32 devices in a mesh: dp: 8 (over z, x), mp: 4 (over y, core).
Axes of the slice: x: 2, y: 2, z: 4, core: 2. Of those that a mesh axis runs over, the one named last changes fastest.
Arguments:
- tokens: bfloat16 [16384, 768], P('dp', 'mp'), may hold values from -6 to 6
- doc_ids: int32 [16, 1024], P('dp'), may hold values from 0 to 7, never falling along the last dimension, each value on 1 to 384 neighbouring positions
- positions_table: bfloat16 [1024, 768], replicated, may hold values from -3 to 3
- norm_gain: bfloat16 [2, 2, 768], replicated, may hold values from 0.5 to 1.5
- norm_shift: bfloat16 [2, 2, 768], replicated, may hold values from -1.5 to 1.5
- joined_projection_weight: bfloat16 [2, 768, 3, 768], P(None, None, None, 'mp'), may hold values from -0.21875 to 0.21875
- qv_bias: bfloat16 [2, 2, 768], P(None, None, 'mp'), may hold values from -1.5 to 1.5
- w_out: bfloat16 [2, 768, 768], P(None, 'mp'), may hold values from -0.625 to 0.625
- out_bias: bfloat16 [2, 2, 768], replicated, may hold values from -1.5 to 1.5
- w_fc: bfloat16 [2, 768, 3072], P(None, None, 'mp'), may hold values from -0.21875 to 0.21875
- fc_bias: bfloat16 [2, 3072], P(None, 'mp'), may hold values from -1.5 to 1.5
- w_proj: bfloat16 [2, 3072, 768], P(None, 'mp'), may hold values from -0.109375 to 0.109375
- cotangent: bfloat16 [16384, 768], P('dp', 'mp'), may hold values from -6 to 6
Outputs:
- out: bfloat16 [16384, 768], P('dp', 'mp')
- grad_tokens: float32 [16384, 768], P('dp', 'mp')
- grad_positions: float32 [1024, 768], P('dp', 'mp')
- grad_norm_gain: float32 [2, 2, 768], P(None, None, 'dp')
- grad_norm_shift: float32 [2, 2, 768], P(None, None, 'dp')
- joined_projection_gradient: float32 [2, 768, 3, 768], P(None, 'dp', None, 'mp')
- grad_qv_bias: float32 [2, 2, 768], P(None, None, ('mp', 'dp'))
- grad_w_out: float32 [2, 768, 768], P(None, 'mp', 'dp')
- grad_out_bias: float32 [2, 2, 768], P(None, None, 'dp')
- grad_w_fc: float32 [2, 768, 3072], P(None, 'dp', 'mp')
- grad_fc_bias: float32 [2, 3072], P(None, ('mp', 'dp'))
- grad_w_proj: float32 [2, 3072, 768], P(None, 'mp', 'dp')
The draws below stay inside these ranges and needn't reach their ends.
Inputs may be any that keep to these rules, and one draw needn't show every extreme that they name: Along each packed row doc_ids never falls; every document has 1 to 384 tokens, and some document has exactly 384.
All inputs are finite; a program needn't handle non-finite values.
Results may differ from the reference program's by a relative error of at most 0.024.
Values may be sent and summed in bfloat16 or wider, within the bound.
No kernel may reach another device: no remote copies, remote signals or barrier semaphores. Data moves between devices by JAX's collectives and lax.ppermute only.
A program may use at most 256 MiB of HBM per device.

```python
import math
import jax
import jax.numpy as jnp
import numpy as np
from jax import lax

D = 768
HEADS = 12
HD = 64
FF = 3072
LEN = 1024
DOCS = 8
DOC_MOST = 384
SEQS = 16
TOKENS = 16384
N_MP = 4


def shard_levels(own_key, dims, split, smallest, high):
    loudness, own = 1.0, jax.random.fold_in(own_key, 6)
    for position, shards_of in split:
        steps = jnp.exp(jax.random.uniform(jax.random.fold_in(own, position), (shards_of,), jnp.float32, smallest / len(split), high / len(split)))
        loudness = loudness * jnp.repeat(steps, dims[position] // shards_of).reshape([-1 if axis == position else 1 for axis in range(len(dims))])
    return loudness


def length_profile(number_of, total, limit, lean):
    weights = [(1 << 20) // math.isqrt(grade ** lean) + 1 for grade in range(2, number_of + 1)]
    rest, holding = total - limit - (number_of - 1), [1] * (number_of - 1)
    while rest > 0:
        free = [i for i in range(number_of - 1) if holding[i] < limit]
        mass, left = sum([weights[i] for i in free]), rest
        for i in free:
            addition = min(limit - holding[i], max(1, left * weights[i] // mass), rest)
            holding[i] = holding[i] + addition
            rest = rest - addition
    return np.array([limit] + holding)


def uneven(own_key, count, total, limit, skew):
    if count == 2:
        one = jax.random.randint(own_key, (), max(1, total - limit), min(limit, total - 1) + 1)
        return jnp.stack([one, total - one])
    sizes = jnp.asarray(length_profile(count, total, limit, skew), jnp.int32)
    pairs = (count - 1) // 2
    donor, taker = sizes[1:1 + 2 * pairs:2], sizes[2:2 + 2 * pairs:2]
    room = jnp.minimum(donor - 1, limit - taker)
    moved = jax.random.randint(jax.random.fold_in(own_key, 1), (pairs,), 0, 1 << 20) % (room + 1)
    sizes = sizes.at[1:1 + 2 * pairs:2].set(donor - moved).at[2:2 + 2 * pairs:2].set(taker + moved)
    return sizes[jax.random.permutation(jax.random.fold_in(own_key, 2), count)]


def bell_draw(rng, dims, spread, most, split=(), held_as=jnp.bfloat16):
    values = spread * jax.random.normal(rng, dims, jnp.float32)
    if split:
        values = values * shard_levels(rng, dims, split, -0.22, 0.18)
    return jnp.clip(values, -most, most).astype(held_as)


def setup_inputs(seed: int = 0) -> dict:
    streams_of = jax.random.split(jax.random.key(seed), 14)
    tokens = bell_draw(streams_of[0], (TOKENS, D), 1.0, 6.0, ((0, 8), (1, 4)))
    doc_ids = jax.vmap(lambda own: jnp.searchsorted(jnp.cumsum(uneven(own, DOCS, LEN, DOC_MOST, 2)), jnp.arange(LEN), side="right"))(jax.random.split(streams_of[1], SEQS)).reshape((SEQS, LEN)).astype(jnp.int32)
    positions_table = bell_draw(streams_of[2], (LEN, D), 0.5, 3.0)
    norm_gain = jnp.clip(1.0 + 0.1 * jax.random.normal(streams_of[3], (2, 2, D), jnp.float32), 0.5, 1.5).astype(jnp.bfloat16)
    norm_shift = bell_draw(streams_of[4], (2, 2, D), 0.3, 1.5)
    joined_projection_weight = bell_draw(streams_of[5], (2, D, 3, D), D ** -0.5, 0.21875, ((3, 4),))
    qv_bias = bell_draw(streams_of[6], (2, 2, D), 0.3, 1.5, ((2, 4),))
    w_out = bell_draw(streams_of[7], (2, D, D), (D // 8) ** -0.5, 0.625, ((1, 4),))
    out_bias = bell_draw(streams_of[8], (2, 2, D), 0.3, 1.5)
    w_fc = bell_draw(streams_of[9], (2, D, FF), D ** -0.5, 0.21875, ((2, 4),))
    fc_bias = bell_draw(streams_of[10], (2, FF), 0.3, 1.5, ((1, 4),))
    w_proj = bell_draw(streams_of[11], (2, FF, D), FF ** -0.5, 0.109375, ((1, 4),))
    cotangent = bell_draw(streams_of[12], (TOKENS, D), 1.0, 6.0, ((0, 8), (1, 4)))
    return dict(tokens=tokens, doc_ids=doc_ids, positions_table=positions_table, norm_gain=norm_gain, norm_shift=norm_shift, joined_projection_weight=joined_projection_weight, qv_bias=qv_bias, w_out=w_out, out_bias=out_bias, w_fc=w_fc, fc_bias=fc_bias, w_proj=w_proj, cotangent=cotangent)


@jax.custom_vjp
def low(v):
    return lax.optimization_barrier(v.astype(jnp.bfloat16)).astype(jnp.float32)

@jax.custom_vjp
def low_back(v):
    return v

def low_keep(v):
    return (low(v), None)

def low_pass(kept, grad):
    return (grad,)

def back_keep(v):
    return (v, None)

def back_low(kept, grad):
    return (low(grad),)
low.defvjp(low_keep, low_pass)
low_back.defvjp(back_keep, back_low)
epsilon = 1e-05

def matmul(left, right):
    return jnp.dot(left, right, precision=lax.Precision.HIGHEST, preferred_element_type=jnp.float32)

def layer_norm(stream, gain_row, shift_row):
    centred = stream - lax.optimization_barrier(jnp.mean(stream, axis=-1, keepdims=True))
    variance = lax.optimization_barrier(jnp.mean(centred * centred, axis=-1, keepdims=True))
    return centred * lax.rsqrt(variance + epsilon) * gain_row + shift_row

def doc_positions(doc_ids):
    row_index = jnp.broadcast_to(jnp.arange(doc_ids.shape[1], dtype=jnp.int32), doc_ids.shape)
    previous = jnp.concatenate([doc_ids[:, :1] - 1, doc_ids[:, :-1]], axis=1)
    starts = jnp.where(doc_ids != previous, row_index, 0).astype(jnp.int32)
    return (row_index - lax.cummax(starts, axis=1)).astype(jnp.int32)

def attend_one(pieces):
    queries, key_rows, value_rows, doc_row = pieces
    scale_factor = 1.0 / math.sqrt(HD)
    scores = jnp.einsum('qhd,khd->hqk', queries, key_rows, precision=lax.Precision.HIGHEST) * scale_factor
    scores = low_back(scores)
    row_index = jnp.arange(doc_row.shape[0], dtype=jnp.int32)
    allowed = (doc_row[:, None] == doc_row[None, :]) & (row_index[None, :] <= row_index[:, None])
    scores = jnp.where(allowed[None], scores, -1e+30)
    attn_probs = low(jax.nn.softmax(scores, axis=-1))
    return jnp.einsum('hqk,khd->qhd', attn_probs, value_rows, precision=lax.Precision.HIGHEST)

def grouped_sum(left, right, members):
    group_width = left.shape[1] // members
    running = jnp.zeros((left.shape[0], right.shape[1]), jnp.float32)
    for part_index in range(members):
        lower = part_index * group_width
        running = running + low(matmul(left[:, lower:lower + group_width], right[lower:lower + group_width]))
    return running

def block(stream, doc_ids, gains, shifts, joined_projection_weight, qv_bias, w_out, out_bias, w_fc, fc_bias, w_proj):
    total_token_count = stream.shape[0]
    normalized_input = low(layer_norm(stream, gains[0], shifts[0]))
    mixed_qkv = matmul(normalized_input, joined_projection_weight.reshape(D, 3 * D)).reshape(total_token_count, 3, D)
    queries = low(low_back(mixed_qkv[:, 0] + qv_bias[0]))
    key_rows = low(low_back(mixed_qkv[:, 1]))
    value_rows = low(low_back(mixed_qkv[:, 2] + qv_bias[1]))
    attended = lax.map(jax.checkpoint(attend_one), (queries.reshape(-1, LEN, HEADS, HD), key_rows.reshape(-1, LEN, HEADS, HD), value_rows.reshape(-1, LEN, HEADS, HD), doc_ids))
    attended = low(low_back(attended.reshape(total_token_count, D)))
    middle = stream + low_back(grouped_sum(attended, w_out, N_MP)) + out_bias[0]
    normed2 = low(layer_norm(middle, gains[1], shifts[1]))
    hidden = low_back(matmul(normed2, w_fc) + fc_bias)
    activated = low(jax.nn.gelu(hidden, approximate=True))
    return middle + low_back(grouped_sum(activated, w_proj, N_MP)) + out_bias[1]

def forward(tokens, table, gains, shifts, joined_projection_weight, qv_bias, w_out, out_bias, w_fc, fc_bias, w_proj, doc_ids):
    places = doc_positions(doc_ids).reshape(-1)
    stream = tokens + table[places]
    for layer_index in range(2):
        stream = block(stream, doc_ids, gains[layer_index], shifts[layer_index], joined_projection_weight[layer_index], qv_bias[layer_index], w_out[layer_index], out_bias[layer_index], w_fc[layer_index], fc_bias[layer_index], w_proj[layer_index])
    return stream

def reference(tokens, doc_ids, positions_table, norm_gain, norm_shift, joined_projection_weight, qv_bias, w_out, out_bias, w_fc, fc_bias, w_proj, cotangent):
    floats = tuple((item.astype(jnp.float32) for item in (tokens, positions_table, norm_gain, norm_shift, joined_projection_weight, qv_bias, w_out, out_bias, w_fc, fc_bias, w_proj)))

    def wrapped(*inputs):
        return forward(*inputs, doc_ids)
    result, pullback = jax.vjp(wrapped, *floats)
    grads = pullback(cotangent.astype(jnp.float32))
    return (result.astype(jnp.bfloat16), grads[0], grads[1], grads[2], grads[3], grads[4], grads[5], grads[6], grads[7], grads[8], grads[9], grads[10])
```

```python
import functools
import math

import jax
import jax.numpy as jnp
from jax import lax
from jax.experimental import pallas as pl
from jax.experimental.pallas import tpu as pltpu
from jax.sharding import PartitionSpec as P

HD = 64
LEN = 1024
DOC_MOST = 384
EPS = 1e-05
BT = 256
QB = 128
KW = QB + DOC_MOST
F32 = jnp.float32
BF16 = jnp.bfloat16
GELU_C = math.sqrt(2.0 / math.pi)


def full_spec(shape):
    return pl.BlockSpec(shape, lambda g: (0,) * len(shape))


def rows_spec(width):
    return pl.BlockSpec((BT, width), lambda g: (g, 0))


def dot(a, b, ca=1, cb=0):
    return lax.dot_general(a, b, (((ca,), (cb,)), ((), ())), preferred_element_type=F32)


def normed_parts(v):
    centred = v - jnp.mean(v, axis=-1, keepdims=True)
    variance = jnp.mean(centred * centred, axis=-1, keepdims=True)
    rstd = lax.rsqrt(variance + EPS)
    return centred * rstd, rstd


def norm_back(g, own, oth, v, gain):
    grad = own.astype(F32) + oth.astype(F32)
    xhat, rstd = normed_parts(v)
    gn = grad * gain
    out = g + rstd * (
        gn
        - jnp.mean(gn, axis=-1, keepdims=True)
        - xhat * jnp.mean(gn * xhat, axis=-1, keepdims=True)
    )
    return out, grad * xhat, grad


def colsum(v):
    return jnp.sum(v, axis=0, keepdims=True)


def head_pair(block):
    lane = lax.broadcasted_iota(jnp.int32, block.shape, 1)
    zero = jnp.zeros_like(block)
    return jnp.concatenate(
        [jnp.where(lane < HD, block, zero), jnp.where(lane < HD, zero, block)], axis=0
    )


def window_bias(start_ref, i, ks):
    kidx = lax.broadcasted_iota(jnp.int32, (KW, QB), 0) + ks
    qidx = lax.broadcasted_iota(jnp.int32, (KW, QB), 1) + i * QB
    first = start_ref[0:1, pl.ds(pl.multiple_of(i * QB, QB), QB)]
    bias = jnp.where((kidx >= first) & (kidx <= qidx), 0.0, -1e30).astype(F32)
    return jnp.concatenate([bias, bias], axis=1)


def attn_fwd_kernel(layer, first, half, *refs):
    if first:
        (tok, emb, start, gain, shift, wqkv, qvb, wout) = refs[:8]
        rest = refs[8:]
        x = tok[...].astype(F32) + emb[...].astype(F32)
    else:
        (mid, own, oth, outb, start, gain, shift, wqkv, qvb, wout) = refs[:10]
        rest = refs[10:]
        x = (
            mid[...]
            + (own[...].astype(F32) + oth[...].astype(F32))
            + outb[layer - 1, 1:2, :].astype(F32)
        )
    x_o, n_o, qkv_o, att_o, lse_o, part_o, v_t, o_t = rest
    g = pl.program_id(0)

    @pl.when(g == 0)
    def _():
        qkv_o[pl.ds(BT, KW - BT), half : 2 * half] = jnp.zeros((KW - BT, half), BF16)
        v_t[:, pl.ds(BT, KW - BT)] = jnp.zeros((half, KW - BT), BF16)
        lse_o[...] = jnp.zeros_like(lse_o)

    x_o[...] = x
    xhat, _ = normed_parts(x)
    normed = (
        xhat * gain[layer, 0:1, :].astype(F32) + shift[layer, 0:1, :].astype(F32)
    ).astype(BF16)
    n_o[...] = normed
    qkv = dot(normed, wqkv[...])
    q = (qkv[:, :half] + qvb[layer, 0:1, :].astype(F32)).astype(BF16)
    k = qkv[:, half : 2 * half].astype(BF16)
    v = qkv[:, 2 * half :] + qvb[layer, 1:2, :].astype(F32)
    rows = pl.ds(pl.multiple_of(g * BT, BT), BT)
    qkv_o[rows, :half] = q
    qkv_o[rows, half : 2 * half] = k
    qkv_o[rows, 2 * half :] = v.astype(BF16)
    v_t[:, rows] = jnp.transpose(v).astype(BF16)
    q = q * jnp.asarray(1.0 / math.sqrt(HD), BF16)
    for s in range(BT // QB):
        i = g * (BT // QB) + s
        ks = pl.multiple_of(jnp.maximum(i - DOC_MOST // QB, 0) * QB, QB)
        bias = window_bias(start, i, ks)
        cols = pl.ds(pl.multiple_of(i * QB, QB), QB)
        for p in range(half // 128):
            lo = 128 * p
            qq = head_pair(q[QB * s : QB * (s + 1), lo : lo + 128])
            kp = qkv_o[pl.ds(ks, KW), half + lo : half + lo + 128]
            scores = dot(kp, qq, 1, 1) + bias
            peak = jnp.max(scores, axis=0, keepdims=True)
            e = jnp.exp(scores - peak)
            total = jnp.sum(e, axis=0, keepdims=True)
            ot = dot(v_t[lo : lo + 128, pl.ds(ks, KW)], e.astype(BF16))
            inv = 1.0 / total
            o_t[lo : lo + HD, :] = ot[:HD, :QB] * inv[:, :QB]
            o_t[lo + HD : lo + 128, :] = ot[HD:, QB:] * inv[:, QB:]
            lse = peak + jnp.log(total)
            lse_o[2 * p : 2 * p + 1, cols] = lse[:, :QB]
            lse_o[2 * p + 1 : 2 * p + 2, cols] = lse[:, QB:]
        att_o[QB * s : QB * (s + 1), :] = jnp.transpose(o_t[...]).astype(BF16)
    part_o[...] = dot(att_o[...], wout[...]).astype(BF16)


def attn_fwd(layer, stream_in, start, gain, shift, wqkv, qvb, wout, outb):
    first = layer == 0
    d = gain.shape[-1]
    half = wqkv.shape[1] // 3
    ins = list(stream_in)
    specs = [rows_spec(d) for _ in ins]
    if not first:
        ins.append(outb)
        specs.append(full_spec(outb.shape))
    for a in (start, gain, shift, wqkv, qvb, wout):
        ins.append(a)
        specs.append(full_spec(a.shape))
    return pl.pallas_call(
        functools.partial(attn_fwd_kernel, layer, first, half),
        grid=(LEN // BT,),
        in_specs=specs,
        out_specs=[
            rows_spec(d),
            rows_spec(d),
            full_spec((LEN, 3 * half)),
            rows_spec(half),
            full_spec((8, LEN)),
            rows_spec(d),
        ],
        out_shape=[
            jax.ShapeDtypeStruct((LEN, d), F32),
            jax.ShapeDtypeStruct((LEN, d), BF16),
            jax.ShapeDtypeStruct((LEN, 3 * half), BF16),
            jax.ShapeDtypeStruct((LEN, half), BF16),
            jax.ShapeDtypeStruct((8, LEN), F32),
            jax.ShapeDtypeStruct((LEN, d), BF16),
        ],
        scratch_shapes=[pltpu.VMEM((half, LEN), BF16), pltpu.VMEM((half, QB), F32)],
        name=f"attn_fwd_{layer}",
    )(*ins)


def mlp_fwd_kernel(layer, x, own, oth, outb, gain, shift, wfc, fcb, wproj, mid_o, n_o, h_o, part_o):
    mid = (
        x[...]
        + (own[...].astype(F32) + oth[...].astype(F32))
        + outb[layer, 0:1, :].astype(F32)
    )
    mid_o[...] = mid
    xhat, _ = normed_parts(mid)
    normed = (
        xhat * gain[layer, 1:2, :].astype(F32) + shift[layer, 1:2, :].astype(F32)
    ).astype(BF16)
    n_o[...] = normed
    hidden = dot(normed, wfc[...]) + fcb[layer : layer + 1, :].astype(F32)
    h_o[...] = hidden.astype(BF16)
    t = jnp.tanh(GELU_C * (hidden + 0.044715 * hidden * hidden * hidden))
    act = (0.5 * hidden * (1.0 + t)).astype(BF16)
    part_o[...] = dot(act, wproj[...]).astype(BF16)


def mlp_fwd(layer, x, own, oth, outb, gain, shift, wfc, fcb, wproj):
    d = x.shape[1]
    f = wfc.shape[1]
    ins = [x, own, oth, outb, gain, shift, wfc, fcb, wproj]
    specs = [rows_spec(d)] * 3 + [full_spec(a.shape) for a in ins[3:]]
    return pl.pallas_call(
        functools.partial(mlp_fwd_kernel, layer),
        grid=(LEN // BT,),
        in_specs=specs,
        out_specs=[rows_spec(d), rows_spec(d), rows_spec(f), rows_spec(d)],
        out_shape=[
            jax.ShapeDtypeStruct((LEN, d), F32),
            jax.ShapeDtypeStruct((LEN, d), BF16),
            jax.ShapeDtypeStruct((LEN, f), BF16),
            jax.ShapeDtypeStruct((LEN, d), BF16),
        ],
        name=f"mlp_fwd_{layer}",
    )(*ins)


def mlp_bwd_kernel(g, h, wfc, wproj, low_o, act_o, gh_o, part_o, sumg_o, sumh_o):
    step = pl.program_id(0)

    @pl.when(step == 0)
    def _():
        sumg_o[...] = jnp.zeros_like(sumg_o)
        sumh_o[...] = jnp.zeros_like(sumh_o)

    grad = g[...].astype(F32)
    low = grad.astype(BF16)
    low_o[...] = low
    grad_act = dot(low, wproj[...], 1, 1)
    v = h[...].astype(F32)
    v2 = v * v
    t = jnp.tanh(GELU_C * v * (1.0 + 0.044715 * v2))
    cdf = 0.5 * (1.0 + t)
    act_o[...] = (v * cdf).astype(BF16)
    slope = cdf + (0.5 * GELU_C) * v * (1.0 - t * t) * (1.0 + (3 * 0.044715) * v2)
    gh = (grad_act * slope).astype(BF16)
    gh_o[...] = gh
    part_o[...] = dot(gh, wfc[...], 1, 1).astype(BF16)
    sumg_o[0:1, :] += colsum(grad)
    sumh_o[0:1, :] += colsum(gh.astype(F32))


def mlp_bwd(layer, g, h, wfc, wproj):
    d, f = wfc.shape
    return pl.pallas_call(
        mlp_bwd_kernel,
        grid=(LEN // BT,),
        in_specs=[rows_spec(d), rows_spec(f), full_spec(wfc.shape), full_spec(wproj.shape)],
        out_specs=[
            rows_spec(d),
            rows_spec(f),
            rows_spec(f),
            rows_spec(d),
            full_spec((8, d)),
            full_spec((8, f)),
        ],
        out_shape=[
            jax.ShapeDtypeStruct((LEN, d), BF16),
            jax.ShapeDtypeStruct((LEN, f), BF16),
            jax.ShapeDtypeStruct((LEN, f), BF16),
            jax.ShapeDtypeStruct((LEN, d), BF16),
            jax.ShapeDtypeStruct((8, d), F32),
            jax.ShapeDtypeStruct((8, f), F32),
        ],
        name=f"mlp_bwd_{layer}",
    )(g, h, wfc, wproj)


def attn_bwd_kernel(layer, half, *refs):
    (g_i, own, oth, mid, qkv, att, lse, start, gain, wout) = refs[:10]
    (gm_o, low_o, dqkv_o, sums_o, qvs_o, k_t, dk, dv, dq_t) = refs[10:]
    g = pl.program_id(0)

    @pl.when(g == 0)
    def _():
        sums_o[...] = jnp.zeros_like(sums_o)
        qvs_o[...] = jnp.zeros_like(qvs_o)
        dk[...] = jnp.zeros_like(dk)
        dv[...] = jnp.zeros_like(dv)
        for b in range(LEN // BT):
            block = qkv[BT * b : BT * (b + 1), half : 2 * half].astype(F32)
            k_t[:, BT * b : BT * (b + 1)] = jnp.transpose(block).astype(BF16)

    gm, g_gain, g_shift = norm_back(
        g_i[...].astype(F32), own[...], oth[...], mid[...], gain[layer, 1:2, :].astype(F32)
    )
    gm_o[...] = gm
    sums_o[0:1, :] += colsum(g_gain)
    sums_o[1:2, :] += colsum(g_shift)
    sums_o[2:3, :] += colsum(gm)
    low = gm.astype(BF16)
    low_o[...] = low
    d_att = dot(low, wout[...], 1, 1).astype(BF16)
    prod = d_att.astype(F32) * att[...].astype(F32)
    head = lax.broadcasted_iota(jnp.int32, (8, half), 1) // HD
    pick = (head == lax.broadcasted_iota(jnp.int32, (8, half), 0)).astype(F32)
    inner = lax.dot_general(
        pick,
        prod,
        (((1,), (1,)), ((), ())),
        preferred_element_type=F32,
        precision=lax.Precision.HIGHEST,
    )
    rows = pl.ds(pl.multiple_of(g * BT, BT), BT)
    q = qkv[rows, :half] * jnp.asarray(1.0 / math.sqrt(HD), BF16)
    for s in range(BT // QB):
        i = g * (BT // QB) + s
        ks = pl.multiple_of(jnp.maximum(i - DOC_MOST // QB, 0) * QB, QB)
        bias = window_bias(start, i, ks)
        cols = pl.ds(pl.multiple_of(i * QB, QB), QB)
        win = pl.ds(ks, KW)
        for p in range(half // 128):
            lo = 128 * p
            qq = head_pair(q[QB * s : QB * (s + 1), lo : lo + 128])
            oo = head_pair(d_att[QB * s : QB * (s + 1), lo : lo + 128])
            kp = qkv[win, half + lo : half + lo + 128]
            vp = qkv[win, 2 * half + lo : 2 * half + lo + 128]
            total = jnp.concatenate(
                [lse[2 * p : 2 * p + 1, cols], lse[2 * p + 1 : 2 * p + 2, cols]], axis=1
            )
            inn = jnp.concatenate(
                [
                    inner[2 * p : 2 * p + 1, QB * s : QB * (s + 1)],
                    inner[2 * p + 1 : 2 * p + 2, QB * s : QB * (s + 1)],
                ],
                axis=1,
            )
            probs = jnp.exp(dot(kp, qq, 1, 1) + bias - total)
            d_probs = dot(vp, oo, 1, 1)
            ds = (probs * (d_probs - inn)).astype(BF16)
            dv[win, lo : lo + 128] += dot(probs.astype(BF16), oo)
            dk[win, lo : lo + 128] += dot(ds, qq)
            dqt = dot(k_t[lo : lo + 128, win], ds)
            dq_t[lo : lo + HD, :] = dqt[:HD, :QB]
            dq_t[lo + HD : lo + 128, :] = dqt[HD:, QB:]
        dq = (jnp.transpose(dq_t[...]) * (1.0 / math.sqrt(HD))).astype(BF16)
        dqkv_o[cols, :half] = dq
        qvs_o[0:1, :] += colsum(dq.astype(F32))

    @pl.when(g == pl.num_programs(0) - 1)
    def _():
        dqkv_o[:, half : 2 * half] = dk[...].astype(BF16)
        dvb = dv[...].astype(BF16)
        dqkv_o[:, 2 * half :] = dvb
        qvs_o[1:2, :] = colsum(dvb.astype(F32))


def attn_bwd(layer, g, own, oth, mid, qkv, att, lse, start, gain, wout):
    d = mid.shape[1]
    half = att.shape[1]
    ins = [g, own, oth, mid, qkv, att, lse, start, gain, wout]
    specs = [rows_spec(d)] * 4 + [full_spec(qkv.shape), rows_spec(half)]
    specs += [full_spec(a.shape) for a in ins[6:]]
    return pl.pallas_call(
        functools.partial(attn_bwd_kernel, layer, half),
        grid=(LEN // BT,),
        in_specs=specs,
        out_specs=[
            rows_spec(d),
            rows_spec(d),
            full_spec((LEN, 3 * half)),
            full_spec((8, d)),
            full_spec((8, half)),
        ],
        out_shape=[
            jax.ShapeDtypeStruct((LEN, d), F32),
            jax.ShapeDtypeStruct((LEN, d), BF16),
            jax.ShapeDtypeStruct((LEN, 3 * half), BF16),
            jax.ShapeDtypeStruct((8, d), F32),
            jax.ShapeDtypeStruct((8, half), F32),
        ],
        scratch_shapes=[
            pltpu.VMEM((half, LEN), BF16),
            pltpu.VMEM((LEN, half), F32),
            pltpu.VMEM((LEN, half), F32),
            pltpu.VMEM((half, QB), F32),
        ],
        name=f"attn_bwd_{layer}",
    )(*ins)


def norm_bwd_kernel(layer, g, own, oth, x, gain, g_o, sums_o):
    @pl.when(pl.program_id(0) == 0)
    def _():
        sums_o[...] = jnp.zeros_like(sums_o)

    out, g_gain, g_shift = norm_back(
        g[...], own[...], oth[...], x[...], gain[layer, 0:1, :].astype(F32)
    )
    g_o[...] = out
    sums_o[0:1, :] += colsum(g_gain)
    sums_o[1:2, :] += colsum(g_shift)


def norm_bwd(layer, g, own, oth, x, gain):
    d = x.shape[1]
    return pl.pallas_call(
        functools.partial(norm_bwd_kernel, layer),
        grid=(LEN // BT,),
        in_specs=[rows_spec(d)] * 4 + [full_spec(gain.shape)],
        out_specs=[rows_spec(d), full_spec((8, d))],
        out_shape=[jax.ShapeDtypeStruct((LEN, d), F32), jax.ShapeDtypeStruct((8, d), F32)],
        name=f"norm_bwd_{layer}",
    )(g, own, oth, x, gain)


def core_swap(a):
    return lax.ppermute(a, "mp", [(i, i ^ 1) for i in range(4)])


def y_swap(a):
    return lax.ppermute(a, "mp", [(i, i ^ 2) for i in range(4)])


def dp_swap(a, bit, n_dp):
    return lax.ppermute(a, "dp", [(i, i ^ (1 << bit)) for i in range(n_dp)])


def pick(flag, zero, one):
    return jnp.where(flag == 0, zero, one)


class Place:
    def __init__(self, n_dp):
        mp = lax.axis_index("mp")
        self.n_dp = n_dp
        self.bits = n_dp.bit_length() - 1
        self.y = mp // 2
        self.c = mp % 2
        self.dp = lax.axis_index("dp")

    def dp_bit(self, b):
        return (self.dp >> b) & 1


def gather_row(a, at):
    rows = a.reshape(2, LEN, a.shape[1])
    mine = pick(at.y, rows[0], rows[1])
    theirs = pick(at.y, rows[1], rows[0])
    far = y_swap(theirs)
    mine_c = core_swap(mine)
    far_c = core_swap(far)

    def joined(here, there):
        return [pick(at.c, here, there), pick(at.c, there, here)]

    near2, far2 = joined(mine, mine_c), joined(far, far_c)
    return jnp.concatenate(
        [pick(at.y, a_, b_) for a_, b_ in zip(near2, far2)]
        + [pick(at.y, b_, a_) for a_, b_ in zip(near2, far2)],
        axis=1,
    )


def own_cols(a, at, other):
    w = a.shape[1] // 4
    halves = (a[:, : 2 * w], a[:, 2 * w :])
    h = pick(at.y, halves[1], halves[0]) if other else pick(at.y, halves[0], halves[1])
    return pick(at.c, h[:, :w], h[:, w:])


def fetch(w, at):
    if at.n_dp == 1:
        return y_swap(w)
    r = w.shape[0] // 2
    b = at.dp_bit(0)
    a1 = y_swap(pick(b, w[:r], w[r:]))
    a2 = dp_swap(a1, 0, at.n_dp)
    return jnp.concatenate([pick(b, a1, a2), pick(b, a2, a1)], axis=0)


def scatter_sum(own, oth, order, at):
    d, width = own.shape
    k = at.bits
    lead = (2,) * k
    a = jnp.stack([own.astype(BF16), oth.astype(BF16)]).reshape(
        (2,) + lead + (d // at.n_dp, width)
    )
    left = ["y"] + [k - 1 - j for j in range(k)]
    order = [o for o in order if o in left] + [o for o in left if o not in order]
    for o in order:
        ax = left.index(o)
        zero = lax.index_in_dim(a, 0, ax, keepdims=False)
        one = lax.index_in_dim(a, 1, ax, keepdims=False)
        if o == "y":
            got = y_swap(one)
            keep = zero
        else:
            b = at.dp_bit(o)
            got = dp_swap(pick(b, one, zero), o, at.n_dp)
            keep = pick(b, zero, one)
        left.pop(ax)
        a = keep.astype(F32) + got.astype(F32)
        if left:
            a = a.astype(BF16)
    return a


def table_scatter(t, at, rows_all):
    a = t[0] + y_swap(t[1].astype(BF16)).astype(F32)
    if at.n_dp == 1:
        return jnp.pad(a, ((0, rows_all - a.shape[0]), (0, 0)))
    top = at.bits - 1
    half = rows_all // 2
    hi = [(i, i ^ (1 << top)) for i in range(at.n_dp) if i >> top & 1]
    a = a + lax.ppermute(a.astype(BF16), "dp", hi).astype(F32)
    a = pick(at.dp_bit(top), a, jnp.zeros_like(a))
    a = jnp.pad(a, ((0, half - a.shape[0]), (0, 0)))
    for b in range(top - 1, -1, -1):
        r = a.shape[0] // 2
        f = at.dp_bit(b)
        got = dp_swap(pick(f, a[r:], a[:r]).astype(BF16), b, at.n_dp)
        a = pick(f, a[:r], a[r:]) + got.astype(F32)
    return a


def small_scatter(shared, own, oth, at):
    n = at.n_dp
    got = y_swap(jnp.concatenate([shared, oth], axis=0))
    a = jnp.concatenate([shared, own], axis=0) + got
    r, d = a.shape
    a = a.reshape(r, n, d // n).transpose(1, 0, 2)
    for b in range(at.bits - 1, -1, -1):
        h = a.shape[0] // 2
        f = at.dp_bit(b)
        a = pick(f, a[:h], a[h:]) + dp_swap(pick(f, a[h:], a[:h]), b, n)
    return a[0]


def doc_positions(doc_ids):
    row_index = jnp.broadcast_to(jnp.arange(doc_ids.shape[1], dtype=jnp.int32), doc_ids.shape)
    previous = jnp.concatenate([doc_ids[:, :1] - 1, doc_ids[:, :-1]], axis=1)
    starts = jnp.where(doc_ids != previous, row_index, 0)
    return lax.cummax(starts, axis=1)


def tok_dot(a, b):
    return lax.dot_general(a, b, (((0,), (0,)), ((), ())), preferred_element_type=F32).astype(BF16)


def on_device(
    n_dp,
    tokens,
    doc_ids,
    positions_table,
    norm_gain,
    norm_shift,
    joined_projection_weight,
    qv_bias,
    w_out,
    out_bias,
    w_fc,
    fc_bias,
    w_proj,
    cotangent,
):
    at = Place(n_dp)
    d = positions_table.shape[1]
    share = joined_projection_weight.shape[-1]
    layers = w_fc.shape[0]

    starts = doc_positions(doc_ids)
    start = pick(at.y, starts[0:1], starts[1:2])
    place = jnp.arange(LEN, dtype=jnp.int32) - start[0]
    hot = (place[:, None] == jnp.arange(DOC_MOST, dtype=jnp.int32)[None, :]).astype(BF16)
    embedded = lax.dot_general(
        hot, positions_table[:DOC_MOST], (((1,), (0,)), ((), ())), preferred_element_type=F32
    ).astype(BF16)
    full_tokens = gather_row(tokens, at)

    small = jnp.concatenate([qv_bias.reshape(-1), fc_bias.reshape(-1)])
    small_o = y_swap(small)
    nq = qv_bias.size
    qvb = jnp.concatenate([qv_bias, small_o[:nq].reshape(qv_bias.shape)], axis=-1)
    fcb = jnp.concatenate([fc_bias, small_o[nq:].reshape(fc_bias.shape)], axis=-1)

    wqkv, wout, wfc, wproj = [], [], [], []
    for l in range(layers):
        own = joined_projection_weight[l]
        flat = own.reshape(d, 3 * share)
        oth = fetch(flat, at).reshape(own.shape)
        wqkv.append(jnp.concatenate([own, oth], axis=-1).reshape(d, 6 * share))
        wout.append(jnp.concatenate([w_out[l], fetch(w_out[l], at)], axis=0))
        wfc.append(jnp.concatenate([w_fc[l], fetch(w_fc[l], at)], axis=1))
        wproj.append(jnp.concatenate([w_proj[l], fetch(w_proj[l], at)], axis=0))

    kept = []
    stream_in = (full_tokens, embedded)
    for l in range(layers):
        x, normed, qkv, att, lse, part = attn_fwd(
            l, stream_in, start, norm_gain, norm_shift, wqkv[l], qvb, wout[l], out_bias
        )
        mid, normed2, hidden, part2 = mlp_fwd(
            l, x, part, core_swap(part), out_bias, norm_gain, norm_shift, wfc[l], fcb, wproj[l]
        )
        stream_in = (mid, part2, core_swap(part2))
        kept.append((x, normed, qkv, att, lse, mid, normed2, hidden))

    result = (
        stream_in[0]
        + (stream_in[1].astype(F32) + stream_in[2].astype(F32))
        + out_bias[layers - 1, 1].astype(F32)
    ).astype(BF16)
    out_far = y_swap(own_cols(result, at, True))
    out_near = own_cols(result, at, False)
    out = jnp.concatenate([pick(at.y, out_near, out_far), pick(at.y, out_far, out_near)], axis=0)

    g = gather_row(cotangent, at)
    grads = [None] * layers
    for l in range(layers - 1, -1, -1):
        x, normed, qkv, att, lse, mid, normed2, hidden = kept[l]
        g_low, act, g_hid, part, sum_g, sum_h = mlp_bwd(l, g, hidden, wfc[l], wproj[l])
        far = core_swap(part)
        d_fc = tok_dot(normed2, g_hid)
        d_proj = tok_dot(g_low, act)
        gm, m_low, dqkv, sums2, qvs = attn_bwd(
            l, g, part, far, mid, qkv, att, lse, start, norm_gain, wout[l]
        )
        part = lax.dot_general(
            dqkv, wqkv[l], (((1,), (1,)), ((), ())), preferred_element_type=F32
        ).astype(BF16)
        far = core_swap(part)
        d_out = tok_dot(m_low, att)
        d_qkv = tok_dot(normed, dqkv)
        g, sums1 = norm_bwd(l, gm, part, far, x, norm_gain)
        f = w_fc.shape[-1]
        q6 = d_qkv.reshape(d, 3, 2, share)
        ao_own = jnp.concatenate([q6[:, j, 0] for j in range(3)] + [d_out[:, :share]], axis=1)
        ao_oth = jnp.concatenate([q6[:, j, 1] for j in range(3)] + [d_out[:, share:]], axis=1)
        r_fc = scatter_sum(d_fc[:, :f], d_fc[:, f:], ["y", 0, 1, 2], at)
        r_proj = scatter_sum(d_proj[:, :f], d_proj[:, f:], [0, 1, "y", 2], at)
        r_ao = scatter_sum(ao_own, ao_oth, [1, "y", 0, 2], at)
        grads[l] = (r_fc, r_proj, r_ao, sums1, sums2, sum_g, sum_h, qvs)

    near = own_cols(g, at, False)
    far_send = own_cols(g, at, True).astype(BF16)
    far = y_swap(far_send).astype(F32)
    grad_tokens = jnp.concatenate([pick(at.y, near, far), pick(at.y, far, near)], axis=0)
    table = lax.dot_general(
        hot,
        jnp.concatenate([near.astype(BF16), far_send], axis=1),
        (((0,), (0,)), ((), ())),
        preferred_element_type=F32,
    )
    grad_positions = table_scatter(
        jnp.stack([table[:, :share], table[:, share:]]), at, positions_table.shape[0]
    )

    def qv_row(qvs, lo):
        parts = jnp.stack([q[j, lo : lo + share] for q in qvs for j in range(2)])
        return parts.reshape(-1, n_dp, share // n_dp).transpose(1, 0, 2).reshape(1, d)

    f = w_fc.shape[-1]
    shared = jnp.stack(
        [grads[l][3][0] if w == 0 else grads[l][4][0] for l in range(layers) for w in range(2)]
        + [grads[l][3][1] if w == 0 else grads[l][4][1] for l in range(layers) for w in range(2)]
        + [grads[l][4][2] if w == 0 else grads[l][5][0] for l in range(layers) for w in range(2)]
    )
    qvs = [grads[l][7] for l in range(layers)]
    own = jnp.concatenate([jnp.stack([grads[l][6][0, :f] for l in range(layers)]), qv_row(qvs, 0)])
    oth = jnp.concatenate(
        [jnp.stack([grads[l][6][0, f:] for l in range(layers)]), qv_row(qvs, share)]
    )
    s = small_scatter(shared, own, oth, at)
    w = d // n_dp
    ao = jnp.stack([grads[l][2] for l in range(layers)])
    return (
        out,
        grad_tokens,
        grad_positions,
        s[0:4].reshape(2, 2, w),
        s[4:8].reshape(2, 2, w),
        ao[..., : 3 * share].reshape(layers, w, 3, share),
        s[14].reshape(2, 2, w // 4),
        jnp.swapaxes(ao[..., 3 * share :], 1, 2),
        s[8:12].reshape(2, 2, w),
        jnp.stack([grads[l][0] for l in range(layers)]),
        s[12:14],
        jnp.stack([grads[l][1].T for l in range(layers)]),
    )


def solution(mesh):
    n_dp = mesh.shape["dp"]
    in_specs = (
        P("dp", "mp"),
        P("dp", None),
        P(),
        P(),
        P(),
        P(None, None, None, "mp"),
        P(None, None, "mp"),
        P(None, "mp", None),
        P(),
        P(None, None, "mp"),
        P(None, "mp"),
        P(None, "mp", None),
        P("dp", "mp"),
    )
    out_specs = (
        P("dp", "mp"),
        P("dp", "mp"),
        P("dp", "mp"),
        P(None, None, "dp"),
        P(None, None, "dp"),
        P(None, "dp", None, "mp"),
        P(None, None, ("mp", "dp")),
        P(None, "mp", "dp"),
        P(None, None, "dp"),
        P(None, "dp", "mp"),
        P(None, ("mp", "dp")),
        P(None, "mp", "dp"),
    )
    return jax.shard_map(
        functools.partial(on_device, n_dp),
        mesh=mesh,
        in_specs=in_specs,
        out_specs=out_specs,
        check_vma=False,
    )
```

```python
import functools
import math

import jax
import jax.numpy as jnp
from jax import lax
from jax.experimental import pallas as pl
from jax.experimental.pallas import tpu as pltpu
from jax.sharding import PartitionSpec as P

HD = 64
LEN = 1024
DOC_MOST = 384
EPS = 1e-05
BT = 256
QB = 128
KW = QB + DOC_MOST
F32 = jnp.float32
BF16 = jnp.bfloat16
GELU_C = math.sqrt(2.0 / math.pi)


ANY = pl.BlockSpec(memory_space=pl.ANY)
SMEM = pl.BlockSpec(memory_space=pltpu.SMEM)


def cost(us):
    return pl.CostEstimate(flops=int(us * 1.15e9), transcendentals=0, bytes_accessed=0)


def full_spec(shape):
    return pl.BlockSpec(shape, lambda g: (0,) * len(shape))


def rows_spec(width):
    return pl.BlockSpec((BT, width), lambda g: (g, 0))


def dot(a, b, ca=1, cb=0):
    return lax.dot_general(a, b, (((ca,), (cb,)), ((), ())), preferred_element_type=F32)


def normed_parts(v):
    centred = v - jnp.mean(v, axis=-1, keepdims=True)
    variance = jnp.mean(centred * centred, axis=-1, keepdims=True)
    rstd = lax.rsqrt(variance + EPS)
    return centred * rstd, rstd


def norm_back(g, own, oth, v, gain):
    grad = own.astype(F32) + oth.astype(F32)
    xhat, rstd = normed_parts(v)
    gn = grad * gain
    out = g + rstd * (
        gn
        - jnp.mean(gn, axis=-1, keepdims=True)
        - xhat * jnp.mean(gn * xhat, axis=-1, keepdims=True)
    )
    return out, grad * xhat, grad


def colsum(v):
    return jnp.sum(v, axis=0, keepdims=True)


def head_pair(block):
    lane = lax.broadcasted_iota(jnp.int32, block.shape, 1)
    zero = jnp.zeros_like(block)
    return jnp.concatenate(
        [jnp.where(lane < HD, block, zero), jnp.where(lane < HD, zero, block)], axis=0
    )


def window_bias(start_ref, i, ks):
    kidx = lax.broadcasted_iota(jnp.int32, (KW, QB), 0) + ks
    qidx = lax.broadcasted_iota(jnp.int32, (KW, QB), 1) + i * QB
    first = start_ref[0:1, pl.ds(pl.multiple_of(i * QB, QB), QB)]
    bias = jnp.where((kidx >= first) & (kidx <= qidx), 0.0, -1e30).astype(F32)
    return jnp.concatenate([bias, bias], axis=1)


def copies(pairs, sems):
    out = [pltpu.make_async_copy(a, b, sems.at[j]) for j, (a, b) in enumerate(pairs)]
    for c in out:
        c.start()
    return out


def join_pieces(flag, plan, refs, dst, cols=slice(None)):
    r = dst.shape[0] // 2
    out = []
    for (lo, n, other, off), ref in zip(plan, refs):
        row = (1 - flag if other else flag) * r + off
        out.append((ref.at[pl.ds(lo, n)], dst.at[pl.ds(pl.multiple_of(row, 8), n), cols]))
    return out


def gelu_parts(v):
    v2 = v * v
    t = jnp.tanh(GELU_C * v * (1.0 + 0.044715 * v2))
    cdf = 0.5 * (1.0 + t)
    slope = cdf + (0.5 * GELU_C) * v * (1.0 - t * t) * (1.0 + (3 * 0.044715) * v2)
    return v * cdf, slope


def gained(xhat, gain, shift, layer, which):
    row = slice(which, which + 1)
    return (xhat * gain[layer, row, :].astype(F32) + shift[layer, row, :].astype(F32)).astype(BF16)


def attn_fwd_kernel(layer, first, half, plan, *refs):
    if first:
        (tok, emb, flag, start, gain, shift, qvb, a_own) = refs[:8]
        rest = refs[8:]
        x = tok[...].astype(F32) + emb[...].astype(F32)
    else:
        (mid, own, oth, outb, flag, start, gain, shift, qvb, a_own) = refs[:10]
        rest = refs[10:]
        x = (
            mid[...]
            + (own[...].astype(F32) + oth[...].astype(F32))
            + outb[layer - 1, 1:2, :].astype(F32)
        )
    a_refs, rest = rest[: len(plan)], rest[len(plan) :]
    x_o, n_o, qkv_o, att_o, lse_o, part_o, w_o, v_t, o_t, a_buf, sems = rest
    g = pl.program_id(0)
    sh = half // 2

    @pl.when(g == 0)
    def _():
        moves = copies(
            [(a_own, a_buf.at[0])] + join_pieces(flag[0], plan, a_refs, a_buf.at[1]), sems
        )
        qkv_o[pl.ds(BT, KW - BT), half : 2 * half] = jnp.zeros((KW - BT, half), BF16)
        v_t[:, pl.ds(BT, KW - BT)] = jnp.zeros((half, KW - BT), BF16)
        lse_o[...] = jnp.zeros_like(lse_o)
        for m in moves:
            m.wait()
        for j in range(4):
            for s in range(2):
                w_o[:, (2 * j + s) * sh : (2 * j + s + 1) * sh] = a_buf[s, :, j * sh : (j + 1) * sh]

    x_o[...] = x
    xhat, _ = normed_parts(x)
    normed = gained(xhat, gain, shift, layer, 0)
    n_o[...] = normed
    qkv = dot(normed, w_o[:, : 3 * half])
    q = (qkv[:, :half] + qvb[layer, 0:1, :].astype(F32)).astype(BF16)
    k = qkv[:, half : 2 * half].astype(BF16)
    v = qkv[:, 2 * half :] + qvb[layer, 1:2, :].astype(F32)
    rows = pl.ds(pl.multiple_of(g * BT, BT), BT)
    qkv_o[rows, :half] = q
    qkv_o[rows, half : 2 * half] = k
    qkv_o[rows, 2 * half :] = v.astype(BF16)
    v_t[:, rows] = jnp.transpose(v).astype(BF16)
    q = q * jnp.asarray(1.0 / math.sqrt(HD), BF16)
    for s in range(BT // QB):
        i = g * (BT // QB) + s
        ks = pl.multiple_of(jnp.maximum(i - DOC_MOST // QB, 0) * QB, QB)
        bias = window_bias(start, i, ks)
        cols = pl.ds(pl.multiple_of(i * QB, QB), QB)
        for p in range(half // 128):
            lo = 128 * p
            qq = head_pair(q[QB * s : QB * (s + 1), lo : lo + 128])
            kp = qkv_o[pl.ds(ks, KW), half + lo : half + lo + 128]
            scores = dot(kp, qq, 1, 1) + bias
            peak = jnp.max(scores, axis=0, keepdims=True)
            e = jnp.exp(scores - peak)
            total = jnp.sum(e, axis=0, keepdims=True)
            ot = dot(v_t[lo : lo + 128, pl.ds(ks, KW)], e.astype(BF16))
            inv = 1.0 / total
            o_t[lo : lo + HD, :] = ot[:HD, :QB] * inv[:, :QB]
            o_t[lo + HD : lo + 128, :] = ot[HD:, QB:] * inv[:, QB:]
            lse = peak + jnp.log(total)
            lse_o[2 * p : 2 * p + 1, cols] = lse[:, :QB]
            lse_o[2 * p + 1 : 2 * p + 2, cols] = lse[:, QB:]
        att_o[QB * s : QB * (s + 1), :] = jnp.transpose(o_t[...]).astype(BF16)
    part_o[...] = dot(att_o[...], w_o[:, 3 * half :], 1, 1).astype(BF16)


def attn_fwd(layer, stream_in, outb, flag, start, gain, shift, qvb, a_own, a_oth):
    first = layer == 0
    d = gain.shape[-1]
    half = a_own.shape[1] // 2
    ins = list(stream_in)
    specs = [rows_spec(d) for _ in ins]
    if not first:
        ins.append(outb)
        specs.append(full_spec(outb.shape))
    plan, arrays = a_oth
    ins += [flag, start, gain, shift, qvb, a_own, *arrays]
    specs += [SMEM] + [full_spec(a.shape) for a in (start, gain, shift, qvb)]
    specs += [ANY] * (1 + len(arrays))
    return pl.pallas_call(
        functools.partial(attn_fwd_kernel, layer, first, half, plan),
        grid=(LEN // BT,),
        in_specs=specs,
        out_specs=[
            rows_spec(d),
            rows_spec(d),
            full_spec((LEN, 3 * half)),
            rows_spec(half),
            full_spec((8, LEN)),
            rows_spec(d),
            full_spec((d, 4 * half)),
        ],
        out_shape=[
            jax.ShapeDtypeStruct((LEN, d), F32),
            jax.ShapeDtypeStruct((LEN, d), BF16),
            jax.ShapeDtypeStruct((LEN, 3 * half), BF16),
            jax.ShapeDtypeStruct((LEN, half), BF16),
            jax.ShapeDtypeStruct((8, LEN), F32),
            jax.ShapeDtypeStruct((LEN, d), BF16),
            jax.ShapeDtypeStruct((d, 4 * half), BF16),
        ],
        scratch_shapes=[
            pltpu.VMEM((half, LEN), BF16),
            pltpu.VMEM((half, QB), F32),
            pltpu.VMEM((2, d, 2 * half), BF16),
            pltpu.SemaphoreType.DMA((1 + len(plan),)),
        ],
        name=f"attn_fwd_{layer}",
        cost_estimate=cost(22),
    )(*ins)


def load_mlp(layer, flag, plans, weights, wfc, wproj, sems):
    d = wfc.shape[0]
    f = wfc.shape[1] // 2
    n = len(plans[0])
    return copies(
        [(weights[0].at[layer], wfc.at[:, pl.ds(0, f)])]
        + join_pieces(flag[0], plans[0], weights[2 : 2 + n], wfc, pl.ds(f, f))
        + [(weights[1].at[layer], wproj.at[pl.ds(0, f)])]
        + join_pieces(flag[0], plans[1], weights[2 + n :], wproj.at[pl.ds(f, f)]),
        sems,
    )


def mlp_scratch(d, f2, plans):
    return [
        pltpu.VMEM((d, f2), BF16),
        pltpu.VMEM((f2, d), BF16),
        pltpu.SemaphoreType.DMA((2 + len(plans[0]) + len(plans[1]),)),
    ]


def mlp_weights(weights):
    w_fc, fc_oth, w_proj, pj_oth = weights
    return (fc_oth[0], pj_oth[0]), [w_fc, w_proj, *fc_oth[1], *pj_oth[1]]


def mlp_fwd_kernel(layer, plans, x, own, oth, outb, gain, shift, fcb, flag, *refs):
    nw = 2 + len(plans[0]) + len(plans[1])
    weights = refs[:nw]
    mid_o, n_o, h_o, part_o, wfc, wproj, sems = refs[nw:]

    @pl.when(pl.program_id(0) == 0)
    def _():
        for m in load_mlp(layer, flag, plans, weights, wfc, wproj, sems):
            m.wait()

    mid = (
        x[...]
        + (own[...].astype(F32) + oth[...].astype(F32))
        + outb[layer, 0:1, :].astype(F32)
    )
    mid_o[...] = mid
    xhat, _ = normed_parts(mid)
    normed = gained(xhat, gain, shift, layer, 1)
    n_o[...] = normed
    hidden = dot(normed, wfc[...]) + fcb[layer : layer + 1, :].astype(F32)
    h_o[...] = hidden.astype(BF16)
    t = jnp.tanh(GELU_C * hidden * (1.0 + 0.044715 * hidden * hidden))
    act = (0.5 * hidden * (1.0 + t)).astype(BF16)
    part_o[...] = dot(act, wproj[...]).astype(BF16)


def mlp_fwd(layer, x, own, oth, outb, gain, shift, fcb, flag, weights):
    d = x.shape[1]
    f = fcb.shape[1]
    plans, arrays = mlp_weights(weights)
    ins = [x, own, oth, outb, gain, shift, fcb, flag, *arrays]
    specs = [rows_spec(d)] * 3 + [full_spec(a.shape) for a in ins[3:7]] + [SMEM] + [ANY] * len(arrays)
    return pl.pallas_call(
        functools.partial(mlp_fwd_kernel, layer, plans),
        grid=(LEN // BT,),
        in_specs=specs,
        out_specs=[rows_spec(d), rows_spec(d), rows_spec(f), rows_spec(d)],
        out_shape=[
            jax.ShapeDtypeStruct((LEN, d), F32),
            jax.ShapeDtypeStruct((LEN, d), BF16),
            jax.ShapeDtypeStruct((LEN, f), BF16),
            jax.ShapeDtypeStruct((LEN, d), BF16),
        ],
        scratch_shapes=mlp_scratch(d, f, plans),
        name=f"mlp_fwd_{layer}",
        cost_estimate=cost(12),
    )(*ins)


def mlp_both_kernel(layer, plans, x, own, oth, cot, outb, gain, shift, fcb, flag, *refs):
    nw = 2 + len(plans[0]) + len(plans[1])
    weights = refs[:nw]
    mid_o, n_o, act_o, gh_o, out_o, part_o, sumg_o, sumh_o, wfc, wproj, sems = refs[nw:]

    @pl.when(pl.program_id(0) == 0)
    def _():
        moves = load_mlp(layer, flag, plans, weights, wfc, wproj, sems)
        sumg_o[...] = jnp.zeros_like(sumg_o)
        sumh_o[...] = jnp.zeros_like(sumh_o)
        for m in moves:
            m.wait()

    mid = (
        x[...]
        + (own[...].astype(F32) + oth[...].astype(F32))
        + outb[layer, 0:1, :].astype(F32)
    )
    mid_o[...] = mid
    xhat, _ = normed_parts(mid)
    normed = gained(xhat, gain, shift, layer, 1)
    n_o[...] = normed
    grad_act = dot(cot[...], wproj[...], 1, 1)
    value, slope = gelu_parts(dot(normed, wfc[...]) + fcb[layer : layer + 1, :].astype(F32))
    act = value.astype(BF16)
    act_o[...] = act
    gh = (grad_act * slope).astype(BF16)
    gh_o[...] = gh
    part_o[...] = dot(gh, wfc[...], 1, 1).astype(BF16)
    out_o[...] = dot(act, wproj[...]).astype(BF16)
    sumg_o[0:1, :] += colsum(cot[...].astype(F32))
    sumh_o[0:1, :] += colsum(gh.astype(F32))


def mlp_both(layer, x, own, oth, cot, outb, gain, shift, fcb, flag, weights):
    d = x.shape[1]
    f = fcb.shape[1]
    plans, arrays = mlp_weights(weights)
    ins = [x, own, oth, cot, outb, gain, shift, fcb, flag, *arrays]
    specs = [rows_spec(d)] * 4 + [full_spec(a.shape) for a in ins[4:8]] + [SMEM] + [ANY] * len(arrays)
    widths = [d, d, f, f, d, d]
    kinds = [F32, BF16, BF16, BF16, BF16, BF16]
    return pl.pallas_call(
        functools.partial(mlp_both_kernel, layer, plans),
        grid=(LEN // BT,),
        in_specs=specs,
        out_specs=[rows_spec(w) for w in widths] + [full_spec((8, d)), full_spec((8, f))],
        out_shape=[jax.ShapeDtypeStruct((LEN, w), k) for w, k in zip(widths, kinds)]
        + [jax.ShapeDtypeStruct((8, d), F32), jax.ShapeDtypeStruct((8, f), F32)],
        scratch_shapes=mlp_scratch(d, f, plans),
        name=f"mlp_both_{layer}",
        cost_estimate=cost(18),
    )(*ins)


def mlp_bwd_kernel(layer, plans, gm, own, oth, x, h, gain, flag, *refs):
    nw = 2 + len(plans[0]) + len(plans[1])
    weights = refs[:nw]
    g_o, low_o, act_o, gh_o, part_o, sums_o, sumh_o, wfc, wproj, sems = refs[nw:]

    @pl.when(pl.program_id(0) == 0)
    def _():
        moves = load_mlp(layer, flag, plans, weights, wfc, wproj, sems)
        sums_o[...] = jnp.zeros_like(sums_o)
        sumh_o[...] = jnp.zeros_like(sumh_o)
        for m in moves:
            m.wait()

    grad, g_gain, g_shift = norm_back(
        gm[...], own[...], oth[...], x[...], gain[layer + 1, 0:1, :].astype(F32)
    )
    sums_o[0:1, :] += colsum(g_gain)
    sums_o[1:2, :] += colsum(g_shift)
    sums_o[2:3, :] += colsum(grad)
    g_o[...] = grad
    low = grad.astype(BF16)
    low_o[...] = low
    grad_act = dot(low, wproj[...], 1, 1)
    value, slope = gelu_parts(h[...].astype(F32))
    act_o[...] = value.astype(BF16)
    gh = (grad_act * slope).astype(BF16)
    gh_o[...] = gh
    part_o[...] = dot(gh, wfc[...], 1, 1).astype(BF16)
    sumh_o[0:1, :] += colsum(gh.astype(F32))


def mlp_bwd(layer, gm, own, oth, x, h, gain, flag, weights):
    d = x.shape[1]
    f = h.shape[1]
    plans, arrays = mlp_weights(weights)
    ins = [gm, own, oth, x, h, gain, flag, *arrays]
    specs = [rows_spec(d)] * 4 + [rows_spec(f), full_spec(gain.shape), SMEM] + [ANY] * len(arrays)
    widths = [d, d, f, f, d]
    kinds = [F32, BF16, BF16, BF16, BF16]
    return pl.pallas_call(
        functools.partial(mlp_bwd_kernel, layer, plans),
        grid=(LEN // BT,),
        in_specs=specs,
        out_specs=[rows_spec(w) for w in widths] + [full_spec((8, d)), full_spec((8, f))],
        out_shape=[jax.ShapeDtypeStruct((LEN, w), k) for w, k in zip(widths, kinds)]
        + [jax.ShapeDtypeStruct((8, d), F32), jax.ShapeDtypeStruct((8, f), F32)],
        scratch_shapes=mlp_scratch(d, f, plans),
        name=f"mlp_bwd_{layer}",
        cost_estimate=cost(16),
    )(*ins)


def spread_rows(out, at, value, order):
    n = len(order)
    r = value.shape[0] >> n
    for c in range(1 << n):
        pos = sum(((c >> b) & 1) << (n - 1 - j) for j, b in enumerate(order))
        out[at, r * pos : r * (pos + 1), :] = value[r * c : r * (c + 1)]


def dw_mlp_kernel(orders, n, low, gh, act, fc_o, pj_o):
    spread_rows(fc_o, 0, dot(n[...], gh[...], 0, 0).astype(BF16), orders[0])
    spread_rows(pj_o, 0, dot(low[...], act[...], 0, 0).astype(BF16), orders[1])


def dw_mlp(layer, n, low, gh, act, orders):
    t, d = n.shape
    f = gh.shape[1] // 2
    out = pl.BlockSpec((1, d, f), lambda j: (j, 0, 0))
    col = pl.BlockSpec((t, f), lambda j: (0, j))
    return pl.pallas_call(
        functools.partial(dw_mlp_kernel, orders),
        grid=(2,),
        in_specs=[full_spec(n.shape), full_spec(low.shape), col, col],
        out_specs=[out, out],
        out_shape=[jax.ShapeDtypeStruct((2, d, f), BF16)] * 2,
        name=f"dw_mlp_{layer}",
        cost_estimate=cost(9),
    )(n, low, gh, act)


def dw_attn_kernel(orders, n, low, dqkv, att, out_a, out_b):
    sh = att.shape[1] // 2
    qkv = dot(n[...], dqkv[...], 0, 0)
    wo = dot(low[...], att[...], 0, 0)
    for s in range(2):
        parts = [qkv[:, (2 * j + s) * sh : (2 * j + s + 1) * sh] for j in range(3)]
        parts.append(wo[:, s * sh : (s + 1) * sh])
        for j, (out, order) in enumerate(zip((out_a, out_b), orders)):
            both = jnp.concatenate(parts[2 * j : 2 * j + 2], axis=1).astype(BF16)
            spread_rows(out, s, both, order)


def dw_attn(layer, n, low, dqkv, att, orders):
    d = n.shape[1]
    ins = (n, low, dqkv, att)
    return pl.pallas_call(
        functools.partial(dw_attn_kernel, orders),
        grid=(1,),
        in_specs=[full_spec(a.shape) for a in ins],
        out_specs=[full_spec((2, d, att.shape[1]))] * 2,
        out_shape=[jax.ShapeDtypeStruct((2, d, att.shape[1]), BF16)] * 2,
        name=f"dw_attn_{layer}",
        cost_estimate=cost(7),
    )(*ins)


def attn_bwd_kernel(layer, half, *refs):
    (g_i, own, oth, mid, qkv, att, lse, start, gain, w) = refs[:10]
    (gm_o, low_o, dqkv_o, part_o, sums_o, qvs_o, k_t, dk, dv, dq_t) = refs[10:]
    g = pl.program_id(0)

    @pl.when(g == 0)
    def _():
        sums_o[...] = jnp.zeros_like(sums_o)
        qvs_o[...] = jnp.zeros_like(qvs_o)
        dk[...] = jnp.zeros_like(dk)
        dv[...] = jnp.zeros_like(dv)
        for b in range(LEN // BT):
            block = qkv[BT * b : BT * (b + 1), half : 2 * half].astype(F32)
            k_t[:, BT * b : BT * (b + 1)] = jnp.transpose(block).astype(BF16)

    gm, g_gain, g_shift = norm_back(
        g_i[...].astype(F32), own[...], oth[...], mid[...], gain[layer, 1:2, :].astype(F32)
    )
    gm_o[...] = gm
    sums_o[0:1, :] += colsum(g_gain)
    sums_o[1:2, :] += colsum(g_shift)
    sums_o[2:3, :] += colsum(gm)
    low = gm.astype(BF16)
    low_o[...] = low
    d_att = dot(low, w[:, 3 * half :]).astype(BF16)
    prod = d_att.astype(F32) * att[...].astype(F32)
    head = lax.broadcasted_iota(jnp.int32, (8, half), 1) // HD
    pick = (head == lax.broadcasted_iota(jnp.int32, (8, half), 0)).astype(F32)
    inner = lax.dot_general(
        pick,
        prod,
        (((1,), (1,)), ((), ())),
        preferred_element_type=F32,
        precision=lax.Precision.HIGHEST,
    )
    rows = pl.ds(pl.multiple_of(g * BT, BT), BT)
    q = qkv[rows, :half] * jnp.asarray(1.0 / math.sqrt(HD), BF16)
    for s in range(BT // QB):
        i = g * (BT // QB) + s
        ks = pl.multiple_of(jnp.maximum(i - DOC_MOST // QB, 0) * QB, QB)
        bias = window_bias(start, i, ks)
        cols = pl.ds(pl.multiple_of(i * QB, QB), QB)
        win = pl.ds(ks, KW)
        for p in range(half // 128):
            lo = 128 * p
            qq = head_pair(q[QB * s : QB * (s + 1), lo : lo + 128])
            oo = head_pair(d_att[QB * s : QB * (s + 1), lo : lo + 128])
            kp = qkv[win, half + lo : half + lo + 128]
            vp = qkv[win, 2 * half + lo : 2 * half + lo + 128]
            total = jnp.concatenate(
                [lse[2 * p : 2 * p + 1, cols], lse[2 * p + 1 : 2 * p + 2, cols]], axis=1
            )
            inn = jnp.concatenate(
                [
                    inner[2 * p : 2 * p + 1, QB * s : QB * (s + 1)],
                    inner[2 * p + 1 : 2 * p + 2, QB * s : QB * (s + 1)],
                ],
                axis=1,
            )
            probs = jnp.exp(dot(kp, qq, 1, 1) + bias - total)
            d_probs = dot(vp, oo, 1, 1)
            ds = (probs * (d_probs - inn)).astype(BF16)
            dv[win, lo : lo + 128] += dot(probs.astype(BF16), oo)
            dk[win, lo : lo + 128] += dot(ds, qq)
            dqt = dot(k_t[lo : lo + 128, win], ds)
            dq_t[lo : lo + HD, :] = dqt[:HD, :QB]
            dq_t[lo + HD : lo + 128, :] = dqt[HD:, QB:]
        dq = (jnp.transpose(dq_t[...]) * (1.0 / math.sqrt(HD))).astype(BF16)
        dqkv_o[cols, :half] = dq
        qvs_o[0:1, :] += colsum(dq.astype(F32))

    @pl.when(g == pl.num_programs(0) - 1)
    def _():
        dqkv_o[:, half : 2 * half] = dk[...].astype(BF16)
        dvb = dv[...].astype(BF16)
        dqkv_o[:, 2 * half :] = dvb
        qvs_o[1:2, :] = colsum(dvb.astype(F32))
        for b in range(LEN // BT):
            part = dot(dqkv_o[BT * b : BT * (b + 1), :], w[:, : 3 * half], 1, 1)
            part_o[BT * b : BT * (b + 1), :] = part.astype(BF16)


def attn_bwd(layer, g, own, oth, mid, qkv, att, lse, start, gain, w):
    d = mid.shape[1]
    half = att.shape[1]
    ins = [g, own, oth, mid, qkv, att, lse, start, gain, w]
    specs = [rows_spec(d)] * 4 + [full_spec(qkv.shape), rows_spec(half)]
    specs += [full_spec(a.shape) for a in ins[6:]]
    return pl.pallas_call(
        functools.partial(attn_bwd_kernel, layer, half),
        grid=(LEN // BT,),
        in_specs=specs,
        out_specs=[
            rows_spec(d),
            rows_spec(d),
            full_spec((LEN, 3 * half)),
            full_spec((LEN, d)),
            full_spec((8, d)),
            full_spec((8, half)),
        ],
        out_shape=[
            jax.ShapeDtypeStruct((LEN, d), F32),
            jax.ShapeDtypeStruct((LEN, d), BF16),
            jax.ShapeDtypeStruct((LEN, 3 * half), BF16),
            jax.ShapeDtypeStruct((LEN, d), BF16),
            jax.ShapeDtypeStruct((8, d), F32),
            jax.ShapeDtypeStruct((8, half), F32),
        ],
        scratch_shapes=[
            pltpu.VMEM((half, LEN), BF16),
            pltpu.VMEM((LEN, half), F32),
            pltpu.VMEM((LEN, half), F32),
            pltpu.VMEM((half, QB), F32),
        ],
        name=f"attn_bwd_{layer}",
        cost_estimate=cost(24),
    )(*ins)


def norm_bwd_kernel(layer, g, own, oth, x, gain, g_o, sums_o):
    @pl.when(pl.program_id(0) == 0)
    def _():
        sums_o[...] = jnp.zeros_like(sums_o)

    out, g_gain, g_shift = norm_back(
        g[...], own[...], oth[...], x[...], gain[layer, 0:1, :].astype(F32)
    )
    g_o[...] = out
    sums_o[0:1, :] += colsum(g_gain)
    sums_o[1:2, :] += colsum(g_shift)


def norm_bwd(layer, g, own, oth, x, gain):
    d = x.shape[1]
    return pl.pallas_call(
        functools.partial(norm_bwd_kernel, layer),
        grid=(LEN // BT,),
        in_specs=[rows_spec(d)] * 4 + [full_spec(gain.shape)],
        out_specs=[rows_spec(d), full_spec((8, d))],
        out_shape=[jax.ShapeDtypeStruct((LEN, d), F32), jax.ShapeDtypeStruct((8, d), F32)],
        name=f"norm_bwd_{layer}",
        cost_estimate=cost(7),
    )(g, own, oth, x, gain)


def core_swap(a):
    return lax.ppermute(a, "mp", [(i, i ^ 1) for i in range(4)])


def y_swap(a):
    return lax.ppermute(a, "mp", [(i, i ^ 2) for i in range(4)])


def dp_swap(a, bit, n_dp):
    return lax.ppermute(a, "dp", [(i, i ^ (1 << bit)) for i in range(n_dp)])


def pick(flag, zero, one):
    return jnp.where(flag == 0, zero, one)


class Place:
    def __init__(self, n_dp):
        mp = lax.axis_index("mp")
        self.n_dp = n_dp
        self.bits = n_dp.bit_length() - 1
        self.y = mp // 2
        self.c = mp % 2
        self.dp = lax.axis_index("dp")

    def dp_bit(self, b):
        return (self.dp >> b) & 1


def row_pieces(a, at):
    rows = a.reshape(2, LEN, a.shape[1])
    return pick(at.y, rows[0], rows[1]), pick(at.y, rows[1], rows[0])


def join_row(mine, far, at):
    mine_c = core_swap(mine)
    far_c = core_swap(far)

    def joined(here, there):
        return [pick(at.c, here, there), pick(at.c, there, here)]

    near2, far2 = joined(mine, mine_c), joined(far, far_c)
    return jnp.concatenate(
        [pick(at.y, a_, b_) for a_, b_ in zip(near2, far2)]
        + [pick(at.y, b_, a_) for a_, b_ in zip(near2, far2)],
        axis=1,
    )


def own_cols(a, at, other):
    w = a.shape[1] // 4
    halves = (a[:, : 2 * w], a[:, 2 * w :])
    h = pick(at.y, halves[1], halves[0]) if other else pick(at.y, halves[0], halves[1])
    return pick(at.c, h[:, :w], h[:, w:])


class Halving:
    def __init__(self, a, order, at):
        self.a, self.order, self.at = a, list(order), at
        self.last = "y" not in order

    def send(self):
        o, at = self.order.pop(0), self.at
        if o == "y":
            self.keep = self.a[0]
            self.got = y_swap(self.a[1])
        else:
            r = self.a.shape[-2] // 2
            b = at.dp_bit(o)
            ax = self.a.ndim - 2
            out = lax.dynamic_slice_in_dim(self.a, (1 - b) * r, r, ax)
            self.keep = lax.dynamic_slice_in_dim(self.a, b * r, r, ax)
            self.got = dp_swap(out, o, at.n_dp)

    def add(self):
        a = self.keep.astype(F32) + self.got.astype(F32)
        self.a = a if self.last and not self.order else a.astype(BF16)

    def finish(self):
        while self.order:
            self.send()
            self.add()
        return self.a


def table_scatter(t, at, rows_all):
    a = t[0] + y_swap(t[1].astype(BF16)).astype(F32)
    top = at.bits - 1
    half = rows_all // 2
    hi = [(i, i ^ (1 << top)) for i in range(at.n_dp) if i >> top & 1]
    a = a + lax.ppermute(a.astype(BF16), "dp", hi).astype(F32)
    a = pick(at.dp_bit(top), a, jnp.zeros_like(a))
    a = jnp.pad(a, ((0, half - a.shape[0]), (0, 0)))
    for b in range(top - 1, -1, -1):
        r = a.shape[0] // 2
        f = at.dp_bit(b)
        got = dp_swap(pick(f, a[r:], a[:r]).astype(BF16), b, at.n_dp)
        a = pick(f, a[:r], a[r:]) + got.astype(F32)
    return a


def small_scatter(shared, own, oth, at):
    n = at.n_dp
    got = y_swap(jnp.concatenate([shared, oth], axis=0))
    a = jnp.concatenate([shared, own], axis=0) + got
    r, d = a.shape
    a = a.reshape(r, n, d // n).transpose(1, 0, 2)
    for b in range(at.bits - 1, -1, -1):
        h = a.shape[0] // 2
        f = at.dp_bit(b)
        a = pick(f, a[:h], a[h:]) + dp_swap(pick(f, a[h:], a[:h]), b, n)
    return a[0]


def bar(*vals):
    return lax.optimization_barrier(vals)


def doc_starts(doc_ids):
    row_index = jnp.broadcast_to(jnp.arange(doc_ids.shape[1], dtype=jnp.int32), doc_ids.shape)
    previous = jnp.concatenate([doc_ids[:, :1] - 1, doc_ids[:, :-1]], axis=1)
    starts = jnp.where(doc_ids != previous, row_index, 0)
    return lax.cummax(starts, axis=1)


def on_device(
    n_dp,
    tokens,
    doc_ids,
    positions_table,
    norm_gain,
    norm_shift,
    joined_projection_weight,
    qv_bias,
    w_out,
    out_bias,
    w_fc,
    fc_bias,
    w_proj,
    cotangent,
):
    at = Place(n_dp)
    d = positions_table.shape[1]
    share = joined_projection_weight.shape[-1]
    f = w_fc.shape[-1]
    bits = list(range(2, at.bits))
    bits = list(range(2, at.bits))

    def dp_only(*orders):
        return [[o for o in order if o != "y"] + bits for order in orders]

    b = at.dp_bit(0) ^ at.dp_bit(1)
    flag = b.reshape(1)
    gain, shift = norm_gain, norm_shift

    a_own = [
        jnp.concatenate([joined_projection_weight[l].reshape(d, 3 * share), w_out[l].T], axis=1)
        for l in range(2)
    ]
    biases = jnp.concatenate([qv_bias.reshape(-1), fc_bias.reshape(-1)]).reshape(-1, d)
    biases = jnp.pad(biases, ((0, -biases.shape[0] % 8), (0, 0)))
    r = d // 2

    def half_rows(w):
        return lax.dynamic_slice_in_dim(w, b * r, r, 0)

    def x_swap(w):
        return dp_swap(w, 0, n_dp)

    def z_swap(w):
        return dp_swap(w, 1, n_dp)

    def by_two(one, lo=0):
        return x_swap(one[lo : lo + r // 2]), z_swap(one[lo + r // 2 : lo + r])

    def plan_one(lo=0):
        return ((lo, r, 0, 0), (0, r, 1, 0))

    def plan_two(lo=0):
        return ((lo, r, 0, 0), (0, r // 2, 1, 0), (0, r // 2, 1, r // 2))

    tok_mine, tok_theirs = row_pieces(tokens, at)
    tok_far = y_swap(tok_theirs)
    a_one0 = y_swap(jnp.concatenate([half_rows(a_own[0]), biases], axis=0))

    starts = doc_starts(doc_ids)
    start = pick(at.y, starts[0:1], starts[1:2])
    place = jnp.arange(LEN, dtype=jnp.int32) - start[0]
    hot = (place[:, None] == jnp.arange(DOC_MOST, dtype=jnp.int32)[None, :]).astype(BF16)
    embedded = dot(hot, positions_table[:DOC_MOST]).astype(BF16)

    tok_far, a_one0, embedded, hot = bar(tok_far, a_one0, embedded, hot)
    a_x, a_z = by_two(a_one0)
    fc_one0 = y_swap(half_rows(w_fc[0]))
    full_tokens = join_row(tok_mine, tok_far, at)
    small = a_one0[r:].reshape(-1)
    nq = qv_bias.size
    qvb = jnp.concatenate([qv_bias, small[:nq].reshape(qv_bias.shape)], axis=-1)
    fcb = jnp.concatenate(
        [fc_bias, small[nq : nq + fc_bias.size].reshape(fc_bias.shape)], axis=-1
    )
    send_y = jnp.concatenate([half_rows(w_proj[0]), half_rows(a_own[1])], axis=0)
    a_x, a_z, fc_one0, full_tokens, send_y = bar(a_x, a_z, fc_one0, full_tokens, send_y)

    fc_two0 = x_swap(fc_one0)
    pj_a1 = y_swap(send_y)
    x0, n0, qkv0, att0, lse0, part, wa0 = attn_fwd(
        0,
        (full_tokens, embedded),
        out_bias,
        flag,
        start,
        gain,
        shift,
        qvb,
        a_own[0],
        (plan_two(), (a_one0, a_x, a_z)),
    )
    part, x0, fc_two0, pj_a1 = bar(part, x0, fc_two0, pj_a1)
    far = core_swap(part)
    pj_x, pj_z = by_two(pj_a1)
    far, pj_x, pj_z = bar(far, pj_x, pj_z)
    mlp0 = (
        w_fc,
        (plan_one(), (fc_one0, fc_two0)),
        w_proj,
        (plan_two(), (pj_a1, pj_x, pj_z)),
    )
    a_two1 = x_swap(pj_a1[r:])
    fc_one1 = y_swap(half_rows(w_fc[1]))
    mid0, nn0, hid0, part2 = mlp_fwd(
        0, x0, part, far, out_bias, gain, shift, fcb, flag, mlp0
    )
    part2, mid0, a_two1, fc_one1 = bar(part2, mid0, a_two1, fc_one1)
    far = core_swap(part2)
    (far,) = bar(far)
    fc_two1 = x_swap(fc_one1)
    pj_one1 = y_swap(half_rows(w_proj[1]))
    cot_mine, cot_theirs = row_pieces(cotangent, at)
    cot_far = y_swap(cot_theirs)
    x1, n1, qkv1, att1, lse1, part, wa1 = attn_fwd(
        1,
        (mid0, part2, far),
        out_bias,
        flag,
        start,
        gain,
        shift,
        qvb,
        a_own[1],
        (plan_one(r), (pj_a1, a_two1)),
    )
    part, x1, fc_two1, cot_far, pj_one1 = bar(part, x1, fc_two1, cot_far, pj_one1)
    far = core_swap(part)
    pj_x, pj_z = by_two(pj_one1)
    cot = join_row(cot_mine, cot_far, at)
    far, cot, pj_x, pj_z = bar(far, cot, pj_x, pj_z)
    mlp1 = (
        w_fc,
        (plan_one(), (fc_one1, fc_two1)),
        w_proj,
        (plan_two(), (pj_one1, pj_x, pj_z)),
    )
    mid1, nn1, act, gh, part_out, part, sumg1, sumh1 = mlp_both(
        1, x1, part, far, cot, out_bias, gain, shift, fcb, flag, mlp1
    )

    part, part_out, mid1, gh, act = bar(part, part_out, mid1, gh, act)
    far = core_swap(part)
    far_out = core_swap(part_out)
    o_fc, o_pj, o_a, o_b = ["y", 1, 0], [0, "y", 1], [0, 1, "y"], [1, "y", 0]
    d_fc, d_pj = dw_mlp(1, nn1, cot, gh, act, dp_only(o_fc, o_pj))
    far, far_out, d_fc, d_pj = bar(far, far_out, d_fc, d_pj)
    fc1, pj1 = Halving(d_fc, o_fc, at), Halving(d_pj, o_pj, at)
    fc1.send()
    pj1.send()
    gm1, m_low, dqkv, part, sums1, qvs1 = attn_bwd(
        1, cot, part, far, mid1, qkv1, att1, lse1, start, gain, wa1
    )
    part, gm1, m_low, dqkv, fc1.got, pj1.got = bar(part, gm1, m_low, dqkv, fc1.got, pj1.got)
    far = core_swap(part)
    d_a, d_b = dw_attn(1, n1, m_low, dqkv, att1, dp_only(o_a, o_b))
    result = (
        mid1 + (part_out.astype(F32) + far_out.astype(F32)) + out_bias[1, 1].astype(F32)
    ).astype(BF16)
    out_near, out_send = own_cols(result, at, False), own_cols(result, at, True)
    fc1.add()
    pj1.add()
    far, d_a, d_b, out_send, fc1.a, pj1.a = bar(far, d_a, d_b, out_send, fc1.a, pj1.a)
    aa1, ab1 = Halving(d_a, o_a, at), Halving(d_b, o_b, at)
    aa1.send()
    fc1.send()
    pj1.send()
    g0, g_low, act, gh, part, sums0b, sumh0 = mlp_bwd(
        0, gm1, part, far, x1, hid0, gain, flag, mlp0
    )
    part, g0, g_low, act, gh, fc1.got, pj1.got, aa1.got = bar(
        part, g0, g_low, act, gh, fc1.got, pj1.got, aa1.got
    )
    far = core_swap(part)
    for h in (fc1, pj1, aa1):
        h.add()
        h.send()
    out_far = y_swap(out_send)
    d_fc, d_pj = dw_mlp(0, nn0, g_low, gh, act, dp_only(o_fc, o_pj))
    far, d_fc, d_pj, out_far, fc1.got, pj1.got, aa1.got = bar(
        far, d_fc, d_pj, out_far, fc1.got, pj1.got, aa1.got
    )
    fc0, pj0 = Halving(d_fc, o_fc, at), Halving(d_pj, o_pj, at)
    fc0.send()
    pj0.send()
    ab1.send()
    aa1.add()
    aa1.send()
    fc1.add()
    pj1.add()
    gm0, m_low, dqkv, part, sums0, qvs0 = attn_bwd(
        0, g0, part, far, mid0, qkv0, att0, lse0, start, gain, wa0
    )
    part, gm0, m_low, dqkv, fc0.got, pj0.got, ab1.got, aa1.got = bar(
        part, gm0, m_low, dqkv, fc0.got, pj0.got, ab1.got, aa1.got
    )
    far = core_swap(part)
    d_a, d_b = dw_attn(0, n0, m_low, dqkv, att0, dp_only(o_a, o_b))
    far, d_a, d_b = bar(far, d_a, d_b)
    aa0, ab0 = Halving(d_a, o_a, at), Halving(d_b, o_b, at)
    aa0.send()
    ab0.send()
    for h in (fc0, pj0, ab1, aa1):
        h.add()
    fc0.send()
    pj0.send()
    ab1.send()
    last1 = Halving(jnp.concatenate([fc1.a, pj1.a, aa1.a], axis=1), bits, at)
    last1.send()
    g, sums0a = norm_bwd(0, gm0, part, far, x0, gain)
    near = own_cols(g, at, False)
    far_send = own_cols(g, at, True).astype(BF16)
    near, far_send, aa0.got, ab0.got, fc0.got, pj0.got, ab1.got = bar(
        near, far_send, aa0.got, ab0.got, fc0.got, pj0.got, ab1.got
    )
    g_far = y_swap(far_send)
    for h in (aa0, ab0, fc0, pj0, ab1):
        h.add()
        h.send()

    def qv_row(lo):
        parts = jnp.stack([q[j, lo : lo + share] for q in (qvs0, qvs1) for j in range(2)])
        return parts.reshape(-1, n_dp, share // n_dp).transpose(1, 0, 2).reshape(1, d)

    shared = jnp.stack(
        [sums0a[0], sums0[0], sums0b[0], sums1[0]]
        + [sums0a[1], sums0[1], sums0b[1], sums1[1]]
        + [sums0[2], sums0b[2], sums1[2], sumg1[0]]
    )
    own = jnp.concatenate([jnp.stack([sumh0[0, :f], sumh1[0, :f]]), qv_row(0)])
    oth = jnp.concatenate([jnp.stack([sumh0[0, f:], sumh1[0, f:]]), qv_row(share)])
    table = lax.dot_general(
        hot,
        jnp.concatenate([near.astype(BF16), far_send], axis=1),
        (((0,), (0,)), ((), ())),
        preferred_element_type=F32,
    )
    table, shared, own, oth, aa0.got, ab0.got, fc0.got, pj0.got, ab1.got, g_far = bar(
        table, shared, own, oth, aa0.got, ab0.got, fc0.got, pj0.got, ab1.got, g_far
    )
    for h in (aa0, ab0, fc0, pj0, ab1):
        h.add()
    aa0.send()
    ab0.send()
    last0 = Halving(jnp.concatenate([fc0.a, pj0.a, ab1.a], axis=1), bits, at)
    last0.send()
    grad_positions = table_scatter(
        jnp.stack([table[:, :share], table[:, share:]]), at, positions_table.shape[0]
    )
    s = small_scatter(shared, own, oth, at)
    last1.add()
    aa0.add()
    ab0.add()
    last2 = Halving(jnp.concatenate([aa0.a, ab0.a], axis=1), bits, at)
    last2.send()
    last0.add()
    last2.add()
    l1, l0, l2 = last1.finish(), last0.finish(), last2.finish()
    h2 = 2 * share
    r_fc = (l0[:, :f], l1[:, :f])
    r_pj = (l0[:, f : 2 * f], l1[:, f : 2 * f])
    r_ao = (
        l2,
        jnp.concatenate([l1[:, 2 * f : 2 * f + h2], l0[:, 2 * f : 2 * f + h2]], axis=1),
    )
    g_far = g_far.astype(F32)
    grad_tokens = jnp.concatenate([pick(at.y, near, g_far), pick(at.y, g_far, near)], axis=0)
    out = jnp.concatenate([pick(at.y, out_near, out_far), pick(at.y, out_far, out_near)], axis=0)
    w = d // n_dp
    ao = jnp.stack(r_ao)
    return (
        out,
        grad_tokens,
        grad_positions,
        s[0:4].reshape(2, 2, w),
        s[4:8].reshape(2, 2, w),
        ao[..., : 3 * share].reshape(2, w, 3, share),
        s[14].reshape(2, 2, w // 4),
        jnp.swapaxes(ao[..., 3 * share :], 1, 2),
        s[8:12].reshape(2, 2, w),
        jnp.stack(r_fc),
        s[12:14],
        jnp.stack([p.T for p in r_pj]),
    )


def solution(mesh):
    n_dp = mesh.shape["dp"]
    in_specs = (
        P("dp", "mp"),
        P("dp", None),
        P(),
        P(),
        P(),
        P(None, None, None, "mp"),
        P(None, None, "mp"),
        P(None, "mp", None),
        P(),
        P(None, None, "mp"),
        P(None, "mp"),
        P(None, "mp", None),
        P("dp", "mp"),
    )
    out_specs = (
        P("dp", "mp"),
        P("dp", "mp"),
        P("dp", "mp"),
        P(None, None, "dp"),
        P(None, None, "dp"),
        P(None, "dp", None, "mp"),
        P(None, None, ("mp", "dp")),
        P(None, "mp", "dp"),
        P(None, None, "dp"),
        P(None, "dp", "mp"),
        P(None, ("mp", "dp")),
        P(None, "mp", "dp"),
    )
    return jax.shard_map(
        functools.partial(on_device, n_dp),
        mesh=mesh,
        in_specs=in_specs,
        out_specs=out_specs,
        check_vma=False,
    )
```

```python
import functools
import math

import jax
import jax.numpy as jnp
from jax import lax
from jax.experimental import pallas as pl
from jax.experimental.pallas import tpu as pltpu
from jax.sharding import PartitionSpec as P

HD = 64
LEN = 1024
DOC_MOST = 384
EPS = 1e-05
BT = 256
QB = 128
KW = QB + DOC_MOST
F32 = jnp.float32
BF16 = jnp.bfloat16
GELU_C = math.sqrt(2.0 / math.pi)


ANY = pl.BlockSpec(memory_space=pl.ANY)
SMEM = pl.BlockSpec(memory_space=pltpu.SMEM)


def cost(us):
    return pl.CostEstimate(flops=int(us * 1.15e9), transcendentals=0, bytes_accessed=0)


def full_spec(shape):
    return pl.BlockSpec(shape, lambda g: (0,) * len(shape))


def rows_spec(width):
    return pl.BlockSpec((BT, width), lambda g: (g, 0))


def dot(a, b, ca=1, cb=0):
    return lax.dot_general(a, b, (((ca,), (cb,)), ((), ())), preferred_element_type=F32)


def normed_parts(v):
    centred = v - jnp.mean(v, axis=-1, keepdims=True)
    variance = jnp.mean(centred * centred, axis=-1, keepdims=True)
    rstd = lax.rsqrt(variance + EPS)
    return centred * rstd, rstd


def norm_back(g, own, oth, v, gain):
    grad = own.astype(F32) + oth.astype(F32)
    xhat, rstd = normed_parts(v)
    gn = grad * gain
    out = g + rstd * (
        gn
        - jnp.mean(gn, axis=-1, keepdims=True)
        - xhat * jnp.mean(gn * xhat, axis=-1, keepdims=True)
    )
    return out, grad * xhat, grad


def colsum(v):
    return jnp.sum(v, axis=0, keepdims=True)


def head_pair(block):
    lane = lax.broadcasted_iota(jnp.int32, block.shape, 1)
    zero = jnp.zeros_like(block)
    return jnp.concatenate(
        [jnp.where(lane < HD, block, zero), jnp.where(lane < HD, zero, block)], axis=0
    )


def window_bias(start_ref, i, ks):
    kidx = lax.broadcasted_iota(jnp.int32, (KW, QB), 0) + ks
    qidx = lax.broadcasted_iota(jnp.int32, (KW, QB), 1) + i * QB
    first = start_ref[0:1, pl.ds(pl.multiple_of(i * QB, QB), QB)]
    bias = jnp.where((kidx >= first) & (kidx <= qidx), 0.0, -1e30).astype(F32)
    return jnp.concatenate([bias, bias], axis=1)


def copies(pairs, sems):
    out = [pltpu.make_async_copy(a, b, sems.at[j]) for j, (a, b) in enumerate(pairs)]
    for c in out:
        c.start()
    return out


def join_pieces(flag, plan, refs, dst, cols=slice(None)):
    r = dst.shape[0] // 2
    out = []
    for (lo, n, other, off), ref in zip(plan, refs):
        row = (1 - flag if other else flag) * r + off
        out.append((ref.at[pl.ds(lo, n)], dst.at[pl.ds(pl.multiple_of(row, 8), n), cols]))
    return out


def gelu_parts(v):
    v2 = v * v
    t = jnp.tanh(GELU_C * v * (1.0 + 0.044715 * v2))
    cdf = 0.5 * (1.0 + t)
    slope = cdf + (0.5 * GELU_C) * v * (1.0 - t * t) * (1.0 + (3 * 0.044715) * v2)
    return v * cdf, slope


def gained(xhat, gain, shift, layer, which):
    row = slice(which, which + 1)
    return (xhat * gain[layer, row, :].astype(F32) + shift[layer, row, :].astype(F32)).astype(BF16)


def attn_fwd_kernel(layer, first, half, plan, *refs):
    if first:
        (tok, emb, flag, start, gain, shift, qvb, a_own) = refs[:8]
        rest = refs[8:]
        x = tok[...].astype(F32) + emb[...].astype(F32)
    else:
        (mid, own, oth, outb, flag, start, gain, shift, qvb, a_own) = refs[:10]
        rest = refs[10:]
        x = (
            mid[...]
            + (own[...].astype(F32) + oth[...].astype(F32))
            + outb[layer - 1, 1:2, :].astype(F32)
        )
    a_refs, rest = rest[: len(plan)], rest[len(plan) :]
    x_o, n_o, qkv_o, att_o, lse_o, part_o, w_o, v_t, o_t, a_buf, sems = rest
    g = pl.program_id(0)
    sh = half // 2

    @pl.when(g == 0)
    def _():
        moves = copies(
            [(a_own, a_buf.at[0])] + join_pieces(flag[0], plan, a_refs, a_buf.at[1]), sems
        )
        qkv_o[pl.ds(BT, KW - BT), half : 2 * half] = jnp.zeros((KW - BT, half), BF16)
        v_t[:, pl.ds(BT, KW - BT)] = jnp.zeros((half, KW - BT), BF16)
        lse_o[...] = jnp.zeros_like(lse_o)
        for m in moves:
            m.wait()
        for j in range(4):
            for s in range(2):
                w_o[:, (2 * j + s) * sh : (2 * j + s + 1) * sh] = a_buf[s, :, j * sh : (j + 1) * sh]

    x_o[...] = x
    xhat, _ = normed_parts(x)
    normed = gained(xhat, gain, shift, layer, 0)
    n_o[...] = normed
    qkv = dot(normed, w_o[:, : 3 * half])
    q = (qkv[:, :half] + qvb[layer, 0:1, :].astype(F32)).astype(BF16)
    k = qkv[:, half : 2 * half].astype(BF16)
    v = qkv[:, 2 * half :] + qvb[layer, 1:2, :].astype(F32)
    rows = pl.ds(pl.multiple_of(g * BT, BT), BT)
    qkv_o[rows, :half] = q
    qkv_o[rows, half : 2 * half] = k
    qkv_o[rows, 2 * half :] = v.astype(BF16)
    v_t[:, rows] = jnp.transpose(v).astype(BF16)
    q = q * jnp.asarray(1.0 / math.sqrt(HD), BF16)
    for s in range(BT // QB):
        i = g * (BT // QB) + s
        ks = pl.multiple_of(jnp.maximum(i - DOC_MOST // QB, 0) * QB, QB)
        bias = window_bias(start, i, ks)
        cols = pl.ds(pl.multiple_of(i * QB, QB), QB)
        for p in range(half // 128):
            lo = 128 * p
            qq = head_pair(q[QB * s : QB * (s + 1), lo : lo + 128])
            kp = qkv_o[pl.ds(ks, KW), half + lo : half + lo + 128]
            scores = dot(kp, qq, 1, 1) + bias
            peak = jnp.max(scores, axis=0, keepdims=True)
            e = jnp.exp(scores - peak)
            total = jnp.sum(e, axis=0, keepdims=True)
            ot = dot(v_t[lo : lo + 128, pl.ds(ks, KW)], e.astype(BF16))
            inv = 1.0 / total
            o_t[lo : lo + HD, :] = ot[:HD, :QB] * inv[:, :QB]
            o_t[lo + HD : lo + 128, :] = ot[HD:, QB:] * inv[:, QB:]
            lse = peak + jnp.log(total)
            lse_o[2 * p : 2 * p + 1, cols] = lse[:, :QB]
            lse_o[2 * p + 1 : 2 * p + 2, cols] = lse[:, QB:]
        att_o[QB * s : QB * (s + 1), :] = jnp.transpose(o_t[...]).astype(BF16)
    part_o[...] = dot(att_o[...], w_o[:, 3 * half :], 1, 1).astype(BF16)


def attn_fwd(layer, stream_in, outb, flag, start, gain, shift, qvb, a_own, a_oth):
    first = layer == 0
    d = gain.shape[-1]
    half = a_own.shape[1] // 2
    ins = list(stream_in)
    specs = [rows_spec(d) for _ in ins]
    if not first:
        ins.append(outb)
        specs.append(full_spec(outb.shape))
    plan, arrays = a_oth
    ins += [flag, start, gain, shift, qvb, a_own, *arrays]
    specs += [SMEM] + [full_spec(a.shape) for a in (start, gain, shift, qvb)]
    specs += [ANY] * (1 + len(arrays))
    return pl.pallas_call(
        functools.partial(attn_fwd_kernel, layer, first, half, plan),
        grid=(LEN // BT,),
        in_specs=specs,
        out_specs=[
            rows_spec(d),
            rows_spec(d),
            full_spec((LEN, 3 * half)),
            rows_spec(half),
            full_spec((8, LEN)),
            rows_spec(d),
            full_spec((d, 4 * half)),
        ],
        out_shape=[
            jax.ShapeDtypeStruct((LEN, d), F32),
            jax.ShapeDtypeStruct((LEN, d), BF16),
            jax.ShapeDtypeStruct((LEN, 3 * half), BF16),
            jax.ShapeDtypeStruct((LEN, half), BF16),
            jax.ShapeDtypeStruct((8, LEN), F32),
            jax.ShapeDtypeStruct((LEN, d), BF16),
            jax.ShapeDtypeStruct((d, 4 * half), BF16),
        ],
        scratch_shapes=[
            pltpu.VMEM((half, LEN), BF16),
            pltpu.VMEM((half, QB), F32),
            pltpu.VMEM((2, d, 2 * half), BF16),
            pltpu.SemaphoreType.DMA((1 + len(plan),)),
        ],
        name=f"attn_fwd_{layer}",
        cost_estimate=cost(22),
    )(*ins)


def load_mlp(layer, flag, plans, weights, wfc, wproj, sems):
    d = wfc.shape[0]
    f = wfc.shape[1] // 2
    n = len(plans[0])
    return copies(
        [(weights[0].at[layer], wfc.at[:, pl.ds(0, f)])]
        + join_pieces(flag[0], plans[0], weights[2 : 2 + n], wfc, pl.ds(f, f))
        + [(weights[1].at[layer], wproj.at[pl.ds(0, f)])]
        + join_pieces(flag[0], plans[1], weights[2 + n :], wproj.at[pl.ds(f, f)]),
        sems,
    )


def mlp_scratch(d, f2, plans):
    return [
        pltpu.VMEM((d, f2), BF16),
        pltpu.VMEM((f2, d), BF16),
        pltpu.SemaphoreType.DMA((2 + len(plans[0]) + len(plans[1]),)),
    ]


def mlp_weights(weights):
    w_fc, fc_oth, w_proj, pj_oth = weights
    return (fc_oth[0], pj_oth[0]), [w_fc, w_proj, *fc_oth[1], *pj_oth[1]]


def mlp_fwd_kernel(layer, plans, x, own, oth, outb, gain, shift, fcb, flag, *refs):
    nw = 2 + len(plans[0]) + len(plans[1])
    weights = refs[:nw]
    mid_o, n_o, h_o, part_o, wfc, wproj, sems = refs[nw:]

    @pl.when(pl.program_id(0) == 0)
    def _():
        for m in load_mlp(layer, flag, plans, weights, wfc, wproj, sems):
            m.wait()

    mid = (
        x[...]
        + (own[...].astype(F32) + oth[...].astype(F32))
        + outb[layer, 0:1, :].astype(F32)
    )
    mid_o[...] = mid
    xhat, _ = normed_parts(mid)
    normed = gained(xhat, gain, shift, layer, 1)
    n_o[...] = normed
    hidden = dot(normed, wfc[...]) + fcb[layer : layer + 1, :].astype(F32)
    h_o[...] = hidden.astype(BF16)
    t = jnp.tanh(GELU_C * hidden * (1.0 + 0.044715 * hidden * hidden))
    act = (0.5 * hidden * (1.0 + t)).astype(BF16)
    part_o[...] = dot(act, wproj[...]).astype(BF16)


def mlp_fwd(layer, x, own, oth, outb, gain, shift, fcb, flag, weights):
    d = x.shape[1]
    f = fcb.shape[1]
    plans, arrays = mlp_weights(weights)
    ins = [x, own, oth, outb, gain, shift, fcb, flag, *arrays]
    specs = [rows_spec(d)] * 3 + [full_spec(a.shape) for a in ins[3:7]] + [SMEM] + [ANY] * len(arrays)
    return pl.pallas_call(
        functools.partial(mlp_fwd_kernel, layer, plans),
        grid=(LEN // BT,),
        in_specs=specs,
        out_specs=[rows_spec(d), rows_spec(d), rows_spec(f), rows_spec(d)],
        out_shape=[
            jax.ShapeDtypeStruct((LEN, d), F32),
            jax.ShapeDtypeStruct((LEN, d), BF16),
            jax.ShapeDtypeStruct((LEN, f), BF16),
            jax.ShapeDtypeStruct((LEN, d), BF16),
        ],
        scratch_shapes=mlp_scratch(d, f, plans),
        name=f"mlp_fwd_{layer}",
        cost_estimate=cost(12),
    )(*ins)


def mlp_both_kernel(layer, plans, x, own, oth, cot, outb, gain, shift, fcb, flag, *refs):
    nw = 2 + len(plans[0]) + len(plans[1])
    weights = refs[:nw]
    mid_o, n_o, act_o, gh_o, out_o, part_o, sumg_o, sumh_o, wfc, wproj, sems = refs[nw:]

    @pl.when(pl.program_id(0) == 0)
    def _():
        moves = load_mlp(layer, flag, plans, weights, wfc, wproj, sems)
        sumg_o[...] = jnp.zeros_like(sumg_o)
        sumh_o[...] = jnp.zeros_like(sumh_o)
        for m in moves:
            m.wait()

    mid = (
        x[...]
        + (own[...].astype(F32) + oth[...].astype(F32))
        + outb[layer, 0:1, :].astype(F32)
    )
    mid_o[...] = mid
    xhat, _ = normed_parts(mid)
    normed = gained(xhat, gain, shift, layer, 1)
    n_o[...] = normed
    grad_act = dot(cot[...], wproj[...], 1, 1)
    value, slope = gelu_parts(dot(normed, wfc[...]) + fcb[layer : layer + 1, :].astype(F32))
    act = value.astype(BF16)
    act_o[...] = act
    gh = (grad_act * slope).astype(BF16)
    gh_o[...] = gh
    part_o[...] = dot(gh, wfc[...], 1, 1).astype(BF16)
    out_o[...] = dot(act, wproj[...]).astype(BF16)
    sumg_o[0:1, :] += colsum(cot[...].astype(F32))
    sumh_o[0:1, :] += colsum(gh.astype(F32))


def mlp_both(layer, x, own, oth, cot, outb, gain, shift, fcb, flag, weights):
    d = x.shape[1]
    f = fcb.shape[1]
    plans, arrays = mlp_weights(weights)
    ins = [x, own, oth, cot, outb, gain, shift, fcb, flag, *arrays]
    specs = [rows_spec(d)] * 4 + [full_spec(a.shape) for a in ins[4:8]] + [SMEM] + [ANY] * len(arrays)
    widths = [d, d, f, f, d, d]
    kinds = [F32, BF16, BF16, BF16, BF16, BF16]
    return pl.pallas_call(
        functools.partial(mlp_both_kernel, layer, plans),
        grid=(LEN // BT,),
        in_specs=specs,
        out_specs=[rows_spec(w) for w in widths] + [full_spec((8, d)), full_spec((8, f))],
        out_shape=[jax.ShapeDtypeStruct((LEN, w), k) for w, k in zip(widths, kinds)]
        + [jax.ShapeDtypeStruct((8, d), F32), jax.ShapeDtypeStruct((8, f), F32)],
        scratch_shapes=mlp_scratch(d, f, plans),
        name=f"mlp_both_{layer}",
        cost_estimate=cost(18),
    )(*ins)


def mlp_bwd_kernel(layer, plans, gm, own, oth, x, h, gain, flag, *refs):
    nw = 2 + len(plans[0]) + len(plans[1])
    weights = refs[:nw]
    g_o, low_o, act_o, gh_o, part_o, sums_o, sumh_o, wfc, wproj, sems = refs[nw:]

    @pl.when(pl.program_id(0) == 0)
    def _():
        moves = load_mlp(layer, flag, plans, weights, wfc, wproj, sems)
        sums_o[...] = jnp.zeros_like(sums_o)
        sumh_o[...] = jnp.zeros_like(sumh_o)
        for m in moves:
            m.wait()

    grad, g_gain, g_shift = norm_back(
        gm[...], own[...], oth[...], x[...], gain[layer + 1, 0:1, :].astype(F32)
    )
    sums_o[0:1, :] += colsum(g_gain)
    sums_o[1:2, :] += colsum(g_shift)
    sums_o[2:3, :] += colsum(grad)
    g_o[...] = grad
    low = grad.astype(BF16)
    low_o[...] = low
    grad_act = dot(low, wproj[...], 1, 1)
    value, slope = gelu_parts(h[...].astype(F32))
    act_o[...] = value.astype(BF16)
    gh = (grad_act * slope).astype(BF16)
    gh_o[...] = gh
    part_o[...] = dot(gh, wfc[...], 1, 1).astype(BF16)
    sumh_o[0:1, :] += colsum(gh.astype(F32))


def mlp_bwd(layer, gm, own, oth, x, h, gain, flag, weights):
    d = x.shape[1]
    f = h.shape[1]
    plans, arrays = mlp_weights(weights)
    ins = [gm, own, oth, x, h, gain, flag, *arrays]
    specs = [rows_spec(d)] * 4 + [rows_spec(f), full_spec(gain.shape), SMEM] + [ANY] * len(arrays)
    widths = [d, d, f, f, d]
    kinds = [F32, BF16, BF16, BF16, BF16]
    return pl.pallas_call(
        functools.partial(mlp_bwd_kernel, layer, plans),
        grid=(LEN // BT,),
        in_specs=specs,
        out_specs=[rows_spec(w) for w in widths] + [full_spec((8, d)), full_spec((8, f))],
        out_shape=[jax.ShapeDtypeStruct((LEN, w), k) for w, k in zip(widths, kinds)]
        + [jax.ShapeDtypeStruct((8, d), F32), jax.ShapeDtypeStruct((8, f), F32)],
        scratch_shapes=mlp_scratch(d, f, plans),
        name=f"mlp_bwd_{layer}",
        cost_estimate=cost(16),
    )(*ins)


def emit(keep, send, slot, value, order, flags):
    dims = [o for o in order if o != "y"]
    n = len(dims)
    r = value.shape[0] >> n
    value = value.astype(BF16)

    def chunks():
        for c in range(1 << n):
            yield sum(((c >> b) & 1) << (n - 1 - j) for j, b in enumerate(dims)), value[r * c : r * (c + 1)]

    def whole(out):
        for pos, v in chunks():
            out[r * pos : r * (pos + 1), :] = v

    if order[0] == "y":
        if isinstance(slot, int):
            whole(send if slot else keep)
        else:
            pl.when(slot == 0)(lambda: whole(keep))
            pl.when(slot == 1)(lambda: whole(send))
        return
    at = slot if isinstance(slot, int) else 0
    half = 1 << (n - 1)

    def split(bit):
        for pos, v in chunks():
            out = keep if pos // half == bit else send
            row = r * (pos % half)
            out[at, row : row + r, :] = v

    pl.when(flags[dims[0]] == 0)(lambda: split(0))
    pl.when(flags[dims[0]] == 1)(lambda: split(1))


def first_shape(order, d, w):
    return (d, w) if order[0] == "y" else (2, d // 2, w)


def dw_mlp_kernel(orders, flags, n, low, gh, act, *outs):
    j = pl.program_id(0)
    emit(outs[0], outs[1], j, dot(n[...], gh[...], 0, 0), orders[0], flags)
    emit(outs[2], outs[3], j, dot(low[...], act[...], 0, 0), orders[1], flags)


def dw_mlp(layer, n, low, gh, act, orders, flags):
    t, d = n.shape
    f = gh.shape[1] // 2
    col = pl.BlockSpec((t, f), lambda j: (0, j))
    shapes = [first_shape(o, d, f) for o in orders for _ in range(2)]
    specs = [
        full_spec(s) if len(s) == 2 else pl.BlockSpec((1,) + s[1:], lambda j: (j, 0, 0))
        for s in shapes
    ]
    k0, s0, k1, s1 = pl.pallas_call(
        functools.partial(dw_mlp_kernel, orders),
        grid=(2,),
        in_specs=[SMEM, full_spec(n.shape), full_spec(low.shape), col, col],
        out_specs=specs,
        out_shape=[jax.ShapeDtypeStruct(s, BF16) for s in shapes],
        name=f"dw_mlp_{layer}",
        cost_estimate=cost(9),
    )(flags, n, low, gh, act)
    return Part(k0, s0, orders[0]), Part(k1, s1, orders[1])


def dw_attn_kernel(orders, flags, n, low, dqkv, att, *outs):
    sh = att.shape[1] // 2
    qkv = dot(n[...], dqkv[...], 0, 0)
    wo = dot(low[...], att[...], 0, 0)
    for s in range(2):
        parts = [qkv[:, (2 * j + s) * sh : (2 * j + s + 1) * sh] for j in range(3)]
        parts.append(wo[:, s * sh : (s + 1) * sh])
        for j, order in enumerate(orders):
            both = jnp.concatenate(parts[2 * j : 2 * j + 2], axis=1)
            emit(outs[2 * j], outs[2 * j + 1], s, both, order, flags)


def dw_attn(layer, n, low, dqkv, att, orders, flags):
    d = n.shape[1]
    ins = (n, low, dqkv, att)
    shapes = [first_shape(o, d, att.shape[1]) for o in orders for _ in range(2)]
    k0, s0, k1, s1 = pl.pallas_call(
        functools.partial(dw_attn_kernel, orders),
        grid=(1,),
        in_specs=[SMEM] + [full_spec(a.shape) for a in ins],
        out_specs=[full_spec(s) for s in shapes],
        out_shape=[jax.ShapeDtypeStruct(s, BF16) for s in shapes],
        name=f"dw_attn_{layer}",
        cost_estimate=cost(7),
    )(flags, *ins)
    return Part(k0, s0, orders[0]), Part(k1, s1, orders[1])


def combine_kernel(steps, merged, flags, *refs):
    ins, outs = refs[: 2 * len(steps)], refs[2 * len(steps) :]
    lo = 0
    for k, o in enumerate(steps):
        keep, got = ins[2 * k : 2 * k + 2]

        def total(at):
            return keep[at].astype(F32) + got[at].astype(F32)

        if o is None:
            outs[k][...] = total(...)
            continue
        dst = outs if merged else outs[2 * k : 2 * k + 2]
        cols = slice(lo, lo + keep.shape[-1]) if merged else slice(None)
        if o == "y":
            halves = [total(0), total(1)]
        else:
            r = keep.shape[-2] // 2
            lead = (slice(None),) * (len(keep.shape) - 2)
            rows = [pl.ds(pl.multiple_of(h * r, 8), r) for h in (flags[o], 1 - flags[o])]
            halves = [total(lead + (row, slice(None))) for row in rows]
        for out, v in zip(dst, halves):
            out[..., cols] = v.astype(BF16)
        if merged:
            lo += keep.shape[-1]


def combine(parts, flags, merged=False):
    steps = [p.order[1] if len(p.order) > 1 else None for p in parts]
    ncol = 1 if merged or parts[0].keep.size < 2**18 else 3

    def spec(shape):
        block = shape[:-1] + (shape[-1] // ncol,)
        return pl.BlockSpec(block, lambda g: (0,) * (len(shape) - 1) + (g,))

    ins, shapes = [], []
    for p, o in zip(parts, steps):
        ins += [p.keep, p.got]
        s = p.keep.shape
        if o is None:
            shapes.append(jax.ShapeDtypeStruct(s, F32))
        else:
            s = s[1:] if o == "y" else s[:-2] + (s[-2] // 2, s[-1])
            shapes += [jax.ShapeDtypeStruct(s, BF16)] * 2
    if merged:
        s = (shapes[0].shape[0], sum(p.keep.shape[-1] for p in parts))
        shapes = [jax.ShapeDtypeStruct(s, BF16)] * 2
    outs = pl.pallas_call(
        functools.partial(combine_kernel, steps, merged),
        grid=(ncol,),
        in_specs=[SMEM] + [spec(a.shape) for a in ins],
        out_specs=[spec(a.shape) for a in shapes],
        out_shape=shapes,
        name="combine",
        cost_estimate=cost(3),
    )(flags, *ins)
    if merged:
        return Part(outs[0], outs[1], parts[0].order[1:])
    if steps[0] is None:
        return list(outs)
    return [
        Part(outs[2 * k], outs[2 * k + 1], p.order[1:]) for k, p in enumerate(parts)
    ]


class Part:
    def __init__(self, keep, send, order):
        self.keep, self.send, self.order = keep, send, list(order)

    def go(self, n_dp):
        o = self.order[0]
        self.got = y_swap(self.send) if o == "y" else dp_swap(self.send, o, n_dp)


def attn_bwd_kernel(layer, half, *refs):
    (g_i, own, oth, mid, qkv, att, lse, start, gain, w) = refs[:10]
    (gm_o, low_o, dqkv_o, part_o, sums_o, qvs_o, k_t, dk, dv, dq_t) = refs[10:]
    g = pl.program_id(0)

    @pl.when(g == 0)
    def _():
        sums_o[...] = jnp.zeros_like(sums_o)
        qvs_o[...] = jnp.zeros_like(qvs_o)
        dk[...] = jnp.zeros_like(dk)
        dv[...] = jnp.zeros_like(dv)
        for b in range(LEN // BT):
            block = qkv[BT * b : BT * (b + 1), half : 2 * half].astype(F32)
            k_t[:, BT * b : BT * (b + 1)] = jnp.transpose(block).astype(BF16)

    gm, g_gain, g_shift = norm_back(
        g_i[...].astype(F32), own[...], oth[...], mid[...], gain[layer, 1:2, :].astype(F32)
    )
    gm_o[...] = gm
    sums_o[0:1, :] += colsum(g_gain)
    sums_o[1:2, :] += colsum(g_shift)
    sums_o[2:3, :] += colsum(gm)
    low = gm.astype(BF16)
    low_o[...] = low
    d_att = dot(low, w[:, 3 * half :]).astype(BF16)
    prod = d_att.astype(F32) * att[...].astype(F32)
    head = lax.broadcasted_iota(jnp.int32, (8, half), 1) // HD
    pick = (head == lax.broadcasted_iota(jnp.int32, (8, half), 0)).astype(F32)
    inner = lax.dot_general(
        pick,
        prod,
        (((1,), (1,)), ((), ())),
        preferred_element_type=F32,
        precision=lax.Precision.HIGHEST,
    )
    rows = pl.ds(pl.multiple_of(g * BT, BT), BT)
    q = qkv[rows, :half] * jnp.asarray(1.0 / math.sqrt(HD), BF16)
    for s in range(BT // QB):
        i = g * (BT // QB) + s
        ks = pl.multiple_of(jnp.maximum(i - DOC_MOST // QB, 0) * QB, QB)
        bias = window_bias(start, i, ks)
        cols = pl.ds(pl.multiple_of(i * QB, QB), QB)
        win = pl.ds(ks, KW)
        for p in range(half // 128):
            lo = 128 * p
            qq = head_pair(q[QB * s : QB * (s + 1), lo : lo + 128])
            oo = head_pair(d_att[QB * s : QB * (s + 1), lo : lo + 128])
            kp = qkv[win, half + lo : half + lo + 128]
            vp = qkv[win, 2 * half + lo : 2 * half + lo + 128]
            total = jnp.concatenate(
                [lse[2 * p : 2 * p + 1, cols], lse[2 * p + 1 : 2 * p + 2, cols]], axis=1
            )
            inn = jnp.concatenate(
                [
                    inner[2 * p : 2 * p + 1, QB * s : QB * (s + 1)],
                    inner[2 * p + 1 : 2 * p + 2, QB * s : QB * (s + 1)],
                ],
                axis=1,
            )
            probs = jnp.exp(dot(kp, qq, 1, 1) + bias - total)
            d_probs = dot(vp, oo, 1, 1)
            ds = (probs * (d_probs - inn)).astype(BF16)
            dv[win, lo : lo + 128] += dot(probs.astype(BF16), oo)
            dk[win, lo : lo + 128] += dot(ds, qq)
            dqt = dot(k_t[lo : lo + 128, win], ds)
            dq_t[lo : lo + HD, :] = dqt[:HD, :QB]
            dq_t[lo + HD : lo + 128, :] = dqt[HD:, QB:]
        dq = (jnp.transpose(dq_t[...]) * (1.0 / math.sqrt(HD))).astype(BF16)
        dqkv_o[cols, :half] = dq
        qvs_o[0:1, :] += colsum(dq.astype(F32))

    @pl.when(g == pl.num_programs(0) - 1)
    def _():
        dqkv_o[:, half : 2 * half] = dk[...].astype(BF16)
        dvb = dv[...].astype(BF16)
        dqkv_o[:, 2 * half :] = dvb
        qvs_o[1:2, :] = colsum(dvb.astype(F32))
        for b in range(LEN // BT):
            part = dot(dqkv_o[BT * b : BT * (b + 1), :], w[:, : 3 * half], 1, 1)
            part_o[BT * b : BT * (b + 1), :] = part.astype(BF16)


def attn_bwd(layer, g, own, oth, mid, qkv, att, lse, start, gain, w):
    d = mid.shape[1]
    half = att.shape[1]
    ins = [g, own, oth, mid, qkv, att, lse, start, gain, w]
    specs = [rows_spec(d)] * 4 + [full_spec(qkv.shape), rows_spec(half)]
    specs += [full_spec(a.shape) for a in ins[6:]]
    return pl.pallas_call(
        functools.partial(attn_bwd_kernel, layer, half),
        grid=(LEN // BT,),
        in_specs=specs,
        out_specs=[
            rows_spec(d),
            rows_spec(d),
            full_spec((LEN, 3 * half)),
            full_spec((LEN, d)),
            full_spec((8, d)),
            full_spec((8, half)),
        ],
        out_shape=[
            jax.ShapeDtypeStruct((LEN, d), F32),
            jax.ShapeDtypeStruct((LEN, d), BF16),
            jax.ShapeDtypeStruct((LEN, 3 * half), BF16),
            jax.ShapeDtypeStruct((LEN, d), BF16),
            jax.ShapeDtypeStruct((8, d), F32),
            jax.ShapeDtypeStruct((8, half), F32),
        ],
        scratch_shapes=[
            pltpu.VMEM((half, LEN), BF16),
            pltpu.VMEM((LEN, half), F32),
            pltpu.VMEM((LEN, half), F32),
            pltpu.VMEM((half, QB), F32),
        ],
        name=f"attn_bwd_{layer}",
        cost_estimate=cost(24),
    )(*ins)


def norm_bwd_kernel(layer, g, own, oth, x, gain, g_o, sums_o):
    @pl.when(pl.program_id(0) == 0)
    def _():
        sums_o[...] = jnp.zeros_like(sums_o)

    out, g_gain, g_shift = norm_back(
        g[...], own[...], oth[...], x[...], gain[layer, 0:1, :].astype(F32)
    )
    g_o[...] = out
    sums_o[0:1, :] += colsum(g_gain)
    sums_o[1:2, :] += colsum(g_shift)


def norm_bwd(layer, g, own, oth, x, gain):
    d = x.shape[1]
    return pl.pallas_call(
        functools.partial(norm_bwd_kernel, layer),
        grid=(LEN // BT,),
        in_specs=[rows_spec(d)] * 4 + [full_spec(gain.shape)],
        out_specs=[rows_spec(d), full_spec((8, d))],
        out_shape=[jax.ShapeDtypeStruct((LEN, d), F32), jax.ShapeDtypeStruct((8, d), F32)],
        name=f"norm_bwd_{layer}",
        cost_estimate=cost(1),
    )(g, own, oth, x, gain)


def core_swap(a):
    return lax.ppermute(a, "mp", [(i, i ^ 1) for i in range(4)])


def y_swap(a):
    return lax.ppermute(a, "mp", [(i, i ^ 2) for i in range(4)])


def dp_swap(a, bit, n_dp):
    return lax.ppermute(a, "dp", [(i, i ^ (1 << bit)) for i in range(n_dp)])


def pick(flag, zero, one):
    return jnp.where(flag == 0, zero, one)


class Place:
    def __init__(self, n_dp):
        mp = lax.axis_index("mp")
        self.n_dp = n_dp
        self.bits = n_dp.bit_length() - 1
        self.y = mp // 2
        self.c = mp % 2
        self.dp = lax.axis_index("dp")

    def dp_bit(self, b):
        return (self.dp >> b) & 1


def row_pieces(a, at):
    rows = a.reshape(2, LEN, a.shape[1])
    return pick(at.y, rows[0], rows[1]), pick(at.y, rows[1], rows[0])


def join_row(mine, far, at):
    mine_c = core_swap(mine)
    far_c = core_swap(far)

    def joined(here, there):
        return [pick(at.c, here, there), pick(at.c, there, here)]

    near2, far2 = joined(mine, mine_c), joined(far, far_c)
    return jnp.concatenate(
        [pick(at.y, a_, b_) for a_, b_ in zip(near2, far2)]
        + [pick(at.y, b_, a_) for a_, b_ in zip(near2, far2)],
        axis=1,
    )


def own_cols(a, at, other):
    w = a.shape[1] // 4
    halves = (a[:, : 2 * w], a[:, 2 * w :])
    h = pick(at.y, halves[1], halves[0]) if other else pick(at.y, halves[0], halves[1])
    return pick(at.c, h[:, :w], h[:, w:])


def table_scatter(t, at, rows_all):
    a = t[0] + y_swap(t[1].astype(BF16)).astype(F32)
    top = at.bits - 1
    half = rows_all // 2
    hi = [(i, i ^ (1 << top)) for i in range(at.n_dp) if i >> top & 1]
    a = a + lax.ppermute(a.astype(BF16), "dp", hi).astype(F32)
    a = pick(at.dp_bit(top), a, jnp.zeros_like(a))
    a = jnp.pad(a, ((0, half - a.shape[0]), (0, 0)))
    for b in range(top - 1, -1, -1):
        r = a.shape[0] // 2
        f = at.dp_bit(b)
        got = dp_swap(pick(f, a[r:], a[:r]).astype(BF16), b, at.n_dp)
        a = pick(f, a[:r], a[r:]) + got.astype(F32)
    return a


def small_scatter(shared, own, oth, at):
    n = at.n_dp
    got = y_swap(jnp.concatenate([shared, oth], axis=0))
    a = jnp.concatenate([shared, own], axis=0) + got
    r, d = a.shape
    a = a.reshape(r, n, d // n).transpose(1, 0, 2)
    for b in range(at.bits - 1, -1, -1):
        h = a.shape[0] // 2
        f = at.dp_bit(b)
        a = pick(f, a[:h], a[h:]) + dp_swap(pick(f, a[h:], a[:h]), b, n)
    return a[0]


def bar(*vals):
    return lax.optimization_barrier(vals)


def doc_starts(doc_ids):
    row_index = jnp.broadcast_to(jnp.arange(doc_ids.shape[1], dtype=jnp.int32), doc_ids.shape)
    previous = jnp.concatenate([doc_ids[:, :1] - 1, doc_ids[:, :-1]], axis=1)
    starts = jnp.where(doc_ids != previous, row_index, 0)
    return lax.cummax(starts, axis=1)


def on_device(
    n_dp,
    tokens,
    doc_ids,
    positions_table,
    norm_gain,
    norm_shift,
    joined_projection_weight,
    qv_bias,
    w_out,
    out_bias,
    w_fc,
    fc_bias,
    w_proj,
    cotangent,
):
    at = Place(n_dp)
    d = positions_table.shape[1]
    share = joined_projection_weight.shape[-1]
    f = w_fc.shape[-1]
    bits = list(range(2, at.bits))
    flags = jnp.stack([at.dp_bit(b) for b in range(at.bits)]).astype(jnp.int32)

    b = at.dp_bit(0) ^ at.dp_bit(1)
    flag = b.reshape(1)
    gain, shift = norm_gain, norm_shift

    a_own = [
        jnp.concatenate([joined_projection_weight[l].reshape(d, 3 * share), w_out[l].T], axis=1)
        for l in range(2)
    ]
    biases = jnp.concatenate([qv_bias.reshape(-1), fc_bias.reshape(-1)]).reshape(-1, d)
    biases = jnp.pad(biases, ((0, -biases.shape[0] % 8), (0, 0)))
    r = d // 2

    def half_rows(w):
        return lax.dynamic_slice_in_dim(w, b * r, r, 0)

    def x_swap(w):
        return dp_swap(w, 0, n_dp)

    def z_swap(w):
        return dp_swap(w, 1, n_dp)

    def by_two(one, lo=0):
        return x_swap(one[lo : lo + r // 2]), z_swap(one[lo + r // 2 : lo + r])

    def plan_one(lo=0):
        return ((lo, r, 0, 0), (0, r, 1, 0))

    def plan_two(lo=0):
        return ((lo, r, 0, 0), (0, r // 2, 1, 0), (0, r // 2, 1, r // 2))

    tok_mine, tok_theirs = row_pieces(tokens, at)
    tok_far = y_swap(tok_theirs)
    a_one0 = y_swap(jnp.concatenate([half_rows(a_own[0]), biases], axis=0))

    starts = doc_starts(doc_ids)
    start = pick(at.y, starts[0:1], starts[1:2])
    place = jnp.arange(LEN, dtype=jnp.int32) - start[0]
    hot = (place[:, None] == jnp.arange(DOC_MOST, dtype=jnp.int32)[None, :]).astype(BF16)
    embedded = dot(hot, positions_table[:DOC_MOST]).astype(BF16)

    tok_far, a_one0, embedded, hot = bar(tok_far, a_one0, embedded, hot)
    a_x, a_z = by_two(a_one0)
    fc_one0 = y_swap(half_rows(w_fc[0]))
    full_tokens = join_row(tok_mine, tok_far, at)
    small = a_one0[r:].reshape(-1)
    nq = qv_bias.size
    qvb = jnp.concatenate([qv_bias, small[:nq].reshape(qv_bias.shape)], axis=-1)
    fcb = jnp.concatenate(
        [fc_bias, small[nq : nq + fc_bias.size].reshape(fc_bias.shape)], axis=-1
    )
    send_y = jnp.concatenate([half_rows(w_proj[0]), half_rows(a_own[1])], axis=0)
    a_x, a_z, fc_one0, full_tokens, send_y = bar(a_x, a_z, fc_one0, full_tokens, send_y)

    fc_two0 = x_swap(fc_one0)
    pj_a1 = y_swap(send_y)
    x0, n0, qkv0, att0, lse0, part, wa0 = attn_fwd(
        0,
        (full_tokens, embedded),
        out_bias,
        flag,
        start,
        gain,
        shift,
        qvb,
        a_own[0],
        (plan_two(), (a_one0, a_x, a_z)),
    )
    part, x0, fc_two0, pj_a1 = bar(part, x0, fc_two0, pj_a1)
    far = core_swap(part)
    pj_x, pj_z = by_two(pj_a1)
    far, pj_x, pj_z = bar(far, pj_x, pj_z)
    mlp0 = (
        w_fc,
        (plan_one(), (fc_one0, fc_two0)),
        w_proj,
        (plan_two(), (pj_a1, pj_x, pj_z)),
    )
    a_two1 = x_swap(pj_a1[r:])
    fc_one1 = y_swap(half_rows(w_fc[1]))
    mid0, nn0, hid0, part2 = mlp_fwd(
        0, x0, part, far, out_bias, gain, shift, fcb, flag, mlp0
    )
    part2, mid0, a_two1, fc_one1 = bar(part2, mid0, a_two1, fc_one1)
    far = core_swap(part2)
    (far,) = bar(far)
    fc_two1 = x_swap(fc_one1)
    pj_one1 = y_swap(half_rows(w_proj[1]))
    cot_mine, cot_theirs = row_pieces(cotangent, at)
    cot_far = y_swap(cot_theirs)
    x1, n1, qkv1, att1, lse1, part, wa1 = attn_fwd(
        1,
        (mid0, part2, far),
        out_bias,
        flag,
        start,
        gain,
        shift,
        qvb,
        a_own[1],
        (plan_one(r), (pj_a1, a_two1)),
    )
    part, x1, fc_two1, cot_far, pj_one1 = bar(part, x1, fc_two1, cot_far, pj_one1)
    far = core_swap(part)
    pj_x, pj_z = by_two(pj_one1)
    cot = join_row(cot_mine, cot_far, at)
    far, cot, pj_x, pj_z = bar(far, cot, pj_x, pj_z)
    mlp1 = (
        w_fc,
        (plan_one(), (fc_one1, fc_two1)),
        w_proj,
        (plan_two(), (pj_one1, pj_x, pj_z)),
    )
    mid1, nn1, act, gh, part_out, part, sumg1, sumh1 = mlp_both(
        1, x1, part, far, cot, out_bias, gain, shift, fcb, flag, mlp1
    )

    def go(*parts):
        for p in parts:
            p.go(n_dp)

    def bar_parts(parts, sent, *vals):
        name = "send" if sent else "got"
        out = bar(*[getattr(p, name) for p in parts], *vals)
        for p, v in zip(parts, out):
            setattr(p, name, v)
        return out[len(parts) :]

    part, part_out, mid1, gh, act = bar(part, part_out, mid1, gh, act)
    far = core_swap(part)
    far_out = core_swap(part_out)
    o_fc, o_pj = ["y", 1, 0] + bits, [0, "y", 1] + bits
    o_a, o_b = [0, 1, "y"] + bits, [1, "y", 0] + bits
    fc1, pj1 = dw_mlp(1, nn1, cot, gh, act, (o_fc, o_pj), flags)
    far, far_out, mid1, part_out = bar_parts([fc1, pj1], True, far, far_out, mid1, part_out)
    go(fc1, pj1)
    gm1, m_low, dqkv, part, sums1, qvs1 = attn_bwd(
        1, cot, part, far, mid1, qkv1, att1, lse1, start, gain, wa1
    )
    part, gm1, m_low, dqkv, far_out, part_out = bar_parts(
        [fc1, pj1], False, part, gm1, m_low, dqkv, far_out, part_out
    )
    far = core_swap(part)
    fc1, pj1 = combine([fc1, pj1], flags)
    result = (
        mid1 + (part_out.astype(F32) + far_out.astype(F32)) + out_bias[1, 1].astype(F32)
    ).astype(BF16)
    out_near, out_send = own_cols(result, at, False), own_cols(result, at, True)
    out_near, out_send, far, m_low = bar_parts([fc1, pj1], True, out_near, out_send, far, m_low)
    out_far = y_swap(out_send)
    aa1, ab1 = dw_attn(1, n1, m_low, dqkv, att1, (o_a, ["y", 1, 0] + bits), flags)
    far, gm1, out_far = bar_parts([aa1, ab1], True, far, gm1, out_far)
    go(fc1, pj1, aa1)
    g0, g_low, act, gh, part, sums0b, sumh0 = mlp_bwd(
        0, gm1, part, far, x1, hid0, gain, flag, mlp0
    )
    part, g0, g_low, act, gh = bar_parts([fc1, pj1, aa1], False, part, g0, g_low, act, gh)
    far = core_swap(part)
    fc1, pj1, aa1 = combine([fc1, pj1, aa1], flags)
    far, g_low, act, gh = bar_parts([fc1, pj1, aa1, ab1], True, far, g_low, act, gh)
    go(ab1, fc1, pj1, aa1)
    fc0, pj0 = dw_mlp(0, nn0, g_low, gh, act, (o_fc, o_pj), flags)
    far, fc0.send, pj0.send, g0 = bar_parts(
        [ab1, fc1, pj1, aa1], False, far, fc0.send, pj0.send, g0
    )
    last1 = combine([fc1, pj1], flags, merged=True)
    aa1, ab1 = combine([aa1, ab1], flags)
    far, g0, part = bar_parts([last1, aa1, ab1, fc0, pj0], True, far, g0, part)
    go(fc0, pj0, aa1, ab1, last1)
    gm0, m_low, dqkv, part, sums0, qvs0 = attn_bwd(
        0, g0, part, far, mid0, qkv0, att0, lse0, start, gain, wa0
    )
    part, gm0, m_low, dqkv, out_near, out_far = bar_parts(
        [fc0, pj0, aa1, ab1, last1], False, part, gm0, m_low, dqkv, out_near, out_far
    )
    far = core_swap(part)
    fc0, pj0 = combine([fc0, pj0], flags)
    (ab1,) = combine([ab1], flags)
    far, m_low, dqkv = bar_parts([fc0, pj0, ab1], True, far, m_low, dqkv)
    go(fc0, pj0, ab1)
    aa0, ab0 = dw_attn(0, n0, m_low, dqkv, att0, (o_a, o_b), flags)
    far, gm0, part = bar_parts([aa0, ab0], True, far, gm0, part)
    go(aa0, ab0)
    g, sums0a = norm_bwd(0, gm0, part, far, x0, gain)
    sums = (sums0a, sums0, sums0b, sums1, sumg1, sumh0, sumh1, qvs0, qvs1)
    g, *sums = bar_parts([fc0, pj0, ab1], False, g, *sums)
    sums0a, sums0, sums0b, sums1, sumg1, sumh0, sumh1, qvs0, qvs1 = sums
    near = own_cols(g, at, False)
    far_send = own_cols(g, at, True).astype(BF16)
    fc0, pj0 = combine([fc0, pj0], flags)
    near, far_send = bar_parts([fc0, pj0], True, near, far_send)
    g_far = y_swap(far_send)
    go(fc0, pj0)

    def qv_row(lo):
        parts = jnp.stack([q[j, lo : lo + share] for q in (qvs0, qvs1) for j in range(2)])
        return parts.reshape(-1, n_dp, share // n_dp).transpose(1, 0, 2).reshape(1, d)

    shared = jnp.stack(
        [sums0a[0], sums0[0], sums0b[0], sums1[0]]
        + [sums0a[1], sums0[1], sums0b[1], sums1[1]]
        + [sums0[2], sums0b[2], sums1[2], sumg1[0]]
    )
    own = jnp.concatenate([jnp.stack([sumh0[0, :f], sumh1[0, :f]]), qv_row(0)])
    oth = jnp.concatenate([jnp.stack([sumh0[0, f:], sumh1[0, f:]]), qv_row(share)])
    table = lax.dot_general(
        hot,
        jnp.concatenate([near.astype(BF16), far_send], axis=1),
        (((0,), (0,)), ((), ())),
        preferred_element_type=F32,
    )
    table, shared, own, oth, near = bar_parts([aa0, ab0], False, table, shared, own, oth, near)
    aa0, ab0 = combine([aa0, ab0], flags)
    go(aa0, ab0)
    grad_positions = table_scatter(
        jnp.stack([table[:, :share], table[:, share:]]), at, positions_table.shape[0]
    )
    s = small_scatter(shared, own, oth, at)
    last0 = combine([fc0, pj0, aa1, ab1], flags, merged=True)
    go(last0)
    aa0, ab0 = combine([aa0, ab0], flags)
    go(aa0, ab0)
    last2 = combine([aa0, ab0], flags, merged=True)
    go(last2)
    lasts = [last1, last0, last2]
    while len(lasts[0].order) > 1:
        lasts = combine(lasts, flags)
        go(*lasts)
    l1, l0, l2 = combine(lasts, flags)
    f2 = 2 * f
    r_fc = (l0[:, :f], l1[:, :f])
    r_pj = (l0[:, f:f2], l1[:, f:])
    r_ao = (l2, l0[:, f2:])
    g_far = g_far.astype(F32)
    grad_tokens = jnp.concatenate([pick(at.y, near, g_far), pick(at.y, g_far, near)], axis=0)
    out = jnp.concatenate([pick(at.y, out_near, out_far), pick(at.y, out_far, out_near)], axis=0)
    w = d // n_dp
    ao = jnp.stack(r_ao)
    return (
        out,
        grad_tokens,
        grad_positions,
        s[0:4].reshape(2, 2, w),
        s[4:8].reshape(2, 2, w),
        ao[..., : 3 * share].reshape(2, w, 3, share),
        s[14].reshape(2, 2, w // 4),
        jnp.swapaxes(ao[..., 3 * share :], 1, 2),
        s[8:12].reshape(2, 2, w),
        jnp.stack(r_fc),
        s[12:14],
        jnp.stack([p.T for p in r_pj]),
    )


def solution(mesh):
    n_dp = mesh.shape["dp"]
    in_specs = (
        P("dp", "mp"),
        P("dp", None),
        P(),
        P(),
        P(),
        P(None, None, None, "mp"),
        P(None, None, "mp"),
        P(None, "mp", None),
        P(),
        P(None, None, "mp"),
        P(None, "mp"),
        P(None, "mp", None),
        P("dp", "mp"),
    )
    out_specs = (
        P("dp", "mp"),
        P("dp", "mp"),
        P("dp", "mp"),
        P(None, None, "dp"),
        P(None, None, "dp"),
        P(None, "dp", None, "mp"),
        P(None, None, ("mp", "dp")),
        P(None, "mp", "dp"),
        P(None, None, "dp"),
        P(None, "dp", "mp"),
        P(None, ("mp", "dp")),
        P(None, "mp", "dp"),
    )
    return jax.shard_map(
        functools.partial(on_device, n_dp),
        mesh=mesh,
        in_specs=in_specs,
        out_specs=out_specs,
        check_vma=False,
    )
```

```python
import functools
import math

import jax
import jax.numpy as jnp
from jax import lax
from jax.experimental import pallas as pl
from jax.experimental.pallas import tpu as pltpu
from jax.sharding import PartitionSpec as P

HD = 64
LEN = 1024
DOC_MOST = 384
EPS = 1e-05
BT = 256
QB = 128
KW = QB + DOC_MOST
F32 = jnp.float32
BF16 = jnp.bfloat16
GELU_C = math.sqrt(2.0 / math.pi)


ANY = pl.BlockSpec(memory_space=pl.ANY)
SMEM = pl.BlockSpec(memory_space=pltpu.SMEM)


def cost(us):
    return pl.CostEstimate(flops=int(us * 1.15e9), transcendentals=0, bytes_accessed=0)


def full_spec(shape):
    return pl.BlockSpec(shape, lambda g: (0,) * len(shape))


def rows_spec(width):
    return pl.BlockSpec((BT, width), lambda g: (g, 0))


def dot(a, b, ca=1, cb=0):
    return lax.dot_general(a, b, (((ca,), (cb,)), ((), ())), preferred_element_type=F32)


def normed_parts(v):
    centred = v - jnp.mean(v, axis=-1, keepdims=True)
    variance = jnp.mean(centred * centred, axis=-1, keepdims=True)
    rstd = lax.rsqrt(variance + EPS)
    return centred * rstd, rstd


def norm_back(g, own, oth, v, gain):
    grad = own.astype(F32) + oth.astype(F32)
    xhat, rstd = normed_parts(v)
    gn = grad * gain
    out = g + rstd * (
        gn
        - jnp.mean(gn, axis=-1, keepdims=True)
        - xhat * jnp.mean(gn * xhat, axis=-1, keepdims=True)
    )
    return out, grad * xhat, grad


def colsum(v):
    return jnp.sum(v, axis=0, keepdims=True)


def head_pair(block):
    lane = lax.broadcasted_iota(jnp.int32, block.shape, 1)
    zero = jnp.zeros_like(block)
    return jnp.concatenate(
        [jnp.where(lane < HD, block, zero), jnp.where(lane < HD, zero, block)], axis=0
    )


def window_bias(start_ref, i, ks):
    kidx = lax.broadcasted_iota(jnp.int32, (KW, QB), 0) + ks
    qidx = lax.broadcasted_iota(jnp.int32, (KW, QB), 1) + i * QB
    first = start_ref[0:1, pl.ds(pl.multiple_of(i * QB, QB), QB)]
    bias = jnp.where((kidx >= first) & (kidx <= qidx), 0.0, -1e30).astype(F32)
    return jnp.concatenate([bias, bias], axis=1)


def copies(pairs, sems):
    out = [pltpu.make_async_copy(a, b, sems.at[j]) for j, (a, b) in enumerate(pairs)]
    for c in out:
        c.start()
    return out


def join_pieces(flag, plan, refs, dst, cols=slice(None)):
    r = dst.shape[0] // 2
    out = []
    for (lo, n, other, off), ref in zip(plan, refs):
        row = (1 - flag if other else flag) * r + off
        out.append((ref.at[pl.ds(lo, n)], dst.at[pl.ds(pl.multiple_of(row, 8), n), cols]))
    return out


def gelu_parts(v):
    v2 = v * v
    t = jnp.tanh(GELU_C * v * (1.0 + 0.044715 * v2))
    cdf = 0.5 * (1.0 + t)
    slope = cdf + (0.5 * GELU_C) * v * (1.0 - t * t) * (1.0 + (3 * 0.044715) * v2)
    return v * cdf, slope


def gained(xhat, gain, shift, layer, which):
    row = slice(which, which + 1)
    return (xhat * gain[layer, row, :].astype(F32) + shift[layer, row, :].astype(F32)).astype(BF16)


def attn_fwd_kernel(layer, first, half, plan, *refs):
    if first:
        (tok, emb, flag, start, gain, shift, qvb, a_own) = refs[:8]
        rest = refs[8:]
        x = tok[...].astype(F32) + emb[...].astype(F32)
    else:
        (mid, own, oth, outb, flag, start, gain, shift, qvb, a_own) = refs[:10]
        rest = refs[10:]
        x = (
            mid[...]
            + (own[...].astype(F32) + oth[...].astype(F32))
            + outb[layer - 1, 1:2, :].astype(F32)
        )
    a_refs, rest = rest[: len(plan)], rest[len(plan) :]
    x_o, n_o, qkv_o, att_o, lse_o, part_o, w_o, v_t, o_t, a_buf, sems = rest
    g = pl.program_id(0)
    sh = half // 2

    @pl.when(g == 0)
    def _():
        moves = copies(
            [(a_own, a_buf.at[0])] + join_pieces(flag[0], plan, a_refs, a_buf.at[1]), sems
        )
        qkv_o[pl.ds(BT, KW - BT), half : 2 * half] = jnp.zeros((KW - BT, half), BF16)
        v_t[:, pl.ds(BT, KW - BT)] = jnp.zeros((half, KW - BT), BF16)
        lse_o[...] = jnp.zeros_like(lse_o)
        for m in moves:
            m.wait()
        for j in range(4):
            for s in range(2):
                w_o[:, (2 * j + s) * sh : (2 * j + s + 1) * sh] = a_buf[s, :, j * sh : (j + 1) * sh]

    x_o[...] = x
    xhat, _ = normed_parts(x)
    normed = gained(xhat, gain, shift, layer, 0)
    n_o[...] = normed
    qkv = dot(normed, w_o[:, : 3 * half])
    q = (qkv[:, :half] + qvb[layer, 0:1, :].astype(F32)).astype(BF16)
    k = qkv[:, half : 2 * half].astype(BF16)
    v = qkv[:, 2 * half :] + qvb[layer, 1:2, :].astype(F32)
    rows = pl.ds(pl.multiple_of(g * BT, BT), BT)
    qkv_o[rows, :half] = q
    qkv_o[rows, half : 2 * half] = k
    qkv_o[rows, 2 * half :] = v.astype(BF16)
    v_t[:, rows] = jnp.transpose(v).astype(BF16)
    q = q * jnp.asarray(1.0 / math.sqrt(HD), BF16)
    for s in range(BT // QB):
        i = g * (BT // QB) + s
        ks = pl.multiple_of(jnp.maximum(i - DOC_MOST // QB, 0) * QB, QB)
        bias = window_bias(start, i, ks)
        cols = pl.ds(pl.multiple_of(i * QB, QB), QB)
        for p in range(half // 128):
            lo = 128 * p
            qq = head_pair(q[QB * s : QB * (s + 1), lo : lo + 128])
            kp = qkv_o[pl.ds(ks, KW), half + lo : half + lo + 128]
            scores = dot(kp, qq, 1, 1) + bias
            peak = jnp.max(scores, axis=0, keepdims=True)
            e = jnp.exp(scores - peak)
            total = jnp.sum(e, axis=0, keepdims=True)
            ot = dot(v_t[lo : lo + 128, pl.ds(ks, KW)], e.astype(BF16))
            inv = 1.0 / total
            o_t[lo : lo + HD, :] = ot[:HD, :QB] * inv[:, :QB]
            o_t[lo + HD : lo + 128, :] = ot[HD:, QB:] * inv[:, QB:]
            lse = peak + jnp.log(total)
            lse_o[2 * p : 2 * p + 1, cols] = lse[:, :QB]
            lse_o[2 * p + 1 : 2 * p + 2, cols] = lse[:, QB:]
        att_o[QB * s : QB * (s + 1), :] = jnp.transpose(o_t[...]).astype(BF16)
    part_o[...] = dot(att_o[...], w_o[:, 3 * half :], 1, 1).astype(BF16)


def attn_fwd(layer, stream_in, outb, flag, start, gain, shift, qvb, a_own, a_oth):
    first = layer == 0
    d = gain.shape[-1]
    half = a_own.shape[1] // 2
    ins = list(stream_in)
    specs = [rows_spec(d) for _ in ins]
    if not first:
        ins.append(outb)
        specs.append(full_spec(outb.shape))
    plan, arrays = a_oth
    ins += [flag, start, gain, shift, qvb, a_own, *arrays]
    specs += [SMEM] + [full_spec(a.shape) for a in (start, gain, shift, qvb)]
    specs += [ANY] * (1 + len(arrays))
    return pl.pallas_call(
        functools.partial(attn_fwd_kernel, layer, first, half, plan),
        grid=(LEN // BT,),
        in_specs=specs,
        out_specs=[
            rows_spec(d),
            rows_spec(d),
            full_spec((LEN, 3 * half)),
            rows_spec(half),
            full_spec((8, LEN)),
            rows_spec(d),
            full_spec((d, 4 * half)),
        ],
        out_shape=[
            jax.ShapeDtypeStruct((LEN, d), F32),
            jax.ShapeDtypeStruct((LEN, d), BF16),
            jax.ShapeDtypeStruct((LEN, 3 * half), BF16),
            jax.ShapeDtypeStruct((LEN, half), BF16),
            jax.ShapeDtypeStruct((8, LEN), F32),
            jax.ShapeDtypeStruct((LEN, d), BF16),
            jax.ShapeDtypeStruct((d, 4 * half), BF16),
        ],
        scratch_shapes=[
            pltpu.VMEM((half, LEN), BF16),
            pltpu.VMEM((half, QB), F32),
            pltpu.VMEM((2, d, 2 * half), BF16),
            pltpu.SemaphoreType.DMA((1 + len(plan),)),
        ],
        name=f"attn_fwd_{layer}",
        cost_estimate=cost(22),
    )(*ins)


def load_mlp(layer, flag, plans, weights, wfc, wproj, sems):
    d = wfc.shape[0]
    f = wfc.shape[1] // 2
    n = len(plans[0])
    return copies(
        [(weights[0].at[layer], wfc.at[:, pl.ds(0, f)])]
        + join_pieces(flag[0], plans[0], weights[2 : 2 + n], wfc, pl.ds(f, f))
        + [(weights[1].at[layer], wproj.at[pl.ds(0, f)])]
        + join_pieces(flag[0], plans[1], weights[2 + n :], wproj.at[pl.ds(f, f)]),
        sems,
    )


def mlp_scratch(d, f2, plans):
    return [
        pltpu.VMEM((d, f2), BF16),
        pltpu.VMEM((f2, d), BF16),
        pltpu.SemaphoreType.DMA((2 + len(plans[0]) + len(plans[1]),)),
    ]


def mlp_weights(weights):
    w_fc, fc_oth, w_proj, pj_oth = weights
    return (fc_oth[0], pj_oth[0]), [w_fc, w_proj, *fc_oth[1], *pj_oth[1]]


def mlp_fwd_kernel(layer, plans, x, own, oth, outb, gain, shift, fcb, flag, *refs):
    nw = 2 + len(plans[0]) + len(plans[1])
    weights = refs[:nw]
    mid_o, n_o, h_o, part_o, wfc, wproj, sems = refs[nw:]

    @pl.when(pl.program_id(0) == 0)
    def _():
        for m in load_mlp(layer, flag, plans, weights, wfc, wproj, sems):
            m.wait()

    mid = (
        x[...]
        + (own[...].astype(F32) + oth[...].astype(F32))
        + outb[layer, 0:1, :].astype(F32)
    )
    mid_o[...] = mid
    xhat, _ = normed_parts(mid)
    normed = gained(xhat, gain, shift, layer, 1)
    n_o[...] = normed
    hidden = dot(normed, wfc[...]) + fcb[layer : layer + 1, :].astype(F32)
    h_o[...] = hidden.astype(BF16)
    t = jnp.tanh(GELU_C * hidden * (1.0 + 0.044715 * hidden * hidden))
    act = (0.5 * hidden * (1.0 + t)).astype(BF16)
    part_o[...] = dot(act, wproj[...]).astype(BF16)


def mlp_fwd(layer, x, own, oth, outb, gain, shift, fcb, flag, weights):
    d = x.shape[1]
    f = fcb.shape[1]
    plans, arrays = mlp_weights(weights)
    ins = [x, own, oth, outb, gain, shift, fcb, flag, *arrays]
    specs = [rows_spec(d)] * 3 + [full_spec(a.shape) for a in ins[3:7]] + [SMEM] + [ANY] * len(arrays)
    return pl.pallas_call(
        functools.partial(mlp_fwd_kernel, layer, plans),
        grid=(LEN // BT,),
        in_specs=specs,
        out_specs=[rows_spec(d), rows_spec(d), rows_spec(f), rows_spec(d)],
        out_shape=[
            jax.ShapeDtypeStruct((LEN, d), F32),
            jax.ShapeDtypeStruct((LEN, d), BF16),
            jax.ShapeDtypeStruct((LEN, f), BF16),
            jax.ShapeDtypeStruct((LEN, d), BF16),
        ],
        scratch_shapes=mlp_scratch(d, f, plans),
        name=f"mlp_fwd_{layer}",
        cost_estimate=cost(12),
    )(*ins)


def mlp_both_kernel(layer, plans, x, own, oth, cot, outb, gain, shift, fcb, flag, *refs):
    nw = 2 + len(plans[0]) + len(plans[1])
    weights = refs[:nw]
    mid_o, n_o, act_o, gh_o, out_o, part_o, sumg_o, sumh_o, wfc, wproj, sems = refs[nw:]

    @pl.when(pl.program_id(0) == 0)
    def _():
        moves = load_mlp(layer, flag, plans, weights, wfc, wproj, sems)
        sumg_o[...] = jnp.zeros_like(sumg_o)
        sumh_o[...] = jnp.zeros_like(sumh_o)
        for m in moves:
            m.wait()

    mid = (
        x[...]
        + (own[...].astype(F32) + oth[...].astype(F32))
        + outb[layer, 0:1, :].astype(F32)
    )
    mid_o[...] = mid
    xhat, _ = normed_parts(mid)
    normed = gained(xhat, gain, shift, layer, 1)
    n_o[...] = normed
    grad_act = dot(cot[...], wproj[...], 1, 1)
    value, slope = gelu_parts(dot(normed, wfc[...]) + fcb[layer : layer + 1, :].astype(F32))
    act = value.astype(BF16)
    act_o[...] = act
    gh = (grad_act * slope).astype(BF16)
    gh_o[...] = gh
    part_o[...] = dot(gh, wfc[...], 1, 1).astype(BF16)
    out_o[...] = dot(act, wproj[...]).astype(BF16)
    sumg_o[0:1, :] += colsum(cot[...].astype(F32))
    sumh_o[0:1, :] += colsum(gh.astype(F32))


def mlp_both(layer, x, own, oth, cot, outb, gain, shift, fcb, flag, weights):
    d = x.shape[1]
    f = fcb.shape[1]
    plans, arrays = mlp_weights(weights)
    ins = [x, own, oth, cot, outb, gain, shift, fcb, flag, *arrays]
    specs = [rows_spec(d)] * 4 + [full_spec(a.shape) for a in ins[4:8]] + [SMEM] + [ANY] * len(arrays)
    widths = [d, d, f, f, d, d]
    kinds = [F32, BF16, BF16, BF16, BF16, BF16]
    return pl.pallas_call(
        functools.partial(mlp_both_kernel, layer, plans),
        grid=(LEN // BT,),
        in_specs=specs,
        out_specs=[rows_spec(w) for w in widths] + [full_spec((8, d)), full_spec((8, f))],
        out_shape=[jax.ShapeDtypeStruct((LEN, w), k) for w, k in zip(widths, kinds)]
        + [jax.ShapeDtypeStruct((8, d), F32), jax.ShapeDtypeStruct((8, f), F32)],
        scratch_shapes=mlp_scratch(d, f, plans),
        name=f"mlp_both_{layer}",
        cost_estimate=cost(18),
    )(*ins)


def mlp_bwd_kernel(layer, plans, gm, own, oth, x, h, gain, flag, *refs):
    nw = 2 + len(plans[0]) + len(plans[1])
    weights = refs[:nw]
    g_o, low_o, act_o, gh_o, part_o, sums_o, sumh_o, wfc, wproj, sems = refs[nw:]

    @pl.when(pl.program_id(0) == 0)
    def _():
        moves = load_mlp(layer, flag, plans, weights, wfc, wproj, sems)
        sums_o[...] = jnp.zeros_like(sums_o)
        sumh_o[...] = jnp.zeros_like(sumh_o)
        for m in moves:
            m.wait()

    grad, g_gain, g_shift = norm_back(
        gm[...], own[...], oth[...], x[...], gain[layer + 1, 0:1, :].astype(F32)
    )
    sums_o[0:1, :] += colsum(g_gain)
    sums_o[1:2, :] += colsum(g_shift)
    sums_o[2:3, :] += colsum(grad)
    g_o[...] = grad
    low = grad.astype(BF16)
    low_o[...] = low
    grad_act = dot(low, wproj[...], 1, 1)
    value, slope = gelu_parts(h[...].astype(F32))
    act_o[...] = value.astype(BF16)
    gh = (grad_act * slope).astype(BF16)
    gh_o[...] = gh
    part_o[...] = dot(gh, wfc[...], 1, 1).astype(BF16)
    sumh_o[0:1, :] += colsum(gh.astype(F32))


def mlp_bwd(layer, gm, own, oth, x, h, gain, flag, weights):
    d = x.shape[1]
    f = h.shape[1]
    plans, arrays = mlp_weights(weights)
    ins = [gm, own, oth, x, h, gain, flag, *arrays]
    specs = [rows_spec(d)] * 4 + [rows_spec(f), full_spec(gain.shape), SMEM] + [ANY] * len(arrays)
    widths = [d, d, f, f, d]
    kinds = [F32, BF16, BF16, BF16, BF16]
    return pl.pallas_call(
        functools.partial(mlp_bwd_kernel, layer, plans),
        grid=(LEN // BT,),
        in_specs=specs,
        out_specs=[rows_spec(w) for w in widths] + [full_spec((8, d)), full_spec((8, f))],
        out_shape=[jax.ShapeDtypeStruct((LEN, w), k) for w, k in zip(widths, kinds)]
        + [jax.ShapeDtypeStruct((8, d), F32), jax.ShapeDtypeStruct((8, f), F32)],
        scratch_shapes=mlp_scratch(d, f, plans),
        name=f"mlp_bwd_{layer}",
        cost_estimate=cost(16),
    )(*ins)


def emit(keep, send, slot, value, order, flags):
    dims = [o for o in order if o != "y"]
    n = len(dims)
    r = value.shape[0] >> n
    value = value.astype(BF16)

    def chunks():
        for c in range(1 << n):
            yield sum(((c >> b) & 1) << (n - 1 - j) for j, b in enumerate(dims)), value[r * c : r * (c + 1)]

    def whole(out):
        for pos, v in chunks():
            out[r * pos : r * (pos + 1), :] = v

    if order[0] == "y":
        if isinstance(slot, int):
            whole(send if slot else keep)
        else:
            pl.when(slot == 0)(lambda: whole(keep))
            pl.when(slot == 1)(lambda: whole(send))
        return
    at = slot if isinstance(slot, int) else 0
    half = 1 << (n - 1)

    def split(bit):
        for pos, v in chunks():
            out = keep if pos // half == bit else send
            row = r * (pos % half)
            out[at, row : row + r, :] = v

    pl.when(flags[dims[0]] == 0)(lambda: split(0))
    pl.when(flags[dims[0]] == 1)(lambda: split(1))


def first_shape(order, d, w):
    return (d, w) if order[0] == "y" else (2, d // 2, w)


def dw_mlp_kernel(orders, flags, n, low, gh, act, *outs):
    j = pl.program_id(0)
    emit(outs[0], outs[1], j, dot(n[...], gh[...], 0, 0), orders[0], flags)
    emit(outs[2], outs[3], j, dot(low[...], act[...], 0, 0), orders[1], flags)


def dw_mlp(layer, n, low, gh, act, orders, flags):
    t, d = n.shape
    f = gh.shape[1] // 2
    col = pl.BlockSpec((t, f), lambda j: (0, j))
    shapes = [first_shape(o, d, f) for o in orders for _ in range(2)]
    specs = [
        full_spec(s) if len(s) == 2 else pl.BlockSpec((1,) + s[1:], lambda j: (j, 0, 0))
        for s in shapes
    ]
    k0, s0, k1, s1 = pl.pallas_call(
        functools.partial(dw_mlp_kernel, orders),
        grid=(2,),
        in_specs=[SMEM, full_spec(n.shape), full_spec(low.shape), col, col],
        out_specs=specs,
        out_shape=[jax.ShapeDtypeStruct(s, BF16) for s in shapes],
        name=f"dw_mlp_{layer}",
        cost_estimate=cost(9),
    )(flags, n, low, gh, act)
    return Part(k0, s0, orders[0]), Part(k1, s1, orders[1])


def dw_attn_kernel(orders, flags, n, low, dqkv, att, *outs):
    sh = att.shape[1] // 2
    qkv = dot(n[...], dqkv[...], 0, 0)
    wo = dot(low[...], att[...], 0, 0)
    for s in range(2):
        parts = [qkv[:, (2 * j + s) * sh : (2 * j + s + 1) * sh] for j in range(3)]
        parts.append(wo[:, s * sh : (s + 1) * sh])
        for j, order in enumerate(orders):
            both = jnp.concatenate(parts[2 * j : 2 * j + 2], axis=1)
            emit(outs[2 * j], outs[2 * j + 1], s, both, order, flags)


def dw_attn(layer, n, low, dqkv, att, orders, flags):
    d = n.shape[1]
    ins = (n, low, dqkv, att)
    shapes = [first_shape(o, d, att.shape[1]) for o in orders for _ in range(2)]
    k0, s0, k1, s1 = pl.pallas_call(
        functools.partial(dw_attn_kernel, orders),
        grid=(1,),
        in_specs=[SMEM] + [full_spec(a.shape) for a in ins],
        out_specs=[full_spec(s) for s in shapes],
        out_shape=[jax.ShapeDtypeStruct(s, BF16) for s in shapes],
        name=f"dw_attn_{layer}",
        cost_estimate=cost(7),
    )(flags, *ins)
    return Part(k0, s0, orders[0]), Part(k1, s1, orders[1])


def combine_kernel(steps, merged, flags, *refs):
    ins, outs = refs[: 2 * len(steps)], refs[2 * len(steps) :]
    lo = 0
    for k, o in enumerate(steps):
        keep, got = ins[2 * k : 2 * k + 2]

        def total(at):
            return keep[at].astype(F32) + got[at].astype(F32)

        if o is None:
            outs[k][...] = total(...)
            continue
        dst = outs if merged else outs[2 * k : 2 * k + 2]
        cols = slice(lo, lo + keep.shape[-1]) if merged else slice(None)
        if o == "y":
            halves = [total(0), total(1)]
        else:
            r = keep.shape[-2] // 2
            lead = (slice(None),) * (len(keep.shape) - 2)
            rows = [pl.ds(pl.multiple_of(h * r, 8), r) for h in (flags[o], 1 - flags[o])]
            halves = [total(lead + (row, slice(None))) for row in rows]
        for out, v in zip(dst, halves):
            out[..., cols] = v.astype(BF16)
        if merged:
            lo += keep.shape[-1]


def combine(parts, flags, merged=False):
    steps = [p.order[1] if len(p.order) > 1 else None for p in parts]
    wide = all(p.keep.shape[-1] % 384 == 0 for p in parts)
    ncol = 3 if wide and not merged and parts[0].keep.size >= 2**18 else 1

    def spec(shape):
        block = shape[:-1] + (shape[-1] // ncol,)
        return pl.BlockSpec(block, lambda g: (0,) * (len(shape) - 1) + (g,))

    ins, shapes = [], []
    for p, o in zip(parts, steps):
        ins += [p.keep, p.got]
        s = p.keep.shape
        if o is None:
            shapes.append(jax.ShapeDtypeStruct(s, F32))
        else:
            s = s[1:] if o == "y" else s[:-2] + (s[-2] // 2, s[-1])
            shapes += [jax.ShapeDtypeStruct(s, BF16)] * 2
    if merged:
        s = (shapes[0].shape[0], sum(p.keep.shape[-1] for p in parts))
        shapes = [jax.ShapeDtypeStruct(s, BF16)] * 2
    outs = pl.pallas_call(
        functools.partial(combine_kernel, steps, merged),
        grid=(ncol,),
        in_specs=[SMEM] + [spec(a.shape) for a in ins],
        out_specs=[spec(a.shape) for a in shapes],
        out_shape=shapes,
        name="combine",
        cost_estimate=cost(0.3),
    )(flags, *ins)
    if merged:
        return Part(outs[0], outs[1], parts[0].order[1:])
    if steps[0] is None:
        return list(outs)
    return [
        Part(outs[2 * k], outs[2 * k + 1], p.order[1:]) for k, p in enumerate(parts)
    ]


class Part:
    def __init__(self, keep, send, order):
        self.keep, self.send, self.order = keep, send, list(order)

    def go(self, n_dp):
        o = self.order[0]
        self.got = y_swap(self.send) if o == "y" else dp_swap(self.send, o, n_dp)


def attn_bwd_kernel(layer, half, *refs):
    (g_i, own, oth, mid, qkv, att, lse, start, gain, w) = refs[:10]
    (gm_o, low_o, dqkv_o, part_o, sums_o, qvs_o, k_t, dk, dv, dq_t) = refs[10:]
    g = pl.program_id(0)

    @pl.when(g == 0)
    def _():
        sums_o[...] = jnp.zeros_like(sums_o)
        qvs_o[...] = jnp.zeros_like(qvs_o)
        dk[...] = jnp.zeros_like(dk)
        dv[...] = jnp.zeros_like(dv)
        for b in range(LEN // BT):
            block = qkv[BT * b : BT * (b + 1), half : 2 * half].astype(F32)
            k_t[:, BT * b : BT * (b + 1)] = jnp.transpose(block).astype(BF16)

    gm, g_gain, g_shift = norm_back(
        g_i[...].astype(F32), own[...], oth[...], mid[...], gain[layer, 1:2, :].astype(F32)
    )
    gm_o[...] = gm
    sums_o[0:1, :] += colsum(g_gain)
    sums_o[1:2, :] += colsum(g_shift)
    sums_o[2:3, :] += colsum(gm)
    low = gm.astype(BF16)
    low_o[...] = low
    d_att = dot(low, w[:, 3 * half :]).astype(BF16)
    prod = d_att.astype(F32) * att[...].astype(F32)
    head = lax.broadcasted_iota(jnp.int32, (8, half), 1) // HD
    pick = (head == lax.broadcasted_iota(jnp.int32, (8, half), 0)).astype(F32)
    inner = lax.dot_general(
        pick,
        prod,
        (((1,), (1,)), ((), ())),
        preferred_element_type=F32,
        precision=lax.Precision.HIGHEST,
    )
    rows = pl.ds(pl.multiple_of(g * BT, BT), BT)
    q = qkv[rows, :half] * jnp.asarray(1.0 / math.sqrt(HD), BF16)
    for s in range(BT // QB):
        i = g * (BT // QB) + s
        ks = pl.multiple_of(jnp.maximum(i - DOC_MOST // QB, 0) * QB, QB)
        bias = window_bias(start, i, ks)
        cols = pl.ds(pl.multiple_of(i * QB, QB), QB)
        win = pl.ds(ks, KW)
        for p in range(half // 128):
            lo = 128 * p
            qq = head_pair(q[QB * s : QB * (s + 1), lo : lo + 128])
            oo = head_pair(d_att[QB * s : QB * (s + 1), lo : lo + 128])
            kp = qkv[win, half + lo : half + lo + 128]
            vp = qkv[win, 2 * half + lo : 2 * half + lo + 128]
            total = jnp.concatenate(
                [lse[2 * p : 2 * p + 1, cols], lse[2 * p + 1 : 2 * p + 2, cols]], axis=1
            )
            inn = jnp.concatenate(
                [
                    inner[2 * p : 2 * p + 1, QB * s : QB * (s + 1)],
                    inner[2 * p + 1 : 2 * p + 2, QB * s : QB * (s + 1)],
                ],
                axis=1,
            )
            probs = jnp.exp(dot(kp, qq, 1, 1) + bias - total)
            d_probs = dot(vp, oo, 1, 1)
            ds = (probs * (d_probs - inn)).astype(BF16)
            dv[win, lo : lo + 128] += dot(probs.astype(BF16), oo)
            dk[win, lo : lo + 128] += dot(ds, qq)
            dqt = dot(k_t[lo : lo + 128, win], ds)
            dq_t[lo : lo + HD, :] = dqt[:HD, :QB]
            dq_t[lo + HD : lo + 128, :] = dqt[HD:, QB:]
        dq = (jnp.transpose(dq_t[...]) * (1.0 / math.sqrt(HD))).astype(BF16)
        dqkv_o[cols, :half] = dq
        qvs_o[0:1, :] += colsum(dq.astype(F32))

    @pl.when(g == pl.num_programs(0) - 1)
    def _():
        dqkv_o[:, half : 2 * half] = dk[...].astype(BF16)
        dvb = dv[...].astype(BF16)
        dqkv_o[:, 2 * half :] = dvb
        qvs_o[1:2, :] = colsum(dvb.astype(F32))
        for b in range(LEN // BT):
            part = dot(dqkv_o[BT * b : BT * (b + 1), :], w[:, : 3 * half], 1, 1)
            part_o[BT * b : BT * (b + 1), :] = part.astype(BF16)


def attn_bwd(layer, g, own, oth, mid, qkv, att, lse, start, gain, w):
    d = mid.shape[1]
    half = att.shape[1]
    ins = [g, own, oth, mid, qkv, att, lse, start, gain, w]
    specs = [rows_spec(d)] * 4 + [full_spec(qkv.shape), rows_spec(half)]
    specs += [full_spec(a.shape) for a in ins[6:]]
    return pl.pallas_call(
        functools.partial(attn_bwd_kernel, layer, half),
        grid=(LEN // BT,),
        in_specs=specs,
        out_specs=[
            rows_spec(d),
            rows_spec(d),
            full_spec((LEN, 3 * half)),
            full_spec((LEN, d)),
            full_spec((8, d)),
            full_spec((8, half)),
        ],
        out_shape=[
            jax.ShapeDtypeStruct((LEN, d), F32),
            jax.ShapeDtypeStruct((LEN, d), BF16),
            jax.ShapeDtypeStruct((LEN, 3 * half), BF16),
            jax.ShapeDtypeStruct((LEN, d), BF16),
            jax.ShapeDtypeStruct((8, d), F32),
            jax.ShapeDtypeStruct((8, half), F32),
        ],
        scratch_shapes=[
            pltpu.VMEM((half, LEN), BF16),
            pltpu.VMEM((LEN, half), F32),
            pltpu.VMEM((LEN, half), F32),
            pltpu.VMEM((half, QB), F32),
        ],
        name=f"attn_bwd_{layer}",
        cost_estimate=cost(24),
    )(*ins)


def norm_bwd_kernel(layer, n_dp, place, g, own, oth, x, gain, hot, *refs):
    sums, (near_o, far_o, own_o, oth_o, acc, table, small) = refs[:8], refs[8:]
    sums0, sums0b, sums1, sumg1, sumh0, sumh1, qvs0, qvs1 = sums
    w = near_o.shape[1]
    step = pl.program_id(0)

    @pl.when(step == 0)
    def _():
        acc[...] = jnp.zeros_like(acc)
        table[...] = jnp.zeros_like(table)
        small[...] = jnp.zeros_like(small)

    out, g_gain, g_shift = norm_back(
        g[...], own[...], oth[...], x[...], gain[layer, 0:1, :].astype(F32)
    )
    acc[0:1, :] += colsum(g_gain)
    acc[1:2, :] += colsum(g_shift)

    def select(q):
        far = q ^ 2
        near_o[...] = out[:, w * q : w * (q + 1)]
        far_o[...] = out[:, w * far : w * (far + 1)].astype(BF16)

    for q in range(4):
        pl.when(place[0] == q)(functools.partial(select, q))
    table[0] += dot(hot[...], near_o[...].astype(BF16), 0, 0)
    table[1] += dot(hot[...], far_o[...], 0, 0)

    @pl.when(step == pl.num_programs(0) - 1)
    def _():
        rows = [(acc, 0), (sums0, 0), (sums0b, 0), (sums1, 0)]
        rows += [(acc, 1), (sums0, 1), (sums0b, 1), (sums1, 1)]
        rows += [(sums0, 2), (sums0b, 2), (sums1, 2), (sumg1, 0)]
        cw, qw, f = acc.shape[1] // n_dp, w // n_dp, sumh0.shape[1] // 2
        for c in range(n_dp):
            for k, (ref, r) in enumerate(rows):
                v = ref[r : r + 1, cw * c : cw * (c + 1)]
                small[0, 16 * c + k : 16 * c + k + 1, 0:cw] = v
                small[1, 16 * c + k : 16 * c + k + 1, 0:cw] = v
            for slot in range(2):
                for k, ref in enumerate((sumh0, sumh1)):
                    lo = f * slot + cw * c
                    row = 16 * c + 12 + k
                    small[slot, row : row + 1, 0:cw] = ref[0:1, lo : lo + cw]
                for k, (ref, r) in enumerate(((qvs0, 0), (qvs0, 1), (qvs1, 0), (qvs1, 1))):
                    lo = w * slot + qw * c
                    row = 16 * c + k
                    small[slot, row : row + 1, cw : cw + qw] = ref[r : r + 1, lo : lo + qw]
        for slot, ref in enumerate((own_o, oth_o)):
            ref[:DOC_MOST, :] = table[slot].astype(BF16)
            ref[DOC_MOST:, :] = small[slot].astype(BF16)


def norm_bwd(layer, n_dp, place, g, own, oth, x, gain, hot, sums):
    d = x.shape[1]
    w = d // 4
    r = DOC_MOST + 16 * n_dp
    return pl.pallas_call(
        functools.partial(norm_bwd_kernel, layer, n_dp),
        grid=(LEN // BT,),
        in_specs=[SMEM]
        + [rows_spec(d)] * 4
        + [full_spec(gain.shape), rows_spec(DOC_MOST)]
        + [full_spec(v.shape) for v in sums],
        out_specs=[rows_spec(w), rows_spec(w), full_spec((r, w)), full_spec((r, w))],
        out_shape=[
            jax.ShapeDtypeStruct((LEN, w), F32),
            jax.ShapeDtypeStruct((LEN, w), BF16),
            jax.ShapeDtypeStruct((r, w), BF16),
            jax.ShapeDtypeStruct((r, w), BF16),
        ],
        scratch_shapes=[
            pltpu.VMEM((8, d), F32),
            pltpu.VMEM((2, DOC_MOST, w), F32),
            pltpu.VMEM((2, 16 * n_dp, w), F32),
        ],
        name=f"norm_bwd_{layer}",
        cost_estimate=cost(1),
    )(place, g, own, oth, x, gain, hot, *sums)


def expand_kernel(order, n_dp, rows, flags, own, got, keep, send):
    total = (own[...].astype(F32) + got[...].astype(F32)).astype(BF16)
    n = len(order)
    half = 1 << (n - 1)
    r = rows + 16

    def split(bit):
        for c in range(n_dp):
            pos = sum(((c >> b) & 1) << (n - 1 - j) for j, b in enumerate(order))
            out = keep if pos // half == bit else send
            row = r * (pos % half)
            if rows * c < DOC_MOST:
                out[row : row + rows, :] = total[rows * c : rows * (c + 1)]
            else:
                out[row : row + rows, :] = jnp.zeros((rows, total.shape[1]), BF16)
            lo = DOC_MOST + 16 * c
            out[row + rows : row + r, :] = total[lo : lo + 16]

    pl.when(flags[order[0]] == 0)(lambda: split(0))
    pl.when(flags[order[0]] == 1)(lambda: split(1))


def expand(own, got, order, n_dp, rows, flags):
    w = own.shape[1]
    shape = (n_dp * (rows + 16) // 2, w)
    keep, send = pl.pallas_call(
        functools.partial(expand_kernel, order, n_dp, rows),
        grid=(1,),
        in_specs=[SMEM, full_spec(own.shape), full_spec(own.shape)],
        out_specs=[full_spec(shape)] * 2,
        out_shape=[jax.ShapeDtypeStruct(shape, BF16)] * 2,
        name="expand",
        cost_estimate=cost(0.3),
    )(flags, own, got)
    return Part(keep, send, order)


def core_swap(a):
    return lax.ppermute(a, "mp", [(i, i ^ 1) for i in range(4)])


def y_swap(a):
    return lax.ppermute(a, "mp", [(i, i ^ 2) for i in range(4)])


def dp_swap(a, bit, n_dp):
    return lax.ppermute(a, "dp", [(i, i ^ (1 << bit)) for i in range(n_dp)])


def pick(flag, zero, one):
    return jnp.where(flag == 0, zero, one)


class Place:
    def __init__(self, n_dp):
        mp = lax.axis_index("mp")
        self.n_dp = n_dp
        self.bits = n_dp.bit_length() - 1
        self.y = mp // 2
        self.c = mp % 2
        self.dp = lax.axis_index("dp")

    def dp_bit(self, b):
        return (self.dp >> b) & 1


def row_pieces(a, at):
    rows = a.reshape(2, LEN, a.shape[1])
    return pick(at.y, rows[0], rows[1]), pick(at.y, rows[1], rows[0])


def join_row(mine, far, at):
    mine_c = core_swap(mine)
    far_c = core_swap(far)

    def joined(here, there):
        return [pick(at.c, here, there), pick(at.c, there, here)]

    near2, far2 = joined(mine, mine_c), joined(far, far_c)
    return jnp.concatenate(
        [pick(at.y, a_, b_) for a_, b_ in zip(near2, far2)]
        + [pick(at.y, b_, a_) for a_, b_ in zip(near2, far2)],
        axis=1,
    )


def own_cols(a, at, other):
    w = a.shape[1] // 4
    halves = (a[:, : 2 * w], a[:, 2 * w :])
    h = pick(at.y, halves[1], halves[0]) if other else pick(at.y, halves[0], halves[1])
    return pick(at.c, h[:, :w], h[:, w:])


def bar(*vals):
    return lax.optimization_barrier(vals)


def doc_starts(doc_ids):
    row_index = jnp.broadcast_to(jnp.arange(doc_ids.shape[1], dtype=jnp.int32), doc_ids.shape)
    previous = jnp.concatenate([doc_ids[:, :1] - 1, doc_ids[:, :-1]], axis=1)
    starts = jnp.where(doc_ids != previous, row_index, 0)
    return lax.cummax(starts, axis=1)


def on_device(
    n_dp,
    tokens,
    doc_ids,
    positions_table,
    norm_gain,
    norm_shift,
    joined_projection_weight,
    qv_bias,
    w_out,
    out_bias,
    w_fc,
    fc_bias,
    w_proj,
    cotangent,
):
    at = Place(n_dp)
    d = positions_table.shape[1]
    share = joined_projection_weight.shape[-1]
    f = w_fc.shape[-1]
    bits = list(range(2, at.bits))
    flags = jnp.stack([at.dp_bit(b) for b in range(at.bits)]).astype(jnp.int32)

    b = at.dp_bit(0) ^ at.dp_bit(1)
    flag = b.reshape(1)
    gain, shift = norm_gain, norm_shift

    a_own = [
        jnp.concatenate([joined_projection_weight[l].reshape(d, 3 * share), w_out[l].T], axis=1)
        for l in range(2)
    ]
    biases = jnp.concatenate([qv_bias.reshape(-1), fc_bias.reshape(-1)]).reshape(-1, d)
    biases = jnp.pad(biases, ((0, -biases.shape[0] % 8), (0, 0)))
    r = d // 2

    def half_rows(w):
        return lax.dynamic_slice_in_dim(w, b * r, r, 0)

    def x_swap(w):
        return dp_swap(w, 0, n_dp)

    def z_swap(w):
        return dp_swap(w, 1, n_dp)

    def by_two(one, lo=0):
        return x_swap(one[lo : lo + r // 2]), z_swap(one[lo + r // 2 : lo + r])

    def plan_one(lo=0):
        return ((lo, r, 0, 0), (0, r, 1, 0))

    def plan_two(lo=0):
        return ((lo, r, 0, 0), (0, r // 2, 1, 0), (0, r // 2, 1, r // 2))

    tok_mine, tok_theirs = row_pieces(tokens, at)
    tok_far = y_swap(tok_theirs)
    a_one0 = y_swap(jnp.concatenate([half_rows(a_own[0]), biases], axis=0))

    starts = doc_starts(doc_ids)
    start = pick(at.y, starts[0:1], starts[1:2])
    place = jnp.arange(LEN, dtype=jnp.int32) - start[0]
    hot = (place[:, None] == jnp.arange(DOC_MOST, dtype=jnp.int32)[None, :]).astype(BF16)
    embedded = dot(hot, positions_table[:DOC_MOST]).astype(BF16)

    tok_far, a_one0, embedded, hot = bar(tok_far, a_one0, embedded, hot)
    a_x, a_z = by_two(a_one0)
    fc_one0 = y_swap(half_rows(w_fc[0]))
    full_tokens = join_row(tok_mine, tok_far, at)
    small = a_one0[r:].reshape(-1)
    nq = qv_bias.size
    qvb = jnp.concatenate([qv_bias, small[:nq].reshape(qv_bias.shape)], axis=-1)
    fcb = jnp.concatenate(
        [fc_bias, small[nq : nq + fc_bias.size].reshape(fc_bias.shape)], axis=-1
    )
    send_y = jnp.concatenate([half_rows(w_proj[0]), half_rows(a_own[1])], axis=0)
    a_x, a_z, fc_one0, full_tokens, send_y = bar(a_x, a_z, fc_one0, full_tokens, send_y)

    fc_two0 = x_swap(fc_one0)
    pj_a1 = y_swap(send_y)
    x0, n0, qkv0, att0, lse0, part, wa0 = attn_fwd(
        0,
        (full_tokens, embedded),
        out_bias,
        flag,
        start,
        gain,
        shift,
        qvb,
        a_own[0],
        (plan_two(), (a_one0, a_x, a_z)),
    )
    part, x0, fc_two0, pj_a1 = bar(part, x0, fc_two0, pj_a1)
    far = core_swap(part)
    pj_x, pj_z = by_two(pj_a1)
    far, pj_x, pj_z = bar(far, pj_x, pj_z)
    mlp0 = (
        w_fc,
        (plan_one(), (fc_one0, fc_two0)),
        w_proj,
        (plan_two(), (pj_a1, pj_x, pj_z)),
    )
    a_two1 = x_swap(pj_a1[r:])
    fc_one1 = y_swap(half_rows(w_fc[1]))
    mid0, nn0, hid0, part2 = mlp_fwd(
        0, x0, part, far, out_bias, gain, shift, fcb, flag, mlp0
    )
    part2, mid0, a_two1, fc_one1 = bar(part2, mid0, a_two1, fc_one1)
    far = core_swap(part2)
    (far,) = bar(far)
    fc_two1 = x_swap(fc_one1)
    pj_one1 = y_swap(half_rows(w_proj[1]))
    cot_mine, cot_theirs = row_pieces(cotangent, at)
    cot_far = y_swap(cot_theirs)
    x1, n1, qkv1, att1, lse1, part, wa1 = attn_fwd(
        1,
        (mid0, part2, far),
        out_bias,
        flag,
        start,
        gain,
        shift,
        qvb,
        a_own[1],
        (plan_one(r), (pj_a1, a_two1)),
    )
    part, x1, fc_two1, cot_far, pj_one1 = bar(part, x1, fc_two1, cot_far, pj_one1)
    far = core_swap(part)
    pj_x, pj_z = by_two(pj_one1)
    cot = join_row(cot_mine, cot_far, at)
    far, cot, pj_x, pj_z = bar(far, cot, pj_x, pj_z)
    mlp1 = (
        w_fc,
        (plan_one(), (fc_one1, fc_two1)),
        w_proj,
        (plan_two(), (pj_one1, pj_x, pj_z)),
    )
    mid1, nn1, act, gh, part_out, part, sumg1, sumh1 = mlp_both(
        1, x1, part, far, cot, out_bias, gain, shift, fcb, flag, mlp1
    )

    def go(*parts):
        for p in parts:
            p.go(n_dp)

    def bar_parts(parts, sent, *vals):
        name = "send" if sent else "got"
        out = bar(*[getattr(p, name) for p in parts], *vals)
        for p, v in zip(parts, out):
            setattr(p, name, v)
        return out[len(parts) :]

    part, part_out, mid1, gh, act = bar(part, part_out, mid1, gh, act)
    far = core_swap(part)
    far_out = core_swap(part_out)
    o_fc, o_pj = ["y", 1, 0] + bits, [0, "y", 1] + bits
    o_a, o_b = [0, 1, "y"] + bits, [1, "y", 0] + bits
    fc1, pj1 = dw_mlp(1, nn1, cot, gh, act, (o_fc, o_pj), flags)
    far, far_out, mid1, part_out = bar_parts([fc1, pj1], True, far, far_out, mid1, part_out)
    go(fc1, pj1)
    gm1, m_low, dqkv, part, sums1, qvs1 = attn_bwd(
        1, cot, part, far, mid1, qkv1, att1, lse1, start, gain, wa1
    )
    part, gm1, m_low, dqkv, far_out, part_out = bar_parts(
        [fc1, pj1], False, part, gm1, m_low, dqkv, far_out, part_out
    )
    far = core_swap(part)
    fc1, pj1 = combine([fc1, pj1], flags)
    result = (
        mid1 + (part_out.astype(F32) + far_out.astype(F32)) + out_bias[1, 1].astype(F32)
    ).astype(BF16)
    out_near, out_send = own_cols(result, at, False), own_cols(result, at, True)
    out_near, out_send, far, m_low = bar_parts([fc1, pj1], True, out_near, out_send, far, m_low)
    out_far = y_swap(out_send)
    aa1, ab1 = dw_attn(1, n1, m_low, dqkv, att1, (o_a, ["y", 1, 0] + bits), flags)
    far, gm1, out_far = bar_parts([aa1, ab1], True, far, gm1, out_far)
    go(fc1, pj1, aa1)
    g0, g_low, act, gh, part, sums0b, sumh0 = mlp_bwd(
        0, gm1, part, far, x1, hid0, gain, flag, mlp0
    )
    part, g0, g_low, act, gh = bar_parts([fc1, pj1, aa1], False, part, g0, g_low, act, gh)
    far = core_swap(part)
    fc1, pj1, aa1 = combine([fc1, pj1, aa1], flags)
    far, g_low, act, gh = bar_parts([fc1, pj1, aa1, ab1], True, far, g_low, act, gh)
    go(ab1, fc1, pj1, aa1)
    fc0, pj0 = dw_mlp(0, nn0, g_low, gh, act, (o_fc, o_pj), flags)
    far, fc0.send, pj0.send, g0 = bar_parts(
        [ab1, fc1, pj1, aa1], False, far, fc0.send, pj0.send, g0
    )
    last1 = combine([fc1, pj1], flags, merged=True)
    aa1, ab1 = combine([aa1, ab1], flags)
    far, g0, part = bar_parts([last1, aa1, ab1, fc0, pj0], True, far, g0, part)
    go(fc0, pj0, aa1, ab1, last1)
    gm0, m_low, dqkv, part, sums0, qvs0 = attn_bwd(
        0, g0, part, far, mid0, qkv0, att0, lse0, start, gain, wa0
    )
    part, gm0, m_low, dqkv, out_near, out_far = bar_parts(
        [fc0, pj0, aa1, ab1, last1], False, part, gm0, m_low, dqkv, out_near, out_far
    )
    far = core_swap(part)
    fc0, pj0 = combine([fc0, pj0], flags)
    (ab1,) = combine([ab1], flags)
    far, m_low, dqkv = bar_parts([fc0, pj0, ab1], True, far, m_low, dqkv)
    go(fc0, pj0, ab1)
    aa0, ab0 = dw_attn(0, n0, m_low, dqkv, att0, (o_a, o_b), flags)
    far, gm0, part = bar_parts([aa0, ab0], True, far, gm0, part)
    go(aa0, ab0)
    quarter = (2 * at.y + at.c).astype(jnp.int32).reshape(1)
    sums = (sums0, sums0b, sums1, sumg1, sumh0, sumh1, qvs0, qvs1)
    near, far_send, pk, pk_send = norm_bwd(0, n_dp, quarter, gm0, part, far, x0, gain, hot, sums)
    near, far_send, pk, pk_send = bar_parts([fc0, pj0, ab1], False, near, far_send, pk, pk_send)
    pk_got = y_swap(pk_send)
    g_far = y_swap(far_send)
    fc0, pj0 = combine([fc0, pj0], flags)
    pk_got, pk = bar_parts([fc0, pj0], True, pk_got, pk)
    go(fc0, pj0)
    rows = positions_table.shape[0] // n_dp
    pk = expand(pk, pk_got, [0, 1] + bits, n_dp, rows, flags)
    (pk.send,) = bar_parts([aa0, ab0], False, pk.send)
    aa0, ab0 = combine([aa0, ab0], flags)
    bar_parts([aa0, ab0, pk], True)
    g_far, near = bar_parts([fc0, pj0], False, g_far, near)
    go(aa0, ab0, pk)
    last0 = combine([fc0, pj0, aa1, ab1], flags, merged=True)
    out = jnp.concatenate([pick(at.y, out_near, out_far), pick(at.y, out_far, out_near)], axis=0)
    last0.send, out = bar_parts([aa0, ab0, pk], False, last0.send, out)
    go(last0)
    aa0, ab0, pk = combine([aa0, ab0, pk], flags)
    g_far, near = bar_parts([aa0, ab0, pk], True, g_far, near)
    go(aa0, ab0, pk)
    g_far = g_far.astype(F32)
    grad_tokens = jnp.concatenate([pick(at.y, near, g_far), pick(at.y, g_far, near)], axis=0)
    (grad_tokens,) = bar_parts([aa0, ab0, pk], False, grad_tokens)
    last2 = combine([aa0, ab0], flags, merged=True)
    (pk,) = combine([pk], flags)
    bar_parts([last2, pk], True)
    go(last2, pk)
    lasts = [last1, last0, last2, pk]
    while len(lasts[0].order) > 1:
        lasts = combine(lasts, flags)
        go(*lasts)
    l1, l0, l2, pk = combine(lasts, flags)
    grad_positions, small = pk[:rows], pk[rows:]
    f2 = 2 * f
    r_fc = (l0[:, :f], l1[:, :f])
    r_pj = (l0[:, f:f2], l1[:, f:])
    r_ao = (l2, l0[:, f2:])
    w = d // n_dp
    s = small[:, :w]
    qv = small[:4, w : w + share // n_dp]
    ao = jnp.stack(r_ao)
    return (
        out,
        grad_tokens,
        grad_positions,
        s[0:4].reshape(2, 2, w),
        s[4:8].reshape(2, 2, w),
        ao[..., : 3 * share].reshape(2, w, 3, share),
        qv.reshape(2, 2, w // 4),
        jnp.swapaxes(ao[..., 3 * share :], 1, 2),
        s[8:12].reshape(2, 2, w),
        jnp.stack(r_fc),
        s[12:14],
        jnp.stack([p.T for p in r_pj]),
    )


def solution(mesh):
    n_dp = mesh.shape["dp"]
    in_specs = (
        P("dp", "mp"),
        P("dp", None),
        P(),
        P(),
        P(),
        P(None, None, None, "mp"),
        P(None, None, "mp"),
        P(None, "mp", None),
        P(),
        P(None, None, "mp"),
        P(None, "mp"),
        P(None, "mp", None),
        P("dp", "mp"),
    )
    out_specs = (
        P("dp", "mp"),
        P("dp", "mp"),
        P("dp", "mp"),
        P(None, None, "dp"),
        P(None, None, "dp"),
        P(None, "dp", None, "mp"),
        P(None, None, ("mp", "dp")),
        P(None, "mp", "dp"),
        P(None, None, "dp"),
        P(None, "dp", "mp"),
        P(None, ("mp", "dp")),
        P(None, "mp", "dp"),
    )
    return jax.shard_map(
        functools.partial(on_device, n_dp),
        mesh=mesh,
        in_specs=in_specs,
        out_specs=out_specs,
        check_vma=False,
    )
```

```python
import functools
import math

import jax
import jax.numpy as jnp
from jax import lax
from jax.experimental import pallas as pl
from jax.experimental.pallas import tpu as pltpu
from jax.sharding import PartitionSpec as P

HD = 64
LEN = 1024
DOC_MOST = 384
EPS = 1e-05
BT = 256
QB = 128
KW = QB + DOC_MOST
F32 = jnp.float32
BF16 = jnp.bfloat16
GELU_C = math.sqrt(2.0 / math.pi)


ANY = pl.BlockSpec(memory_space=pl.ANY)
SMEM = pl.BlockSpec(memory_space=pltpu.SMEM)


def cost(us):
    return pl.CostEstimate(flops=int(us * 1.15e9), transcendentals=0, bytes_accessed=0)


def full_spec(shape):
    return pl.BlockSpec(shape, lambda g: (0,) * len(shape))


def rows_spec(width):
    return pl.BlockSpec((BT, width), lambda g: (g, 0))


def dot(a, b, ca=1, cb=0):
    return lax.dot_general(a, b, (((ca,), (cb,)), ((), ())), preferred_element_type=F32)


def normed_parts(v):
    centred = v - jnp.mean(v, axis=-1, keepdims=True)
    variance = jnp.mean(centred * centred, axis=-1, keepdims=True)
    rstd = lax.rsqrt(variance + EPS)
    return centred * rstd, rstd


def norm_back(g, own, oth, v, gain):
    grad = own.astype(F32) + oth.astype(F32)
    xhat, rstd = normed_parts(v)
    gn = grad * gain
    out = g + rstd * (
        gn
        - jnp.mean(gn, axis=-1, keepdims=True)
        - xhat * jnp.mean(gn * xhat, axis=-1, keepdims=True)
    )
    return out, grad * xhat, grad


def colsum(v):
    return jnp.sum(v, axis=0, keepdims=True)


def head_pair(block):
    lane = lax.broadcasted_iota(jnp.int32, block.shape, 1)
    zero = jnp.zeros_like(block)
    return jnp.concatenate(
        [jnp.where(lane < HD, block, zero), jnp.where(lane < HD, zero, block)], axis=0
    )


def window_bias(start_ref, i, ks):
    kidx = lax.broadcasted_iota(jnp.int32, (KW, QB), 0) + ks
    qidx = lax.broadcasted_iota(jnp.int32, (KW, QB), 1) + i * QB
    first = start_ref[0:1, pl.ds(pl.multiple_of(i * QB, QB), QB)]
    bias = jnp.where((kidx >= first) & (kidx <= qidx), 0.0, -1e30).astype(F32)
    return jnp.concatenate([bias, bias], axis=1)


def copies(pairs, sems):
    out = [pltpu.make_async_copy(a, b, sems.at[j]) for j, (a, b) in enumerate(pairs)]
    for c in out:
        c.start()
    return out


def join_pieces(flag, plan, refs, dst, cols=slice(None)):
    r = dst.shape[0] // 2
    out = []
    for (lo, n, other, off), ref in zip(plan, refs):
        row = (1 - flag if other else flag) * r + off
        out.append((ref.at[pl.ds(lo, n)], dst.at[pl.ds(pl.multiple_of(row, 8), n), cols]))
    return out


def gelu_parts(v):
    v2 = v * v
    t = jnp.tanh(GELU_C * v * (1.0 + 0.044715 * v2))
    cdf = 0.5 * (1.0 + t)
    slope = cdf + (0.5 * GELU_C) * v * (1.0 - t * t) * (1.0 + (3 * 0.044715) * v2)
    return v * cdf, slope


def gained(xhat, gain, shift, layer, which):
    row = slice(which, which + 1)
    return (xhat * gain[layer, row, :].astype(F32) + shift[layer, row, :].astype(F32)).astype(BF16)


def attn_fwd_kernel(layer, first, half, plan, *refs):
    if first:
        (tok, emb, flag, start, gain, shift, qvb, a_own) = refs[:8]
        rest = refs[8:]
        x = tok[...].astype(F32) + emb[...].astype(F32)
    else:
        (mid, own, oth, outb, flag, start, gain, shift, qvb, a_own) = refs[:10]
        rest = refs[10:]
        x = (
            mid[...]
            + (own[...].astype(F32) + oth[...].astype(F32))
            + outb[layer - 1, 1:2, :].astype(F32)
        )
    a_refs, rest = rest[: len(plan)], rest[len(plan) :]
    x_o, n_o, qkv_o, att_o, lse_o, part_o, w_o, v_t, o_t, a_buf, sems = rest
    g = pl.program_id(0)
    sh = half // 2

    @pl.when(g == 0)
    def _():
        moves = copies(
            [(a_own, a_buf.at[0])] + join_pieces(flag[0], plan, a_refs, a_buf.at[1]), sems
        )
        qkv_o[pl.ds(BT, KW - BT), half : 2 * half] = jnp.zeros((KW - BT, half), BF16)
        v_t[:, pl.ds(BT, KW - BT)] = jnp.zeros((half, KW - BT), BF16)
        lse_o[...] = jnp.zeros_like(lse_o)
        for m in moves:
            m.wait()
        for j in range(4):
            for s in range(2):
                w_o[:, (2 * j + s) * sh : (2 * j + s + 1) * sh] = a_buf[s, :, j * sh : (j + 1) * sh]

    x_o[...] = x
    xhat, _ = normed_parts(x)
    normed = gained(xhat, gain, shift, layer, 0)
    n_o[...] = normed
    qkv = dot(normed, w_o[:, : 3 * half])
    q = (qkv[:, :half] + qvb[layer, 0:1, :].astype(F32)).astype(BF16)
    k = qkv[:, half : 2 * half].astype(BF16)
    v = qkv[:, 2 * half :] + qvb[layer, 1:2, :].astype(F32)
    rows = pl.ds(pl.multiple_of(g * BT, BT), BT)
    qkv_o[rows, :half] = q
    qkv_o[rows, half : 2 * half] = k
    qkv_o[rows, 2 * half :] = v.astype(BF16)
    v_t[:, rows] = jnp.transpose(v).astype(BF16)
    q = q * jnp.asarray(1.0 / math.sqrt(HD), BF16)
    for s in range(BT // QB):
        i = g * (BT // QB) + s
        ks = pl.multiple_of(jnp.maximum(i - DOC_MOST // QB, 0) * QB, QB)
        bias = window_bias(start, i, ks)
        cols = pl.ds(pl.multiple_of(i * QB, QB), QB)
        for p in range(half // 128):
            lo = 128 * p
            qq = head_pair(q[QB * s : QB * (s + 1), lo : lo + 128])
            kp = qkv_o[pl.ds(ks, KW), half + lo : half + lo + 128]
            scores = dot(kp, qq, 1, 1) + bias
            peak = jnp.max(scores, axis=0, keepdims=True)
            e = jnp.exp(scores - peak)
            total = jnp.sum(e, axis=0, keepdims=True)
            ot = dot(v_t[lo : lo + 128, pl.ds(ks, KW)], e.astype(BF16))
            inv = 1.0 / total
            o_t[lo : lo + HD, :] = ot[:HD, :QB] * inv[:, :QB]
            o_t[lo + HD : lo + 128, :] = ot[HD:, QB:] * inv[:, QB:]
            lse = peak + jnp.log(total)
            lse_o[2 * p : 2 * p + 1, cols] = lse[:, :QB]
            lse_o[2 * p + 1 : 2 * p + 2, cols] = lse[:, QB:]
        att_o[QB * s : QB * (s + 1), :] = jnp.transpose(o_t[...]).astype(BF16)
    part_o[...] = dot(att_o[...], w_o[:, 3 * half :], 1, 1).astype(BF16)


def attn_fwd(layer, stream_in, outb, flag, start, gain, shift, qvb, a_own, a_oth):
    first = layer == 0
    d = gain.shape[-1]
    half = a_own.shape[1] // 2
    ins = list(stream_in)
    specs = [rows_spec(d) for _ in ins]
    if not first:
        ins.append(outb)
        specs.append(full_spec(outb.shape))
    plan, arrays = a_oth
    ins += [flag, start, gain, shift, qvb, a_own, *arrays]
    specs += [SMEM] + [full_spec(a.shape) for a in (start, gain, shift, qvb)]
    specs += [ANY] * (1 + len(arrays))
    return pl.pallas_call(
        functools.partial(attn_fwd_kernel, layer, first, half, plan),
        grid=(LEN // BT,),
        in_specs=specs,
        out_specs=[
            rows_spec(d),
            rows_spec(d),
            full_spec((LEN, 3 * half)),
            rows_spec(half),
            full_spec((8, LEN)),
            rows_spec(d),
            full_spec((d, 4 * half)),
        ],
        out_shape=[
            jax.ShapeDtypeStruct((LEN, d), F32),
            jax.ShapeDtypeStruct((LEN, d), BF16),
            jax.ShapeDtypeStruct((LEN, 3 * half), BF16),
            jax.ShapeDtypeStruct((LEN, half), BF16),
            jax.ShapeDtypeStruct((8, LEN), F32),
            jax.ShapeDtypeStruct((LEN, d), BF16),
            jax.ShapeDtypeStruct((d, 4 * half), BF16),
        ],
        scratch_shapes=[
            pltpu.VMEM((half, LEN), BF16),
            pltpu.VMEM((half, QB), F32),
            pltpu.VMEM((2, d, 2 * half), BF16),
            pltpu.SemaphoreType.DMA((1 + len(plan),)),
        ],
        name=f"attn_fwd_{layer}",
        cost_estimate=cost(22),
    )(*ins)


def load_mlp(layer, flag, plans, weights, wfc, wproj, sems):
    d = wfc.shape[0]
    f = wfc.shape[1] // 2
    n = len(plans[0])
    return copies(
        [(weights[0].at[layer], wfc.at[:, pl.ds(0, f)])]
        + join_pieces(flag[0], plans[0], weights[2 : 2 + n], wfc, pl.ds(f, f))
        + [(weights[1].at[layer], wproj.at[pl.ds(0, f)])]
        + join_pieces(flag[0], plans[1], weights[2 + n :], wproj.at[pl.ds(f, f)]),
        sems,
    )


def mlp_scratch(d, f2, plans):
    return [
        pltpu.VMEM((d, f2), BF16),
        pltpu.VMEM((f2, d), BF16),
        pltpu.SemaphoreType.DMA((2 + len(plans[0]) + len(plans[1]),)),
    ]


def mlp_weights(weights):
    w_fc, fc_oth, w_proj, pj_oth = weights
    return (fc_oth[0], pj_oth[0]), [w_fc, w_proj, *fc_oth[1], *pj_oth[1]]


def mlp_fwd_kernel(layer, plans, x, own, oth, outb, gain, shift, fcb, flag, *refs):
    nw = 2 + len(plans[0]) + len(plans[1])
    weights = refs[:nw]
    mid_o, n_o, h_o, part_o, wfc, wproj, sems = refs[nw:]

    @pl.when(pl.program_id(0) == 0)
    def _():
        for m in load_mlp(layer, flag, plans, weights, wfc, wproj, sems):
            m.wait()

    mid = (
        x[...]
        + (own[...].astype(F32) + oth[...].astype(F32))
        + outb[layer, 0:1, :].astype(F32)
    )
    mid_o[...] = mid
    xhat, _ = normed_parts(mid)
    normed = gained(xhat, gain, shift, layer, 1)
    n_o[...] = normed
    hidden = dot(normed, wfc[...]) + fcb[layer : layer + 1, :].astype(F32)
    h_o[...] = hidden.astype(BF16)
    t = jnp.tanh(GELU_C * hidden * (1.0 + 0.044715 * hidden * hidden))
    act = (0.5 * hidden * (1.0 + t)).astype(BF16)
    part_o[...] = dot(act, wproj[...]).astype(BF16)


def mlp_fwd(layer, x, own, oth, outb, gain, shift, fcb, flag, weights):
    d = x.shape[1]
    f = fcb.shape[1]
    plans, arrays = mlp_weights(weights)
    ins = [x, own, oth, outb, gain, shift, fcb, flag, *arrays]
    specs = [rows_spec(d)] * 3 + [full_spec(a.shape) for a in ins[3:7]] + [SMEM] + [ANY] * len(arrays)
    return pl.pallas_call(
        functools.partial(mlp_fwd_kernel, layer, plans),
        grid=(LEN // BT,),
        in_specs=specs,
        out_specs=[rows_spec(d), rows_spec(d), rows_spec(f), rows_spec(d)],
        out_shape=[
            jax.ShapeDtypeStruct((LEN, d), F32),
            jax.ShapeDtypeStruct((LEN, d), BF16),
            jax.ShapeDtypeStruct((LEN, f), BF16),
            jax.ShapeDtypeStruct((LEN, d), BF16),
        ],
        scratch_shapes=mlp_scratch(d, f, plans),
        name=f"mlp_fwd_{layer}",
        cost_estimate=cost(12),
    )(*ins)


def mlp_both_kernel(layer, plans, x, own, oth, cot, outb, gain, shift, fcb, flag, *refs):
    nw = 2 + len(plans[0]) + len(plans[1])
    weights = refs[:nw]
    mid_o, n_o, act_o, gh_o, out_o, part_o, sumg_o, sumh_o, wfc, wproj, sems = refs[nw:]

    @pl.when(pl.program_id(0) == 0)
    def _():
        moves = load_mlp(layer, flag, plans, weights, wfc, wproj, sems)
        sumg_o[...] = jnp.zeros_like(sumg_o)
        sumh_o[...] = jnp.zeros_like(sumh_o)
        for m in moves:
            m.wait()

    mid = (
        x[...]
        + (own[...].astype(F32) + oth[...].astype(F32))
        + outb[layer, 0:1, :].astype(F32)
    )
    mid_o[...] = mid
    xhat, _ = normed_parts(mid)
    normed = gained(xhat, gain, shift, layer, 1)
    n_o[...] = normed
    grad_act = dot(cot[...], wproj[...], 1, 1)
    value, slope = gelu_parts(dot(normed, wfc[...]) + fcb[layer : layer + 1, :].astype(F32))
    act = value.astype(BF16)
    act_o[...] = act
    gh = (grad_act * slope).astype(BF16)
    gh_o[...] = gh
    part_o[...] = dot(gh, wfc[...], 1, 1).astype(BF16)
    out_o[...] = dot(act, wproj[...]).astype(BF16)
    sumg_o[0:1, :] += colsum(cot[...].astype(F32))
    sumh_o[0:1, :] += colsum(gh.astype(F32))


def mlp_both(layer, x, own, oth, cot, outb, gain, shift, fcb, flag, weights):
    d = x.shape[1]
    f = fcb.shape[1]
    plans, arrays = mlp_weights(weights)
    ins = [x, own, oth, cot, outb, gain, shift, fcb, flag, *arrays]
    specs = [rows_spec(d)] * 4 + [full_spec(a.shape) for a in ins[4:8]] + [SMEM] + [ANY] * len(arrays)
    widths = [d, d, f, f, d, d]
    kinds = [F32, BF16, BF16, BF16, BF16, BF16]
    return pl.pallas_call(
        functools.partial(mlp_both_kernel, layer, plans),
        grid=(LEN // BT,),
        in_specs=specs,
        out_specs=[rows_spec(w) for w in widths] + [full_spec((8, d)), full_spec((8, f))],
        out_shape=[jax.ShapeDtypeStruct((LEN, w), k) for w, k in zip(widths, kinds)]
        + [jax.ShapeDtypeStruct((8, d), F32), jax.ShapeDtypeStruct((8, f), F32)],
        scratch_shapes=mlp_scratch(d, f, plans),
        name=f"mlp_both_{layer}",
        cost_estimate=cost(18),
    )(*ins)


def mlp_bwd_kernel(layer, plans, gm, own, oth, x, h, gain, flag, *refs):
    nw = 2 + len(plans[0]) + len(plans[1])
    weights = refs[:nw]
    g_o, low_o, act_o, gh_o, part_o, sums_o, sumh_o, wfc, wproj, sems = refs[nw:]

    @pl.when(pl.program_id(0) == 0)
    def _():
        moves = load_mlp(layer, flag, plans, weights, wfc, wproj, sems)
        sums_o[...] = jnp.zeros_like(sums_o)
        sumh_o[...] = jnp.zeros_like(sumh_o)
        for m in moves:
            m.wait()

    grad, g_gain, g_shift = norm_back(
        gm[...], own[...], oth[...], x[...], gain[layer + 1, 0:1, :].astype(F32)
    )
    sums_o[0:1, :] += colsum(g_gain)
    sums_o[1:2, :] += colsum(g_shift)
    sums_o[2:3, :] += colsum(grad)
    g_o[...] = grad
    low = grad.astype(BF16)
    low_o[...] = low
    grad_act = dot(low, wproj[...], 1, 1)
    value, slope = gelu_parts(h[...].astype(F32))
    act_o[...] = value.astype(BF16)
    gh = (grad_act * slope).astype(BF16)
    gh_o[...] = gh
    part_o[...] = dot(gh, wfc[...], 1, 1).astype(BF16)
    sumh_o[0:1, :] += colsum(gh.astype(F32))


def mlp_bwd(layer, gm, own, oth, x, h, gain, flag, weights):
    d = x.shape[1]
    f = h.shape[1]
    plans, arrays = mlp_weights(weights)
    ins = [gm, own, oth, x, h, gain, flag, *arrays]
    specs = [rows_spec(d)] * 4 + [rows_spec(f), full_spec(gain.shape), SMEM] + [ANY] * len(arrays)
    widths = [d, d, f, f, d]
    kinds = [F32, BF16, BF16, BF16, BF16]
    return pl.pallas_call(
        functools.partial(mlp_bwd_kernel, layer, plans),
        grid=(LEN // BT,),
        in_specs=specs,
        out_specs=[rows_spec(w) for w in widths] + [full_spec((8, d)), full_spec((8, f))],
        out_shape=[jax.ShapeDtypeStruct((LEN, w), k) for w, k in zip(widths, kinds)]
        + [jax.ShapeDtypeStruct((8, d), F32), jax.ShapeDtypeStruct((8, f), F32)],
        scratch_shapes=mlp_scratch(d, f, plans),
        name=f"mlp_bwd_{layer}",
        cost_estimate=cost(16),
    )(*ins)


def stage(buf, value, order):
    dims = [o for o in order if o != "y"]
    n = len(dims)
    r = value.shape[0] >> n
    for c in range(1 << n):
        pos = sum(((c >> b) & 1) << (n - 1 - j) for j, b in enumerate(dims))
        buf[r * pos : r * (pos + 1), :] = value[r * c : r * (c + 1)].astype(BF16)


def ship(buf, keep, send, slot, order, flags, sems):
    if order[0] == "y":
        pairs = [(buf, send if slot else keep)]
    else:
        half = buf.shape[0] // 2
        f = flags[order[0]]
        lo = [pl.multiple_of(h * half, 16) for h in (f, 1 - f)]
        pairs = [
            (buf.at[pl.ds(lo[0], half)], keep.at[slot]),
            (buf.at[pl.ds(lo[1], half)], send.at[slot]),
        ]
    return [pltpu.make_async_copy(a, b, sems.at[j]) for j, (a, b) in enumerate(pairs)]


def first_shape(order, d, w):
    return (d, w) if order[0] == "y" else (2, d // 2, w)


def dw_mlp_kernel(orders, flags, n, low, gh, act, *refs):
    outs, (bufs, sems) = refs[:4], refs[4:]
    j = pl.program_id(0)

    def moves(t, slot):
        keep, send = outs[2 * t : 2 * t + 2]
        return ship(bufs.at[t, slot], keep, send, slot, orders[t], flags, sems.at[t, slot])

    for t, (a, b) in enumerate(((n, gh), (low, act))):
        stage(bufs.at[t, j], dot(a[...], b[...], 0, 0), orders[t])
        for slot in range(2):

            @pl.when(j == slot)
            def _():
                for m in moves(t, slot):
                    m.start()

    @pl.when(j == 1)
    def _():
        for t in range(2):
            for slot in range(2):
                for m in moves(t, slot):
                    m.wait()


def dw_mlp(layer, n, low, gh, act, orders, flags):
    t, d = n.shape
    f = gh.shape[1] // 2
    col = pl.BlockSpec((t, f), lambda j: (0, j))
    shapes = [first_shape(o, d, f) for o in orders for _ in range(2)]
    k0, s0, k1, s1 = pl.pallas_call(
        functools.partial(dw_mlp_kernel, orders),
        grid=(2,),
        in_specs=[SMEM, full_spec(n.shape), full_spec(low.shape), col, col],
        out_specs=[ANY] * 4,
        out_shape=[jax.ShapeDtypeStruct(s, BF16) for s in shapes],
        scratch_shapes=[pltpu.VMEM((2, 2, d, f), BF16), pltpu.SemaphoreType.DMA((2, 2, 2))],
        name=f"dw_mlp_{layer}",
        cost_estimate=cost(9),
    )(flags, n, low, gh, act)
    return Part(k0, s0, orders[0]), Part(k1, s1, orders[1])


def dw_attn_kernel(orders, flags, n, low, dqkv, att, *refs):
    outs, (bufs, sems) = refs[:4], refs[4:]
    sh = att.shape[1] // 2
    moves = []

    def send_off(t, values):
        for slot in range(2):
            both = jnp.concatenate(
                [v[:, (2 * j + slot) * sh : (2 * j + slot + 1) * sh] for v, j in values], axis=1
            )
            stage(bufs.at[t, slot], both, orders[t])
            keep, send = outs[2 * t : 2 * t + 2]
            for m in ship(
                bufs.at[t, slot], keep, send, slot, orders[t], flags, sems.at[t, slot]
            ):
                m.start()
                moves.append(m)

    half = 2 * sh
    qk = dot(n[...], dqkv[:, : 2 * half], 0, 0)
    send_off(0, [(qk, 0), (qk, 1)])
    v = dot(n[...], dqkv[:, 2 * half :], 0, 0)
    wo = dot(low[...], att[...], 0, 0)
    send_off(1, [(v, 0), (wo, 0)])
    for m in moves:
        m.wait()


def dw_attn(layer, n, low, dqkv, att, orders, flags):
    d = n.shape[1]
    w = att.shape[1]
    ins = (n, low, dqkv, att)
    shapes = [first_shape(o, d, w) for o in orders for _ in range(2)]
    k0, s0, k1, s1 = pl.pallas_call(
        functools.partial(dw_attn_kernel, orders),
        grid=(1,),
        in_specs=[SMEM] + [full_spec(a.shape) for a in ins],
        out_specs=[ANY] * 4,
        out_shape=[jax.ShapeDtypeStruct(s, BF16) for s in shapes],
        scratch_shapes=[pltpu.VMEM((2, 2, d, w), BF16), pltpu.SemaphoreType.DMA((2, 2, 2))],
        name=f"dw_attn_{layer}",
        cost_estimate=cost(7),
    )(flags, *ins)
    return Part(k0, s0, orders[0]), Part(k1, s1, orders[1])


def combine_kernel(steps, merged, flags, *refs):
    ins, outs = refs[: 2 * len(steps)], refs[2 * len(steps) :]
    lo = 0
    for k, o in enumerate(steps):
        keep, got = ins[2 * k : 2 * k + 2]

        def total(at):
            return keep[at].astype(F32) + got[at].astype(F32)

        if o is None:
            outs[k][...] = total(...)
            continue
        dst = outs if merged else outs[2 * k : 2 * k + 2]
        cols = slice(lo, lo + keep.shape[-1]) if merged else slice(None)
        if o == "y":
            halves = [total(0), total(1)]
        else:
            r = keep.shape[-2] // 2
            lead = (slice(None),) * (len(keep.shape) - 2)
            rows = [pl.ds(pl.multiple_of(h * r, 8), r) for h in (flags[o], 1 - flags[o])]
            halves = [total(lead + (row, slice(None))) for row in rows]
        for out, v in zip(dst, halves):
            out[..., cols] = v.astype(BF16)
        if merged:
            lo += keep.shape[-1]


def combine(parts, flags, merged=False):
    steps = [p.order[1] if len(p.order) > 1 else None for p in parts]
    wide = all(p.keep.shape[-1] % 384 == 0 for p in parts)
    ncol = 3 if wide and not merged and parts[0].keep.size >= 2**18 else 1

    def spec(shape):
        block = shape[:-1] + (shape[-1] // ncol,)
        return pl.BlockSpec(block, lambda g: (0,) * (len(shape) - 1) + (g,))

    ins, shapes = [], []
    for p, o in zip(parts, steps):
        ins += [p.keep, p.got]
        s = p.keep.shape
        if o is None:
            shapes.append(jax.ShapeDtypeStruct(s, F32))
        else:
            s = s[1:] if o == "y" else s[:-2] + (s[-2] // 2, s[-1])
            shapes += [jax.ShapeDtypeStruct(s, BF16)] * 2
    if merged:
        s = (shapes[0].shape[0], sum(p.keep.shape[-1] for p in parts))
        shapes = [jax.ShapeDtypeStruct(s, BF16)] * 2
    outs = pl.pallas_call(
        functools.partial(combine_kernel, steps, merged),
        grid=(ncol,),
        in_specs=[SMEM] + [spec(a.shape) for a in ins],
        out_specs=[spec(a.shape) for a in shapes],
        out_shape=shapes,
        name="combine",
        cost_estimate=cost(0.3),
    )(flags, *ins)
    if merged:
        return Part(outs[0], outs[1], parts[0].order[1:])
    if steps[0] is None:
        return list(outs)
    return [
        Part(outs[2 * k], outs[2 * k + 1], p.order[1:]) for k, p in enumerate(parts)
    ]


def final_kernel(f, share, *refs):
    (m1, m0, a1, a0, pk), outs = [
        (refs[2 * k], refs[2 * k + 1]) for k in range(5)
    ], refs[10:]
    fc_o, pj_o, qkv_o, wo_o, pos_o, small_o = outs

    def total(pair, cols=slice(None)):
        return pair[0][:, cols].astype(F32) + pair[1][:, cols].astype(F32)

    for l, (m, a) in enumerate(((m0, a0), (m1, a1))):
        fc_o[l] = total(m, slice(0, f))
        pj_o[l] = total(m, slice(f, 2 * f))
        v = total(a)
        for j in range(3):
            qkv_o[l, j] = v[:, share * j : share * (j + 1)]
        wo_o[l] = jnp.transpose(v[:, 3 * share :])
    v = total(pk)
    rows = pos_o.shape[1]
    pos_o[...] = jnp.transpose(v[:rows])
    small_o[...] = v[rows:]


def final(parts, f, share, rows):
    r = parts[0].keep.shape[0]
    ins = [v for p in parts for v in (p.keep, p.got)]
    shapes = [(2, r, f), (2, r, f), (2, 3, r, share), (2, share, r), (share, rows), (16, share)]
    return pl.pallas_call(
        functools.partial(final_kernel, f, share),
        grid=(1,),
        in_specs=[full_spec(v.shape) for v in ins],
        out_specs=[full_spec(v) for v in shapes],
        out_shape=[jax.ShapeDtypeStruct(v, F32) for v in shapes],
        name="final",
        cost_estimate=cost(3),
    )(*ins)


class Part:
    def __init__(self, keep, send, order):
        self.keep, self.send, self.order = keep, send, list(order)

    def go(self, n_dp):
        o = self.order[0]
        self.got = y_swap(self.send) if o == "y" else dp_swap(self.send, o, n_dp)


def attn_bwd_kernel(layer, half, *refs):
    (g_i, own, oth, mid, qkv, att, lse, start, gain, w) = refs[:10]
    (gm_o, low_o, dqkv_o, part_o, sums_o, qvs_o, k_t, dk, dv, dq_t) = refs[10:]
    g = pl.program_id(0)

    @pl.when(g == 0)
    def _():
        sums_o[...] = jnp.zeros_like(sums_o)
        qvs_o[...] = jnp.zeros_like(qvs_o)
        dk[...] = jnp.zeros_like(dk)
        dv[...] = jnp.zeros_like(dv)
        for b in range(LEN // BT):
            block = qkv[BT * b : BT * (b + 1), half : 2 * half].astype(F32)
            k_t[:, BT * b : BT * (b + 1)] = jnp.transpose(block).astype(BF16)

    gm, g_gain, g_shift = norm_back(
        g_i[...].astype(F32), own[...], oth[...], mid[...], gain[layer, 1:2, :].astype(F32)
    )
    gm_o[...] = gm
    sums_o[0:1, :] += colsum(g_gain)
    sums_o[1:2, :] += colsum(g_shift)
    sums_o[2:3, :] += colsum(gm)
    low = gm.astype(BF16)
    low_o[...] = low
    d_att = dot(low, w[:, 3 * half :]).astype(BF16)
    prod = d_att.astype(F32) * att[...].astype(F32)
    head = lax.broadcasted_iota(jnp.int32, (8, half), 1) // HD
    pick = (head == lax.broadcasted_iota(jnp.int32, (8, half), 0)).astype(F32)
    inner = lax.dot_general(
        pick,
        prod,
        (((1,), (1,)), ((), ())),
        preferred_element_type=F32,
        precision=lax.Precision.HIGHEST,
    )
    rows = pl.ds(pl.multiple_of(g * BT, BT), BT)
    q = qkv[rows, :half] * jnp.asarray(1.0 / math.sqrt(HD), BF16)
    for s in range(BT // QB):
        i = g * (BT // QB) + s
        ks = pl.multiple_of(jnp.maximum(i - DOC_MOST // QB, 0) * QB, QB)
        bias = window_bias(start, i, ks)
        cols = pl.ds(pl.multiple_of(i * QB, QB), QB)
        win = pl.ds(ks, KW)
        for p in range(half // 128):
            lo = 128 * p
            qq = head_pair(q[QB * s : QB * (s + 1), lo : lo + 128])
            oo = head_pair(d_att[QB * s : QB * (s + 1), lo : lo + 128])
            kp = qkv[win, half + lo : half + lo + 128]
            vp = qkv[win, 2 * half + lo : 2 * half + lo + 128]
            total = jnp.concatenate(
                [lse[2 * p : 2 * p + 1, cols], lse[2 * p + 1 : 2 * p + 2, cols]], axis=1
            )
            inn = jnp.concatenate(
                [
                    inner[2 * p : 2 * p + 1, QB * s : QB * (s + 1)],
                    inner[2 * p + 1 : 2 * p + 2, QB * s : QB * (s + 1)],
                ],
                axis=1,
            )
            probs = jnp.exp(dot(kp, qq, 1, 1) + bias - total)
            d_probs = dot(vp, oo, 1, 1)
            ds = (probs * (d_probs - inn)).astype(BF16)
            dv[win, lo : lo + 128] += dot(probs.astype(BF16), oo)
            dk[win, lo : lo + 128] += dot(ds, qq)
            dqt = dot(k_t[lo : lo + 128, win], ds)
            dq_t[lo : lo + HD, :] = dqt[:HD, :QB]
            dq_t[lo + HD : lo + 128, :] = dqt[HD:, QB:]
        dq = (jnp.transpose(dq_t[...]) * (1.0 / math.sqrt(HD))).astype(BF16)
        dqkv_o[cols, :half] = dq
        qvs_o[0:1, :] += colsum(dq.astype(F32))

    @pl.when(g == pl.num_programs(0) - 1)
    def _():
        dqkv_o[:, half : 2 * half] = dk[...].astype(BF16)
        dvb = dv[...].astype(BF16)
        dqkv_o[:, 2 * half :] = dvb
        qvs_o[1:2, :] = colsum(dvb.astype(F32))
        for b in range(LEN // BT):
            part = dot(dqkv_o[BT * b : BT * (b + 1), :], w[:, : 3 * half], 1, 1)
            part_o[BT * b : BT * (b + 1), :] = part.astype(BF16)


def attn_bwd(layer, g, own, oth, mid, qkv, att, lse, start, gain, w):
    d = mid.shape[1]
    half = att.shape[1]
    ins = [g, own, oth, mid, qkv, att, lse, start, gain, w]
    specs = [rows_spec(d)] * 4 + [full_spec(qkv.shape), rows_spec(half)]
    specs += [full_spec(a.shape) for a in ins[6:]]
    return pl.pallas_call(
        functools.partial(attn_bwd_kernel, layer, half),
        grid=(LEN // BT,),
        in_specs=specs,
        out_specs=[
            rows_spec(d),
            rows_spec(d),
            full_spec((LEN, 3 * half)),
            full_spec((LEN, d)),
            full_spec((8, d)),
            full_spec((8, half)),
        ],
        out_shape=[
            jax.ShapeDtypeStruct((LEN, d), F32),
            jax.ShapeDtypeStruct((LEN, d), BF16),
            jax.ShapeDtypeStruct((LEN, 3 * half), BF16),
            jax.ShapeDtypeStruct((LEN, d), BF16),
            jax.ShapeDtypeStruct((8, d), F32),
            jax.ShapeDtypeStruct((8, half), F32),
        ],
        scratch_shapes=[
            pltpu.VMEM((half, LEN), BF16),
            pltpu.VMEM((LEN, half), F32),
            pltpu.VMEM((LEN, half), F32),
            pltpu.VMEM((half, QB), F32),
        ],
        name=f"attn_bwd_{layer}",
        cost_estimate=cost(24),
    )(*ins)


def norm_bwd_kernel(layer, n_dp, place, g, own, oth, x, gain, hot, *refs):
    sums, (near_o, far_o, own_o, oth_o, acc, table, small) = refs[:8], refs[8:]
    sums0, sums0b, sums1, sumg1, sumh0, sumh1, qvs0, qvs1 = sums
    w = near_o.shape[1]
    step = pl.program_id(0)

    @pl.when(step == 0)
    def _():
        acc[...] = jnp.zeros_like(acc)
        table[...] = jnp.zeros_like(table)
        small[...] = jnp.zeros_like(small)

    out, g_gain, g_shift = norm_back(
        g[...], own[...], oth[...], x[...], gain[layer, 0:1, :].astype(F32)
    )
    acc[0:1, :] += colsum(g_gain)
    acc[1:2, :] += colsum(g_shift)

    def select(q):
        far = q ^ 2
        near_o[...] = out[:, w * q : w * (q + 1)]
        far_o[...] = out[:, w * far : w * (far + 1)].astype(BF16)

    for q in range(4):
        pl.when(place[0] == q)(functools.partial(select, q))
    table[0] += dot(hot[...], near_o[...].astype(BF16), 0, 0)
    table[1] += dot(hot[...], far_o[...], 0, 0)

    @pl.when(step == pl.num_programs(0) - 1)
    def _():
        rows = [(acc, 0), (sums0, 0), (sums0b, 0), (sums1, 0)]
        rows += [(acc, 1), (sums0, 1), (sums0b, 1), (sums1, 1)]
        rows += [(sums0, 2), (sums0b, 2), (sums1, 2), (sumg1, 0)]
        cw, qw, f = acc.shape[1] // n_dp, w // n_dp, sumh0.shape[1] // 2
        for c in range(n_dp):
            for k, (ref, r) in enumerate(rows):
                v = ref[r : r + 1, cw * c : cw * (c + 1)]
                small[0, 16 * c + k : 16 * c + k + 1, 0:cw] = v
                small[1, 16 * c + k : 16 * c + k + 1, 0:cw] = v
            for slot in range(2):
                for k, ref in enumerate((sumh0, sumh1)):
                    lo = f * slot + cw * c
                    row = 16 * c + 12 + k
                    small[slot, row : row + 1, 0:cw] = ref[0:1, lo : lo + cw]
                for k, (ref, r) in enumerate(((qvs0, 0), (qvs0, 1), (qvs1, 0), (qvs1, 1))):
                    lo = w * slot + qw * c
                    row = 16 * c + k
                    small[slot, row : row + 1, cw : cw + qw] = ref[r : r + 1, lo : lo + qw]
        for slot, ref in enumerate((own_o, oth_o)):
            ref[:DOC_MOST, :] = table[slot].astype(BF16)
            ref[DOC_MOST:, :] = small[slot].astype(BF16)


def norm_bwd(layer, n_dp, place, g, own, oth, x, gain, hot, sums):
    d = x.shape[1]
    w = d // 4
    r = DOC_MOST + 16 * n_dp
    return pl.pallas_call(
        functools.partial(norm_bwd_kernel, layer, n_dp),
        grid=(LEN // BT,),
        in_specs=[SMEM]
        + [rows_spec(d)] * 4
        + [full_spec(gain.shape), rows_spec(DOC_MOST)]
        + [full_spec(v.shape) for v in sums],
        out_specs=[rows_spec(w), rows_spec(w), full_spec((r, w)), full_spec((r, w))],
        out_shape=[
            jax.ShapeDtypeStruct((LEN, w), F32),
            jax.ShapeDtypeStruct((LEN, w), BF16),
            jax.ShapeDtypeStruct((r, w), BF16),
            jax.ShapeDtypeStruct((r, w), BF16),
        ],
        scratch_shapes=[
            pltpu.VMEM((8, d), F32),
            pltpu.VMEM((2, DOC_MOST, w), F32),
            pltpu.VMEM((2, 16 * n_dp, w), F32),
        ],
        name=f"norm_bwd_{layer}",
        cost_estimate=cost(1),
    )(place, g, own, oth, x, gain, hot, *sums)


def expand_kernel(order, n_dp, rows, flags, own, got, keep, send):
    total = (own[...].astype(F32) + got[...].astype(F32)).astype(BF16)
    n = len(order)
    half = 1 << (n - 1)
    r = rows + 16

    def split(bit):
        for c in range(n_dp):
            pos = sum(((c >> b) & 1) << (n - 1 - j) for j, b in enumerate(order))
            out = keep if pos // half == bit else send
            row = r * (pos % half)
            if rows * c < DOC_MOST:
                out[row : row + rows, :] = total[rows * c : rows * (c + 1)]
            else:
                out[row : row + rows, :] = jnp.zeros((rows, total.shape[1]), BF16)
            lo = DOC_MOST + 16 * c
            out[row + rows : row + r, :] = total[lo : lo + 16]

    pl.when(flags[order[0]] == 0)(lambda: split(0))
    pl.when(flags[order[0]] == 1)(lambda: split(1))


def expand(own, got, order, n_dp, rows, flags):
    w = own.shape[1]
    shape = (n_dp * (rows + 16) // 2, w)
    keep, send = pl.pallas_call(
        functools.partial(expand_kernel, order, n_dp, rows),
        grid=(1,),
        in_specs=[SMEM, full_spec(own.shape), full_spec(own.shape)],
        out_specs=[full_spec(shape)] * 2,
        out_shape=[jax.ShapeDtypeStruct(shape, BF16)] * 2,
        name="expand",
        cost_estimate=cost(0.3),
    )(flags, own, got)
    return Part(keep, send, order)


def core_swap(a):
    return lax.ppermute(a, "mp", [(i, i ^ 1) for i in range(4)])


def y_swap(a):
    return lax.ppermute(a, "mp", [(i, i ^ 2) for i in range(4)])


def dp_swap(a, bit, n_dp):
    return lax.ppermute(a, "dp", [(i, i ^ (1 << bit)) for i in range(n_dp)])


def pick(flag, zero, one):
    return jnp.where(flag == 0, zero, one)


class Place:
    def __init__(self, n_dp):
        mp = lax.axis_index("mp")
        self.n_dp = n_dp
        self.bits = n_dp.bit_length() - 1
        self.y = mp // 2
        self.c = mp % 2
        self.dp = lax.axis_index("dp")

    def dp_bit(self, b):
        return (self.dp >> b) & 1


def row_pieces(a, at):
    rows = a.reshape(2, LEN, a.shape[1])
    return pick(at.y, rows[0], rows[1]), pick(at.y, rows[1], rows[0])


def join_row(mine, far, at):
    mine_c = core_swap(mine)
    far_c = core_swap(far)

    def joined(here, there):
        return [pick(at.c, here, there), pick(at.c, there, here)]

    near2, far2 = joined(mine, mine_c), joined(far, far_c)
    return jnp.concatenate(
        [pick(at.y, a_, b_) for a_, b_ in zip(near2, far2)]
        + [pick(at.y, b_, a_) for a_, b_ in zip(near2, far2)],
        axis=1,
    )


def own_cols(a, at, other):
    w = a.shape[1] // 4
    halves = (a[:, : 2 * w], a[:, 2 * w :])
    h = pick(at.y, halves[1], halves[0]) if other else pick(at.y, halves[0], halves[1])
    return pick(at.c, h[:, :w], h[:, w:])


def bar(*vals):
    return lax.optimization_barrier(vals)


def doc_starts(doc_ids):
    row_index = jnp.broadcast_to(jnp.arange(doc_ids.shape[1], dtype=jnp.int32), doc_ids.shape)
    previous = jnp.concatenate([doc_ids[:, :1] - 1, doc_ids[:, :-1]], axis=1)
    starts = jnp.where(doc_ids != previous, row_index, 0)
    return lax.cummax(starts, axis=1)


def on_device(
    n_dp,
    tokens,
    doc_ids,
    positions_table,
    norm_gain,
    norm_shift,
    joined_projection_weight,
    qv_bias,
    w_out,
    out_bias,
    w_fc,
    fc_bias,
    w_proj,
    cotangent,
):
    at = Place(n_dp)
    d = positions_table.shape[1]
    share = joined_projection_weight.shape[-1]
    f = w_fc.shape[-1]
    bits = list(range(2, at.bits))
    flags = jnp.stack([at.dp_bit(b) for b in range(at.bits)]).astype(jnp.int32)

    b = at.dp_bit(0) ^ at.dp_bit(1)
    flag = b.reshape(1)
    gain, shift = norm_gain, norm_shift

    a_own = [
        jnp.concatenate([joined_projection_weight[l].reshape(d, 3 * share), w_out[l].T], axis=1)
        for l in range(2)
    ]
    biases = jnp.concatenate([qv_bias.reshape(-1), fc_bias.reshape(-1)]).reshape(-1, d)
    biases = jnp.pad(biases, ((0, -biases.shape[0] % 8), (0, 0)))
    r = d // 2

    def half_rows(w):
        return lax.dynamic_slice_in_dim(w, b * r, r, 0)

    def x_swap(w):
        return dp_swap(w, 0, n_dp)

    def z_swap(w):
        return dp_swap(w, 1, n_dp)

    def by_two(one, lo=0):
        return x_swap(one[lo : lo + r // 2]), z_swap(one[lo + r // 2 : lo + r])

    def plan_one(lo=0):
        return ((lo, r, 0, 0), (0, r, 1, 0))

    def plan_two(lo=0):
        return ((lo, r, 0, 0), (0, r // 2, 1, 0), (0, r // 2, 1, r // 2))

    tok_mine, tok_theirs = row_pieces(tokens, at)
    tok_far = y_swap(tok_theirs)
    a_one0 = y_swap(jnp.concatenate([half_rows(a_own[0]), biases], axis=0))

    starts = doc_starts(doc_ids)
    start = pick(at.y, starts[0:1], starts[1:2])
    place = jnp.arange(LEN, dtype=jnp.int32) - start[0]
    hot = (place[:, None] == jnp.arange(DOC_MOST, dtype=jnp.int32)[None, :]).astype(BF16)
    embedded = dot(hot, positions_table[:DOC_MOST]).astype(BF16)

    tok_far, a_one0, embedded, hot = bar(tok_far, a_one0, embedded, hot)
    a_x, a_z = by_two(a_one0)
    fc_one0 = y_swap(half_rows(w_fc[0]))
    full_tokens = join_row(tok_mine, tok_far, at)
    small = a_one0[r:].reshape(-1)
    nq = qv_bias.size
    qvb = jnp.concatenate([qv_bias, small[:nq].reshape(qv_bias.shape)], axis=-1)
    fcb = jnp.concatenate(
        [fc_bias, small[nq : nq + fc_bias.size].reshape(fc_bias.shape)], axis=-1
    )
    send_y = jnp.concatenate([half_rows(w_proj[0]), half_rows(a_own[1])], axis=0)
    a_x, a_z, fc_one0, full_tokens, send_y = bar(a_x, a_z, fc_one0, full_tokens, send_y)

    fc_two0 = x_swap(fc_one0)
    pj_a1 = y_swap(send_y)
    x0, n0, qkv0, att0, lse0, part, wa0 = attn_fwd(
        0,
        (full_tokens, embedded),
        out_bias,
        flag,
        start,
        gain,
        shift,
        qvb,
        a_own[0],
        (plan_two(), (a_one0, a_x, a_z)),
    )
    part, x0, fc_two0, pj_a1 = bar(part, x0, fc_two0, pj_a1)
    far = core_swap(part)
    pj_x, pj_z = by_two(pj_a1)
    far, pj_x, pj_z = bar(far, pj_x, pj_z)
    mlp0 = (
        w_fc,
        (plan_one(), (fc_one0, fc_two0)),
        w_proj,
        (plan_two(), (pj_a1, pj_x, pj_z)),
    )
    a_two1 = x_swap(pj_a1[r:])
    fc_one1 = y_swap(half_rows(w_fc[1]))
    mid0, nn0, hid0, part2 = mlp_fwd(
        0, x0, part, far, out_bias, gain, shift, fcb, flag, mlp0
    )
    part2, mid0, a_two1, fc_one1 = bar(part2, mid0, a_two1, fc_one1)
    far = core_swap(part2)
    (far,) = bar(far)
    fc_two1 = x_swap(fc_one1)
    pj_one1 = y_swap(half_rows(w_proj[1]))
    cot_mine, cot_theirs = row_pieces(cotangent, at)
    cot_far = y_swap(cot_theirs)
    x1, n1, qkv1, att1, lse1, part, wa1 = attn_fwd(
        1,
        (mid0, part2, far),
        out_bias,
        flag,
        start,
        gain,
        shift,
        qvb,
        a_own[1],
        (plan_one(r), (pj_a1, a_two1)),
    )
    part, x1, fc_two1, cot_far, pj_one1 = bar(part, x1, fc_two1, cot_far, pj_one1)
    far = core_swap(part)
    pj_x, pj_z = by_two(pj_one1)
    cot = join_row(cot_mine, cot_far, at)
    far, cot, pj_x, pj_z = bar(far, cot, pj_x, pj_z)
    mlp1 = (
        w_fc,
        (plan_one(), (fc_one1, fc_two1)),
        w_proj,
        (plan_two(), (pj_one1, pj_x, pj_z)),
    )
    mid1, nn1, act, gh, part_out, part, sumg1, sumh1 = mlp_both(
        1, x1, part, far, cot, out_bias, gain, shift, fcb, flag, mlp1
    )

    def go(*parts):
        for p in parts:
            p.go(n_dp)

    def bar_parts(parts, sent, *vals):
        name = "send" if sent else "got"
        out = bar(*[getattr(p, name) for p in parts], *vals)
        for p, v in zip(parts, out):
            setattr(p, name, v)
        return out[len(parts) :]

    part, part_out, mid1, gh, act = bar(part, part_out, mid1, gh, act)
    far = core_swap(part)
    far_out = core_swap(part_out)
    o_fc, o_pj = ["y", 1, 0] + bits, [0, "y", 1] + bits
    o_a, o_b = [0, 1, "y"] + bits, [1, "y", 0] + bits
    fc1, pj1 = dw_mlp(1, nn1, cot, gh, act, (o_fc, o_pj), flags)
    far, far_out, mid1, part_out = bar_parts([fc1, pj1], True, far, far_out, mid1, part_out)
    go(fc1, pj1)
    gm1, m_low, dqkv, part, sums1, qvs1 = attn_bwd(
        1, cot, part, far, mid1, qkv1, att1, lse1, start, gain, wa1
    )
    part, gm1, m_low, dqkv, far_out, part_out = bar_parts(
        [fc1, pj1], False, part, gm1, m_low, dqkv, far_out, part_out
    )
    far = core_swap(part)
    fc1, pj1 = combine([fc1, pj1], flags)
    result = (
        mid1 + (part_out.astype(F32) + far_out.astype(F32)) + out_bias[1, 1].astype(F32)
    ).astype(BF16)
    out_near, out_send = own_cols(result, at, False), own_cols(result, at, True)
    out_near, out_send, far, m_low = bar_parts([fc1, pj1], True, out_near, out_send, far, m_low)
    out_far = y_swap(out_send)
    aa1, ab1 = dw_attn(1, n1, m_low, dqkv, att1, (o_a, ["y", 1, 0] + bits), flags)
    far, gm1 = bar_parts([aa1, ab1], True, far, gm1)
    go(fc1, pj1, aa1)
    g0, g_low, act, gh, part, sums0b, sumh0 = mlp_bwd(
        0, gm1, part, far, x1, hid0, gain, flag, mlp0
    )
    part, g0, g_low, act, gh, out_far = bar_parts(
        [fc1, pj1, aa1], False, part, g0, g_low, act, gh, out_far
    )
    far = core_swap(part)
    fc1, pj1, aa1 = combine([fc1, pj1, aa1], flags)
    far, g_low, act, gh = bar_parts([fc1, pj1, aa1, ab1], True, far, g_low, act, gh)
    go(ab1, fc1, pj1, aa1)
    fc0, pj0 = dw_mlp(0, nn0, g_low, gh, act, (o_fc, o_pj), flags)
    far, fc0.send, pj0.send, g0 = bar_parts(
        [ab1, fc1, pj1, aa1], False, far, fc0.send, pj0.send, g0
    )
    last1 = combine([fc1, pj1], flags, merged=True)
    aa1, ab1 = combine([aa1, ab1], flags)
    far, g0, part = bar_parts([last1, aa1, ab1, fc0, pj0], True, far, g0, part)
    go(fc0, pj0, aa1, ab1, last1)
    gm0, m_low, dqkv, part, sums0, qvs0 = attn_bwd(
        0, g0, part, far, mid0, qkv0, att0, lse0, start, gain, wa0
    )
    part, gm0, m_low, dqkv, out_near, out_far = bar_parts(
        [fc0, pj0, aa1, ab1, last1], False, part, gm0, m_low, dqkv, out_near, out_far
    )
    far = core_swap(part)
    fc0, pj0 = combine([fc0, pj0], flags)
    (ab1,) = combine([ab1], flags)
    far, m_low, dqkv = bar_parts([fc0, pj0, ab1], True, far, m_low, dqkv)
    go(fc0, pj0, ab1)
    aa0, ab0 = dw_attn(0, n0, m_low, dqkv, att0, (o_a, o_b), flags)
    far, gm0, part = bar_parts([aa0, ab0], True, far, gm0, part)
    go(aa0, ab0)
    quarter = (2 * at.y + at.c).astype(jnp.int32).reshape(1)
    sums = (sums0, sums0b, sums1, sumg1, sumh0, sumh1, qvs0, qvs1)
    near, far_send, pk, pk_send = norm_bwd(0, n_dp, quarter, gm0, part, far, x0, gain, hot, sums)
    near, far_send, pk, pk_send = bar_parts([fc0, pj0], False, near, far_send, pk, pk_send)
    pk_got = y_swap(pk_send)
    g_far = y_swap(far_send)
    fc0, pj0 = combine([fc0, pj0], flags)
    fc0.send, pj0.send, pk_got, pk = bar_parts([ab1], False, fc0.send, pj0.send, pk_got, pk)
    go(fc0, pj0)
    last3 = combine([aa1, ab1], flags, merged=True)
    go(last3)
    rows = positions_table.shape[0] // n_dp
    pk = expand(pk, pk_got, [0, 1] + bits, n_dp, rows, flags)
    (pk.send,) = bar_parts([aa0, ab0], False, pk.send)
    aa0, ab0 = combine([aa0, ab0], flags)
    bar_parts([aa0, ab0, pk], True)
    g_far, near = bar_parts([fc0, pj0], False, g_far, near)
    go(aa0, ab0, pk)
    last0 = combine([fc0, pj0], flags, merged=True)
    out = jnp.concatenate([pick(at.y, out_near, out_far), pick(at.y, out_far, out_near)], axis=0)
    last0.send, out = bar_parts([aa0, ab0, pk], False, last0.send, out)
    go(last0)
    aa0, ab0, pk = combine([aa0, ab0, pk], flags)
    g_far, near = bar_parts([aa0, ab0, pk], True, g_far, near)
    go(aa0, ab0, pk)
    g_far = g_far.astype(F32)
    grad_tokens = jnp.concatenate([pick(at.y, near, g_far), pick(at.y, g_far, near)], axis=0)
    (grad_tokens,) = bar_parts([aa0, ab0, pk], False, grad_tokens)
    last2 = combine([aa0, ab0], flags, merged=True)
    (pk,) = combine([pk], flags)
    bar_parts([last2, pk], True)
    go(last2, pk)
    lasts = [last1, last0, last3, last2, pk]
    while len(lasts[0].order) > 1:
        lasts = combine(lasts, flags)
        go(*lasts)
    g_fc, g_pj, g_qkv, g_wo, g_pos, small = final(lasts, f, share, rows)
    w = d // n_dp
    s = small[:, :w]
    qv = small[:4, w : w + share // n_dp]
    return (
        out,
        grad_tokens,
        g_pos.T,
        s[0:4].reshape(2, 2, w),
        s[4:8].reshape(2, 2, w),
        g_qkv.transpose(0, 2, 1, 3),
        qv.reshape(2, 2, w // 4),
        g_wo,
        s[8:12].reshape(2, 2, w),
        g_fc,
        s[12:14],
        g_pj.transpose(0, 2, 1),
    )


def solution(mesh):
    n_dp = mesh.shape["dp"]
    in_specs = (
        P("dp", "mp"),
        P("dp", None),
        P(),
        P(),
        P(),
        P(None, None, None, "mp"),
        P(None, None, "mp"),
        P(None, "mp", None),
        P(),
        P(None, None, "mp"),
        P(None, "mp"),
        P(None, "mp", None),
        P("dp", "mp"),
    )
    out_specs = (
        P("dp", "mp"),
        P("dp", "mp"),
        P("dp", "mp"),
        P(None, None, "dp"),
        P(None, None, "dp"),
        P(None, "dp", None, "mp"),
        P(None, None, ("mp", "dp")),
        P(None, "mp", "dp"),
        P(None, None, "dp"),
        P(None, "dp", "mp"),
        P(None, ("mp", "dp")),
        P(None, "mp", "dp"),
    )
    return jax.shard_map(
        functools.partial(on_device, n_dp),
        mesh=mesh,
        in_specs=in_specs,
        out_specs=out_specs,
        check_vma=False,
    )
```

```python
import functools
import math

import jax
import jax.numpy as jnp
from jax import lax
from jax.experimental import pallas as pl
from jax.experimental.pallas import tpu as pltpu
from jax.sharding import PartitionSpec as P

HD = 64
LEN = 1024
DOC_MOST = 384
EPS = 1e-05
BT = 256
QB = 128
KW = QB + DOC_MOST
F32 = jnp.float32
BF16 = jnp.bfloat16
GELU_C = math.sqrt(2.0 / math.pi)


ANY = pl.BlockSpec(memory_space=pl.ANY)
SMEM = pl.BlockSpec(memory_space=pltpu.SMEM)


def cost(us):
    return pl.CostEstimate(flops=int(us * 1.15e9), transcendentals=0, bytes_accessed=0)


def full_spec(shape):
    return pl.BlockSpec(shape, lambda g: (0,) * len(shape))


def rows_spec(width):
    return pl.BlockSpec((BT, width), lambda g: (g, 0))


def dot(a, b, ca=1, cb=0):
    return lax.dot_general(a, b, (((ca,), (cb,)), ((), ())), preferred_element_type=F32)


def normed_parts(v):
    centred = v - jnp.mean(v, axis=-1, keepdims=True)
    variance = jnp.mean(centred * centred, axis=-1, keepdims=True)
    rstd = lax.rsqrt(variance + EPS)
    return centred * rstd, rstd


def norm_back(g, own, oth, v, gain):
    grad = own.astype(F32) + oth.astype(F32)
    xhat, rstd = normed_parts(v)
    gn = grad * gain
    out = g + rstd * (
        gn
        - jnp.mean(gn, axis=-1, keepdims=True)
        - xhat * jnp.mean(gn * xhat, axis=-1, keepdims=True)
    )
    return out, grad * xhat, grad


def colsum(v):
    return jnp.sum(v, axis=0, keepdims=True)


def head_pair(block):
    lane = lax.broadcasted_iota(jnp.int32, block.shape, 1)
    zero = jnp.zeros_like(block)
    return jnp.concatenate(
        [jnp.where(lane < HD, block, zero), jnp.where(lane < HD, zero, block)], axis=0
    )


def window_bias(start_ref, i, ks):
    kidx = lax.broadcasted_iota(jnp.int32, (KW, QB), 0) + ks
    qidx = lax.broadcasted_iota(jnp.int32, (KW, QB), 1) + i * QB
    first = start_ref[0:1, pl.ds(pl.multiple_of(i * QB, QB), QB)]
    bias = jnp.where((kidx >= first) & (kidx <= qidx), 0.0, -1e30).astype(F32)
    return jnp.concatenate([bias, bias], axis=1)


def copies(pairs, sems):
    out = [pltpu.make_async_copy(a, b, sems.at[j]) for j, (a, b) in enumerate(pairs)]
    for c in out:
        c.start()
    return out


def join_pieces(flag, plan, refs, dst, cols=slice(None)):
    r = dst.shape[0] // 2
    out = []
    for (lo, n, other, off), ref in zip(plan, refs):
        row = (1 - flag if other else flag) * r + off
        out.append((ref.at[pl.ds(lo, n)], dst.at[pl.ds(pl.multiple_of(row, 8), n), cols]))
    return out


def gelu_parts(v):
    v2 = v * v
    t = jnp.tanh(GELU_C * v * (1.0 + 0.044715 * v2))
    cdf = 0.5 * (1.0 + t)
    slope = cdf + (0.5 * GELU_C) * v * (1.0 - t * t) * (1.0 + (3 * 0.044715) * v2)
    return v * cdf, slope


def gained(xhat, gain, shift, layer, which):
    row = slice(which, which + 1)
    return (xhat * gain[layer, row, :].astype(F32) + shift[layer, row, :].astype(F32)).astype(BF16)


def attn_fwd_kernel(layer, first, half, plan, *refs):
    if first:
        (tok, emb, flag, start, gain, shift, qvb, a_own) = refs[:8]
        rest = refs[8:]
        x = tok[...].astype(F32) + emb[...].astype(F32)
    else:
        (mid, own, oth, outb, flag, start, gain, shift, qvb, a_own) = refs[:10]
        rest = refs[10:]
        x = (
            mid[...]
            + (own[...].astype(F32) + oth[...].astype(F32))
            + outb[layer - 1, 1:2, :].astype(F32)
        )
    a_refs, rest = rest[: len(plan)], rest[len(plan) :]
    x_o, n_o, qkv_o, att_o, lse_o, part_o, w_o, v_t, o_t, a_buf, sems = rest
    g = pl.program_id(0)
    sh = half // 2

    @pl.when(g == 0)
    def _():
        moves = copies(
            [(a_own, a_buf.at[0])] + join_pieces(flag[0], plan, a_refs, a_buf.at[1]), sems
        )
        qkv_o[pl.ds(BT, KW - BT), half : 2 * half] = jnp.zeros((KW - BT, half), BF16)
        v_t[:, pl.ds(BT, KW - BT)] = jnp.zeros((half, KW - BT), BF16)
        lse_o[...] = jnp.zeros_like(lse_o)
        for m in moves:
            m.wait()
        for j in range(4):
            for s in range(2):
                w_o[:, (2 * j + s) * sh : (2 * j + s + 1) * sh] = a_buf[s, :, j * sh : (j + 1) * sh]

    x_o[...] = x
    xhat, _ = normed_parts(x)
    normed = gained(xhat, gain, shift, layer, 0)
    n_o[...] = normed
    qkv = dot(normed, w_o[:, : 3 * half])
    q = (qkv[:, :half] + qvb[layer, 0:1, :].astype(F32)).astype(BF16)
    k = qkv[:, half : 2 * half].astype(BF16)
    v = qkv[:, 2 * half :] + qvb[layer, 1:2, :].astype(F32)
    rows = pl.ds(pl.multiple_of(g * BT, BT), BT)
    qkv_o[rows, :half] = q
    qkv_o[rows, half : 2 * half] = k
    qkv_o[rows, 2 * half :] = v.astype(BF16)
    v_t[:, rows] = jnp.transpose(v).astype(BF16)
    q = q * jnp.asarray(1.0 / math.sqrt(HD), BF16)
    for s in range(BT // QB):
        i = g * (BT // QB) + s
        ks = pl.multiple_of(jnp.maximum(i - DOC_MOST // QB, 0) * QB, QB)
        bias = window_bias(start, i, ks)
        cols = pl.ds(pl.multiple_of(i * QB, QB), QB)
        for p in range(half // 128):
            lo = 128 * p
            qq = head_pair(q[QB * s : QB * (s + 1), lo : lo + 128])
            kp = qkv_o[pl.ds(ks, KW), half + lo : half + lo + 128]
            scores = dot(kp, qq, 1, 1) + bias
            peak = jnp.max(scores, axis=0, keepdims=True)
            e = jnp.exp(scores - peak)
            total = jnp.sum(e, axis=0, keepdims=True)
            ot = dot(v_t[lo : lo + 128, pl.ds(ks, KW)], e.astype(BF16))
            inv = 1.0 / total
            o_t[lo : lo + HD, :] = ot[:HD, :QB] * inv[:, :QB]
            o_t[lo + HD : lo + 128, :] = ot[HD:, QB:] * inv[:, QB:]
            lse = peak + jnp.log(total)
            lse_o[2 * p : 2 * p + 1, cols] = lse[:, :QB]
            lse_o[2 * p + 1 : 2 * p + 2, cols] = lse[:, QB:]
        att_o[QB * s : QB * (s + 1), :] = jnp.transpose(o_t[...]).astype(BF16)
    part_o[...] = dot(att_o[...], w_o[:, 3 * half :], 1, 1).astype(BF16)


def attn_fwd(layer, stream_in, outb, flag, start, gain, shift, qvb, a_own, a_oth):
    first = layer == 0
    d = gain.shape[-1]
    half = a_own.shape[1] // 2
    ins = list(stream_in)
    specs = [rows_spec(d) for _ in ins]
    if not first:
        ins.append(outb)
        specs.append(full_spec(outb.shape))
    plan, arrays = a_oth
    ins += [flag, start, gain, shift, qvb, a_own, *arrays]
    specs += [SMEM] + [full_spec(a.shape) for a in (start, gain, shift, qvb)]
    specs += [ANY] * (1 + len(arrays))
    return pl.pallas_call(
        functools.partial(attn_fwd_kernel, layer, first, half, plan),
        grid=(LEN // BT,),
        in_specs=specs,
        out_specs=[
            rows_spec(d),
            rows_spec(d),
            full_spec((LEN, 3 * half)),
            rows_spec(half),
            full_spec((8, LEN)),
            rows_spec(d),
            full_spec((d, 4 * half)),
        ],
        out_shape=[
            jax.ShapeDtypeStruct((LEN, d), F32),
            jax.ShapeDtypeStruct((LEN, d), BF16),
            jax.ShapeDtypeStruct((LEN, 3 * half), BF16),
            jax.ShapeDtypeStruct((LEN, half), BF16),
            jax.ShapeDtypeStruct((8, LEN), F32),
            jax.ShapeDtypeStruct((LEN, d), BF16),
            jax.ShapeDtypeStruct((d, 4 * half), BF16),
        ],
        scratch_shapes=[
            pltpu.VMEM((half, LEN), BF16),
            pltpu.VMEM((half, QB), F32),
            pltpu.VMEM((2, d, 2 * half), BF16),
            pltpu.SemaphoreType.DMA((1 + len(plan),)),
        ],
        name=f"attn_fwd_{layer}",
        cost_estimate=cost(22),
    )(*ins)


def load_mlp(layer, flag, plans, weights, wfc, wproj, sems):
    d = wfc.shape[0]
    f = wfc.shape[1] // 2
    n = len(plans[0])
    return copies(
        [(weights[0].at[layer], wfc.at[:, pl.ds(0, f)])]
        + join_pieces(flag[0], plans[0], weights[2 : 2 + n], wfc, pl.ds(f, f))
        + [(weights[1].at[layer], wproj.at[pl.ds(0, f)])]
        + join_pieces(flag[0], plans[1], weights[2 + n :], wproj.at[pl.ds(f, f)]),
        sems,
    )


def mlp_scratch(d, f2, plans):
    return [
        pltpu.VMEM((d, f2), BF16),
        pltpu.VMEM((f2, d), BF16),
        pltpu.SemaphoreType.DMA((2 + len(plans[0]) + len(plans[1]),)),
    ]


def mlp_weights(weights):
    w_fc, fc_oth, w_proj, pj_oth = weights
    return (fc_oth[0], pj_oth[0]), [w_fc, w_proj, *fc_oth[1], *pj_oth[1]]


def mlp_fwd_kernel(layer, plans, x, own, oth, outb, gain, shift, fcb, flag, *refs):
    nw = 2 + len(plans[0]) + len(plans[1])
    weights = refs[:nw]
    mid_o, n_o, h_o, part_o, wfc, wproj, sems = refs[nw:]

    @pl.when(pl.program_id(0) == 0)
    def _():
        for m in load_mlp(layer, flag, plans, weights, wfc, wproj, sems):
            m.wait()

    mid = (
        x[...]
        + (own[...].astype(F32) + oth[...].astype(F32))
        + outb[layer, 0:1, :].astype(F32)
    )
    mid_o[...] = mid
    xhat, _ = normed_parts(mid)
    normed = gained(xhat, gain, shift, layer, 1)
    n_o[...] = normed
    hidden = dot(normed, wfc[...]) + fcb[layer : layer + 1, :].astype(F32)
    h_o[...] = hidden.astype(BF16)
    t = jnp.tanh(GELU_C * hidden * (1.0 + 0.044715 * hidden * hidden))
    act = (0.5 * hidden * (1.0 + t)).astype(BF16)
    part_o[...] = dot(act, wproj[...]).astype(BF16)


def mlp_fwd(layer, x, own, oth, outb, gain, shift, fcb, flag, weights):
    d = x.shape[1]
    f = fcb.shape[1]
    plans, arrays = mlp_weights(weights)
    ins = [x, own, oth, outb, gain, shift, fcb, flag, *arrays]
    specs = [rows_spec(d)] * 3 + [full_spec(a.shape) for a in ins[3:7]] + [SMEM] + [ANY] * len(arrays)
    return pl.pallas_call(
        functools.partial(mlp_fwd_kernel, layer, plans),
        grid=(LEN // BT,),
        in_specs=specs,
        out_specs=[rows_spec(d), rows_spec(d), rows_spec(f), rows_spec(d)],
        out_shape=[
            jax.ShapeDtypeStruct((LEN, d), F32),
            jax.ShapeDtypeStruct((LEN, d), BF16),
            jax.ShapeDtypeStruct((LEN, f), BF16),
            jax.ShapeDtypeStruct((LEN, d), BF16),
        ],
        scratch_shapes=mlp_scratch(d, f, plans),
        name=f"mlp_fwd_{layer}",
        cost_estimate=cost(12),
    )(*ins)


def mlp_both_kernel(layer, plans, x, own, oth, cot, outb, gain, shift, fcb, flag, *refs):
    nw = 2 + len(plans[0]) + len(plans[1])
    weights = refs[:nw]
    mid_o, n_o, act_o, gh_o, out_o, part_o, sumg_o, sumh_o, wfc, wproj, sems = refs[nw:]

    @pl.when(pl.program_id(0) == 0)
    def _():
        moves = load_mlp(layer, flag, plans, weights, wfc, wproj, sems)
        sumg_o[...] = jnp.zeros_like(sumg_o)
        sumh_o[...] = jnp.zeros_like(sumh_o)
        for m in moves:
            m.wait()

    mid = (
        x[...]
        + (own[...].astype(F32) + oth[...].astype(F32))
        + outb[layer, 0:1, :].astype(F32)
    )
    mid_o[...] = mid
    xhat, _ = normed_parts(mid)
    normed = gained(xhat, gain, shift, layer, 1)
    n_o[...] = normed
    grad_act = dot(cot[...], wproj[...], 1, 1)
    value, slope = gelu_parts(dot(normed, wfc[...]) + fcb[layer : layer + 1, :].astype(F32))
    act = value.astype(BF16)
    act_o[...] = act
    gh = (grad_act * slope).astype(BF16)
    gh_o[...] = gh
    part_o[...] = dot(gh, wfc[...], 1, 1).astype(BF16)
    out_o[...] = dot(act, wproj[...]).astype(BF16)
    sumg_o[0:1, :] += colsum(cot[...].astype(F32))
    sumh_o[0:1, :] += colsum(gh.astype(F32))


def mlp_both(layer, x, own, oth, cot, outb, gain, shift, fcb, flag, weights):
    d = x.shape[1]
    f = fcb.shape[1]
    plans, arrays = mlp_weights(weights)
    ins = [x, own, oth, cot, outb, gain, shift, fcb, flag, *arrays]
    specs = [rows_spec(d)] * 4 + [full_spec(a.shape) for a in ins[4:8]] + [SMEM] + [ANY] * len(arrays)
    widths = [d, d, f, f, d, d]
    kinds = [F32, BF16, BF16, BF16, BF16, BF16]
    return pl.pallas_call(
        functools.partial(mlp_both_kernel, layer, plans),
        grid=(LEN // BT,),
        in_specs=specs,
        out_specs=[rows_spec(w) for w in widths] + [full_spec((8, d)), full_spec((8, f))],
        out_shape=[jax.ShapeDtypeStruct((LEN, w), k) for w, k in zip(widths, kinds)]
        + [jax.ShapeDtypeStruct((8, d), F32), jax.ShapeDtypeStruct((8, f), F32)],
        scratch_shapes=mlp_scratch(d, f, plans),
        name=f"mlp_both_{layer}",
        cost_estimate=cost(18),
    )(*ins)


def mlp_bwd_kernel(layer, plans, gm, own, oth, x, h, gain, flag, *refs):
    nw = 2 + len(plans[0]) + len(plans[1])
    weights = refs[:nw]
    g_o, low_o, act_o, gh_o, part_o, sums_o, sumh_o, wfc, wproj, sems = refs[nw:]

    @pl.when(pl.program_id(0) == 0)
    def _():
        moves = load_mlp(layer, flag, plans, weights, wfc, wproj, sems)
        sums_o[...] = jnp.zeros_like(sums_o)
        sumh_o[...] = jnp.zeros_like(sumh_o)
        for m in moves:
            m.wait()

    grad, g_gain, g_shift = norm_back(
        gm[...], own[...], oth[...], x[...], gain[layer + 1, 0:1, :].astype(F32)
    )
    sums_o[0:1, :] += colsum(g_gain)
    sums_o[1:2, :] += colsum(g_shift)
    sums_o[2:3, :] += colsum(grad)
    g_o[...] = grad
    low = grad.astype(BF16)
    low_o[...] = low
    grad_act = dot(low, wproj[...], 1, 1)
    value, slope = gelu_parts(h[...].astype(F32))
    act_o[...] = value.astype(BF16)
    gh = (grad_act * slope).astype(BF16)
    gh_o[...] = gh
    part_o[...] = dot(gh, wfc[...], 1, 1).astype(BF16)
    sumh_o[0:1, :] += colsum(gh.astype(F32))


def mlp_bwd(layer, gm, own, oth, x, h, gain, flag, weights):
    d = x.shape[1]
    f = h.shape[1]
    plans, arrays = mlp_weights(weights)
    ins = [gm, own, oth, x, h, gain, flag, *arrays]
    specs = [rows_spec(d)] * 4 + [rows_spec(f), full_spec(gain.shape), SMEM] + [ANY] * len(arrays)
    widths = [d, d, f, f, d]
    kinds = [F32, BF16, BF16, BF16, BF16]
    return pl.pallas_call(
        functools.partial(mlp_bwd_kernel, layer, plans),
        grid=(LEN // BT,),
        in_specs=specs,
        out_specs=[rows_spec(w) for w in widths] + [full_spec((8, d)), full_spec((8, f))],
        out_shape=[jax.ShapeDtypeStruct((LEN, w), k) for w, k in zip(widths, kinds)]
        + [jax.ShapeDtypeStruct((8, d), F32), jax.ShapeDtypeStruct((8, f), F32)],
        scratch_shapes=mlp_scratch(d, f, plans),
        name=f"mlp_bwd_{layer}",
        cost_estimate=cost(16),
    )(*ins)


def stage(buf, value, order):
    dims = [o for o in order if o != "y"]
    n = len(dims)
    r = value.shape[0] >> n
    for c in range(1 << n):
        pos = sum(((c >> b) & 1) << (n - 1 - j) for j, b in enumerate(dims))
        buf[r * pos : r * (pos + 1), :] = value[r * c : r * (c + 1)].astype(BF16)


def ship(buf, keep, send, slot, order, flags, sems):
    if order[0] == "y":
        pairs = [(buf, send if slot else keep)]
    else:
        half = buf.shape[0] // 2
        f = flags[order[0]]
        lo = [pl.multiple_of(h * half, 16) for h in (f, 1 - f)]
        pairs = [
            (buf.at[pl.ds(lo[0], half)], keep.at[slot]),
            (buf.at[pl.ds(lo[1], half)], send.at[slot]),
        ]
    return [pltpu.make_async_copy(a, b, sems.at[j]) for j, (a, b) in enumerate(pairs)]


def first_shape(order, d, w):
    return (d, w) if order[0] == "y" else (2, d // 2, w)


def dw_mlp_kernel(orders, flags, n, low, gh, act, *refs):
    outs, (bufs, sems) = refs[:4], refs[4:]
    j = pl.program_id(0)

    def moves(t, slot):
        keep, send = outs[2 * t : 2 * t + 2]
        return ship(bufs.at[t, slot], keep, send, slot, orders[t], flags, sems.at[t, slot])

    for t, (a, b) in enumerate(((n, gh), (low, act))):
        stage(bufs.at[t, j], dot(a[...], b[...], 0, 0), orders[t])
        for slot in range(2):

            @pl.when(j == slot)
            def _():
                for m in moves(t, slot):
                    m.start()

    @pl.when(j == 1)
    def _():
        for t in range(2):
            for slot in range(2):
                for m in moves(t, slot):
                    m.wait()


def dw_mlp(layer, n, low, gh, act, orders, flags):
    t, d = n.shape
    f = gh.shape[1] // 2
    col = pl.BlockSpec((t, f), lambda j: (0, j))
    shapes = [first_shape(o, d, f) for o in orders for _ in range(2)]
    k0, s0, k1, s1 = pl.pallas_call(
        functools.partial(dw_mlp_kernel, orders),
        grid=(2,),
        in_specs=[SMEM, full_spec(n.shape), full_spec(low.shape), col, col],
        out_specs=[ANY] * 4,
        out_shape=[jax.ShapeDtypeStruct(s, BF16) for s in shapes],
        scratch_shapes=[pltpu.VMEM((2, 2, d, f), BF16), pltpu.SemaphoreType.DMA((2, 2, 2))],
        name=f"dw_mlp_{layer}",
        cost_estimate=cost(9),
    )(flags, n, low, gh, act)
    return Part(k0, s0, orders[0]), Part(k1, s1, orders[1])


def dw_attn_kernel(orders, flags, n, low, dqkv, att, *refs):
    outs, (bufs, sems) = refs[:4], refs[4:]
    sh = att.shape[1] // 2
    moves = []

    def send_off(t, values):
        for slot in range(2):
            both = jnp.concatenate(
                [v[:, (2 * j + slot) * sh : (2 * j + slot + 1) * sh] for v, j in values], axis=1
            )
            stage(bufs.at[t, slot], both, orders[t])
            keep, send = outs[2 * t : 2 * t + 2]
            for m in ship(
                bufs.at[t, slot], keep, send, slot, orders[t], flags, sems.at[t, slot]
            ):
                m.start()
                moves.append(m)

    half = 2 * sh
    qk = dot(n[...], dqkv[:, : 2 * half], 0, 0)
    send_off(0, [(qk, 0), (qk, 1)])
    v = dot(n[...], dqkv[:, 2 * half :], 0, 0)
    wo = dot(low[...], att[...], 0, 0)
    send_off(1, [(v, 0), (wo, 0)])
    for m in moves:
        m.wait()


def dw_attn(layer, n, low, dqkv, att, orders, flags):
    d = n.shape[1]
    w = att.shape[1]
    ins = (n, low, dqkv, att)
    shapes = [first_shape(o, d, w) for o in orders for _ in range(2)]
    k0, s0, k1, s1 = pl.pallas_call(
        functools.partial(dw_attn_kernel, orders),
        grid=(1,),
        in_specs=[SMEM] + [full_spec(a.shape) for a in ins],
        out_specs=[ANY] * 4,
        out_shape=[jax.ShapeDtypeStruct(s, BF16) for s in shapes],
        scratch_shapes=[pltpu.VMEM((2, 2, d, w), BF16), pltpu.SemaphoreType.DMA((2, 2, 2))],
        name=f"dw_attn_{layer}",
        cost_estimate=cost(7),
    )(flags, *ins)
    return Part(k0, s0, orders[0]), Part(k1, s1, orders[1])


def combine_kernel(steps, merged, flags, *refs):
    ins, outs = refs[: 2 * len(steps)], refs[2 * len(steps) :]
    lo = 0
    for k, o in enumerate(steps):
        keep, got = ins[2 * k : 2 * k + 2]

        def total(at):
            return keep[at].astype(F32) + got[at].astype(F32)

        if o is None:
            outs[k][...] = total(...)
            continue
        dst = outs if merged else outs[2 * k : 2 * k + 2]
        cols = slice(lo, lo + keep.shape[-1]) if merged else slice(None)
        if o == "y":
            halves = [total(0), total(1)]
        else:
            r = keep.shape[-2] // 2
            lead = (slice(None),) * (len(keep.shape) - 2)
            rows = [pl.ds(pl.multiple_of(h * r, 8), r) for h in (flags[o], 1 - flags[o])]
            halves = [total(lead + (row, slice(None))) for row in rows]
        for out, v in zip(dst, halves):
            out[..., cols] = v.astype(BF16)
        if merged:
            lo += keep.shape[-1]


def combine(parts, flags, merged=False):
    steps = [p.order[1] if len(p.order) > 1 else None for p in parts]
    wide = all(p.keep.shape[-1] % 384 == 0 for p in parts)
    ncol = 3 if wide and not merged and parts[0].keep.size >= 2**18 else 1

    def spec(shape):
        block = shape[:-1] + (shape[-1] // ncol,)
        return pl.BlockSpec(block, lambda g: (0,) * (len(shape) - 1) + (g,))

    ins, shapes = [], []
    for p, o in zip(parts, steps):
        ins += [p.keep, p.got]
        s = p.keep.shape
        if o is None:
            shapes.append(jax.ShapeDtypeStruct(s, F32))
        else:
            s = s[1:] if o == "y" else s[:-2] + (s[-2] // 2, s[-1])
            shapes += [jax.ShapeDtypeStruct(s, BF16)] * 2
    if merged:
        s = (shapes[0].shape[0], sum(p.keep.shape[-1] for p in parts))
        shapes = [jax.ShapeDtypeStruct(s, BF16)] * 2
    outs = pl.pallas_call(
        functools.partial(combine_kernel, steps, merged),
        grid=(ncol,),
        in_specs=[SMEM] + [spec(a.shape) for a in ins],
        out_specs=[spec(a.shape) for a in shapes],
        out_shape=shapes,
        name="combine",
        cost_estimate=cost(0.3),
    )(flags, *ins)
    if merged:
        return Part(outs[0], outs[1], parts[0].order[1:])
    if steps[0] is None:
        return list(outs)
    return [
        Part(outs[2 * k], outs[2 * k + 1], p.order[1:]) for k, p in enumerate(parts)
    ]


def final_kernel(f, share, *refs):
    (m1, m0, a0, pk), outs = [(refs[2 * k], refs[2 * k + 1]) for k in range(4)], refs[8:]
    fc_o, pj_o, qkv_o, wo_o, pos_o, gain_o, shift_o, bias_o, fcb_o, qvb_o = outs

    def total(pair, lo, n):
        return pair[0][:, lo : lo + n].astype(F32) + pair[1][:, lo : lo + n].astype(F32)

    for l, (m, a, lo) in enumerate(((m0, a0, 0), (m1, m0, 2 * f))):
        fc_o[l] = total(m, 0, f)
        pj_o[l] = total(m, f, f)
        v = total(a, lo, 4 * share)
        for j in range(3):
            qkv_o[l, j] = v[:, share * j : share * (j + 1)]
        wo_o[l] = jnp.transpose(v[:, 3 * share :])
    v = total(pk, 0, share)
    rows = pos_o.shape[1]
    pos_o[...] = jnp.transpose(v[:rows])
    v = v[rows:]
    w = gain_o.shape[2]
    for l in range(2):
        for k, ref in enumerate((gain_o, shift_o, bias_o)):
            ref[l] = v[4 * k + 2 * l : 4 * k + 2 * l + 2, :w]
        qvb_o[l] = v[2 * l : 2 * l + 2, w : w + qvb_o.shape[2]]
    fcb_o[...] = v[12:14, :w]


def final(parts, f, share, rows, n_dp):
    r = parts[0].keep.shape[0]
    ins = [v for p in parts for v in (p.keep, p.got)]
    shapes = [(2, r, f), (2, r, f), (2, 3, r, share), (2, share, r), (share, rows)]
    shapes += [(2, 2, r)] * 3 + [(2, r), (2, 2, share // n_dp)]
    return pl.pallas_call(
        functools.partial(final_kernel, f, share),
        grid=(1,),
        in_specs=[full_spec(v.shape) for v in ins],
        out_specs=[full_spec(v) for v in shapes],
        out_shape=[jax.ShapeDtypeStruct(v, F32) for v in shapes],
        name="final",
        cost_estimate=cost(3),
    )(*ins)


class Part:
    def __init__(self, keep, send, order):
        self.keep, self.send, self.order = keep, send, list(order)

    def go(self, n_dp):
        o = self.order[0]
        self.got = y_swap(self.send) if o == "y" else dp_swap(self.send, o, n_dp)


def attn_bwd_kernel(layer, half, *refs):
    (g_i, own, oth, mid, qkv, att, lse, start, gain, w) = refs[:10]
    (gm_o, low_o, dqkv_o, part_o, sums_o, qvs_o, k_t, dk, dv, dq_t) = refs[10:]
    g = pl.program_id(0)

    @pl.when(g == 0)
    def _():
        sums_o[...] = jnp.zeros_like(sums_o)
        qvs_o[...] = jnp.zeros_like(qvs_o)
        dk[...] = jnp.zeros_like(dk)
        dv[...] = jnp.zeros_like(dv)
        for b in range(LEN // BT):
            block = qkv[BT * b : BT * (b + 1), half : 2 * half].astype(F32)
            k_t[:, BT * b : BT * (b + 1)] = jnp.transpose(block).astype(BF16)

    gm, g_gain, g_shift = norm_back(
        g_i[...].astype(F32), own[...], oth[...], mid[...], gain[layer, 1:2, :].astype(F32)
    )
    gm_o[...] = gm
    sums_o[0:1, :] += colsum(g_gain)
    sums_o[1:2, :] += colsum(g_shift)
    sums_o[2:3, :] += colsum(gm)
    low = gm.astype(BF16)
    low_o[...] = low
    d_att = dot(low, w[:, 3 * half :]).astype(BF16)
    prod = d_att.astype(F32) * att[...].astype(F32)
    head = lax.broadcasted_iota(jnp.int32, (8, half), 1) // HD
    pick = (head == lax.broadcasted_iota(jnp.int32, (8, half), 0)).astype(F32)
    inner = lax.dot_general(
        pick,
        prod,
        (((1,), (1,)), ((), ())),
        preferred_element_type=F32,
        precision=lax.Precision.HIGHEST,
    )
    rows = pl.ds(pl.multiple_of(g * BT, BT), BT)
    q = qkv[rows, :half] * jnp.asarray(1.0 / math.sqrt(HD), BF16)
    for s in range(BT // QB):
        i = g * (BT // QB) + s
        ks = pl.multiple_of(jnp.maximum(i - DOC_MOST // QB, 0) * QB, QB)
        bias = window_bias(start, i, ks)
        cols = pl.ds(pl.multiple_of(i * QB, QB), QB)
        win = pl.ds(ks, KW)
        for p in range(half // 128):
            lo = 128 * p
            qq = head_pair(q[QB * s : QB * (s + 1), lo : lo + 128])
            oo = head_pair(d_att[QB * s : QB * (s + 1), lo : lo + 128])
            kp = qkv[win, half + lo : half + lo + 128]
            vp = qkv[win, 2 * half + lo : 2 * half + lo + 128]
            total = jnp.concatenate(
                [lse[2 * p : 2 * p + 1, cols], lse[2 * p + 1 : 2 * p + 2, cols]], axis=1
            )
            inn = jnp.concatenate(
                [
                    inner[2 * p : 2 * p + 1, QB * s : QB * (s + 1)],
                    inner[2 * p + 1 : 2 * p + 2, QB * s : QB * (s + 1)],
                ],
                axis=1,
            )
            probs = jnp.exp(dot(kp, qq, 1, 1) + bias - total)
            d_probs = dot(vp, oo, 1, 1)
            ds = (probs * (d_probs - inn)).astype(BF16)
            dv[win, lo : lo + 128] += dot(probs.astype(BF16), oo)
            dk[win, lo : lo + 128] += dot(ds, qq)
            dqt = dot(k_t[lo : lo + 128, win], ds)
            dq_t[lo : lo + HD, :] = dqt[:HD, :QB]
            dq_t[lo + HD : lo + 128, :] = dqt[HD:, QB:]
        dq = (jnp.transpose(dq_t[...]) * (1.0 / math.sqrt(HD))).astype(BF16)
        dqkv_o[cols, :half] = dq
        qvs_o[0:1, :] += colsum(dq.astype(F32))

    @pl.when(g == pl.num_programs(0) - 1)
    def _():
        dqkv_o[:, half : 2 * half] = dk[...].astype(BF16)
        dvb = dv[...].astype(BF16)
        dqkv_o[:, 2 * half :] = dvb
        qvs_o[1:2, :] = colsum(dvb.astype(F32))
        for b in range(LEN // BT):
            part = dot(dqkv_o[BT * b : BT * (b + 1), :], w[:, : 3 * half], 1, 1)
            part_o[BT * b : BT * (b + 1), :] = part.astype(BF16)


def attn_bwd(layer, g, own, oth, mid, qkv, att, lse, start, gain, w):
    d = mid.shape[1]
    half = att.shape[1]
    ins = [g, own, oth, mid, qkv, att, lse, start, gain, w]
    specs = [rows_spec(d)] * 4 + [full_spec(qkv.shape), rows_spec(half)]
    specs += [full_spec(a.shape) for a in ins[6:]]
    return pl.pallas_call(
        functools.partial(attn_bwd_kernel, layer, half),
        grid=(LEN // BT,),
        in_specs=specs,
        out_specs=[
            rows_spec(d),
            rows_spec(d),
            full_spec((LEN, 3 * half)),
            full_spec((LEN, d)),
            full_spec((8, d)),
            full_spec((8, half)),
        ],
        out_shape=[
            jax.ShapeDtypeStruct((LEN, d), F32),
            jax.ShapeDtypeStruct((LEN, d), BF16),
            jax.ShapeDtypeStruct((LEN, 3 * half), BF16),
            jax.ShapeDtypeStruct((LEN, d), BF16),
            jax.ShapeDtypeStruct((8, d), F32),
            jax.ShapeDtypeStruct((8, half), F32),
        ],
        scratch_shapes=[
            pltpu.VMEM((half, LEN), BF16),
            pltpu.VMEM((LEN, half), F32),
            pltpu.VMEM((LEN, half), F32),
            pltpu.VMEM((half, QB), F32),
        ],
        name=f"attn_bwd_{layer}",
        cost_estimate=cost(24),
    )(*ins)


def norm_bwd_kernel(layer, n_dp, place, g, own, oth, x, gain, hot, *refs):
    sums, (near_o, far_o, own_o, oth_o, acc, table, small) = refs[:8], refs[8:]
    sums0, sums0b, sums1, sumg1, sumh0, sumh1, qvs0, qvs1 = sums
    w = near_o.shape[1]
    step = pl.program_id(0)

    @pl.when(step == 0)
    def _():
        acc[...] = jnp.zeros_like(acc)
        table[...] = jnp.zeros_like(table)
        small[...] = jnp.zeros_like(small)

    out, g_gain, g_shift = norm_back(
        g[...], own[...], oth[...], x[...], gain[layer, 0:1, :].astype(F32)
    )
    acc[0:1, :] += colsum(g_gain)
    acc[1:2, :] += colsum(g_shift)

    def select(q):
        far = q ^ 2
        near_o[...] = out[:, w * q : w * (q + 1)]
        far_o[...] = out[:, w * far : w * (far + 1)].astype(BF16)

    for q in range(4):
        pl.when(place[0] == q)(functools.partial(select, q))
    table[0] += dot(hot[...], near_o[...].astype(BF16), 0, 0)
    table[1] += dot(hot[...], far_o[...], 0, 0)

    @pl.when(step == pl.num_programs(0) - 1)
    def _():
        rows = [(acc, 0), (sums0, 0), (sums0b, 0), (sums1, 0)]
        rows += [(acc, 1), (sums0, 1), (sums0b, 1), (sums1, 1)]
        rows += [(sums0, 2), (sums0b, 2), (sums1, 2), (sumg1, 0)]
        cw, qw, f = acc.shape[1] // n_dp, w // n_dp, sumh0.shape[1] // 2
        for c in range(n_dp):
            for k, (ref, r) in enumerate(rows):
                v = ref[r : r + 1, cw * c : cw * (c + 1)]
                small[0, 16 * c + k : 16 * c + k + 1, 0:cw] = v
                small[1, 16 * c + k : 16 * c + k + 1, 0:cw] = v
            for slot in range(2):
                for k, ref in enumerate((sumh0, sumh1)):
                    lo = f * slot + cw * c
                    row = 16 * c + 12 + k
                    small[slot, row : row + 1, 0:cw] = ref[0:1, lo : lo + cw]
                for k, (ref, r) in enumerate(((qvs0, 0), (qvs0, 1), (qvs1, 0), (qvs1, 1))):
                    lo = w * slot + qw * c
                    row = 16 * c + k
                    small[slot, row : row + 1, cw : cw + qw] = ref[r : r + 1, lo : lo + qw]
        for slot, ref in enumerate((own_o, oth_o)):
            ref[:DOC_MOST, :] = table[slot].astype(BF16)
            ref[DOC_MOST:, :] = small[slot].astype(BF16)


def norm_bwd(layer, n_dp, place, g, own, oth, x, gain, hot, sums):
    d = x.shape[1]
    w = d // 4
    r = DOC_MOST + 16 * n_dp
    return pl.pallas_call(
        functools.partial(norm_bwd_kernel, layer, n_dp),
        grid=(LEN // BT,),
        in_specs=[SMEM]
        + [rows_spec(d)] * 4
        + [full_spec(gain.shape), rows_spec(DOC_MOST)]
        + [full_spec(v.shape) for v in sums],
        out_specs=[rows_spec(w), rows_spec(w), full_spec((r, w)), full_spec((r, w))],
        out_shape=[
            jax.ShapeDtypeStruct((LEN, w), F32),
            jax.ShapeDtypeStruct((LEN, w), BF16),
            jax.ShapeDtypeStruct((r, w), BF16),
            jax.ShapeDtypeStruct((r, w), BF16),
        ],
        scratch_shapes=[
            pltpu.VMEM((8, d), F32),
            pltpu.VMEM((2, DOC_MOST, w), F32),
            pltpu.VMEM((2, 16 * n_dp, w), F32),
        ],
        name=f"norm_bwd_{layer}",
        cost_estimate=cost(1),
    )(place, g, own, oth, x, gain, hot, *sums)


def expand_kernel(order, n_dp, rows, flags, own, got, keep, send):
    total = (own[...].astype(F32) + got[...].astype(F32)).astype(BF16)
    n = len(order)
    half = 1 << (n - 1)
    r = rows + 16

    def split(bit):
        for c in range(n_dp):
            pos = sum(((c >> b) & 1) << (n - 1 - j) for j, b in enumerate(order))
            out = keep if pos // half == bit else send
            row = r * (pos % half)
            if rows * c < DOC_MOST:
                out[row : row + rows, :] = total[rows * c : rows * (c + 1)]
            else:
                out[row : row + rows, :] = jnp.zeros((rows, total.shape[1]), BF16)
            lo = DOC_MOST + 16 * c
            out[row + rows : row + r, :] = total[lo : lo + 16]

    pl.when(flags[order[0]] == 0)(lambda: split(0))
    pl.when(flags[order[0]] == 1)(lambda: split(1))


def expand(own, got, order, n_dp, rows, flags):
    w = own.shape[1]
    shape = (n_dp * (rows + 16) // 2, w)
    keep, send = pl.pallas_call(
        functools.partial(expand_kernel, order, n_dp, rows),
        grid=(1,),
        in_specs=[SMEM, full_spec(own.shape), full_spec(own.shape)],
        out_specs=[full_spec(shape)] * 2,
        out_shape=[jax.ShapeDtypeStruct(shape, BF16)] * 2,
        name="expand",
        cost_estimate=cost(0.3),
    )(flags, own, got)
    return Part(keep, send, order)


def core_swap(a):
    return lax.ppermute(a, "mp", [(i, i ^ 1) for i in range(4)])


def y_swap(a):
    return lax.ppermute(a, "mp", [(i, i ^ 2) for i in range(4)])


def dp_swap(a, bit, n_dp):
    return lax.ppermute(a, "dp", [(i, i ^ (1 << bit)) for i in range(n_dp)])


def pick(flag, zero, one):
    return jnp.where(flag == 0, zero, one)


class Place:
    def __init__(self, n_dp):
        mp = lax.axis_index("mp")
        self.n_dp = n_dp
        self.bits = n_dp.bit_length() - 1
        self.y = mp // 2
        self.c = mp % 2
        self.dp = lax.axis_index("dp")

    def dp_bit(self, b):
        return (self.dp >> b) & 1


def row_pieces(a, at):
    rows = a.reshape(2, LEN, a.shape[1])
    return pick(at.y, rows[0], rows[1]), pick(at.y, rows[1], rows[0])


def join_row(mine, far, at):
    mine_c = core_swap(mine)
    far_c = core_swap(far)

    def joined(here, there):
        return [pick(at.c, here, there), pick(at.c, there, here)]

    near2, far2 = joined(mine, mine_c), joined(far, far_c)
    return jnp.concatenate(
        [pick(at.y, a_, b_) for a_, b_ in zip(near2, far2)]
        + [pick(at.y, b_, a_) for a_, b_ in zip(near2, far2)],
        axis=1,
    )


def own_cols(a, at, other):
    w = a.shape[1] // 4
    halves = (a[:, : 2 * w], a[:, 2 * w :])
    h = pick(at.y, halves[1], halves[0]) if other else pick(at.y, halves[0], halves[1])
    return pick(at.c, h[:, :w], h[:, w:])


def bar(*vals):
    return lax.optimization_barrier(vals)


def doc_starts(doc_ids):
    row_index = jnp.broadcast_to(jnp.arange(doc_ids.shape[1], dtype=jnp.int32), doc_ids.shape)
    previous = jnp.concatenate([doc_ids[:, :1] - 1, doc_ids[:, :-1]], axis=1)
    starts = jnp.where(doc_ids != previous, row_index, 0)
    return lax.cummax(starts, axis=1)


def on_device(
    n_dp,
    tokens,
    doc_ids,
    positions_table,
    norm_gain,
    norm_shift,
    joined_projection_weight,
    qv_bias,
    w_out,
    out_bias,
    w_fc,
    fc_bias,
    w_proj,
    cotangent,
):
    at = Place(n_dp)
    d = positions_table.shape[1]
    share = joined_projection_weight.shape[-1]
    f = w_fc.shape[-1]
    bits = list(range(2, at.bits))
    flags = jnp.stack([at.dp_bit(b) for b in range(at.bits)]).astype(jnp.int32)

    b = at.dp_bit(0) ^ at.dp_bit(1)
    flag = b.reshape(1)
    gain, shift = norm_gain, norm_shift

    a_own = [
        jnp.concatenate([joined_projection_weight[l].reshape(d, 3 * share), w_out[l].T], axis=1)
        for l in range(2)
    ]
    biases = jnp.concatenate([qv_bias.reshape(-1), fc_bias.reshape(-1)]).reshape(-1, d)
    biases = jnp.pad(biases, ((0, -biases.shape[0] % 8), (0, 0)))
    r = d // 2

    def half_rows(w):
        return lax.dynamic_slice_in_dim(w, b * r, r, 0)

    def x_swap(w):
        return dp_swap(w, 0, n_dp)

    def z_swap(w):
        return dp_swap(w, 1, n_dp)

    def by_two(one, lo=0):
        return x_swap(one[lo : lo + r // 2]), z_swap(one[lo + r // 2 : lo + r])

    def plan_one(lo=0):
        return ((lo, r, 0, 0), (0, r, 1, 0))

    def plan_two(lo=0):
        return ((lo, r, 0, 0), (0, r // 2, 1, 0), (0, r // 2, 1, r // 2))

    tok_mine, tok_theirs = row_pieces(tokens, at)
    tok_far = y_swap(tok_theirs)
    a_one0 = y_swap(jnp.concatenate([half_rows(a_own[0]), biases], axis=0))

    starts = doc_starts(doc_ids)
    start = pick(at.y, starts[0:1], starts[1:2])
    place = jnp.arange(LEN, dtype=jnp.int32) - start[0]
    hot = (place[:, None] == jnp.arange(DOC_MOST, dtype=jnp.int32)[None, :]).astype(BF16)
    embedded = dot(hot, positions_table[:DOC_MOST]).astype(BF16)

    tok_far, a_one0, embedded, hot = bar(tok_far, a_one0, embedded, hot)
    a_x, a_z = by_two(a_one0)
    fc_one0 = y_swap(half_rows(w_fc[0]))
    full_tokens = join_row(tok_mine, tok_far, at)
    small = a_one0[r:].reshape(-1)
    nq = qv_bias.size
    qvb = jnp.concatenate([qv_bias, small[:nq].reshape(qv_bias.shape)], axis=-1)
    fcb = jnp.concatenate(
        [fc_bias, small[nq : nq + fc_bias.size].reshape(fc_bias.shape)], axis=-1
    )
    send_y = jnp.concatenate([half_rows(w_proj[0]), half_rows(a_own[1])], axis=0)
    a_x, a_z, fc_one0, full_tokens, send_y = bar(a_x, a_z, fc_one0, full_tokens, send_y)

    fc_two0 = x_swap(fc_one0)
    pj_a1 = y_swap(send_y)
    x0, n0, qkv0, att0, lse0, part, wa0 = attn_fwd(
        0,
        (full_tokens, embedded),
        out_bias,
        flag,
        start,
        gain,
        shift,
        qvb,
        a_own[0],
        (plan_two(), (a_one0, a_x, a_z)),
    )
    part, x0, fc_two0, pj_a1 = bar(part, x0, fc_two0, pj_a1)
    far = core_swap(part)
    pj_x, pj_z = by_two(pj_a1)
    far, pj_x, pj_z = bar(far, pj_x, pj_z)
    mlp0 = (
        w_fc,
        (plan_one(), (fc_one0, fc_two0)),
        w_proj,
        (plan_two(), (pj_a1, pj_x, pj_z)),
    )
    a_two1 = x_swap(pj_a1[r:])
    fc_one1 = y_swap(half_rows(w_fc[1]))
    mid0, nn0, hid0, part2 = mlp_fwd(
        0, x0, part, far, out_bias, gain, shift, fcb, flag, mlp0
    )
    part2, mid0, a_two1, fc_one1 = bar(part2, mid0, a_two1, fc_one1)
    far = core_swap(part2)
    (far,) = bar(far)
    fc_two1 = x_swap(fc_one1)
    pj_one1 = y_swap(half_rows(w_proj[1]))
    cot_mine, cot_theirs = row_pieces(cotangent, at)
    cot_far = y_swap(cot_theirs)
    x1, n1, qkv1, att1, lse1, part, wa1 = attn_fwd(
        1,
        (mid0, part2, far),
        out_bias,
        flag,
        start,
        gain,
        shift,
        qvb,
        a_own[1],
        (plan_one(r), (pj_a1, a_two1)),
    )
    part, x1, fc_two1, cot_far, pj_one1 = bar(part, x1, fc_two1, cot_far, pj_one1)
    far = core_swap(part)
    pj_x, pj_z = by_two(pj_one1)
    cot = join_row(cot_mine, cot_far, at)
    far, cot, pj_x, pj_z = bar(far, cot, pj_x, pj_z)
    mlp1 = (
        w_fc,
        (plan_one(), (fc_one1, fc_two1)),
        w_proj,
        (plan_two(), (pj_one1, pj_x, pj_z)),
    )
    mid1, nn1, act, gh, part_out, part, sumg1, sumh1 = mlp_both(
        1, x1, part, far, cot, out_bias, gain, shift, fcb, flag, mlp1
    )

    def go(*parts):
        for p in parts:
            p.go(n_dp)

    def bar_parts(parts, sent, *vals):
        name = "send" if sent else "got"
        out = bar(*[getattr(p, name) for p in parts], *vals)
        for p, v in zip(parts, out):
            setattr(p, name, v)
        return out[len(parts) :]

    part, part_out, mid1, gh, act = bar(part, part_out, mid1, gh, act)
    far = core_swap(part)
    far_out = core_swap(part_out)
    o_fc, o_pj = ["y", 1, 0] + bits, [0, "y", 1] + bits
    o_a, o_b = [0, 1, "y"] + bits, [1, "y", 0] + bits
    fc1, pj1 = dw_mlp(1, nn1, cot, gh, act, (o_fc, o_pj), flags)
    far, far_out, mid1, part_out = bar_parts([fc1, pj1], True, far, far_out, mid1, part_out)
    go(fc1, pj1)
    gm1, m_low, dqkv, part, sums1, qvs1 = attn_bwd(
        1, cot, part, far, mid1, qkv1, att1, lse1, start, gain, wa1
    )
    part, gm1, m_low, dqkv, far_out, part_out = bar_parts(
        [fc1, pj1], False, part, gm1, m_low, dqkv, far_out, part_out
    )
    far = core_swap(part)
    fc1, pj1 = combine([fc1, pj1], flags)
    result = (
        mid1 + (part_out.astype(F32) + far_out.astype(F32)) + out_bias[1, 1].astype(F32)
    ).astype(BF16)
    out_near, out_send = own_cols(result, at, False), own_cols(result, at, True)
    out_near, out_send, far, m_low = bar_parts([fc1, pj1], True, out_near, out_send, far, m_low)
    aa1, ab1 = dw_attn(1, n1, m_low, dqkv, att1, (o_a, ["y", 1, 0] + bits), flags)
    far, gm1 = bar_parts([aa1, ab1], True, far, gm1)
    go(fc1, pj1, aa1)
    g0, g_low, act, gh, part, sums0b, sumh0 = mlp_bwd(
        0, gm1, part, far, x1, hid0, gain, flag, mlp0
    )
    part, g0, g_low, act, gh = bar_parts([fc1, pj1, aa1], False, part, g0, g_low, act, gh)
    far = core_swap(part)
    fc1, pj1, aa1 = combine([fc1, pj1, aa1], flags)
    far, g_low, act, gh = bar_parts([fc1, pj1, aa1, ab1], True, far, g_low, act, gh)
    go(ab1, fc1, pj1, aa1)
    fc0, pj0 = dw_mlp(0, nn0, g_low, gh, act, (o_fc, o_pj), flags)
    far, fc0.send, pj0.send, g0 = bar_parts(
        [ab1, fc1, pj1, aa1], False, far, fc0.send, pj0.send, g0
    )
    last1 = combine([fc1, pj1], flags, merged=True)
    aa1, ab1 = combine([aa1, ab1], flags)
    far, g0, part = bar_parts([last1, aa1, ab1, fc0, pj0], True, far, g0, part)
    go(fc0, pj0, aa1, ab1, last1)
    gm0, m_low, dqkv, part, sums0, qvs0 = attn_bwd(
        0, g0, part, far, mid0, qkv0, att0, lse0, start, gain, wa0
    )
    part, gm0, m_low, dqkv = bar_parts(
        [fc0, pj0, aa1, ab1, last1], False, part, gm0, m_low, dqkv
    )
    far = core_swap(part)
    fc0, pj0 = combine([fc0, pj0], flags)
    (ab1,) = combine([ab1], flags)
    far, m_low, dqkv = bar_parts([fc0, pj0, ab1], True, far, m_low, dqkv)
    go(fc0, pj0, ab1)
    aa0, ab0 = dw_attn(0, n0, m_low, dqkv, att0, (o_a, o_b), flags)
    far, gm0, part = bar_parts([aa0, ab0], True, far, gm0, part)
    go(aa0, ab0)
    quarter = (2 * at.y + at.c).astype(jnp.int32).reshape(1)
    sums = (sums0, sums0b, sums1, sumg1, sumh0, sumh1, qvs0, qvs1)
    near, far_send, pk, pk_send = norm_bwd(0, n_dp, quarter, gm0, part, far, x0, gain, hot, sums)
    near, far_send, pk, pk_send = bar_parts([fc0, pj0], False, near, far_send, pk, pk_send)
    pk_got = y_swap(pk_send)
    fc0, pj0 = combine([fc0, pj0], flags)
    fc0.send, pj0.send, pk_got, pk, far_send = bar_parts(
        [ab1], False, fc0.send, pj0.send, pk_got, pk, far_send
    )
    go(fc0, pj0)
    g_far = y_swap(far_send)
    rows = positions_table.shape[0] // n_dp
    pk = expand(pk, pk_got, [0, 1] + bits, n_dp, rows, flags)
    (pk.send,) = bar_parts([aa0, ab0], False, pk.send)
    aa0, ab0 = combine([aa0, ab0], flags)
    aa0.send, ab0.send, pk.send, out_send, out_near = bar_parts(
        [fc0, pj0], False, aa0.send, ab0.send, pk.send, out_send, out_near
    )
    go(aa0, ab0, pk)
    last0 = combine([fc0, pj0, aa1, ab1], flags, merged=True)
    last0.send, g_far, near = bar_parts([aa0, ab0, pk], False, last0.send, g_far, near)
    go(last0)
    aa0, ab0, pk = combine([aa0, ab0, pk], flags)
    out_send, out_near = bar_parts([aa0, ab0, pk], True, out_send, out_near)
    go(aa0, ab0, pk)
    g_far = g_far.astype(F32)
    grad_tokens = jnp.concatenate([pick(at.y, near, g_far), pick(at.y, g_far, near)], axis=0)
    out_send, out_near = bar_parts([aa0, ab0, pk], False, out_send, out_near)
    last2 = combine([aa0, ab0], flags, merged=True)
    (pk,) = combine([pk], flags)
    out_send, out_near, grad_tokens = bar_parts([last2, pk], True, out_send, out_near, grad_tokens)
    out_far = y_swap(out_send)
    go(last2, pk)
    out = jnp.concatenate([pick(at.y, out_near, out_far), pick(at.y, out_far, out_near)], axis=0)
    lasts = [last1, last0, last2, pk]
    while len(lasts[0].order) > 1:
        lasts = combine(lasts, flags)
        go(*lasts)
    g_fc, g_pj, g_qkv, g_wo, g_pos, g_gain, g_shift, g_bias, g_fcb, g_qvb = final(
        lasts, f, share, rows, n_dp
    )
    return (
        out,
        grad_tokens,
        g_pos.T,
        g_gain,
        g_shift,
        g_qkv.transpose(0, 2, 1, 3),
        g_qvb,
        g_wo,
        g_bias,
        g_fc,
        g_fcb,
        g_pj.transpose(0, 2, 1),
    )


def solution(mesh):
    n_dp = mesh.shape["dp"]
    in_specs = (
        P("dp", "mp"),
        P("dp", None),
        P(),
        P(),
        P(),
        P(None, None, None, "mp"),
        P(None, None, "mp"),
        P(None, "mp", None),
        P(),
        P(None, None, "mp"),
        P(None, "mp"),
        P(None, "mp", None),
        P("dp", "mp"),
    )
    out_specs = (
        P("dp", "mp"),
        P("dp", "mp"),
        P("dp", "mp"),
        P(None, None, "dp"),
        P(None, None, "dp"),
        P(None, "dp", None, "mp"),
        P(None, None, ("mp", "dp")),
        P(None, "mp", "dp"),
        P(None, None, "dp"),
        P(None, "dp", "mp"),
        P(None, ("mp", "dp")),
        P(None, "mp", "dp"),
    )
    return jax.shard_map(
        functools.partial(on_device, n_dp),
        mesh=mesh,
        in_specs=in_specs,
        out_specs=out_specs,
        check_vma=False,
    )
```

```python
import functools
import math

import jax
import jax.numpy as jnp
from jax import lax
from jax.experimental import pallas as pl
from jax.experimental.pallas import tpu as pltpu
from jax.sharding import PartitionSpec as P

HD = 64
LEN = 1024
DOC_MOST = 384
EPS = 1e-05
BT = 256
QB = 128
KW = QB + DOC_MOST
F32 = jnp.float32
BF16 = jnp.bfloat16
GELU_C = math.sqrt(2.0 / math.pi)


ANY = pl.BlockSpec(memory_space=pl.ANY)
SMEM = pl.BlockSpec(memory_space=pltpu.SMEM)


def cost(us):
    return pl.CostEstimate(flops=int(us * 1.15e9), transcendentals=0, bytes_accessed=0)


def full_spec(shape):
    return pl.BlockSpec(shape, lambda g: (0,) * len(shape))


def rows_spec(width):
    return pl.BlockSpec((BT, width), lambda g: (g, 0))


def dot(a, b, ca=1, cb=0):
    return lax.dot_general(a, b, (((ca,), (cb,)), ((), ())), preferred_element_type=F32)


def normed_parts(v):
    centred = v - jnp.mean(v, axis=-1, keepdims=True)
    variance = jnp.mean(centred * centred, axis=-1, keepdims=True)
    rstd = lax.rsqrt(variance + EPS)
    return centred * rstd, rstd


def norm_back(g, own, oth, v, gain):
    grad = own.astype(F32) + oth.astype(F32)
    xhat, rstd = normed_parts(v)
    gn = grad * gain
    out = g + rstd * (
        gn
        - jnp.mean(gn, axis=-1, keepdims=True)
        - xhat * jnp.mean(gn * xhat, axis=-1, keepdims=True)
    )
    return out, grad * xhat, grad


def colsum(v):
    return jnp.sum(v, axis=0, keepdims=True)


def head_pair(block):
    lane = lax.broadcasted_iota(jnp.int32, block.shape, 1)
    zero = jnp.zeros_like(block)
    return jnp.concatenate(
        [jnp.where(lane < HD, block, zero), jnp.where(lane < HD, zero, block)], axis=0
    )


def window_bias(start_ref, i, ks):
    kidx = lax.broadcasted_iota(jnp.int32, (KW, QB), 0) + ks
    qidx = lax.broadcasted_iota(jnp.int32, (KW, QB), 1) + i * QB
    first = start_ref[0:1, pl.ds(pl.multiple_of(i * QB, QB), QB)]
    bias = jnp.where((kidx >= first) & (kidx <= qidx), 0.0, -1e30).astype(F32)
    return jnp.concatenate([bias, bias], axis=1)


def copies(pairs, sems):
    out = [pltpu.make_async_copy(a, b, sems.at[j]) for j, (a, b) in enumerate(pairs)]
    for c in out:
        c.start()
    return out


def join_pieces(flag, plan, refs, dst, cols=slice(None)):
    r = dst.shape[0] // 2
    out = []
    for (lo, n, other, off), ref in zip(plan, refs):
        row = (1 - flag if other else flag) * r + off
        out.append((ref.at[pl.ds(lo, n)], dst.at[pl.ds(pl.multiple_of(row, 8), n), cols]))
    return out


def join_quarters(place, pieces, dst):
    w = pieces[0].shape[1]

    def put(q):
        for k, piece in enumerate(pieces):
            lo = w * (q ^ k)
            dst[:, lo : lo + w] = piece[...]

    for q in range(4):
        pl.when(place[0] == q)(functools.partial(put, q))


def gelu_parts(v):
    v2 = v * v
    t = jnp.tanh(GELU_C * v * (1.0 + 0.044715 * v2))
    cdf = 0.5 * (1.0 + t)
    slope = cdf + (0.5 * GELU_C) * v * (1.0 - t * t) * (1.0 + (3 * 0.044715) * v2)
    return v * cdf, slope


def gained(xhat, gain, shift, layer, which):
    row = slice(which, which + 1)
    return (xhat * gain[layer, row, :].astype(F32) + shift[layer, row, :].astype(F32)).astype(BF16)


def attn_fwd_kernel(layer, first, half, plan, *refs):
    if first:
        pieces, (emb, place, flag, start, gain, shift, qvb, a_own) = refs[:4], refs[4:12]
        rest, tok = refs[12:-1], refs[-1]
        join_quarters(place, pieces, tok)
        x = tok[...].astype(F32) + emb[...].astype(F32)
    else:
        (mid, own, oth, outb, flag, start, gain, shift, qvb, a_own) = refs[:10]
        rest = refs[10:]
        x = (
            mid[...]
            + (own[...].astype(F32) + oth[...].astype(F32))
            + outb[layer - 1, 1:2, :].astype(F32)
        )
    a_refs, rest = rest[: len(plan)], rest[len(plan) :]
    x_o, n_o, qkv_o, att_o, lse_o, part_o, w_o, v_t, o_t, a_buf, sems = rest
    g = pl.program_id(0)
    sh = half // 2

    @pl.when(g == 0)
    def _():
        moves = copies(
            [(a_own, a_buf.at[0])] + join_pieces(flag[0], plan, a_refs, a_buf.at[1]), sems
        )
        qkv_o[pl.ds(BT, KW - BT), half : 2 * half] = jnp.zeros((KW - BT, half), BF16)
        v_t[:, pl.ds(BT, KW - BT)] = jnp.zeros((half, KW - BT), BF16)
        lse_o[...] = jnp.zeros_like(lse_o)
        for m in moves:
            m.wait()
        for j in range(4):
            for s in range(2):
                w_o[:, (2 * j + s) * sh : (2 * j + s + 1) * sh] = a_buf[s, :, j * sh : (j + 1) * sh]

    x_o[...] = x
    xhat, _ = normed_parts(x)
    normed = gained(xhat, gain, shift, layer, 0)
    n_o[...] = normed
    qkv = dot(normed, w_o[:, : 3 * half])
    q = (qkv[:, :half] + qvb[layer, 0:1, :].astype(F32)).astype(BF16)
    k = qkv[:, half : 2 * half].astype(BF16)
    v = qkv[:, 2 * half :] + qvb[layer, 1:2, :].astype(F32)
    rows = pl.ds(pl.multiple_of(g * BT, BT), BT)
    qkv_o[rows, :half] = q
    qkv_o[rows, half : 2 * half] = k
    qkv_o[rows, 2 * half :] = v.astype(BF16)
    v_t[:, rows] = jnp.transpose(v).astype(BF16)
    q = q * jnp.asarray(1.0 / math.sqrt(HD), BF16)
    for s in range(BT // QB):
        i = g * (BT // QB) + s
        ks = pl.multiple_of(jnp.maximum(i - DOC_MOST // QB, 0) * QB, QB)
        bias = window_bias(start, i, ks)
        cols = pl.ds(pl.multiple_of(i * QB, QB), QB)
        for p in range(half // 128):
            lo = 128 * p
            qq = head_pair(q[QB * s : QB * (s + 1), lo : lo + 128])
            kp = qkv_o[pl.ds(ks, KW), half + lo : half + lo + 128]
            scores = dot(kp, qq, 1, 1) + bias
            peak = jnp.max(scores, axis=0, keepdims=True)
            e = jnp.exp(scores - peak)
            total = jnp.sum(e, axis=0, keepdims=True)
            ot = dot(v_t[lo : lo + 128, pl.ds(ks, KW)], e.astype(BF16))
            inv = 1.0 / total
            o_t[lo : lo + HD, :] = ot[:HD, :QB] * inv[:, :QB]
            o_t[lo + HD : lo + 128, :] = ot[HD:, QB:] * inv[:, QB:]
            lse = peak + jnp.log(total)
            lse_o[2 * p : 2 * p + 1, cols] = lse[:, :QB]
            lse_o[2 * p + 1 : 2 * p + 2, cols] = lse[:, QB:]
        att_o[QB * s : QB * (s + 1), :] = jnp.transpose(o_t[...]).astype(BF16)
    part_o[...] = dot(att_o[...], w_o[:, 3 * half :], 1, 1).astype(BF16)


def attn_fwd(layer, stream_in, outb, flag, start, gain, shift, qvb, a_own, a_oth):
    first = layer == 0
    d = gain.shape[-1]
    half = a_own.shape[1] // 2
    ins = list(stream_in)
    specs = [SMEM if a.ndim == 1 else rows_spec(a.shape[1]) for a in ins]
    if not first:
        ins.append(outb)
        specs.append(full_spec(outb.shape))
    plan, arrays = a_oth
    ins += [flag, start, gain, shift, qvb, a_own, *arrays]
    specs += [SMEM] + [full_spec(a.shape) for a in (start, gain, shift, qvb)]
    specs += [ANY] * (1 + len(arrays))
    return pl.pallas_call(
        functools.partial(attn_fwd_kernel, layer, first, half, plan),
        grid=(LEN // BT,),
        in_specs=specs,
        out_specs=[
            rows_spec(d),
            rows_spec(d),
            full_spec((LEN, 3 * half)),
            rows_spec(half),
            full_spec((8, LEN)),
            rows_spec(d),
            full_spec((d, 4 * half)),
        ],
        out_shape=[
            jax.ShapeDtypeStruct((LEN, d), F32),
            jax.ShapeDtypeStruct((LEN, d), BF16),
            jax.ShapeDtypeStruct((LEN, 3 * half), BF16),
            jax.ShapeDtypeStruct((LEN, half), BF16),
            jax.ShapeDtypeStruct((8, LEN), F32),
            jax.ShapeDtypeStruct((LEN, d), BF16),
            jax.ShapeDtypeStruct((d, 4 * half), BF16),
        ],
        scratch_shapes=[
            pltpu.VMEM((half, LEN), BF16),
            pltpu.VMEM((half, QB), F32),
            pltpu.VMEM((2, d, 2 * half), BF16),
            pltpu.SemaphoreType.DMA((1 + len(plan),)),
        ]
        + ([pltpu.VMEM((BT, d), BF16)] if first else []),
        name=f"attn_fwd_{layer}",
        cost_estimate=cost(22),
    )(*ins)


def load_mlp(layer, flag, plans, weights, wfc, wproj, sems):
    d = wfc.shape[0]
    f = wfc.shape[1] // 2
    n = len(plans[0])
    return copies(
        [(weights[0].at[layer], wfc.at[:, pl.ds(0, f)])]
        + join_pieces(flag[0], plans[0], weights[2 : 2 + n], wfc, pl.ds(f, f))
        + [(weights[1].at[layer], wproj.at[pl.ds(0, f)])]
        + join_pieces(flag[0], plans[1], weights[2 + n :], wproj.at[pl.ds(f, f)]),
        sems,
    )


def mlp_scratch(d, f2, plans):
    return [
        pltpu.VMEM((d, f2), BF16),
        pltpu.VMEM((f2, d), BF16),
        pltpu.SemaphoreType.DMA((2 + len(plans[0]) + len(plans[1]),)),
    ]


def mlp_weights(weights):
    w_fc, fc_oth, w_proj, pj_oth = weights
    return (fc_oth[0], pj_oth[0]), [w_fc, w_proj, *fc_oth[1], *pj_oth[1]]


def mlp_fwd_kernel(layer, plans, x, own, oth, outb, gain, shift, fcb, flag, *refs):
    nw = 2 + len(plans[0]) + len(plans[1])
    weights = refs[:nw]
    mid_o, n_o, h_o, part_o, wfc, wproj, sems = refs[nw:]

    @pl.when(pl.program_id(0) == 0)
    def _():
        for m in load_mlp(layer, flag, plans, weights, wfc, wproj, sems):
            m.wait()

    mid = (
        x[...]
        + (own[...].astype(F32) + oth[...].astype(F32))
        + outb[layer, 0:1, :].astype(F32)
    )
    mid_o[...] = mid
    xhat, _ = normed_parts(mid)
    normed = gained(xhat, gain, shift, layer, 1)
    n_o[...] = normed
    hidden = dot(normed, wfc[...]) + fcb[layer : layer + 1, :].astype(F32)
    h_o[...] = hidden.astype(BF16)
    t = jnp.tanh(GELU_C * hidden * (1.0 + 0.044715 * hidden * hidden))
    act = (0.5 * hidden * (1.0 + t)).astype(BF16)
    part_o[...] = dot(act, wproj[...]).astype(BF16)


def mlp_fwd(layer, x, own, oth, outb, gain, shift, fcb, flag, weights):
    d = x.shape[1]
    f = fcb.shape[1]
    plans, arrays = mlp_weights(weights)
    ins = [x, own, oth, outb, gain, shift, fcb, flag, *arrays]
    specs = [rows_spec(d)] * 3 + [full_spec(a.shape) for a in ins[3:7]] + [SMEM] + [ANY] * len(arrays)
    return pl.pallas_call(
        functools.partial(mlp_fwd_kernel, layer, plans),
        grid=(LEN // BT,),
        in_specs=specs,
        out_specs=[rows_spec(d), rows_spec(d), rows_spec(f), rows_spec(d)],
        out_shape=[
            jax.ShapeDtypeStruct((LEN, d), F32),
            jax.ShapeDtypeStruct((LEN, d), BF16),
            jax.ShapeDtypeStruct((LEN, f), BF16),
            jax.ShapeDtypeStruct((LEN, d), BF16),
        ],
        scratch_shapes=mlp_scratch(d, f, plans),
        name=f"mlp_fwd_{layer}",
        cost_estimate=cost(12),
    )(*ins)


def mlp_both_kernel(
    layer, plans, x, own, oth, c0, c1, c2, c3, place, outb, gain, shift, fcb, flag, *refs
):
    nw = 2 + len(plans[0]) + len(plans[1])
    weights = refs[:nw]
    mid_o, n_o, act_o, gh_o, out_o, part_o, cot, sumg_o, sumh_o, wfc, wproj, sems = refs[nw:]
    join_quarters(place, (c0, c1, c2, c3), cot)

    @pl.when(pl.program_id(0) == 0)
    def _():
        moves = load_mlp(layer, flag, plans, weights, wfc, wproj, sems)
        sumg_o[...] = jnp.zeros_like(sumg_o)
        sumh_o[...] = jnp.zeros_like(sumh_o)
        for m in moves:
            m.wait()

    mid = (
        x[...]
        + (own[...].astype(F32) + oth[...].astype(F32))
        + outb[layer, 0:1, :].astype(F32)
    )
    mid_o[...] = mid
    xhat, _ = normed_parts(mid)
    normed = gained(xhat, gain, shift, layer, 1)
    n_o[...] = normed
    grad_act = dot(cot[...], wproj[...], 1, 1)
    value, slope = gelu_parts(dot(normed, wfc[...]) + fcb[layer : layer + 1, :].astype(F32))
    act = value.astype(BF16)
    act_o[...] = act
    gh = (grad_act * slope).astype(BF16)
    gh_o[...] = gh
    part_o[...] = dot(gh, wfc[...], 1, 1).astype(BF16)
    out_o[...] = dot(act, wproj[...]).astype(BF16)
    sumg_o[0:1, :] += colsum(cot[...].astype(F32))
    sumh_o[0:1, :] += colsum(gh.astype(F32))


def mlp_both(layer, x, own, oth, cot, outb, gain, shift, fcb, flag, weights):
    d = x.shape[1]
    f = fcb.shape[1]
    plans, arrays = mlp_weights(weights)
    ins = [x, own, oth, *cot, outb, gain, shift, fcb, flag, *arrays]
    specs = [rows_spec(d)] * 3 + [rows_spec(d // 4)] * 4 + [SMEM]
    specs += [full_spec(a.shape) for a in ins[8:12]] + [SMEM] + [ANY] * len(arrays)
    widths = [d, d, f, f, d, d, d]
    kinds = [F32, BF16, BF16, BF16, BF16, BF16, BF16]
    return pl.pallas_call(
        functools.partial(mlp_both_kernel, layer, plans),
        grid=(LEN // BT,),
        in_specs=specs,
        out_specs=[rows_spec(w) for w in widths] + [full_spec((8, d)), full_spec((8, f))],
        out_shape=[jax.ShapeDtypeStruct((LEN, w), k) for w, k in zip(widths, kinds)]
        + [jax.ShapeDtypeStruct((8, d), F32), jax.ShapeDtypeStruct((8, f), F32)],
        scratch_shapes=mlp_scratch(d, f, plans),
        name=f"mlp_both_{layer}",
        cost_estimate=cost(18),
    )(*ins)


def mlp_bwd_kernel(layer, plans, gm, own, oth, x, h, gain, flag, *refs):
    nw = 2 + len(plans[0]) + len(plans[1])
    weights = refs[:nw]
    g_o, low_o, act_o, gh_o, part_o, sums_o, sumh_o, wfc, wproj, sems = refs[nw:]

    @pl.when(pl.program_id(0) == 0)
    def _():
        moves = load_mlp(layer, flag, plans, weights, wfc, wproj, sems)
        sums_o[...] = jnp.zeros_like(sums_o)
        sumh_o[...] = jnp.zeros_like(sumh_o)
        for m in moves:
            m.wait()

    grad, g_gain, g_shift = norm_back(
        gm[...], own[...], oth[...], x[...], gain[layer + 1, 0:1, :].astype(F32)
    )
    sums_o[0:1, :] += colsum(g_gain)
    sums_o[1:2, :] += colsum(g_shift)
    sums_o[2:3, :] += colsum(grad)
    g_o[...] = grad
    low = grad.astype(BF16)
    low_o[...] = low
    grad_act = dot(low, wproj[...], 1, 1)
    value, slope = gelu_parts(h[...].astype(F32))
    act_o[...] = value.astype(BF16)
    gh = (grad_act * slope).astype(BF16)
    gh_o[...] = gh
    part_o[...] = dot(gh, wfc[...], 1, 1).astype(BF16)
    sumh_o[0:1, :] += colsum(gh.astype(F32))


def mlp_bwd(layer, gm, own, oth, x, h, gain, flag, weights):
    d = x.shape[1]
    f = h.shape[1]
    plans, arrays = mlp_weights(weights)
    ins = [gm, own, oth, x, h, gain, flag, *arrays]
    specs = [rows_spec(d)] * 4 + [rows_spec(f), full_spec(gain.shape), SMEM] + [ANY] * len(arrays)
    widths = [d, d, f, f, d]
    kinds = [F32, BF16, BF16, BF16, BF16]
    return pl.pallas_call(
        functools.partial(mlp_bwd_kernel, layer, plans),
        grid=(LEN // BT,),
        in_specs=specs,
        out_specs=[rows_spec(w) for w in widths] + [full_spec((8, d)), full_spec((8, f))],
        out_shape=[jax.ShapeDtypeStruct((LEN, w), k) for w, k in zip(widths, kinds)]
        + [jax.ShapeDtypeStruct((8, d), F32), jax.ShapeDtypeStruct((8, f), F32)],
        scratch_shapes=mlp_scratch(d, f, plans),
        name=f"mlp_bwd_{layer}",
        cost_estimate=cost(16),
    )(*ins)


def stage(buf, value, order):
    dims = [o for o in order if o != "y"]
    n = len(dims)
    r = value.shape[0] >> n
    for c in range(1 << n):
        pos = sum(((c >> b) & 1) << (n - 1 - j) for j, b in enumerate(dims))
        buf[r * pos : r * (pos + 1), :] = value[r * c : r * (c + 1)].astype(BF16)


def ship(buf, keep, send, slot, order, flags, sems):
    if order[0] == "y":
        pairs = [(buf, send if slot else keep)]
    else:
        half = buf.shape[0] // 2
        f = flags[order[0]]
        lo = [pl.multiple_of(h * half, 16) for h in (f, 1 - f)]
        pairs = [
            (buf.at[pl.ds(lo[0], half)], keep.at[slot]),
            (buf.at[pl.ds(lo[1], half)], send.at[slot]),
        ]
    return [pltpu.make_async_copy(a, b, sems.at[j]) for j, (a, b) in enumerate(pairs)]


def first_shape(order, d, w):
    return (d, w) if order[0] == "y" else (2, d // 2, w)


def dw_mlp_kernel(orders, flags, n, low, gh, act, *refs):
    outs, (bufs, sems) = refs[:4], refs[4:]
    j = pl.program_id(0)

    def moves(t, slot):
        keep, send = outs[2 * t : 2 * t + 2]
        return ship(bufs.at[t, slot], keep, send, slot, orders[t], flags, sems.at[t, slot])

    for t, (a, b) in enumerate(((n, gh), (low, act))):
        stage(bufs.at[t, j], dot(a[...], b[...], 0, 0), orders[t])
        for slot in range(2):

            @pl.when(j == slot)
            def _():
                for m in moves(t, slot):
                    m.start()

    @pl.when(j == 1)
    def _():
        for t in range(2):
            for slot in range(2):
                for m in moves(t, slot):
                    m.wait()


def dw_mlp(layer, n, low, gh, act, orders, flags):
    t, d = n.shape
    f = gh.shape[1] // 2
    col = pl.BlockSpec((t, f), lambda j: (0, j))
    shapes = [first_shape(o, d, f) for o in orders for _ in range(2)]
    k0, s0, k1, s1 = pl.pallas_call(
        functools.partial(dw_mlp_kernel, orders),
        grid=(2,),
        in_specs=[SMEM, full_spec(n.shape), full_spec(low.shape), col, col],
        out_specs=[ANY] * 4,
        out_shape=[jax.ShapeDtypeStruct(s, BF16) for s in shapes],
        scratch_shapes=[pltpu.VMEM((2, 2, d, f), BF16), pltpu.SemaphoreType.DMA((2, 2, 2))],
        name=f"dw_mlp_{layer}",
        cost_estimate=cost(9),
    )(flags, n, low, gh, act)
    return Part(k0, s0, orders[0]), Part(k1, s1, orders[1])


def dw_attn_kernel(orders, flags, n, low, dqkv, att, *refs):
    outs, (bufs, sems) = refs[:4], refs[4:]
    sh = att.shape[1] // 2
    moves = []

    def send_off(t, values):
        for slot in range(2):
            both = jnp.concatenate(
                [v[:, (2 * j + slot) * sh : (2 * j + slot + 1) * sh] for v, j in values], axis=1
            )
            stage(bufs.at[t, slot], both, orders[t])
            keep, send = outs[2 * t : 2 * t + 2]
            for m in ship(
                bufs.at[t, slot], keep, send, slot, orders[t], flags, sems.at[t, slot]
            ):
                m.start()
                moves.append(m)

    half = 2 * sh
    qk = dot(n[...], dqkv[:, : 2 * half], 0, 0)
    send_off(0, [(qk, 0), (qk, 1)])
    v = dot(n[...], dqkv[:, 2 * half :], 0, 0)
    wo = dot(low[...], att[...], 0, 0)
    send_off(1, [(v, 0), (wo, 0)])
    for m in moves:
        m.wait()


def dw_attn(layer, n, low, dqkv, att, orders, flags):
    d = n.shape[1]
    w = att.shape[1]
    ins = (n, low, dqkv, att)
    shapes = [first_shape(o, d, w) for o in orders for _ in range(2)]
    k0, s0, k1, s1 = pl.pallas_call(
        functools.partial(dw_attn_kernel, orders),
        grid=(1,),
        in_specs=[SMEM] + [full_spec(a.shape) for a in ins],
        out_specs=[ANY] * 4,
        out_shape=[jax.ShapeDtypeStruct(s, BF16) for s in shapes],
        scratch_shapes=[pltpu.VMEM((2, 2, d, w), BF16), pltpu.SemaphoreType.DMA((2, 2, 2))],
        name=f"dw_attn_{layer}",
        cost_estimate=cost(7),
    )(flags, *ins)
    return Part(k0, s0, orders[0]), Part(k1, s1, orders[1])


def combine_kernel(steps, merged, flags, *refs):
    ins, outs = refs[: 2 * len(steps)], refs[2 * len(steps) :]
    lo = 0
    for k, o in enumerate(steps):
        keep, got = ins[2 * k : 2 * k + 2]

        def total(at):
            return keep[at].astype(F32) + got[at].astype(F32)

        if o is None:
            outs[k][...] = total(...)
            continue
        dst = outs if merged else outs[2 * k : 2 * k + 2]
        cols = slice(lo, lo + keep.shape[-1]) if merged else slice(None)
        if o == "y":
            halves = [total(0), total(1)]
        else:
            r = keep.shape[-2] // 2
            lead = (slice(None),) * (len(keep.shape) - 2)
            rows = [pl.ds(pl.multiple_of(h * r, 8), r) for h in (flags[o], 1 - flags[o])]
            halves = [total(lead + (row, slice(None))) for row in rows]
        for out, v in zip(dst, halves):
            out[..., cols] = v.astype(BF16)
        if merged:
            lo += keep.shape[-1]


def combine(parts, flags, merged=False):
    steps = [p.order[1] if len(p.order) > 1 else None for p in parts]
    wide = all(p.keep.shape[-1] % 384 == 0 for p in parts)
    ncol = 3 if wide and not merged and parts[0].keep.size >= 2**18 else 1

    def spec(shape):
        block = shape[:-1] + (shape[-1] // ncol,)
        return pl.BlockSpec(block, lambda g: (0,) * (len(shape) - 1) + (g,))

    ins, shapes = [], []
    for p, o in zip(parts, steps):
        ins += [p.keep, p.got]
        s = p.keep.shape
        if o is None:
            shapes.append(jax.ShapeDtypeStruct(s, F32))
        else:
            s = s[1:] if o == "y" else s[:-2] + (s[-2] // 2, s[-1])
            shapes += [jax.ShapeDtypeStruct(s, BF16)] * 2
    if merged:
        s = (shapes[0].shape[0], sum(p.keep.shape[-1] for p in parts))
        shapes = [jax.ShapeDtypeStruct(s, BF16)] * 2
    outs = pl.pallas_call(
        functools.partial(combine_kernel, steps, merged),
        grid=(ncol,),
        in_specs=[SMEM] + [spec(a.shape) for a in ins],
        out_specs=[spec(a.shape) for a in shapes],
        out_shape=shapes,
        name="combine",
        cost_estimate=cost(0.3),
    )(flags, *ins)
    if merged:
        return Part(outs[0], outs[1], parts[0].order[1:])
    if steps[0] is None:
        return list(outs)
    return [
        Part(outs[2 * k], outs[2 * k + 1], p.order[1:]) for k, p in enumerate(parts)
    ]


def final_kernel(f, share, *refs):
    (m1, m0, a1, a0, pk), outs = [refs[2 * k : 2 * k + 2] for k in range(5)], refs[10:]
    fc_o, pj_o, qkv_o, wo_o, pos_o, gain_o, shift_o, bias_o, fcb_o, qvb_o = outs

    def total(pair, lo, n):
        return pair[0][:, lo : lo + n].astype(F32) + pair[1][:, lo : lo + n].astype(F32)

    for l, (m, a) in enumerate(((m0, a0), (m1, a1))):
        fc_o[l] = total(m, 0, f)
        pj_o[l] = total(m, f, f)
        v = total(a, 0, 4 * share)
        for j in range(3):
            qkv_o[l, j] = v[:, share * j : share * (j + 1)]
        wo_o[l] = jnp.transpose(v[:, 3 * share :])
    v = total(pk, 0, share)
    rows = pos_o.shape[1]
    pos_o[...] = jnp.transpose(v[:rows])
    v = v[rows:]
    w = gain_o.shape[2]
    for l in range(2):
        for k, ref in enumerate((gain_o, shift_o, bias_o)):
            ref[l] = v[4 * k + 2 * l : 4 * k + 2 * l + 2, :w]
        qvb_o[l] = v[2 * l : 2 * l + 2, w : w + qvb_o.shape[2]]
    fcb_o[...] = v[12:14, :w]


def final(parts, f, share, rows, n_dp):
    r = parts[0].keep.shape[0]
    ins = [v for p in parts for v in (p.keep, p.got)]
    shapes = [(2, r, f), (2, r, f), (2, 3, r, share), (2, share, r), (share, rows)]
    shapes += [(2, 2, r)] * 3 + [(2, r), (2, 2, share // n_dp)]
    return pl.pallas_call(
        functools.partial(final_kernel, f, share),
        grid=(1,),
        in_specs=[full_spec(v.shape) for v in ins],
        out_specs=[full_spec(v) for v in shapes],
        out_shape=[jax.ShapeDtypeStruct(v, F32) for v in shapes],
        name="final",
        cost_estimate=cost(3),
    )(*ins)


class Part:
    def __init__(self, keep, send, order):
        self.keep, self.send, self.order = keep, send, list(order)

    def go(self, n_dp):
        o = self.order[0]
        self.got = y_swap(self.send) if o == "y" else dp_swap(self.send, o, n_dp)


def attn_bwd_kernel(layer, half, *refs):
    (g_i, own, oth, mid, qkv, att, lse, start, gain, w) = refs[:10]
    (gm_o, low_o, dqkv_o, part_o, sums_o, qvs_o, k_t, dk, dv, dq_t) = refs[10:]
    g = pl.program_id(0)

    @pl.when(g == 0)
    def _():
        sums_o[...] = jnp.zeros_like(sums_o)
        qvs_o[...] = jnp.zeros_like(qvs_o)
        dk[...] = jnp.zeros_like(dk)
        dv[...] = jnp.zeros_like(dv)
        for b in range(LEN // BT):
            block = qkv[BT * b : BT * (b + 1), half : 2 * half].astype(F32)
            k_t[:, BT * b : BT * (b + 1)] = jnp.transpose(block).astype(BF16)

    gm, g_gain, g_shift = norm_back(
        g_i[...].astype(F32), own[...], oth[...], mid[...], gain[layer, 1:2, :].astype(F32)
    )
    gm_o[...] = gm
    sums_o[0:1, :] += colsum(g_gain)
    sums_o[1:2, :] += colsum(g_shift)
    sums_o[2:3, :] += colsum(gm)
    low = gm.astype(BF16)
    low_o[...] = low
    d_att = dot(low, w[:, 3 * half :]).astype(BF16)
    prod = d_att.astype(F32) * att[...].astype(F32)
    head = lax.broadcasted_iota(jnp.int32, (8, half), 1) // HD
    pick = (head == lax.broadcasted_iota(jnp.int32, (8, half), 0)).astype(F32)
    inner = lax.dot_general(
        pick,
        prod,
        (((1,), (1,)), ((), ())),
        preferred_element_type=F32,
        precision=lax.Precision.HIGHEST,
    )
    rows = pl.ds(pl.multiple_of(g * BT, BT), BT)
    q = qkv[rows, :half] * jnp.asarray(1.0 / math.sqrt(HD), BF16)
    for s in range(BT // QB):
        i = g * (BT // QB) + s
        ks = pl.multiple_of(jnp.maximum(i - DOC_MOST // QB, 0) * QB, QB)
        bias = window_bias(start, i, ks)
        cols = pl.ds(pl.multiple_of(i * QB, QB), QB)
        win = pl.ds(ks, KW)
        for p in range(half // 128):
            lo = 128 * p
            qq = head_pair(q[QB * s : QB * (s + 1), lo : lo + 128])
            oo = head_pair(d_att[QB * s : QB * (s + 1), lo : lo + 128])
            kp = qkv[win, half + lo : half + lo + 128]
            vp = qkv[win, 2 * half + lo : 2 * half + lo + 128]
            total = jnp.concatenate(
                [lse[2 * p : 2 * p + 1, cols], lse[2 * p + 1 : 2 * p + 2, cols]], axis=1
            )
            inn = jnp.concatenate(
                [
                    inner[2 * p : 2 * p + 1, QB * s : QB * (s + 1)],
                    inner[2 * p + 1 : 2 * p + 2, QB * s : QB * (s + 1)],
                ],
                axis=1,
            )
            probs = jnp.exp(dot(kp, qq, 1, 1) + bias - total)
            d_probs = dot(vp, oo, 1, 1)
            ds = (probs * (d_probs - inn)).astype(BF16)
            dv[win, lo : lo + 128] += dot(probs.astype(BF16), oo)
            dk[win, lo : lo + 128] += dot(ds, qq)
            dqt = dot(k_t[lo : lo + 128, win], ds)
            dq_t[lo : lo + HD, :] = dqt[:HD, :QB]
            dq_t[lo + HD : lo + 128, :] = dqt[HD:, QB:]
        dq = (jnp.transpose(dq_t[...]) * (1.0 / math.sqrt(HD))).astype(BF16)
        dqkv_o[cols, :half] = dq
        qvs_o[0:1, :] += colsum(dq.astype(F32))

    @pl.when(g == pl.num_programs(0) - 1)
    def _():
        dqkv_o[:, half : 2 * half] = dk[...].astype(BF16)
        dvb = dv[...].astype(BF16)
        dqkv_o[:, 2 * half :] = dvb
        qvs_o[1:2, :] = colsum(dvb.astype(F32))
        for b in range(LEN // BT):
            part = dot(dqkv_o[BT * b : BT * (b + 1), :], w[:, : 3 * half], 1, 1)
            part_o[BT * b : BT * (b + 1), :] = part.astype(BF16)


def attn_bwd(layer, g, own, oth, mid, qkv, att, lse, start, gain, w):
    d = mid.shape[1]
    half = att.shape[1]
    ins = [g, own, oth, mid, qkv, att, lse, start, gain, w]
    specs = [rows_spec(d)] * 4 + [full_spec(qkv.shape), rows_spec(half)]
    specs += [full_spec(a.shape) for a in ins[6:]]
    return pl.pallas_call(
        functools.partial(attn_bwd_kernel, layer, half),
        grid=(LEN // BT,),
        in_specs=specs,
        out_specs=[
            rows_spec(d),
            rows_spec(d),
            full_spec((LEN, 3 * half)),
            full_spec((LEN, d)),
            full_spec((8, d)),
            full_spec((8, half)),
        ],
        out_shape=[
            jax.ShapeDtypeStruct((LEN, d), F32),
            jax.ShapeDtypeStruct((LEN, d), BF16),
            jax.ShapeDtypeStruct((LEN, 3 * half), BF16),
            jax.ShapeDtypeStruct((LEN, d), BF16),
            jax.ShapeDtypeStruct((8, d), F32),
            jax.ShapeDtypeStruct((8, half), F32),
        ],
        scratch_shapes=[
            pltpu.VMEM((half, LEN), BF16),
            pltpu.VMEM((LEN, half), F32),
            pltpu.VMEM((LEN, half), F32),
            pltpu.VMEM((half, QB), F32),
        ],
        name=f"attn_bwd_{layer}",
        cost_estimate=cost(24),
    )(*ins)


def norm_bwd_kernel(layer, n_dp, place, g, own, oth, x, gain, hot, *refs):
    sums, (near_o, far_o, own_o, oth_o, acc, table, small) = refs[:8], refs[8:]
    sums0, sums0b, sums1, sumg1, sumh0, sumh1, qvs0, qvs1 = sums
    w = near_o.shape[1]
    step = pl.program_id(0)

    @pl.when(step == 0)
    def _():
        acc[...] = jnp.zeros_like(acc)
        table[...] = jnp.zeros_like(table)
        small[...] = jnp.zeros_like(small)

    out, g_gain, g_shift = norm_back(
        g[...], own[...], oth[...], x[...], gain[layer, 0:1, :].astype(F32)
    )
    acc[0:1, :] += colsum(g_gain)
    acc[1:2, :] += colsum(g_shift)

    def select(q):
        far = q ^ 2
        near_o[...] = out[:, w * q : w * (q + 1)]
        far_o[...] = out[:, w * far : w * (far + 1)].astype(BF16)

    for q in range(4):
        pl.when(place[0] == q)(functools.partial(select, q))
    table[0] += dot(hot[...], near_o[...].astype(BF16), 0, 0)
    table[1] += dot(hot[...], far_o[...], 0, 0)

    @pl.when(step == pl.num_programs(0) - 1)
    def _():
        rows = [(acc, 0), (sums0, 0), (sums0b, 0), (sums1, 0)]
        rows += [(acc, 1), (sums0, 1), (sums0b, 1), (sums1, 1)]
        rows += [(sums0, 2), (sums0b, 2), (sums1, 2), (sumg1, 0)]
        cw, qw, f = acc.shape[1] // n_dp, w // n_dp, sumh0.shape[1] // 2
        for c in range(n_dp):
            for k, (ref, r) in enumerate(rows):
                v = ref[r : r + 1, cw * c : cw * (c + 1)]
                small[0, 16 * c + k : 16 * c + k + 1, 0:cw] = v
                small[1, 16 * c + k : 16 * c + k + 1, 0:cw] = v
            for slot in range(2):
                for k, ref in enumerate((sumh0, sumh1)):
                    lo = f * slot + cw * c
                    row = 16 * c + 12 + k
                    small[slot, row : row + 1, 0:cw] = ref[0:1, lo : lo + cw]
                for k, (ref, r) in enumerate(((qvs0, 0), (qvs0, 1), (qvs1, 0), (qvs1, 1))):
                    lo = w * slot + qw * c
                    row = 16 * c + k
                    small[slot, row : row + 1, cw : cw + qw] = ref[r : r + 1, lo : lo + qw]
        for slot, ref in enumerate((own_o, oth_o)):
            ref[:DOC_MOST, :] = table[slot].astype(BF16)
            ref[DOC_MOST:, :] = small[slot].astype(BF16)


def norm_bwd(layer, n_dp, place, g, own, oth, x, gain, hot, sums):
    d = x.shape[1]
    w = d // 4
    r = DOC_MOST + 16 * n_dp
    return pl.pallas_call(
        functools.partial(norm_bwd_kernel, layer, n_dp),
        grid=(LEN // BT,),
        in_specs=[SMEM]
        + [rows_spec(d)] * 4
        + [full_spec(gain.shape), rows_spec(DOC_MOST)]
        + [full_spec(v.shape) for v in sums],
        out_specs=[rows_spec(w), rows_spec(w), full_spec((r, w)), full_spec((r, w))],
        out_shape=[
            jax.ShapeDtypeStruct((LEN, w), F32),
            jax.ShapeDtypeStruct((LEN, w), BF16),
            jax.ShapeDtypeStruct((r, w), BF16),
            jax.ShapeDtypeStruct((r, w), BF16),
        ],
        scratch_shapes=[
            pltpu.VMEM((8, d), F32),
            pltpu.VMEM((2, DOC_MOST, w), F32),
            pltpu.VMEM((2, 16 * n_dp, w), F32),
        ],
        name=f"norm_bwd_{layer}",
        cost_estimate=cost(1),
    )(place, g, own, oth, x, gain, hot, *sums)


def expand_kernel(order, n_dp, rows, flags, own, got, keep, send):
    total = (own[...].astype(F32) + got[...].astype(F32)).astype(BF16)
    n = len(order)
    half = 1 << (n - 1)
    r = rows + 16

    def split(bit):
        for c in range(n_dp):
            pos = sum(((c >> b) & 1) << (n - 1 - j) for j, b in enumerate(order))
            out = keep if pos // half == bit else send
            row = r * (pos % half)
            if rows * c < DOC_MOST:
                out[row : row + rows, :] = total[rows * c : rows * (c + 1)]
            else:
                out[row : row + rows, :] = jnp.zeros((rows, total.shape[1]), BF16)
            lo = DOC_MOST + 16 * c
            out[row + rows : row + r, :] = total[lo : lo + 16]

    pl.when(flags[order[0]] == 0)(lambda: split(0))
    pl.when(flags[order[0]] == 1)(lambda: split(1))


def expand(own, got, order, n_dp, rows, flags):
    w = own.shape[1]
    shape = (n_dp * (rows + 16) // 2, w)
    keep, send = pl.pallas_call(
        functools.partial(expand_kernel, order, n_dp, rows),
        grid=(1,),
        in_specs=[SMEM, full_spec(own.shape), full_spec(own.shape)],
        out_specs=[full_spec(shape)] * 2,
        out_shape=[jax.ShapeDtypeStruct(shape, BF16)] * 2,
        name="expand",
        cost_estimate=cost(0.3),
    )(flags, own, got)
    return Part(keep, send, order)


def core_swap(a):
    return lax.ppermute(a, "mp", [(i, i ^ 1) for i in range(4)])


def y_swap(a):
    return lax.ppermute(a, "mp", [(i, i ^ 2) for i in range(4)])


def dp_swap(a, bit, n_dp):
    return lax.ppermute(a, "dp", [(i, i ^ (1 << bit)) for i in range(n_dp)])


def pick(flag, zero, one):
    return jnp.where(flag == 0, zero, one)


class Place:
    def __init__(self, n_dp):
        mp = lax.axis_index("mp")
        self.n_dp = n_dp
        self.bits = n_dp.bit_length() - 1
        self.y = mp // 2
        self.c = mp % 2
        self.dp = lax.axis_index("dp")

    def dp_bit(self, b):
        return (self.dp >> b) & 1


def row_pieces(a, at):
    rows = a.reshape(2, LEN, a.shape[1])
    return pick(at.y, rows[0], rows[1]), pick(at.y, rows[1], rows[0])


def own_cols(a, at, other):
    w = a.shape[1] // 4
    halves = (a[:, : 2 * w], a[:, 2 * w :])
    h = pick(at.y, halves[1], halves[0]) if other else pick(at.y, halves[0], halves[1])
    return pick(at.c, h[:, :w], h[:, w:])


def bar(*vals):
    return lax.optimization_barrier(vals)


def doc_starts(doc_ids):
    row_index = jnp.broadcast_to(jnp.arange(doc_ids.shape[1], dtype=jnp.int32), doc_ids.shape)
    previous = jnp.concatenate([doc_ids[:, :1] - 1, doc_ids[:, :-1]], axis=1)
    starts = jnp.where(doc_ids != previous, row_index, 0)
    return lax.cummax(starts, axis=1)


def on_device(
    n_dp,
    tokens,
    doc_ids,
    positions_table,
    norm_gain,
    norm_shift,
    joined_projection_weight,
    qv_bias,
    w_out,
    out_bias,
    w_fc,
    fc_bias,
    w_proj,
    cotangent,
):
    at = Place(n_dp)
    d = positions_table.shape[1]
    share = joined_projection_weight.shape[-1]
    f = w_fc.shape[-1]
    bits = list(range(2, at.bits))
    flags = jnp.stack([at.dp_bit(b) for b in range(at.bits)]).astype(jnp.int32)

    b = at.dp_bit(0) ^ at.dp_bit(1)
    flag = b.reshape(1)
    quarter = (2 * at.y + at.c).astype(jnp.int32).reshape(1)
    gain, shift = norm_gain, norm_shift

    a_own = [
        jnp.concatenate([joined_projection_weight[l].reshape(d, 3 * share), w_out[l].T], axis=1)
        for l in range(2)
    ]
    biases = jnp.concatenate([qv_bias.reshape(-1), fc_bias.reshape(-1)]).reshape(-1, d)
    biases = jnp.pad(biases, ((0, -biases.shape[0] % 8), (0, 0)))
    r = d // 2

    def half_rows(w):
        return lax.dynamic_slice_in_dim(w, b * r, r, 0)

    def x_swap(w):
        return dp_swap(w, 0, n_dp)

    def z_swap(w):
        return dp_swap(w, 1, n_dp)

    def by_two(one, lo=0):
        return x_swap(one[lo : lo + r // 2]), z_swap(one[lo + r // 2 : lo + r])

    def plan_one(lo=0):
        return ((lo, r, 0, 0), (0, r, 1, 0))

    def plan_two(lo=0):
        return ((lo, r, 0, 0), (0, r // 2, 1, 0), (0, r // 2, 1, r // 2))

    tok_mine, tok_theirs = row_pieces(tokens, at)
    tok_far = y_swap(tok_theirs)
    a_one0 = y_swap(jnp.concatenate([half_rows(a_own[0]), biases], axis=0))

    starts = doc_starts(doc_ids)
    start = pick(at.y, starts[0:1], starts[1:2])
    place = jnp.arange(LEN, dtype=jnp.int32) - start[0]
    hot = (place[:, None] == jnp.arange(DOC_MOST, dtype=jnp.int32)[None, :]).astype(BF16)
    fc_half, a_own[1] = bar(half_rows(w_fc[0]), a_own[1])
    fc_one0 = y_swap(fc_half)
    tok_far, a_one0, hot, a_own[1] = bar(tok_far, a_one0, hot, a_own[1])
    embedded = dot(hot, positions_table[:DOC_MOST]).astype(BF16)

    a_x, a_z = by_two(a_one0)
    tok = [tok_mine, core_swap(tok_mine), tok_far, core_swap(tok_far)]
    small = a_one0[r:].reshape(-1)
    nq = qv_bias.size
    qvb = jnp.concatenate([qv_bias, small[:nq].reshape(qv_bias.shape)], axis=-1)
    fcb = jnp.concatenate(
        [fc_bias, small[nq : nq + fc_bias.size].reshape(fc_bias.shape)], axis=-1
    )
    send_y = jnp.concatenate([half_rows(w_proj[0]), half_rows(a_own[1])], axis=0)
    a_x, a_z, fc_one0, send_y, embedded, *tok = bar(a_x, a_z, fc_one0, send_y, embedded, *tok)

    fc_two0 = x_swap(fc_one0)
    pj_a1 = y_swap(send_y)
    x0, n0, qkv0, att0, lse0, part, wa0 = attn_fwd(
        0,
        (*tok, embedded, quarter),
        out_bias,
        flag,
        start,
        gain,
        shift,
        qvb,
        a_own[0],
        (plan_two(), (a_one0, a_x, a_z)),
    )
    part, x0, fc_two0, pj_a1 = bar(part, x0, fc_two0, pj_a1)
    far = core_swap(part)
    pj_x, pj_z = by_two(pj_a1)
    far, pj_x, pj_z = bar(far, pj_x, pj_z)
    mlp0 = (
        w_fc,
        (plan_one(), (fc_one0, fc_two0)),
        w_proj,
        (plan_two(), (pj_a1, pj_x, pj_z)),
    )
    a_two1 = x_swap(pj_a1[r:])
    fc_one1 = y_swap(half_rows(w_fc[1]))
    mid0, nn0, hid0, part2 = mlp_fwd(
        0, x0, part, far, out_bias, gain, shift, fcb, flag, mlp0
    )
    part2, mid0, a_two1, fc_one1 = bar(part2, mid0, a_two1, fc_one1)
    far = core_swap(part2)
    (far,) = bar(far)
    fc_two1 = x_swap(fc_one1)
    pj_one1 = y_swap(half_rows(w_proj[1]))
    cot_mine, cot_theirs = row_pieces(cotangent, at)
    cot_far = y_swap(cot_theirs)
    x1, n1, qkv1, att1, lse1, part, wa1 = attn_fwd(
        1,
        (mid0, part2, far),
        out_bias,
        flag,
        start,
        gain,
        shift,
        qvb,
        a_own[1],
        (plan_one(r), (pj_a1, a_two1)),
    )
    part, x1, fc_two1, cot_far, pj_one1 = bar(part, x1, fc_two1, cot_far, pj_one1)
    far = core_swap(part)
    pj_x, pj_z = by_two(pj_one1)
    cot = [cot_mine, core_swap(cot_mine), cot_far, core_swap(cot_far)]
    far, pj_x, pj_z, *cot = bar(far, pj_x, pj_z, *cot)
    mlp1 = (
        w_fc,
        (plan_one(), (fc_one1, fc_two1)),
        w_proj,
        (plan_two(), (pj_one1, pj_x, pj_z)),
    )
    mid1, nn1, act, gh, part_out, part, cot, sumg1, sumh1 = mlp_both(
        1, x1, part, far, (*cot, quarter), out_bias, gain, shift, fcb, flag, mlp1
    )

    def go(*parts):
        for p in parts:
            p.go(n_dp)

    def bar_parts(parts, sent, *vals):
        name = "send" if sent else "got"
        out = bar(*[getattr(p, name) for p in parts], *vals)
        for p, v in zip(parts, out):
            setattr(p, name, v)
        return out[len(parts) :]

    part, part_out, mid1, gh, act = bar(part, part_out, mid1, gh, act)
    far = core_swap(part)
    far_out = core_swap(part_out)
    o_fc, o_pj = ["y", 1, 0] + bits, [0, "y", 1] + bits
    o_a, o_b = [0, 1, "y"] + bits, [1, "y", 0] + bits
    fc1, pj1 = dw_mlp(1, nn1, cot, gh, act, (o_fc, o_pj), flags)
    far, far_out, mid1, part_out = bar_parts([fc1, pj1], True, far, far_out, mid1, part_out)
    go(fc1, pj1)
    gm1, m_low, dqkv, part, sums1, qvs1 = attn_bwd(
        1, cot, part, far, mid1, qkv1, att1, lse1, start, gain, wa1
    )
    part, gm1, m_low, dqkv, far_out, part_out = bar_parts(
        [fc1, pj1], False, part, gm1, m_low, dqkv, far_out, part_out
    )
    far = core_swap(part)
    fc1, pj1 = combine([fc1, pj1], flags)
    result = (
        mid1 + (part_out.astype(F32) + far_out.astype(F32)) + out_bias[1, 1].astype(F32)
    ).astype(BF16)
    out_near, out_send = own_cols(result, at, False), own_cols(result, at, True)
    out_near, out_send, far, m_low = bar_parts([fc1, pj1], True, out_near, out_send, far, m_low)
    aa1, ab1 = dw_attn(1, n1, m_low, dqkv, att1, (o_a, ["y", 1, 0] + bits), flags)
    far, gm1 = bar_parts([aa1, ab1], True, far, gm1)
    go(fc1, pj1, aa1)
    g0, g_low, act, gh, part, sums0b, sumh0 = mlp_bwd(
        0, gm1, part, far, x1, hid0, gain, flag, mlp0
    )
    part, g0, g_low, act, gh = bar_parts([fc1, pj1, aa1], False, part, g0, g_low, act, gh)
    far = core_swap(part)
    fc1, pj1, aa1 = combine([fc1, pj1, aa1], flags)
    far, g_low, act, gh = bar_parts([fc1, pj1, aa1, ab1], True, far, g_low, act, gh)
    go(ab1, fc1, pj1, aa1)
    fc0, pj0 = dw_mlp(0, nn0, g_low, gh, act, (o_fc, o_pj), flags)
    far, fc0.send, pj0.send, g0 = bar_parts(
        [ab1, fc1, pj1, aa1], False, far, fc0.send, pj0.send, g0
    )
    last1 = combine([fc1, pj1], flags, merged=True)
    aa1, ab1 = combine([aa1, ab1], flags)
    far, g0, part = bar_parts([last1, aa1, ab1, fc0, pj0], True, far, g0, part)
    go(fc0, pj0, aa1, ab1, last1)
    gm0, m_low, dqkv, part, sums0, qvs0 = attn_bwd(
        0, g0, part, far, mid0, qkv0, att0, lse0, start, gain, wa0
    )
    part, gm0, m_low, dqkv = bar_parts(
        [fc0, pj0, aa1, ab1, last1], False, part, gm0, m_low, dqkv
    )
    far = core_swap(part)
    fc0, pj0 = combine([fc0, pj0], flags)
    (ab1,) = combine([ab1], flags)
    far, m_low, dqkv = bar_parts([fc0, pj0, ab1], True, far, m_low, dqkv)
    go(fc0, pj0, ab1)
    aa0, ab0 = dw_attn(0, n0, m_low, dqkv, att0, (o_a, o_b), flags)
    aa0.send, ab0.send, far, gm0, part = bar_parts([ab1], False, aa0.send, ab0.send, far, gm0, part)
    last3 = combine([aa1, ab1], flags, merged=True)
    far, gm0, part = bar_parts([aa0, ab0, last3], True, far, gm0, part)
    go(aa0, ab0, last3)
    sums = (sums0, sums0b, sums1, sumg1, sumh0, sumh1, qvs0, qvs1)
    near, far_send, pk, pk_send = norm_bwd(0, n_dp, quarter, gm0, part, far, x0, gain, hot, sums)
    near, far_send, pk, pk_send = bar_parts([fc0, pj0], False, near, far_send, pk, pk_send)
    pk_got = y_swap(pk_send)
    fc0, pj0 = combine([fc0, pj0], flags)
    pk_got, pk, far_send = bar_parts([fc0, pj0], True, pk_got, pk, far_send)
    go(fc0, pj0)
    g_far = y_swap(far_send)
    rows = positions_table.shape[0] // n_dp
    pk = expand(pk, pk_got, [0, 1] + bits, n_dp, rows, flags)
    (pk.send,) = bar_parts([aa0, ab0], False, pk.send)
    aa0, ab0 = combine([aa0, ab0], flags)
    aa0.send, ab0.send, pk.send, out_send, out_near = bar_parts(
        [fc0, pj0, last3], False, aa0.send, ab0.send, pk.send, out_send, out_near
    )
    go(aa0, ab0, pk)
    last0 = combine([fc0, pj0], flags, merged=True)
    last0.send, g_far, near = bar_parts([aa0, ab0, pk], False, last0.send, g_far, near)
    go(last0)
    aa0, ab0, pk = combine([aa0, ab0, pk], flags)
    out_send, out_near = bar_parts([aa0, ab0, pk], True, out_send, out_near)
    go(aa0, ab0, pk)
    g_far = g_far.astype(F32)
    grad_tokens = jnp.concatenate([pick(at.y, near, g_far), pick(at.y, g_far, near)], axis=0)
    out_send, out_near = bar_parts([aa0, ab0, pk], False, out_send, out_near)
    last2 = combine([aa0, ab0], flags, merged=True)
    (pk,) = combine([pk], flags)
    out_send, out_near, grad_tokens = bar_parts([last2, pk], True, out_send, out_near, grad_tokens)
    out_far = y_swap(out_send)
    go(last2, pk)
    out = jnp.concatenate([pick(at.y, out_near, out_far), pick(at.y, out_far, out_near)], axis=0)
    lasts = [last1, last0, last3, last2, pk]
    while len(lasts[0].order) > 1:
        lasts = combine(lasts, flags)
        go(*lasts)
    g_fc, g_pj, g_qkv, g_wo, g_pos, g_gain, g_shift, g_bias, g_fcb, g_qvb = final(
        lasts, f, share, rows, n_dp
    )
    return (
        out,
        grad_tokens,
        g_pos.T,
        g_gain,
        g_shift,
        g_qkv.transpose(0, 2, 1, 3),
        g_qvb,
        g_wo,
        g_bias,
        g_fc,
        g_fcb,
        g_pj.transpose(0, 2, 1),
    )


def solution(mesh):
    n_dp = mesh.shape["dp"]
    in_specs = (
        P("dp", "mp"),
        P("dp", None),
        P(),
        P(),
        P(),
        P(None, None, None, "mp"),
        P(None, None, "mp"),
        P(None, "mp", None),
        P(),
        P(None, None, "mp"),
        P(None, "mp"),
        P(None, "mp", None),
        P("dp", "mp"),
    )
    out_specs = (
        P("dp", "mp"),
        P("dp", "mp"),
        P("dp", "mp"),
        P(None, None, "dp"),
        P(None, None, "dp"),
        P(None, "dp", None, "mp"),
        P(None, None, ("mp", "dp")),
        P(None, "mp", "dp"),
        P(None, None, "dp"),
        P(None, "dp", "mp"),
        P(None, ("mp", "dp")),
        P(None, "mp", "dp"),
    )
    return jax.shard_map(
        functools.partial(on_device, n_dp),
        mesh=mesh,
        in_specs=in_specs,
        out_specs=out_specs,
        check_vma=False,
    )
```

```python
import functools
import math

import jax
import jax.numpy as jnp
from jax import lax
from jax.experimental import pallas as pl
from jax.experimental.pallas import tpu as pltpu
from jax.sharding import PartitionSpec as P

HD = 64
LEN = 1024
DOC_MOST = 384
EPS = 1e-05
BT = 256
QB = 128
KW = QB + DOC_MOST
F32 = jnp.float32
BF16 = jnp.bfloat16
GELU_C = math.sqrt(2.0 / math.pi)


ANY = pl.BlockSpec(memory_space=pl.ANY)
SMEM = pl.BlockSpec(memory_space=pltpu.SMEM)


def cost(us):
    return pl.CostEstimate(flops=int(us * 1.15e9), transcendentals=0, bytes_accessed=0)


def full_spec(shape):
    return pl.BlockSpec(shape, lambda g: (0,) * len(shape))


def rows_spec(width):
    return pl.BlockSpec((BT, width), lambda g: (g, 0))


def dot(a, b, ca=1, cb=0):
    return lax.dot_general(a, b, (((ca,), (cb,)), ((), ())), preferred_element_type=F32)


def normed_parts(v):
    centred = v - jnp.mean(v, axis=-1, keepdims=True)
    variance = jnp.mean(centred * centred, axis=-1, keepdims=True)
    rstd = lax.rsqrt(variance + EPS)
    return centred * rstd, rstd


def norm_back(g, own, oth, v, gain):
    grad = own.astype(F32) + oth.astype(F32)
    xhat, rstd = normed_parts(v)
    gn = grad * gain
    out = g + rstd * (
        gn
        - jnp.mean(gn, axis=-1, keepdims=True)
        - xhat * jnp.mean(gn * xhat, axis=-1, keepdims=True)
    )
    return out, grad * xhat, grad


def colsum(v):
    return jnp.sum(v, axis=0, keepdims=True)


def head_pair(block):
    lane = lax.broadcasted_iota(jnp.int32, block.shape, 1)
    zero = jnp.zeros_like(block)
    return jnp.concatenate(
        [jnp.where(lane < HD, block, zero), jnp.where(lane < HD, zero, block)], axis=0
    )


def window_bias(start_ref, i, ks):
    kidx = lax.broadcasted_iota(jnp.int32, (KW, QB), 0) + ks
    qidx = lax.broadcasted_iota(jnp.int32, (KW, QB), 1) + i * QB
    first = start_ref[0:1, pl.ds(pl.multiple_of(i * QB, QB), QB)]
    bias = jnp.where((kidx >= first) & (kidx <= qidx), 0.0, -1e30).astype(F32)
    return jnp.concatenate([bias, bias], axis=1)


def copies(pairs, sems):
    out = [pltpu.make_async_copy(a, b, sems.at[j]) for j, (a, b) in enumerate(pairs)]
    for c in out:
        c.start()
    return out


def join_pieces(flag, plan, refs, dst, cols=slice(None)):
    r = dst.shape[0] // 2
    out = []
    for (lo, n, other, off), ref in zip(plan, refs):
        row = (1 - flag if other else flag) * r + off
        out.append((ref.at[pl.ds(lo, n)], dst.at[pl.ds(pl.multiple_of(row, 8), n), cols]))
    return out


def join_quarters(place, pieces, dst):
    w = pieces[0].shape[1]

    def put(q):
        for k, piece in enumerate(pieces):
            lo = w * (q ^ k)
            dst[:, lo : lo + w] = piece[...]

    for q in range(4):
        pl.when(place[0] == q)(functools.partial(put, q))


def gelu_parts(v):
    v2 = v * v
    t = jnp.tanh(GELU_C * v * (1.0 + 0.044715 * v2))
    cdf = 0.5 * (1.0 + t)
    slope = cdf + (0.5 * GELU_C) * v * (1.0 - t * t) * (1.0 + (3 * 0.044715) * v2)
    return v * cdf, slope


def gained(xhat, gain, shift, layer, which):
    row = slice(which, which + 1)
    return (xhat * gain[layer, row, :].astype(F32) + shift[layer, row, :].astype(F32)).astype(BF16)


def attn_fwd_kernel(layer, first, half, plan, *refs):
    if first:
        pieces, (emb, place, flag, start, gain, shift, qvb, a_own) = refs[:4], refs[4:12]
        rest, tok = refs[12:-1], refs[-1]
        join_quarters(place, pieces, tok)
        x = tok[...].astype(F32) + emb[...].astype(F32)
    else:
        (mid, own, oth, outb, flag, start, gain, shift, qvb, a_own) = refs[:10]
        rest = refs[10:]
        x = (
            mid[...]
            + (own[...].astype(F32) + oth[...].astype(F32))
            + outb[layer - 1, 1:2, :].astype(F32)
        )
    a_refs, rest = rest[: len(plan)], rest[len(plan) :]
    x_o, n_o, qkv_h, att_o, lse_o, part_o, w_h, v_t, o_t, a_buf, sems = rest[:11]
    qkv_o, w_o, osems = rest[11:]
    nb = LEN // BT

    def out_rows(b):
        at = pl.ds(pl.multiple_of(b * BT, BT), BT)
        return pltpu.make_async_copy(qkv_o.at[at], qkv_h.at[at], osems.at[b])

    out_w = pltpu.make_async_copy(w_o, w_h, osems.at[nb])
    g = pl.program_id(0)
    sh = half // 2

    @pl.when(g == 0)
    def _():
        moves = copies(
            [(a_own, a_buf.at[0])] + join_pieces(flag[0], plan, a_refs, a_buf.at[1]), sems
        )
        qkv_o[pl.ds(BT, KW - BT), half : 2 * half] = jnp.zeros((KW - BT, half), BF16)
        v_t[:, pl.ds(BT, KW - BT)] = jnp.zeros((half, KW - BT), BF16)
        lse_o[...] = jnp.zeros_like(lse_o)
        for m in moves:
            m.wait()
        for j in range(4):
            for s in range(2):
                w_o[:, (2 * j + s) * sh : (2 * j + s + 1) * sh] = a_buf[s, :, j * sh : (j + 1) * sh]
        out_w.start()

    x_o[...] = x
    xhat, _ = normed_parts(x)
    normed = gained(xhat, gain, shift, layer, 0)
    n_o[...] = normed
    qkv = dot(normed, w_o[:, : 3 * half])
    q = (qkv[:, :half] + qvb[layer, 0:1, :].astype(F32)).astype(BF16)
    k = qkv[:, half : 2 * half].astype(BF16)
    v = qkv[:, 2 * half :] + qvb[layer, 1:2, :].astype(F32)
    rows = pl.ds(pl.multiple_of(g * BT, BT), BT)
    qkv_o[rows, :half] = q
    qkv_o[rows, half : 2 * half] = k
    qkv_o[rows, 2 * half :] = v.astype(BF16)
    out_rows(g).start()
    v_t[:, rows] = jnp.transpose(v).astype(BF16)
    q = q * jnp.asarray(1.0 / math.sqrt(HD), BF16)
    for s in range(BT // QB):
        i = g * (BT // QB) + s
        ks = pl.multiple_of(jnp.maximum(i - DOC_MOST // QB, 0) * QB, QB)
        bias = window_bias(start, i, ks)
        cols = pl.ds(pl.multiple_of(i * QB, QB), QB)
        for p in range(half // 128):
            lo = 128 * p
            qq = head_pair(q[QB * s : QB * (s + 1), lo : lo + 128])
            kp = qkv_o[pl.ds(ks, KW), half + lo : half + lo + 128]
            scores = dot(kp, qq, 1, 1) + bias
            peak = jnp.max(scores, axis=0, keepdims=True)
            e = jnp.exp(scores - peak)
            total = jnp.sum(e, axis=0, keepdims=True)
            ot = dot(v_t[lo : lo + 128, pl.ds(ks, KW)], e.astype(BF16))
            inv = 1.0 / total
            o_t[lo : lo + HD, :] = ot[:HD, :QB] * inv[:, :QB]
            o_t[lo + HD : lo + 128, :] = ot[HD:, QB:] * inv[:, QB:]
            lse = peak + jnp.log(total)
            lse_o[2 * p : 2 * p + 1, cols] = lse[:, :QB]
            lse_o[2 * p + 1 : 2 * p + 2, cols] = lse[:, QB:]
        att_o[QB * s : QB * (s + 1), :] = jnp.transpose(o_t[...]).astype(BF16)
    part_o[...] = dot(att_o[...], w_o[:, 3 * half :], 1, 1).astype(BF16)

    @pl.when(g == nb - 1)
    def _():
        for b in range(nb):
            out_rows(b).wait()
        out_w.wait()


def attn_fwd(layer, stream_in, outb, flag, start, gain, shift, qvb, a_own, a_oth):
    first = layer == 0
    d = gain.shape[-1]
    half = a_own.shape[1] // 2
    ins = list(stream_in)
    specs = [SMEM if a.ndim == 1 else rows_spec(a.shape[1]) for a in ins]
    if not first:
        ins.append(outb)
        specs.append(full_spec(outb.shape))
    plan, arrays = a_oth
    ins += [flag, start, gain, shift, qvb, a_own, *arrays]
    specs += [SMEM] + [full_spec(a.shape) for a in (start, gain, shift, qvb)]
    specs += [ANY] * (1 + len(arrays))
    return pl.pallas_call(
        functools.partial(attn_fwd_kernel, layer, first, half, plan),
        grid=(LEN // BT,),
        in_specs=specs,
        out_specs=[
            rows_spec(d),
            rows_spec(d),
            ANY,
            rows_spec(half),
            full_spec((8, LEN)),
            rows_spec(d),
            ANY,
        ],
        out_shape=[
            jax.ShapeDtypeStruct((LEN, d), F32),
            jax.ShapeDtypeStruct((LEN, d), BF16),
            jax.ShapeDtypeStruct((LEN, 3 * half), BF16),
            jax.ShapeDtypeStruct((LEN, half), BF16),
            jax.ShapeDtypeStruct((8, LEN), F32),
            jax.ShapeDtypeStruct((LEN, d), BF16),
            jax.ShapeDtypeStruct((d, 4 * half), BF16),
        ],
        scratch_shapes=[
            pltpu.VMEM((half, LEN), BF16),
            pltpu.VMEM((half, QB), F32),
            pltpu.VMEM((2, d, 2 * half), BF16),
            pltpu.SemaphoreType.DMA((1 + len(plan),)),
            pltpu.VMEM((LEN, 3 * half), BF16),
            pltpu.VMEM((d, 4 * half), BF16),
            pltpu.SemaphoreType.DMA((LEN // BT + 1,)),
        ]
        + ([pltpu.VMEM((BT, d), BF16)] if first else []),
        name=f"attn_fwd_{layer}",
        cost_estimate=cost(22),
    )(*ins)


def load_mlp(layer, flag, plans, weights, wfc, wproj, sems):
    d = wfc.shape[0]
    f = wfc.shape[1] // 2
    n = len(plans[0])
    return copies(
        [(weights[0].at[layer], wfc.at[:, pl.ds(0, f)])]
        + join_pieces(flag[0], plans[0], weights[2 : 2 + n], wfc, pl.ds(f, f))
        + [(weights[1].at[layer], wproj.at[pl.ds(0, f)])]
        + join_pieces(flag[0], plans[1], weights[2 + n :], wproj.at[pl.ds(f, f)]),
        sems,
    )


def mlp_scratch(d, f2, plans):
    return [
        pltpu.VMEM((d, f2), BF16),
        pltpu.VMEM((f2, d), BF16),
        pltpu.SemaphoreType.DMA((2 + len(plans[0]) + len(plans[1]),)),
    ]


def mlp_weights(weights):
    w_fc, fc_oth, w_proj, pj_oth = weights
    return (fc_oth[0], pj_oth[0]), [w_fc, w_proj, *fc_oth[1], *pj_oth[1]]


def mlp_fwd_kernel(layer, plans, x, own, oth, outb, gain, shift, fcb, flag, *refs):
    nw = 2 + len(plans[0]) + len(plans[1])
    weights = refs[:nw]
    mid_o, n_o, h_o, part_o, wfc, wproj, sems = refs[nw:]

    @pl.when(pl.program_id(0) == 0)
    def _():
        for m in load_mlp(layer, flag, plans, weights, wfc, wproj, sems):
            m.wait()

    mid = (
        x[...]
        + (own[...].astype(F32) + oth[...].astype(F32))
        + outb[layer, 0:1, :].astype(F32)
    )
    mid_o[...] = mid
    xhat, _ = normed_parts(mid)
    normed = gained(xhat, gain, shift, layer, 1)
    n_o[...] = normed
    hidden = dot(normed, wfc[...]) + fcb[layer : layer + 1, :].astype(F32)
    h_o[...] = hidden.astype(BF16)
    t = jnp.tanh(GELU_C * hidden * (1.0 + 0.044715 * hidden * hidden))
    act = (0.5 * hidden * (1.0 + t)).astype(BF16)
    part_o[...] = dot(act, wproj[...]).astype(BF16)


def mlp_fwd(layer, x, own, oth, outb, gain, shift, fcb, flag, weights):
    d = x.shape[1]
    f = fcb.shape[1]
    plans, arrays = mlp_weights(weights)
    ins = [x, own, oth, outb, gain, shift, fcb, flag, *arrays]
    specs = [rows_spec(d)] * 3 + [full_spec(a.shape) for a in ins[3:7]] + [SMEM] + [ANY] * len(arrays)
    return pl.pallas_call(
        functools.partial(mlp_fwd_kernel, layer, plans),
        grid=(LEN // BT,),
        in_specs=specs,
        out_specs=[rows_spec(d), rows_spec(d), rows_spec(f), rows_spec(d)],
        out_shape=[
            jax.ShapeDtypeStruct((LEN, d), F32),
            jax.ShapeDtypeStruct((LEN, d), BF16),
            jax.ShapeDtypeStruct((LEN, f), BF16),
            jax.ShapeDtypeStruct((LEN, d), BF16),
        ],
        scratch_shapes=mlp_scratch(d, f, plans),
        name=f"mlp_fwd_{layer}",
        cost_estimate=cost(12),
    )(*ins)


def mlp_both_kernel(
    layer, plans, x, own, oth, c0, c1, c2, c3, place, outb, gain, shift, fcb, flag, *refs
):
    nw = 2 + len(plans[0]) + len(plans[1])
    weights = refs[:nw]
    mid_o, n_o, act_o, gh_o, out_o, part_o, cot, sumg_o, sumh_o, wfc, wproj, sems = refs[nw:]
    join_quarters(place, (c0, c1, c2, c3), cot)

    @pl.when(pl.program_id(0) == 0)
    def _():
        moves = load_mlp(layer, flag, plans, weights, wfc, wproj, sems)
        sumg_o[...] = jnp.zeros_like(sumg_o)
        sumh_o[...] = jnp.zeros_like(sumh_o)
        for m in moves:
            m.wait()

    mid = (
        x[...]
        + (own[...].astype(F32) + oth[...].astype(F32))
        + outb[layer, 0:1, :].astype(F32)
    )
    mid_o[...] = mid
    xhat, _ = normed_parts(mid)
    normed = gained(xhat, gain, shift, layer, 1)
    n_o[...] = normed
    grad_act = dot(cot[...], wproj[...], 1, 1)
    value, slope = gelu_parts(dot(normed, wfc[...]) + fcb[layer : layer + 1, :].astype(F32))
    act = value.astype(BF16)
    act_o[...] = act
    gh = (grad_act * slope).astype(BF16)
    gh_o[...] = gh
    part_o[...] = dot(gh, wfc[...], 1, 1).astype(BF16)
    out_o[...] = dot(act, wproj[...]).astype(BF16)
    sumg_o[0:1, :] += colsum(cot[...].astype(F32))
    sumh_o[0:1, :] += colsum(gh.astype(F32))


def mlp_both(layer, x, own, oth, cot, outb, gain, shift, fcb, flag, weights):
    d = x.shape[1]
    f = fcb.shape[1]
    plans, arrays = mlp_weights(weights)
    ins = [x, own, oth, *cot, outb, gain, shift, fcb, flag, *arrays]
    specs = [rows_spec(d)] * 3 + [rows_spec(d // 4)] * 4 + [SMEM]
    specs += [full_spec(a.shape) for a in ins[8:12]] + [SMEM] + [ANY] * len(arrays)
    widths = [d, d, f, f, d, d, d]
    kinds = [F32, BF16, BF16, BF16, BF16, BF16, BF16]
    return pl.pallas_call(
        functools.partial(mlp_both_kernel, layer, plans),
        grid=(LEN // BT,),
        in_specs=specs,
        out_specs=[rows_spec(w) for w in widths] + [full_spec((8, d)), full_spec((8, f))],
        out_shape=[jax.ShapeDtypeStruct((LEN, w), k) for w, k in zip(widths, kinds)]
        + [jax.ShapeDtypeStruct((8, d), F32), jax.ShapeDtypeStruct((8, f), F32)],
        scratch_shapes=mlp_scratch(d, f, plans),
        name=f"mlp_both_{layer}",
        cost_estimate=cost(18),
    )(*ins)


def mlp_bwd_kernel(layer, plans, gm, own, oth, x, h, gain, flag, *refs):
    nw = 2 + len(plans[0]) + len(plans[1])
    weights = refs[:nw]
    g_o, low_o, act_o, gh_o, part_o, sums_o, sumh_o, wfc, wproj, sems = refs[nw:]

    @pl.when(pl.program_id(0) == 0)
    def _():
        moves = load_mlp(layer, flag, plans, weights, wfc, wproj, sems)
        sums_o[...] = jnp.zeros_like(sums_o)
        sumh_o[...] = jnp.zeros_like(sumh_o)
        for m in moves:
            m.wait()

    grad, g_gain, g_shift = norm_back(
        gm[...], own[...], oth[...], x[...], gain[layer + 1, 0:1, :].astype(F32)
    )
    sums_o[0:1, :] += colsum(g_gain)
    sums_o[1:2, :] += colsum(g_shift)
    sums_o[2:3, :] += colsum(grad)
    g_o[...] = grad
    low = grad.astype(BF16)
    low_o[...] = low
    grad_act = dot(low, wproj[...], 1, 1)
    value, slope = gelu_parts(h[...].astype(F32))
    act_o[...] = value.astype(BF16)
    gh = (grad_act * slope).astype(BF16)
    gh_o[...] = gh
    part_o[...] = dot(gh, wfc[...], 1, 1).astype(BF16)
    sumh_o[0:1, :] += colsum(gh.astype(F32))


def mlp_bwd(layer, gm, own, oth, x, h, gain, flag, weights):
    d = x.shape[1]
    f = h.shape[1]
    plans, arrays = mlp_weights(weights)
    ins = [gm, own, oth, x, h, gain, flag, *arrays]
    specs = [rows_spec(d)] * 4 + [rows_spec(f), full_spec(gain.shape), SMEM] + [ANY] * len(arrays)
    widths = [d, d, f, f, d]
    kinds = [F32, BF16, BF16, BF16, BF16]
    return pl.pallas_call(
        functools.partial(mlp_bwd_kernel, layer, plans),
        grid=(LEN // BT,),
        in_specs=specs,
        out_specs=[rows_spec(w) for w in widths] + [full_spec((8, d)), full_spec((8, f))],
        out_shape=[jax.ShapeDtypeStruct((LEN, w), k) for w, k in zip(widths, kinds)]
        + [jax.ShapeDtypeStruct((8, d), F32), jax.ShapeDtypeStruct((8, f), F32)],
        scratch_shapes=mlp_scratch(d, f, plans),
        name=f"mlp_bwd_{layer}",
        cost_estimate=cost(16),
    )(*ins)


def stage(buf, value, order):
    dims = [o for o in order if o != "y"]
    n = len(dims)
    r = value.shape[0] >> n
    for c in range(1 << n):
        pos = sum(((c >> b) & 1) << (n - 1 - j) for j, b in enumerate(dims))
        buf[r * pos : r * (pos + 1), :] = value[r * c : r * (c + 1)].astype(BF16)


def ship(buf, keep, send, slot, order, flags, sems):
    if order[0] == "y":
        pairs = [(buf, send if slot else keep)]
    else:
        half = buf.shape[0] // 2
        f = flags[order[0]]
        lo = [pl.multiple_of(h * half, 16) for h in (f, 1 - f)]
        pairs = [
            (buf.at[pl.ds(lo[0], half)], keep.at[slot]),
            (buf.at[pl.ds(lo[1], half)], send.at[slot]),
        ]
    return [pltpu.make_async_copy(a, b, sems.at[j]) for j, (a, b) in enumerate(pairs)]


def first_shape(order, d, w):
    return (d, w) if order[0] == "y" else (2, d // 2, w)


def dw_mlp_kernel(orders, flags, n, low, gh, act, *refs):
    outs, (bufs, sems) = refs[:4], refs[4:]
    j = pl.program_id(0)

    def moves(t, slot):
        keep, send = outs[2 * t : 2 * t + 2]
        return ship(bufs.at[t, slot], keep, send, slot, orders[t], flags, sems.at[t, slot])

    for t, (a, b) in enumerate(((n, gh), (low, act))):
        stage(bufs.at[t, j], dot(a[...], b[...], 0, 0), orders[t])
        for slot in range(2):

            @pl.when(j == slot)
            def _():
                for m in moves(t, slot):
                    m.start()

    @pl.when(j == 1)
    def _():
        for t in range(2):
            for slot in range(2):
                for m in moves(t, slot):
                    m.wait()


def dw_mlp(layer, n, low, gh, act, orders, flags):
    t, d = n.shape
    f = gh.shape[1] // 2
    col = pl.BlockSpec((t, f), lambda j: (0, j))
    shapes = [first_shape(o, d, f) for o in orders for _ in range(2)]
    k0, s0, k1, s1 = pl.pallas_call(
        functools.partial(dw_mlp_kernel, orders),
        grid=(2,),
        in_specs=[SMEM, full_spec(n.shape), full_spec(low.shape), col, col],
        out_specs=[ANY] * 4,
        out_shape=[jax.ShapeDtypeStruct(s, BF16) for s in shapes],
        scratch_shapes=[pltpu.VMEM((2, 2, d, f), BF16), pltpu.SemaphoreType.DMA((2, 2, 2))],
        name=f"dw_mlp_{layer}",
        cost_estimate=cost(9),
    )(flags, n, low, gh, act)
    return Part(k0, s0, orders[0]), Part(k1, s1, orders[1])


def dw_attn_kernel(orders, flags, n, low, dqkv, att, *refs):
    outs, (bufs, sems) = refs[:4], refs[4:]
    sh = att.shape[1] // 2
    moves = []

    def send_off(t, values):
        for slot in range(2):
            both = jnp.concatenate(
                [v[:, (2 * j + slot) * sh : (2 * j + slot + 1) * sh] for v, j in values], axis=1
            )
            stage(bufs.at[t, slot], both, orders[t])
            keep, send = outs[2 * t : 2 * t + 2]
            for m in ship(
                bufs.at[t, slot], keep, send, slot, orders[t], flags, sems.at[t, slot]
            ):
                m.start()
                moves.append(m)

    half = 2 * sh
    qk = dot(n[...], dqkv[:, : 2 * half], 0, 0)
    send_off(0, [(qk, 0), (qk, 1)])
    v = dot(n[...], dqkv[:, 2 * half :], 0, 0)
    wo = dot(low[...], att[...], 0, 0)
    send_off(1, [(v, 0), (wo, 0)])
    for m in moves:
        m.wait()


def dw_attn(layer, n, low, dqkv, att, orders, flags):
    d = n.shape[1]
    w = att.shape[1]
    ins = (n, low, dqkv, att)
    shapes = [first_shape(o, d, w) for o in orders for _ in range(2)]
    k0, s0, k1, s1 = pl.pallas_call(
        functools.partial(dw_attn_kernel, orders),
        grid=(1,),
        in_specs=[SMEM] + [full_spec(a.shape) for a in ins],
        out_specs=[ANY] * 4,
        out_shape=[jax.ShapeDtypeStruct(s, BF16) for s in shapes],
        scratch_shapes=[pltpu.VMEM((2, 2, d, w), BF16), pltpu.SemaphoreType.DMA((2, 2, 2))],
        name=f"dw_attn_{layer}",
        cost_estimate=cost(7),
    )(flags, *ins)
    return Part(k0, s0, orders[0]), Part(k1, s1, orders[1])


def combine_kernel(steps, merged, flags, *refs):
    ins, outs = refs[: 2 * len(steps)], refs[2 * len(steps) :]
    lo = 0
    for k, o in enumerate(steps):
        keep, got = ins[2 * k : 2 * k + 2]

        def total(at):
            return keep[at].astype(F32) + got[at].astype(F32)

        if o is None:
            outs[k][...] = total(...)
            continue
        dst = outs if merged else outs[2 * k : 2 * k + 2]
        cols = slice(lo, lo + keep.shape[-1]) if merged else slice(None)
        if o == "y":
            halves = [total(0), total(1)]
        else:
            r = keep.shape[-2] // 2
            lead = (slice(None),) * (len(keep.shape) - 2)
            rows = [pl.ds(pl.multiple_of(h * r, 8), r) for h in (flags[o], 1 - flags[o])]
            halves = [total(lead + (row, slice(None))) for row in rows]
        for out, v in zip(dst, halves):
            out[..., cols] = v.astype(BF16)
        if merged:
            lo += keep.shape[-1]


def combine(parts, flags, merged=False):
    steps = [p.order[1] if len(p.order) > 1 else None for p in parts]
    wide = all(p.keep.shape[-1] % 384 == 0 for p in parts)
    ncol = 3 if wide and not merged and parts[0].keep.size >= 2**18 else 1

    def spec(shape):
        block = shape[:-1] + (shape[-1] // ncol,)
        return pl.BlockSpec(block, lambda g: (0,) * (len(shape) - 1) + (g,))

    ins, shapes = [], []
    for p, o in zip(parts, steps):
        ins += [p.keep, p.got]
        s = p.keep.shape
        if o is None:
            shapes.append(jax.ShapeDtypeStruct(s, F32))
        else:
            s = s[1:] if o == "y" else s[:-2] + (s[-2] // 2, s[-1])
            shapes += [jax.ShapeDtypeStruct(s, BF16)] * 2
    if merged:
        s = (shapes[0].shape[0], sum(p.keep.shape[-1] for p in parts))
        shapes = [jax.ShapeDtypeStruct(s, BF16)] * 2
    outs = pl.pallas_call(
        functools.partial(combine_kernel, steps, merged),
        grid=(ncol,),
        in_specs=[SMEM] + [spec(a.shape) for a in ins],
        out_specs=[spec(a.shape) for a in shapes],
        out_shape=shapes,
        name="combine",
        cost_estimate=cost(0.3),
    )(flags, *ins)
    if merged:
        return Part(outs[0], outs[1], parts[0].order[1:])
    if steps[0] is None:
        return list(outs)
    return [
        Part(outs[2 * k], outs[2 * k + 1], p.order[1:]) for k, p in enumerate(parts)
    ]


def final_kernel(f, share, *refs):
    (m1, m0, a1, a0, pk), outs = [refs[2 * k : 2 * k + 2] for k in range(5)], refs[10:]
    fc_o, pj_o, qkv_o, wo_o, pos_o, gain_o, shift_o, bias_o, fcb_o, qvb_o = outs

    def total(pair, lo, n):
        return pair[0][:, lo : lo + n].astype(F32) + pair[1][:, lo : lo + n].astype(F32)

    for l, (m, a) in enumerate(((m0, a0), (m1, a1))):
        fc_o[l] = total(m, 0, f)
        pj_o[l] = total(m, f, f)
        v = total(a, 0, 4 * share)
        for j in range(3):
            qkv_o[l, j] = v[:, share * j : share * (j + 1)]
        wo_o[l] = jnp.transpose(v[:, 3 * share :])
    v = total(pk, 0, share)
    rows = pos_o.shape[1]
    pos_o[...] = jnp.transpose(v[:rows])
    v = v[rows:]
    w = gain_o.shape[2]
    for l in range(2):
        for k, ref in enumerate((gain_o, shift_o, bias_o)):
            ref[l] = v[4 * k + 2 * l : 4 * k + 2 * l + 2, :w]
        qvb_o[l] = v[2 * l : 2 * l + 2, w : w + qvb_o.shape[2]]
    fcb_o[...] = v[12:14, :w]


def final(parts, f, share, rows, n_dp):
    r = parts[0].keep.shape[0]
    ins = [v for p in parts for v in (p.keep, p.got)]
    shapes = [(2, r, f), (2, r, f), (2, 3, r, share), (2, share, r), (share, rows)]
    shapes += [(2, 2, r)] * 3 + [(2, r), (2, 2, share // n_dp)]
    return pl.pallas_call(
        functools.partial(final_kernel, f, share),
        grid=(1,),
        in_specs=[full_spec(v.shape) for v in ins],
        out_specs=[full_spec(v) for v in shapes],
        out_shape=[jax.ShapeDtypeStruct(v, F32) for v in shapes],
        name="final",
        cost_estimate=cost(3),
    )(*ins)


class Part:
    def __init__(self, keep, send, order):
        self.keep, self.send, self.order = keep, send, list(order)

    def go(self, n_dp):
        o = self.order[0]
        self.got = y_swap(self.send) if o == "y" else dp_swap(self.send, o, n_dp)


def attn_bwd_kernel(layer, half, *refs):
    (g_i, own, oth, mid, qkv, att, lse, start, gain, w) = refs[:10]
    (gm_o, low_o, dqkv_h, part_h, sums_o, qvs_o, k_t, dk, dv, dq_t) = refs[10:20]
    dqkv_o, part_o, osems = refs[20:]
    g = pl.program_id(0)

    @pl.when(g == 0)
    def _():
        sums_o[...] = jnp.zeros_like(sums_o)
        qvs_o[...] = jnp.zeros_like(qvs_o)
        dk[...] = jnp.zeros_like(dk)
        dv[...] = jnp.zeros_like(dv)
        for b in range(LEN // BT):
            block = qkv[BT * b : BT * (b + 1), half : 2 * half].astype(F32)
            k_t[:, BT * b : BT * (b + 1)] = jnp.transpose(block).astype(BF16)

    gm, g_gain, g_shift = norm_back(
        g_i[...].astype(F32), own[...], oth[...], mid[...], gain[layer, 1:2, :].astype(F32)
    )
    gm_o[...] = gm
    sums_o[0:1, :] += colsum(g_gain)
    sums_o[1:2, :] += colsum(g_shift)
    sums_o[2:3, :] += colsum(gm)
    low = gm.astype(BF16)
    low_o[...] = low
    d_att = dot(low, w[:, 3 * half :]).astype(BF16)
    prod = d_att.astype(F32) * att[...].astype(F32)
    head = lax.broadcasted_iota(jnp.int32, (8, half), 1) // HD
    pick = (head == lax.broadcasted_iota(jnp.int32, (8, half), 0)).astype(F32)
    inner = lax.dot_general(
        pick,
        prod,
        (((1,), (1,)), ((), ())),
        preferred_element_type=F32,
        precision=lax.Precision.HIGHEST,
    )
    rows = pl.ds(pl.multiple_of(g * BT, BT), BT)
    q = qkv[rows, :half] * jnp.asarray(1.0 / math.sqrt(HD), BF16)
    for s in range(BT // QB):
        i = g * (BT // QB) + s
        ks = pl.multiple_of(jnp.maximum(i - DOC_MOST // QB, 0) * QB, QB)
        bias = window_bias(start, i, ks)
        cols = pl.ds(pl.multiple_of(i * QB, QB), QB)
        win = pl.ds(ks, KW)
        for p in range(half // 128):
            lo = 128 * p
            qq = head_pair(q[QB * s : QB * (s + 1), lo : lo + 128])
            oo = head_pair(d_att[QB * s : QB * (s + 1), lo : lo + 128])
            kp = qkv[win, half + lo : half + lo + 128]
            vp = qkv[win, 2 * half + lo : 2 * half + lo + 128]
            total = jnp.concatenate(
                [lse[2 * p : 2 * p + 1, cols], lse[2 * p + 1 : 2 * p + 2, cols]], axis=1
            )
            inn = jnp.concatenate(
                [
                    inner[2 * p : 2 * p + 1, QB * s : QB * (s + 1)],
                    inner[2 * p + 1 : 2 * p + 2, QB * s : QB * (s + 1)],
                ],
                axis=1,
            )
            probs = jnp.exp(dot(kp, qq, 1, 1) + bias - total)
            d_probs = dot(vp, oo, 1, 1)
            ds = (probs * (d_probs - inn)).astype(BF16)
            dv[win, lo : lo + 128] += dot(probs.astype(BF16), oo)
            dk[win, lo : lo + 128] += dot(ds, qq)
            dqt = dot(k_t[lo : lo + 128, win], ds)
            dq_t[lo : lo + HD, :] = dqt[:HD, :QB]
            dq_t[lo + HD : lo + 128, :] = dqt[HD:, QB:]
        dq = (jnp.transpose(dq_t[...]) * (1.0 / math.sqrt(HD))).astype(BF16)
        dqkv_o[cols, :half] = dq
        qvs_o[0:1, :] += colsum(dq.astype(F32))

    @pl.when(g == pl.num_programs(0) - 1)
    def _():
        moves = []
        total = jnp.zeros((1, half), F32)
        for b in range(LEN // BT):
            at = pl.ds(BT * b, BT)
            dqkv_o[at, half : 2 * half] = dk[at, :].astype(BF16)
            dvb = dv[at, :].astype(BF16)
            dqkv_o[at, 2 * half :] = dvb
            total += colsum(dvb.astype(F32))
            moves += copies([(dqkv_o.at[at], dqkv_h.at[at])], osems.at[b, 0:1])
            part_o[at, :] = dot(dqkv_o[at, :], w[:, : 3 * half], 1, 1).astype(BF16)
            moves += copies([(part_o.at[at], part_h.at[at])], osems.at[b, 1:2])
        qvs_o[1:2, :] = total
        for m in moves:
            m.wait()


def attn_bwd(layer, g, own, oth, mid, qkv, att, lse, start, gain, w):
    d = mid.shape[1]
    half = att.shape[1]
    ins = [g, own, oth, mid, qkv, att, lse, start, gain, w]
    specs = [rows_spec(d)] * 4 + [full_spec(qkv.shape), rows_spec(half)]
    specs += [full_spec(a.shape) for a in ins[6:]]
    return pl.pallas_call(
        functools.partial(attn_bwd_kernel, layer, half),
        grid=(LEN // BT,),
        in_specs=specs,
        out_specs=[
            rows_spec(d),
            rows_spec(d),
            ANY,
            ANY,
            full_spec((8, d)),
            full_spec((8, half)),
        ],
        out_shape=[
            jax.ShapeDtypeStruct((LEN, d), F32),
            jax.ShapeDtypeStruct((LEN, d), BF16),
            jax.ShapeDtypeStruct((LEN, 3 * half), BF16),
            jax.ShapeDtypeStruct((LEN, d), BF16),
            jax.ShapeDtypeStruct((8, d), F32),
            jax.ShapeDtypeStruct((8, half), F32),
        ],
        scratch_shapes=[
            pltpu.VMEM((half, LEN), BF16),
            pltpu.VMEM((LEN, half), F32),
            pltpu.VMEM((LEN, half), F32),
            pltpu.VMEM((half, QB), F32),
            pltpu.VMEM((LEN, 3 * half), BF16),
            pltpu.VMEM((LEN, d), BF16),
            pltpu.SemaphoreType.DMA((LEN // BT, 2)),
        ],
        name=f"attn_bwd_{layer}",
        cost_estimate=cost(24),
    )(*ins)


def norm_bwd_kernel(layer, n_dp, place, g, own, oth, x, gain, hot, *refs):
    sums, (near_o, far_o, own_o, oth_o, acc, table, small) = refs[:8], refs[8:]
    sums0, sums0b, sums1, sumg1, sumh0, sumh1, qvs0, qvs1 = sums
    w = near_o.shape[1]
    step = pl.program_id(0)

    @pl.when(step == 0)
    def _():
        acc[...] = jnp.zeros_like(acc)
        table[...] = jnp.zeros_like(table)
        small[...] = jnp.zeros_like(small)

    out, g_gain, g_shift = norm_back(
        g[...], own[...], oth[...], x[...], gain[layer, 0:1, :].astype(F32)
    )
    acc[0:1, :] += colsum(g_gain)
    acc[1:2, :] += colsum(g_shift)

    def select(q):
        far = q ^ 2
        near_o[...] = out[:, w * q : w * (q + 1)]
        far_o[...] = out[:, w * far : w * (far + 1)].astype(BF16)

    for q in range(4):
        pl.when(place[0] == q)(functools.partial(select, q))
    table[0] += dot(hot[...], near_o[...].astype(BF16), 0, 0)
    table[1] += dot(hot[...], far_o[...], 0, 0)

    @pl.when(step == pl.num_programs(0) - 1)
    def _():
        rows = [(acc, 0), (sums0, 0), (sums0b, 0), (sums1, 0)]
        rows += [(acc, 1), (sums0, 1), (sums0b, 1), (sums1, 1)]
        rows += [(sums0, 2), (sums0b, 2), (sums1, 2), (sumg1, 0)]
        cw, qw, f = acc.shape[1] // n_dp, w // n_dp, sumh0.shape[1] // 2
        for c in range(n_dp):
            for k, (ref, r) in enumerate(rows):
                v = ref[r : r + 1, cw * c : cw * (c + 1)]
                small[0, 16 * c + k : 16 * c + k + 1, 0:cw] = v
                small[1, 16 * c + k : 16 * c + k + 1, 0:cw] = v
            for slot in range(2):
                for k, ref in enumerate((sumh0, sumh1)):
                    lo = f * slot + cw * c
                    row = 16 * c + 12 + k
                    small[slot, row : row + 1, 0:cw] = ref[0:1, lo : lo + cw]
                for k, (ref, r) in enumerate(((qvs0, 0), (qvs0, 1), (qvs1, 0), (qvs1, 1))):
                    lo = w * slot + qw * c
                    row = 16 * c + k
                    small[slot, row : row + 1, cw : cw + qw] = ref[r : r + 1, lo : lo + qw]
        for slot, ref in enumerate((own_o, oth_o)):
            ref[:DOC_MOST, :] = table[slot].astype(BF16)
            ref[DOC_MOST:, :] = small[slot].astype(BF16)


def norm_bwd(layer, n_dp, place, g, own, oth, x, gain, hot, sums):
    d = x.shape[1]
    w = d // 4
    r = DOC_MOST + 16 * n_dp
    return pl.pallas_call(
        functools.partial(norm_bwd_kernel, layer, n_dp),
        grid=(LEN // BT,),
        in_specs=[SMEM]
        + [rows_spec(d)] * 4
        + [full_spec(gain.shape), rows_spec(DOC_MOST)]
        + [full_spec(v.shape) for v in sums],
        out_specs=[rows_spec(w), rows_spec(w), full_spec((r, w)), full_spec((r, w))],
        out_shape=[
            jax.ShapeDtypeStruct((LEN, w), F32),
            jax.ShapeDtypeStruct((LEN, w), BF16),
            jax.ShapeDtypeStruct((r, w), BF16),
            jax.ShapeDtypeStruct((r, w), BF16),
        ],
        scratch_shapes=[
            pltpu.VMEM((8, d), F32),
            pltpu.VMEM((2, DOC_MOST, w), F32),
            pltpu.VMEM((2, 16 * n_dp, w), F32),
        ],
        name=f"norm_bwd_{layer}",
        cost_estimate=cost(1),
    )(place, g, own, oth, x, gain, hot, *sums)


def expand_kernel(order, n_dp, rows, flags, own, got, keep, send):
    total = (own[...].astype(F32) + got[...].astype(F32)).astype(BF16)
    n = len(order)
    half = 1 << (n - 1)
    r = rows + 16

    def split(bit):
        for c in range(n_dp):
            pos = sum(((c >> b) & 1) << (n - 1 - j) for j, b in enumerate(order))
            out = keep if pos // half == bit else send
            row = r * (pos % half)
            if rows * c < DOC_MOST:
                out[row : row + rows, :] = total[rows * c : rows * (c + 1)]
            else:
                out[row : row + rows, :] = jnp.zeros((rows, total.shape[1]), BF16)
            lo = DOC_MOST + 16 * c
            out[row + rows : row + r, :] = total[lo : lo + 16]

    pl.when(flags[order[0]] == 0)(lambda: split(0))
    pl.when(flags[order[0]] == 1)(lambda: split(1))


def expand(own, got, order, n_dp, rows, flags):
    w = own.shape[1]
    shape = (n_dp * (rows + 16) // 2, w)
    keep, send = pl.pallas_call(
        functools.partial(expand_kernel, order, n_dp, rows),
        grid=(1,),
        in_specs=[SMEM, full_spec(own.shape), full_spec(own.shape)],
        out_specs=[full_spec(shape)] * 2,
        out_shape=[jax.ShapeDtypeStruct(shape, BF16)] * 2,
        name="expand",
        cost_estimate=cost(0.3),
    )(flags, own, got)
    return Part(keep, send, order)


def core_swap(a):
    return lax.ppermute(a, "mp", [(i, i ^ 1) for i in range(4)])


def y_swap(a):
    return lax.ppermute(a, "mp", [(i, i ^ 2) for i in range(4)])


def dp_swap(a, bit, n_dp):
    return lax.ppermute(a, "dp", [(i, i ^ (1 << bit)) for i in range(n_dp)])


def pick(flag, zero, one):
    return jnp.where(flag == 0, zero, one)


class Place:
    def __init__(self, n_dp):
        mp = lax.axis_index("mp")
        self.n_dp = n_dp
        self.bits = n_dp.bit_length() - 1
        self.y = mp // 2
        self.c = mp % 2
        self.dp = lax.axis_index("dp")

    def dp_bit(self, b):
        return (self.dp >> b) & 1


def row_pieces(a, at):
    rows = a.reshape(2, LEN, a.shape[1])
    return pick(at.y, rows[0], rows[1]), pick(at.y, rows[1], rows[0])


def own_cols(a, at, other):
    w = a.shape[1] // 4
    halves = (a[:, : 2 * w], a[:, 2 * w :])
    h = pick(at.y, halves[1], halves[0]) if other else pick(at.y, halves[0], halves[1])
    return pick(at.c, h[:, :w], h[:, w:])


def bar(*vals):
    return lax.optimization_barrier(vals)


def doc_starts(doc_ids):
    row_index = jnp.broadcast_to(jnp.arange(doc_ids.shape[1], dtype=jnp.int32), doc_ids.shape)
    previous = jnp.concatenate([doc_ids[:, :1] - 1, doc_ids[:, :-1]], axis=1)
    starts = jnp.where(doc_ids != previous, row_index, 0)
    return lax.cummax(starts, axis=1)


def on_device(
    n_dp,
    tokens,
    doc_ids,
    positions_table,
    norm_gain,
    norm_shift,
    joined_projection_weight,
    qv_bias,
    w_out,
    out_bias,
    w_fc,
    fc_bias,
    w_proj,
    cotangent,
):
    at = Place(n_dp)
    d = positions_table.shape[1]
    share = joined_projection_weight.shape[-1]
    f = w_fc.shape[-1]
    bits = list(range(2, at.bits))
    flags = jnp.stack([at.dp_bit(b) for b in range(at.bits)]).astype(jnp.int32)

    b = at.dp_bit(0) ^ at.dp_bit(1)
    flag = b.reshape(1)
    quarter = (2 * at.y + at.c).astype(jnp.int32).reshape(1)
    gain, shift = norm_gain, norm_shift

    a_own = [
        jnp.concatenate([joined_projection_weight[l].reshape(d, 3 * share), w_out[l].T], axis=1)
        for l in range(2)
    ]
    biases = jnp.concatenate([qv_bias.reshape(-1), fc_bias.reshape(-1)]).reshape(-1, d)
    biases = jnp.pad(biases, ((0, -biases.shape[0] % 8), (0, 0)))
    r = d // 2

    def half_rows(w):
        return lax.dynamic_slice_in_dim(w, b * r, r, 0)

    def x_swap(w):
        return dp_swap(w, 0, n_dp)

    def z_swap(w):
        return dp_swap(w, 1, n_dp)

    def by_two(one, lo=0):
        return x_swap(one[lo : lo + r // 2]), z_swap(one[lo + r // 2 : lo + r])

    def plan_one(lo=0):
        return ((lo, r, 0, 0), (0, r, 1, 0))

    def plan_two(lo=0):
        return ((lo, r, 0, 0), (0, r // 2, 1, 0), (0, r // 2, 1, r // 2))

    tok_mine, tok_theirs = row_pieces(tokens, at)
    tok_far = y_swap(tok_theirs)
    a_one0 = y_swap(jnp.concatenate([half_rows(a_own[0]), biases], axis=0))

    starts = doc_starts(doc_ids)
    start = pick(at.y, starts[0:1], starts[1:2])
    place = jnp.arange(LEN, dtype=jnp.int32) - start[0]
    hot = (place[:, None] == jnp.arange(DOC_MOST, dtype=jnp.int32)[None, :]).astype(BF16)
    fc_half = half_rows(w_fc[0])
    tok_far, a_one0, hot, a_own[1], fc_half = bar(tok_far, a_one0, hot, a_own[1], fc_half)
    fc_one0 = y_swap(fc_half)
    embedded = dot(hot, positions_table[:DOC_MOST]).astype(BF16)

    a_x, a_z = by_two(a_one0)
    tok = [tok_mine, core_swap(tok_mine), tok_far, core_swap(tok_far)]
    small = a_one0[r:].reshape(-1)
    nq = qv_bias.size
    qvb = jnp.concatenate([qv_bias, small[:nq].reshape(qv_bias.shape)], axis=-1)
    fcb = jnp.concatenate(
        [fc_bias, small[nq : nq + fc_bias.size].reshape(fc_bias.shape)], axis=-1
    )
    send_y = jnp.concatenate([half_rows(w_proj[0]), half_rows(a_own[1])], axis=0)
    a_x, a_z, fc_one0, send_y, embedded, *tok = bar(a_x, a_z, fc_one0, send_y, embedded, *tok)

    fc_two0 = x_swap(fc_one0)
    pj_a1 = y_swap(send_y)
    x0, n0, qkv0, att0, lse0, part, wa0 = attn_fwd(
        0,
        (*tok, embedded, quarter),
        out_bias,
        flag,
        start,
        gain,
        shift,
        qvb,
        a_own[0],
        (plan_two(), (a_one0, a_x, a_z)),
    )
    part, x0, fc_two0, pj_a1 = bar(part, x0, fc_two0, pj_a1)
    far = core_swap(part)
    pj_x, pj_z = by_two(pj_a1)
    far, pj_x, pj_z = bar(far, pj_x, pj_z)
    mlp0 = (
        w_fc,
        (plan_one(), (fc_one0, fc_two0)),
        w_proj,
        (plan_two(), (pj_a1, pj_x, pj_z)),
    )
    a_two1 = x_swap(pj_a1[r:])
    fc_one1 = y_swap(half_rows(w_fc[1]))
    mid0, nn0, hid0, part2 = mlp_fwd(
        0, x0, part, far, out_bias, gain, shift, fcb, flag, mlp0
    )
    part2, mid0, a_two1, fc_one1 = bar(part2, mid0, a_two1, fc_one1)
    far = core_swap(part2)
    (far,) = bar(far)
    fc_two1 = x_swap(fc_one1)
    pj_one1 = y_swap(half_rows(w_proj[1]))
    cot_mine, cot_theirs = row_pieces(cotangent, at)
    cot_far = y_swap(cot_theirs)
    x1, n1, qkv1, att1, lse1, part, wa1 = attn_fwd(
        1,
        (mid0, part2, far),
        out_bias,
        flag,
        start,
        gain,
        shift,
        qvb,
        a_own[1],
        (plan_one(r), (pj_a1, a_two1)),
    )
    part, x1, fc_two1, cot_far, pj_one1 = bar(part, x1, fc_two1, cot_far, pj_one1)
    far = core_swap(part)
    pj_x, pj_z = by_two(pj_one1)
    cot = [cot_mine, core_swap(cot_mine), cot_far, core_swap(cot_far)]
    far, pj_x, pj_z, *cot = bar(far, pj_x, pj_z, *cot)
    mlp1 = (
        w_fc,
        (plan_one(), (fc_one1, fc_two1)),
        w_proj,
        (plan_two(), (pj_one1, pj_x, pj_z)),
    )
    mid1, nn1, act, gh, part_out, part, cot, sumg1, sumh1 = mlp_both(
        1, x1, part, far, (*cot, quarter), out_bias, gain, shift, fcb, flag, mlp1
    )

    def go(*parts):
        for p in parts:
            p.go(n_dp)

    def bar_parts(parts, sent, *vals):
        name = "send" if sent else "got"
        out = bar(*[getattr(p, name) for p in parts], *vals)
        for p, v in zip(parts, out):
            setattr(p, name, v)
        return out[len(parts) :]

    part, part_out, mid1, gh, act = bar(part, part_out, mid1, gh, act)
    far = core_swap(part)
    far_out = core_swap(part_out)
    o_fc, o_pj = ["y", 1, 0] + bits, [0, "y", 1] + bits
    o_a, o_b = [0, 1, "y"] + bits, [1, "y", 0] + bits
    fc1, pj1 = dw_mlp(1, nn1, cot, gh, act, (o_fc, o_pj), flags)
    far, far_out, mid1, part_out = bar_parts([fc1, pj1], True, far, far_out, mid1, part_out)
    go(fc1, pj1)
    gm1, m_low, dqkv, part, sums1, qvs1 = attn_bwd(
        1, cot, part, far, mid1, qkv1, att1, lse1, start, gain, wa1
    )
    part, gm1, m_low, dqkv, far_out, part_out = bar_parts(
        [fc1, pj1], False, part, gm1, m_low, dqkv, far_out, part_out
    )
    far = core_swap(part)
    fc1, pj1 = combine([fc1, pj1], flags)
    result = (
        mid1 + (part_out.astype(F32) + far_out.astype(F32)) + out_bias[1, 1].astype(F32)
    ).astype(BF16)
    out_near, out_send = own_cols(result, at, False), own_cols(result, at, True)
    out_near, out_send, far, m_low = bar_parts([fc1, pj1], True, out_near, out_send, far, m_low)
    aa1, ab1 = dw_attn(1, n1, m_low, dqkv, att1, (o_a, ["y", 1, 0] + bits), flags)
    far, gm1 = bar_parts([aa1, ab1], True, far, gm1)
    go(fc1, pj1, aa1)
    g0, g_low, act, gh, part, sums0b, sumh0 = mlp_bwd(
        0, gm1, part, far, x1, hid0, gain, flag, mlp0
    )
    part, g0, g_low, act, gh = bar_parts([fc1, pj1, aa1], False, part, g0, g_low, act, gh)
    far = core_swap(part)
    fc1, pj1, aa1 = combine([fc1, pj1, aa1], flags)
    far, g_low, act, gh = bar_parts([fc1, pj1, aa1, ab1], True, far, g_low, act, gh)
    go(ab1, fc1, pj1, aa1)
    fc0, pj0 = dw_mlp(0, nn0, g_low, gh, act, (o_fc, o_pj), flags)
    far, fc0.send, pj0.send, g0 = bar_parts(
        [ab1, fc1, pj1, aa1], False, far, fc0.send, pj0.send, g0
    )
    last1 = combine([fc1, pj1], flags, merged=True)
    aa1, ab1 = combine([aa1, ab1], flags)
    far, g0, part = bar_parts([last1, aa1, ab1, fc0, pj0], True, far, g0, part)
    go(fc0, pj0, aa1, ab1, last1)
    gm0, m_low, dqkv, part, sums0, qvs0 = attn_bwd(
        0, g0, part, far, mid0, qkv0, att0, lse0, start, gain, wa0
    )
    part, gm0, m_low, dqkv = bar_parts(
        [fc0, pj0, aa1, ab1, last1], False, part, gm0, m_low, dqkv
    )
    far = core_swap(part)
    fc0, pj0 = combine([fc0, pj0], flags)
    (ab1,) = combine([ab1], flags)
    far, m_low, dqkv = bar_parts([fc0, pj0, ab1], True, far, m_low, dqkv)
    go(fc0, pj0, ab1)
    aa0, ab0 = dw_attn(0, n0, m_low, dqkv, att0, (o_a, o_b), flags)
    aa0.send, ab0.send, far, gm0, part = bar_parts([ab1], False, aa0.send, ab0.send, far, gm0, part)
    last3 = combine([aa1, ab1], flags, merged=True)
    far, gm0, part = bar_parts([aa0, ab0, last3], True, far, gm0, part)
    go(aa0, ab0, last3)
    sums = (sums0, sums0b, sums1, sumg1, sumh0, sumh1, qvs0, qvs1)
    near, far_send, pk, pk_send = norm_bwd(0, n_dp, quarter, gm0, part, far, x0, gain, hot, sums)
    near, far_send, pk, pk_send = bar_parts([fc0, pj0], False, near, far_send, pk, pk_send)
    pk_got = y_swap(pk_send)
    fc0, pj0 = combine([fc0, pj0], flags)
    pk_got, pk, far_send = bar_parts([fc0, pj0], True, pk_got, pk, far_send)
    go(fc0, pj0)
    g_far = y_swap(far_send)
    rows = positions_table.shape[0] // n_dp
    pk = expand(pk, pk_got, [0, 1] + bits, n_dp, rows, flags)
    (pk.send,) = bar_parts([aa0, ab0], False, pk.send)
    aa0, ab0 = combine([aa0, ab0], flags)
    aa0.send, ab0.send, pk.send, out_send, out_near = bar_parts(
        [fc0, pj0, last3], False, aa0.send, ab0.send, pk.send, out_send, out_near
    )
    go(aa0, ab0, pk)
    last0 = combine([fc0, pj0], flags, merged=True)
    last0.send, g_far, near = bar_parts([aa0, ab0, pk], False, last0.send, g_far, near)
    go(last0)
    aa0, ab0, pk = combine([aa0, ab0, pk], flags)
    out_send, out_near = bar_parts([aa0, ab0, pk], True, out_send, out_near)
    go(aa0, ab0, pk)
    g_far = g_far.astype(F32)
    grad_tokens = jnp.concatenate([pick(at.y, near, g_far), pick(at.y, g_far, near)], axis=0)
    out_send, out_near = bar_parts([aa0, ab0, pk], False, out_send, out_near)
    last2 = combine([aa0, ab0], flags, merged=True)
    (pk,) = combine([pk], flags)
    out_send, out_near, grad_tokens = bar_parts([last2, pk], True, out_send, out_near, grad_tokens)
    out_far = y_swap(out_send)
    go(last2, pk)
    out = jnp.concatenate([pick(at.y, out_near, out_far), pick(at.y, out_far, out_near)], axis=0)
    lasts = [last1, last0, last3, last2, pk]
    while len(lasts[0].order) > 1:
        lasts = combine(lasts, flags)
        go(*lasts)
    g_fc, g_pj, g_qkv, g_wo, g_pos, g_gain, g_shift, g_bias, g_fcb, g_qvb = final(
        lasts, f, share, rows, n_dp
    )
    return (
        out,
        grad_tokens,
        g_pos.T,
        g_gain,
        g_shift,
        g_qkv.transpose(0, 2, 1, 3),
        g_qvb,
        g_wo,
        g_bias,
        g_fc,
        g_fcb,
        g_pj.transpose(0, 2, 1),
    )


def solution(mesh):
    n_dp = mesh.shape["dp"]
    in_specs = (
        P("dp", "mp"),
        P("dp", None),
        P(),
        P(),
        P(),
        P(None, None, None, "mp"),
        P(None, None, "mp"),
        P(None, "mp", None),
        P(),
        P(None, None, "mp"),
        P(None, "mp"),
        P(None, "mp", None),
        P("dp", "mp"),
    )
    out_specs = (
        P("dp", "mp"),
        P("dp", "mp"),
        P("dp", "mp"),
        P(None, None, "dp"),
        P(None, None, "dp"),
        P(None, "dp", None, "mp"),
        P(None, None, ("mp", "dp")),
        P(None, "mp", "dp"),
        P(None, None, "dp"),
        P(None, "dp", "mp"),
        P(None, ("mp", "dp")),
        P(None, "mp", "dp"),
    )
    return jax.shard_map(
        functools.partial(on_device, n_dp),
        mesh=mesh,
        in_specs=in_specs,
        out_specs=out_specs,
        check_vma=False,
    )
```

```python
import functools
import math

import jax
import jax.numpy as jnp
from jax import lax
from jax.experimental import pallas as pl
from jax.experimental.pallas import tpu as pltpu
from jax.sharding import PartitionSpec as P

HD = 64
LEN = 1024
DOC_MOST = 384
EPS = 1e-05
BT = 256
QB = 128
KW = QB + DOC_MOST
F32 = jnp.float32
BF16 = jnp.bfloat16
GELU_C = math.sqrt(2.0 / math.pi)


ANY = pl.BlockSpec(memory_space=pl.ANY)
SMEM = pl.BlockSpec(memory_space=pltpu.SMEM)


def cost(us):
    return pl.CostEstimate(flops=int(us * 1.15e9), transcendentals=0, bytes_accessed=0)


def full_spec(shape):
    return pl.BlockSpec(shape, lambda g: (0,) * len(shape))


def rows_spec(width):
    return pl.BlockSpec((BT, width), lambda g: (g, 0))


def dot(a, b, ca=1, cb=0):
    return lax.dot_general(a, b, (((ca,), (cb,)), ((), ())), preferred_element_type=F32)


def normed_parts(v):
    centred = v - jnp.mean(v, axis=-1, keepdims=True)
    variance = jnp.mean(centred * centred, axis=-1, keepdims=True)
    rstd = lax.rsqrt(variance + EPS)
    return centred * rstd, rstd


def norm_back(g, own, oth, v, gain):
    grad = own.astype(F32) + oth.astype(F32)
    xhat, rstd = normed_parts(v)
    gn = grad * gain
    out = g + rstd * (
        gn
        - jnp.mean(gn, axis=-1, keepdims=True)
        - xhat * jnp.mean(gn * xhat, axis=-1, keepdims=True)
    )
    return out, grad * xhat, grad


def colsum(v):
    return jnp.sum(v, axis=0, keepdims=True)


def head_pair(block):
    lane = lax.broadcasted_iota(jnp.int32, block.shape, 1)
    zero = jnp.zeros_like(block)
    return jnp.concatenate(
        [jnp.where(lane < HD, block, zero), jnp.where(lane < HD, zero, block)], axis=0
    )


def window_bias(start_ref, i, ks):
    kidx = lax.broadcasted_iota(jnp.int32, (KW, QB), 0) + ks
    qidx = lax.broadcasted_iota(jnp.int32, (KW, QB), 1) + i * QB
    first = start_ref[0:1, pl.ds(pl.multiple_of(i * QB, QB), QB)]
    bias = jnp.where((kidx >= first) & (kidx <= qidx), 0.0, -1e30).astype(F32)
    return jnp.concatenate([bias, bias], axis=1)


def copies(pairs, sems):
    out = [pltpu.make_async_copy(a, b, sems.at[j]) for j, (a, b) in enumerate(pairs)]
    for c in out:
        c.start()
    return out


def join_pieces(flag, plan, refs, dst, cols=slice(None)):
    r = dst.shape[0] // 2
    out = []
    for (lo, n, other, off), ref in zip(plan, refs):
        row = (1 - flag if other else flag) * r + off
        out.append((ref.at[pl.ds(lo, n)], dst.at[pl.ds(pl.multiple_of(row, 8), n), cols]))
    return out


def join_quarters(place, pieces, dst):
    w = pieces[0].shape[1]

    def put(q):
        for k, piece in enumerate(pieces):
            lo = w * (q ^ k)
            dst[:, lo : lo + w] = piece[...]

    for q in range(4):
        pl.when(place[0] == q)(functools.partial(put, q))


def gelu_parts(v):
    v2 = v * v
    t = jnp.tanh(GELU_C * v * (1.0 + 0.044715 * v2))
    cdf = 0.5 * (1.0 + t)
    slope = cdf + (0.5 * GELU_C) * v * (1.0 - t * t) * (1.0 + (3 * 0.044715) * v2)
    return v * cdf, slope


def gained(xhat, gain, shift, layer, which):
    row = slice(which, which + 1)
    return (xhat * gain[layer, row, :].astype(F32) + shift[layer, row, :].astype(F32)).astype(BF16)


def attn_fwd_kernel(layer, first, half, plan, *refs):
    if first:
        pieces, (emb, place, flag, start, gain, shift, qvb, a_own) = refs[:4], refs[4:12]
        rest, tok = refs[12:-1], refs[-1]
        join_quarters(place, pieces, tok)
        x = tok[...].astype(F32) + emb[...].astype(F32)
    else:
        (mid, own, oth, outb, flag, start, gain, shift, qvb, a_own) = refs[:10]
        rest = refs[10:]
        x = (
            mid[...]
            + (own[...].astype(F32) + oth[...].astype(F32))
            + outb[layer - 1, 1:2, :].astype(F32)
        )
    a_refs, rest = rest[: len(plan)], rest[len(plan) :]
    x_o, n_o, qkv_h, att_o, lse_o, part_o, w_h, v_t, o_t, a_buf, sems = rest[:11]
    qkv_o, w_o, osems = rest[11:]
    nb = LEN // BT

    def out_rows(b):
        at = pl.ds(pl.multiple_of(b * BT, BT), BT)
        return pltpu.make_async_copy(qkv_o.at[at], qkv_h.at[at], osems.at[b])

    out_w = pltpu.make_async_copy(w_o, w_h, osems.at[nb])
    g = pl.program_id(0)
    sh = half // 2

    @pl.when(g == 0)
    def _():
        moves = copies(
            [(a_own, a_buf.at[0])] + join_pieces(flag[0], plan, a_refs, a_buf.at[1]), sems
        )
        qkv_o[pl.ds(BT, KW - BT), half : 2 * half] = jnp.zeros((KW - BT, half), BF16)
        v_t[:, pl.ds(BT, KW - BT)] = jnp.zeros((half, KW - BT), BF16)
        lse_o[...] = jnp.zeros_like(lse_o)
        for m in moves:
            m.wait()
        for j in range(4):
            for s in range(2):
                w_o[:, (2 * j + s) * sh : (2 * j + s + 1) * sh] = a_buf[s, :, j * sh : (j + 1) * sh]
        out_w.start()

    x_o[...] = x
    xhat, _ = normed_parts(x)
    normed = gained(xhat, gain, shift, layer, 0)
    n_o[...] = normed
    qkv = dot(normed, w_o[:, : 3 * half])
    q = (qkv[:, :half] + qvb[layer, 0:1, :].astype(F32)).astype(BF16)
    k = qkv[:, half : 2 * half].astype(BF16)
    v = qkv[:, 2 * half :] + qvb[layer, 1:2, :].astype(F32)
    rows = pl.ds(pl.multiple_of(g * BT, BT), BT)
    qkv_o[rows, :half] = q
    qkv_o[rows, half : 2 * half] = k
    qkv_o[rows, 2 * half :] = v.astype(BF16)
    out_rows(g).start()
    v_t[:, rows] = jnp.transpose(v).astype(BF16)
    q = q * jnp.asarray(1.0 / math.sqrt(HD), BF16)
    for s in range(BT // QB):
        i = g * (BT // QB) + s
        ks = pl.multiple_of(jnp.maximum(i - DOC_MOST // QB, 0) * QB, QB)
        bias = window_bias(start, i, ks)
        cols = pl.ds(pl.multiple_of(i * QB, QB), QB)
        for p in range(half // 128):
            lo = 128 * p
            qq = head_pair(q[QB * s : QB * (s + 1), lo : lo + 128])
            kp = qkv_o[pl.ds(ks, KW), half + lo : half + lo + 128]
            scores = dot(kp, qq, 1, 1) + bias
            peak = jnp.max(scores, axis=0, keepdims=True)
            e = jnp.exp(scores - peak)
            total = jnp.sum(e, axis=0, keepdims=True)
            ot = dot(v_t[lo : lo + 128, pl.ds(ks, KW)], e.astype(BF16))
            inv = 1.0 / total
            o_t[lo : lo + HD, :] = ot[:HD, :QB] * inv[:, :QB]
            o_t[lo + HD : lo + 128, :] = ot[HD:, QB:] * inv[:, QB:]
            lse = peak + jnp.log(total)
            lse_o[2 * p : 2 * p + 1, cols] = lse[:, :QB]
            lse_o[2 * p + 1 : 2 * p + 2, cols] = lse[:, QB:]
        att_o[QB * s : QB * (s + 1), :] = jnp.transpose(o_t[...]).astype(BF16)
    part_o[...] = dot(att_o[...], w_o[:, 3 * half :], 1, 1).astype(BF16)

    @pl.when(g == nb - 1)
    def _():
        for b in range(nb):
            out_rows(b).wait()
        out_w.wait()


def attn_fwd(layer, stream_in, outb, flag, start, gain, shift, qvb, a_own, a_oth):
    first = layer == 0
    d = gain.shape[-1]
    half = a_own.shape[1] // 2
    ins = list(stream_in)
    specs = [SMEM if a.ndim == 1 else rows_spec(a.shape[1]) for a in ins]
    if not first:
        ins.append(outb)
        specs.append(full_spec(outb.shape))
    plan, arrays = a_oth
    ins += [flag, start, gain, shift, qvb, a_own, *arrays]
    specs += [SMEM] + [full_spec(a.shape) for a in (start, gain, shift, qvb)]
    specs += [ANY] * (1 + len(arrays))
    return pl.pallas_call(
        functools.partial(attn_fwd_kernel, layer, first, half, plan),
        grid=(LEN // BT,),
        in_specs=specs,
        out_specs=[
            rows_spec(d),
            rows_spec(d),
            ANY,
            rows_spec(half),
            full_spec((8, LEN)),
            rows_spec(d),
            ANY,
        ],
        out_shape=[
            jax.ShapeDtypeStruct((LEN, d), F32),
            jax.ShapeDtypeStruct((LEN, d), BF16),
            jax.ShapeDtypeStruct((LEN, 3 * half), BF16),
            jax.ShapeDtypeStruct((LEN, half), BF16),
            jax.ShapeDtypeStruct((8, LEN), F32),
            jax.ShapeDtypeStruct((LEN, d), BF16),
            jax.ShapeDtypeStruct((d, 4 * half), BF16),
        ],
        scratch_shapes=[
            pltpu.VMEM((half, LEN), BF16),
            pltpu.VMEM((half, QB), F32),
            pltpu.VMEM((2, d, 2 * half), BF16),
            pltpu.SemaphoreType.DMA((1 + len(plan),)),
            pltpu.VMEM((LEN, 3 * half), BF16),
            pltpu.VMEM((d, 4 * half), BF16),
            pltpu.SemaphoreType.DMA((LEN // BT + 1,)),
        ]
        + ([pltpu.VMEM((BT, d), BF16)] if first else []),
        name=f"attn_fwd_{layer}",
        cost_estimate=cost(22),
    )(*ins)


def load_mlp(layer, flag, plans, weights, wfc, wproj, sems):
    d = wfc.shape[0]
    f = wfc.shape[1] // 2
    n = len(plans[0])
    return copies(
        [(weights[0].at[layer], wfc.at[:, pl.ds(0, f)])]
        + join_pieces(flag[0], plans[0], weights[2 : 2 + n], wfc, pl.ds(f, f))
        + [(weights[1].at[layer], wproj.at[pl.ds(0, f)])]
        + join_pieces(flag[0], plans[1], weights[2 + n :], wproj.at[pl.ds(f, f)]),
        sems,
    )


def mlp_scratch(d, f2, plans):
    return [
        pltpu.VMEM((d, f2), BF16),
        pltpu.VMEM((f2, d), BF16),
        pltpu.SemaphoreType.DMA((2 + len(plans[0]) + len(plans[1]),)),
    ]


def mlp_weights(weights):
    w_fc, fc_oth, w_proj, pj_oth = weights
    return (fc_oth[0], pj_oth[0]), [w_fc, w_proj, *fc_oth[1], *pj_oth[1]]


def mlp_fwd_kernel(layer, plans, x, own, oth, outb, gain, shift, fcb, flag, *refs):
    nw = 2 + len(plans[0]) + len(plans[1])
    weights = refs[:nw]
    mid_o, n_o, h_o, part_o, wfc, wproj, sems = refs[nw:]

    @pl.when(pl.program_id(0) == 0)
    def _():
        for m in load_mlp(layer, flag, plans, weights, wfc, wproj, sems):
            m.wait()

    mid = (
        x[...]
        + (own[...].astype(F32) + oth[...].astype(F32))
        + outb[layer, 0:1, :].astype(F32)
    )
    mid_o[...] = mid
    xhat, _ = normed_parts(mid)
    normed = gained(xhat, gain, shift, layer, 1)
    n_o[...] = normed
    hidden = dot(normed, wfc[...]) + fcb[layer : layer + 1, :].astype(F32)
    h_o[...] = hidden.astype(BF16)
    t = jnp.tanh(GELU_C * hidden * (1.0 + 0.044715 * hidden * hidden))
    act = (0.5 * hidden * (1.0 + t)).astype(BF16)
    part_o[...] = dot(act, wproj[...]).astype(BF16)


def mlp_fwd(layer, x, own, oth, outb, gain, shift, fcb, flag, weights):
    d = x.shape[1]
    f = fcb.shape[1]
    plans, arrays = mlp_weights(weights)
    ins = [x, own, oth, outb, gain, shift, fcb, flag, *arrays]
    specs = [rows_spec(d)] * 3 + [full_spec(a.shape) for a in ins[3:7]] + [SMEM] + [ANY] * len(arrays)
    return pl.pallas_call(
        functools.partial(mlp_fwd_kernel, layer, plans),
        grid=(LEN // BT,),
        in_specs=specs,
        out_specs=[rows_spec(d), rows_spec(d), rows_spec(f), rows_spec(d)],
        out_shape=[
            jax.ShapeDtypeStruct((LEN, d), F32),
            jax.ShapeDtypeStruct((LEN, d), BF16),
            jax.ShapeDtypeStruct((LEN, f), BF16),
            jax.ShapeDtypeStruct((LEN, d), BF16),
        ],
        scratch_shapes=mlp_scratch(d, f, plans),
        name=f"mlp_fwd_{layer}",
        cost_estimate=cost(12),
    )(*ins)


def mlp_both_kernel(
    layer, plans, x, own, oth, c0, c1, c2, c3, place, outb, gain, shift, fcb, flag, *refs
):
    nw = 2 + len(plans[0]) + len(plans[1])
    weights = refs[:nw]
    mid_o, n_o, act_o, gh_o, out_o, part_o, cot, sumg_o, sumh_o, wfc, wproj, sems = refs[nw:]
    join_quarters(place, (c0, c1, c2, c3), cot)

    @pl.when(pl.program_id(0) == 0)
    def _():
        moves = load_mlp(layer, flag, plans, weights, wfc, wproj, sems)
        sumg_o[...] = jnp.zeros_like(sumg_o)
        sumh_o[...] = jnp.zeros_like(sumh_o)
        for m in moves:
            m.wait()

    mid = (
        x[...]
        + (own[...].astype(F32) + oth[...].astype(F32))
        + outb[layer, 0:1, :].astype(F32)
    )
    mid_o[...] = mid
    xhat, _ = normed_parts(mid)
    normed = gained(xhat, gain, shift, layer, 1)
    n_o[...] = normed
    grad_act = dot(cot[...], wproj[...], 1, 1)
    value, slope = gelu_parts(dot(normed, wfc[...]) + fcb[layer : layer + 1, :].astype(F32))
    act = value.astype(BF16)
    act_o[...] = act
    gh = (grad_act * slope).astype(BF16)
    gh_o[...] = gh
    part_o[...] = dot(gh, wfc[...], 1, 1).astype(BF16)
    out_o[...] = dot(act, wproj[...]).astype(BF16)
    sumg_o[0:1, :] += colsum(cot[...].astype(F32))
    sumh_o[0:1, :] += colsum(gh.astype(F32))


def mlp_both(layer, x, own, oth, cot, outb, gain, shift, fcb, flag, weights):
    d = x.shape[1]
    f = fcb.shape[1]
    plans, arrays = mlp_weights(weights)
    ins = [x, own, oth, *cot, outb, gain, shift, fcb, flag, *arrays]
    specs = [rows_spec(d)] * 3 + [rows_spec(d // 4)] * 4 + [SMEM]
    specs += [full_spec(a.shape) for a in ins[8:12]] + [SMEM] + [ANY] * len(arrays)
    widths = [d, d, f, f, d, d, d]
    kinds = [F32, BF16, BF16, BF16, BF16, BF16, BF16]
    return pl.pallas_call(
        functools.partial(mlp_both_kernel, layer, plans),
        grid=(LEN // BT,),
        in_specs=specs,
        out_specs=[rows_spec(w) for w in widths] + [full_spec((8, d)), full_spec((8, f))],
        out_shape=[jax.ShapeDtypeStruct((LEN, w), k) for w, k in zip(widths, kinds)]
        + [jax.ShapeDtypeStruct((8, d), F32), jax.ShapeDtypeStruct((8, f), F32)],
        scratch_shapes=mlp_scratch(d, f, plans),
        name=f"mlp_both_{layer}",
        cost_estimate=cost(18),
    )(*ins)


def mlp_bwd_kernel(layer, plans, gm, own, oth, x, h, gain, flag, *refs):
    nw = 2 + len(plans[0]) + len(plans[1])
    weights = refs[:nw]
    g_o, low_o, act_o, gh_o, part_o, sums_o, sumh_o, wfc, wproj, sems = refs[nw:]

    @pl.when(pl.program_id(0) == 0)
    def _():
        moves = load_mlp(layer, flag, plans, weights, wfc, wproj, sems)
        sums_o[...] = jnp.zeros_like(sums_o)
        sumh_o[...] = jnp.zeros_like(sumh_o)
        for m in moves:
            m.wait()

    grad, g_gain, g_shift = norm_back(
        gm[...], own[...], oth[...], x[...], gain[layer + 1, 0:1, :].astype(F32)
    )
    sums_o[0:1, :] += colsum(g_gain)
    sums_o[1:2, :] += colsum(g_shift)
    sums_o[2:3, :] += colsum(grad)
    g_o[...] = grad
    low = grad.astype(BF16)
    low_o[...] = low
    grad_act = dot(low, wproj[...], 1, 1)
    value, slope = gelu_parts(h[...].astype(F32))
    act_o[...] = value.astype(BF16)
    gh = (grad_act * slope).astype(BF16)
    gh_o[...] = gh
    part_o[...] = dot(gh, wfc[...], 1, 1).astype(BF16)
    sumh_o[0:1, :] += colsum(gh.astype(F32))


def mlp_bwd(layer, gm, own, oth, x, h, gain, flag, weights):
    d = x.shape[1]
    f = h.shape[1]
    plans, arrays = mlp_weights(weights)
    ins = [gm, own, oth, x, h, gain, flag, *arrays]
    specs = [rows_spec(d)] * 4 + [rows_spec(f), full_spec(gain.shape), SMEM] + [ANY] * len(arrays)
    widths = [d, d, f, f, d]
    kinds = [F32, BF16, BF16, BF16, BF16]
    return pl.pallas_call(
        functools.partial(mlp_bwd_kernel, layer, plans),
        grid=(LEN // BT,),
        in_specs=specs,
        out_specs=[rows_spec(w) for w in widths] + [full_spec((8, d)), full_spec((8, f))],
        out_shape=[jax.ShapeDtypeStruct((LEN, w), k) for w, k in zip(widths, kinds)]
        + [jax.ShapeDtypeStruct((8, d), F32), jax.ShapeDtypeStruct((8, f), F32)],
        scratch_shapes=mlp_scratch(d, f, plans),
        name=f"mlp_bwd_{layer}",
        cost_estimate=cost(16),
    )(*ins)


def stage(buf, value, order):
    dims = [o for o in order if o != "y"]
    n = len(dims)
    r = value.shape[0] >> n
    for c in range(1 << n):
        pos = sum(((c >> b) & 1) << (n - 1 - j) for j, b in enumerate(dims))
        buf[r * pos : r * (pos + 1), :] = value[r * c : r * (c + 1)].astype(BF16)


def ship(buf, keep, send, slot, order, flags, sems):
    if order[0] == "y":
        pairs = [(buf, send if slot else keep)]
    else:
        half = buf.shape[0] // 2
        f = flags[order[0]]
        lo = [pl.multiple_of(h * half, 16) for h in (f, 1 - f)]
        pairs = [
            (buf.at[pl.ds(lo[0], half)], keep.at[slot]),
            (buf.at[pl.ds(lo[1], half)], send.at[slot]),
        ]
    return [pltpu.make_async_copy(a, b, sems.at[j]) for j, (a, b) in enumerate(pairs)]


def first_shape(order, d, w):
    return (d, w) if order[0] == "y" else (2, d // 2, w)


def dw_mlp_kernel(orders, flags, n, low, gh, act, *refs):
    outs, (bufs, sems) = refs[:4], refs[4:]
    j = pl.program_id(0)

    def moves(t, slot):
        keep, send = outs[2 * t : 2 * t + 2]
        return ship(bufs.at[t, slot], keep, send, slot, orders[t], flags, sems.at[t, slot])

    for t, (a, b) in enumerate(((n, gh), (low, act))):
        stage(bufs.at[t, j], dot(a[...], b[...], 0, 0), orders[t])
        for slot in range(2):

            @pl.when(j == slot)
            def _():
                for m in moves(t, slot):
                    m.start()

    @pl.when(j == 1)
    def _():
        for t in range(2):
            for slot in range(2):
                for m in moves(t, slot):
                    m.wait()


def dw_mlp(layer, n, low, gh, act, orders, flags):
    t, d = n.shape
    f = gh.shape[1] // 2
    col = pl.BlockSpec((t, f), lambda j: (0, j))
    shapes = [first_shape(o, d, f) for o in orders for _ in range(2)]
    k0, s0, k1, s1 = pl.pallas_call(
        functools.partial(dw_mlp_kernel, orders),
        grid=(2,),
        in_specs=[SMEM, full_spec(n.shape), full_spec(low.shape), col, col],
        out_specs=[ANY] * 4,
        out_shape=[jax.ShapeDtypeStruct(s, BF16) for s in shapes],
        scratch_shapes=[pltpu.VMEM((2, 2, d, f), BF16), pltpu.SemaphoreType.DMA((2, 2, 2))],
        name=f"dw_mlp_{layer}",
        cost_estimate=cost(9),
    )(flags, n, low, gh, act)
    return Part(k0, s0, orders[0]), Part(k1, s1, orders[1])


def dw_attn_kernel(orders, flags, n, low, dqkv, att, *refs):
    outs, (bufs, sems) = refs[:4], refs[4:]
    sh = att.shape[1] // 2
    moves = []

    def send_off(t, values):
        for slot in range(2):
            both = jnp.concatenate(
                [v[:, (2 * j + slot) * sh : (2 * j + slot + 1) * sh] for v, j in values], axis=1
            )
            stage(bufs.at[t, slot], both, orders[t])
            keep, send = outs[2 * t : 2 * t + 2]
            for m in ship(
                bufs.at[t, slot], keep, send, slot, orders[t], flags, sems.at[t, slot]
            ):
                m.start()
                moves.append(m)

    half = 2 * sh
    qk = dot(n[...], dqkv[:, : 2 * half], 0, 0)
    send_off(0, [(qk, 0), (qk, 1)])
    v = dot(n[...], dqkv[:, 2 * half :], 0, 0)
    wo = dot(low[...], att[...], 0, 0)
    send_off(1, [(v, 0), (wo, 0)])
    for m in moves:
        m.wait()


def dw_attn(layer, n, low, dqkv, att, orders, flags):
    d = n.shape[1]
    w = att.shape[1]
    ins = (n, low, dqkv, att)
    shapes = [first_shape(o, d, w) for o in orders for _ in range(2)]
    k0, s0, k1, s1 = pl.pallas_call(
        functools.partial(dw_attn_kernel, orders),
        grid=(1,),
        in_specs=[SMEM] + [full_spec(a.shape) for a in ins],
        out_specs=[ANY] * 4,
        out_shape=[jax.ShapeDtypeStruct(s, BF16) for s in shapes],
        scratch_shapes=[pltpu.VMEM((2, 2, d, w), BF16), pltpu.SemaphoreType.DMA((2, 2, 2))],
        name=f"dw_attn_{layer}",
        cost_estimate=cost(7),
    )(flags, *ins)
    return Part(k0, s0, orders[0]), Part(k1, s1, orders[1])


def combine_kernel(steps, merged, flags, *refs):
    ins, outs = refs[: 2 * len(steps)], refs[2 * len(steps) :]
    lo = 0
    for k, o in enumerate(steps):
        keep, got = ins[2 * k : 2 * k + 2]

        def total(at):
            return keep[at].astype(F32) + got[at].astype(F32)

        if o is None:
            outs[k][...] = total(...)
            continue
        dst = outs if merged else outs[2 * k : 2 * k + 2]
        cols = slice(lo, lo + keep.shape[-1]) if merged else slice(None)
        if o == "y":
            halves = [total(0), total(1)]
        else:
            r = keep.shape[-2] // 2
            lead = (slice(None),) * (len(keep.shape) - 2)
            rows = [pl.ds(pl.multiple_of(h * r, 8), r) for h in (flags[o], 1 - flags[o])]
            halves = [total(lead + (row, slice(None))) for row in rows]
        for out, v in zip(dst, halves):
            out[..., cols] = v.astype(BF16)
        if merged:
            lo += keep.shape[-1]


def combine(parts, flags, merged=False):
    steps = [p.order[1] if len(p.order) > 1 else None for p in parts]
    wide = all(p.keep.shape[-1] % 384 == 0 for p in parts)
    ncol = 3 if wide and not merged and parts[0].keep.size >= 2**18 else 1

    def spec(shape):
        block = shape[:-1] + (shape[-1] // ncol,)
        return pl.BlockSpec(block, lambda g: (0,) * (len(shape) - 1) + (g,))

    ins, shapes = [], []
    for p, o in zip(parts, steps):
        ins += [p.keep, p.got]
        s = p.keep.shape
        if o is None:
            shapes.append(jax.ShapeDtypeStruct(s, F32))
        else:
            s = s[1:] if o == "y" else s[:-2] + (s[-2] // 2, s[-1])
            shapes += [jax.ShapeDtypeStruct(s, BF16)] * 2
    if merged:
        s = (shapes[0].shape[0], sum(p.keep.shape[-1] for p in parts))
        shapes = [jax.ShapeDtypeStruct(s, BF16)] * 2
    outs = pl.pallas_call(
        functools.partial(combine_kernel, steps, merged),
        grid=(ncol,),
        in_specs=[SMEM] + [spec(a.shape) for a in ins],
        out_specs=[spec(a.shape) for a in shapes],
        out_shape=shapes,
        name="combine",
        cost_estimate=cost(0.3),
    )(flags, *ins)
    if merged:
        return Part(outs[0], outs[1], parts[0].order[1:])
    if steps[0] is None:
        return list(outs)
    return [
        Part(outs[2 * k], outs[2 * k + 1], p.order[1:]) for k, p in enumerate(parts)
    ]


def final_kernel(f, share, *refs):
    (m1, m0, a1, a0, pk), outs = [refs[2 * k : 2 * k + 2] for k in range(5)], refs[10:]
    fc_o, pj_o, qkv_o, wo_o, pos_o, gain_o, shift_o, bias_o, fcb_o, qvb_o = outs

    def total(pair, lo, n):
        return pair[0][:, lo : lo + n].astype(F32) + pair[1][:, lo : lo + n].astype(F32)

    for l, (m, a) in enumerate(((m0, a0), (m1, a1))):
        fc_o[l] = total(m, 0, f)
        pj_o[l] = total(m, f, f)
        v = total(a, 0, 4 * share)
        for j in range(3):
            qkv_o[l, j] = v[:, share * j : share * (j + 1)]
        wo_o[l] = jnp.transpose(v[:, 3 * share :])
    v = total(pk, 0, share)
    rows = pos_o.shape[1]
    pos_o[...] = jnp.transpose(v[:rows])
    v = v[rows:]
    w = gain_o.shape[2]
    for l in range(2):
        for k, ref in enumerate((gain_o, shift_o, bias_o)):
            ref[l] = v[4 * k + 2 * l : 4 * k + 2 * l + 2, :w]
        qvb_o[l] = v[2 * l : 2 * l + 2, w : w + qvb_o.shape[2]]
    fcb_o[...] = v[12:14, :w]


def final(parts, f, share, rows, n_dp):
    r = parts[0].keep.shape[0]
    ins = [v for p in parts for v in (p.keep, p.got)]
    shapes = [(2, r, f), (2, r, f), (2, 3, r, share), (2, share, r), (share, rows)]
    shapes += [(2, 2, r)] * 3 + [(2, r), (2, 2, share // n_dp)]
    return pl.pallas_call(
        functools.partial(final_kernel, f, share),
        grid=(1,),
        in_specs=[full_spec(v.shape) for v in ins],
        out_specs=[full_spec(v) for v in shapes],
        out_shape=[jax.ShapeDtypeStruct(v, F32) for v in shapes],
        name="final",
        cost_estimate=cost(3),
    )(*ins)


class Part:
    def __init__(self, keep, send, order):
        self.keep, self.send, self.order = keep, send, list(order)

    def go(self, n_dp):
        o = self.order[0]
        self.got = y_swap(self.send) if o == "y" else dp_swap(self.send, o, n_dp)


def attn_bwd_kernel(layer, half, *refs):
    (g_i, own, oth, mid, qkv, att, lse, start, gain, w) = refs[:10]
    (gm_o, low_o, dqkv_h, part_h, sums_o, qvs_o, k_t, dk, dv, dq_t) = refs[10:20]
    dqkv_o, part_o, osems = refs[20:]
    g = pl.program_id(0)

    @pl.when(g == 0)
    def _():
        sums_o[...] = jnp.zeros_like(sums_o)
        qvs_o[...] = jnp.zeros_like(qvs_o)
        dk[...] = jnp.zeros_like(dk)
        dv[...] = jnp.zeros_like(dv)
        for b in range(LEN // BT):
            block = qkv[BT * b : BT * (b + 1), half : 2 * half].astype(F32)
            k_t[:, BT * b : BT * (b + 1)] = jnp.transpose(block).astype(BF16)

    gm, g_gain, g_shift = norm_back(
        g_i[...].astype(F32), own[...], oth[...], mid[...], gain[layer, 1:2, :].astype(F32)
    )
    gm_o[...] = gm
    sums_o[0:1, :] += colsum(g_gain)
    sums_o[1:2, :] += colsum(g_shift)
    sums_o[2:3, :] += colsum(gm)
    low = gm.astype(BF16)
    low_o[...] = low
    d_att = dot(low, w[:, 3 * half :]).astype(BF16)
    prod = d_att.astype(F32) * att[...].astype(F32)
    head = lax.broadcasted_iota(jnp.int32, (8, half), 1) // HD
    pick = (head == lax.broadcasted_iota(jnp.int32, (8, half), 0)).astype(F32)
    inner = lax.dot_general(
        pick,
        prod,
        (((1,), (1,)), ((), ())),
        preferred_element_type=F32,
        precision=lax.Precision.HIGHEST,
    )
    rows = pl.ds(pl.multiple_of(g * BT, BT), BT)
    q = qkv[rows, :half] * jnp.asarray(1.0 / math.sqrt(HD), BF16)
    for s in range(BT // QB):
        i = g * (BT // QB) + s
        ks = pl.multiple_of(jnp.maximum(i - DOC_MOST // QB, 0) * QB, QB)
        bias = window_bias(start, i, ks)
        cols = pl.ds(pl.multiple_of(i * QB, QB), QB)
        win = pl.ds(ks, KW)
        for p in range(half // 128):
            lo = 128 * p
            qq = head_pair(q[QB * s : QB * (s + 1), lo : lo + 128])
            oo = head_pair(d_att[QB * s : QB * (s + 1), lo : lo + 128])
            kp = qkv[win, half + lo : half + lo + 128]
            vp = qkv[win, 2 * half + lo : 2 * half + lo + 128]
            total = jnp.concatenate(
                [lse[2 * p : 2 * p + 1, cols], lse[2 * p + 1 : 2 * p + 2, cols]], axis=1
            )
            inn = jnp.concatenate(
                [
                    inner[2 * p : 2 * p + 1, QB * s : QB * (s + 1)],
                    inner[2 * p + 1 : 2 * p + 2, QB * s : QB * (s + 1)],
                ],
                axis=1,
            )
            probs = jnp.exp(dot(kp, qq, 1, 1) + bias - total)
            d_probs = dot(vp, oo, 1, 1)
            ds = (probs * (d_probs - inn)).astype(BF16)
            dv[win, lo : lo + 128] += dot(probs.astype(BF16), oo)
            dk[win, lo : lo + 128] += dot(ds, qq)
            dqt = dot(k_t[lo : lo + 128, win], ds)
            dq_t[lo : lo + HD, :] = dqt[:HD, :QB]
            dq_t[lo + HD : lo + 128, :] = dqt[HD:, QB:]
        dq = (jnp.transpose(dq_t[...]) * (1.0 / math.sqrt(HD))).astype(BF16)
        dqkv_o[cols, :half] = dq
        qvs_o[0:1, :] += colsum(dq.astype(F32))

    @pl.when(g == pl.num_programs(0) - 1)
    def _():
        moves = []
        total = jnp.zeros((1, half), F32)
        for b in range(LEN // BT):
            at = pl.ds(BT * b, BT)
            dqkv_o[at, half : 2 * half] = dk[at, :].astype(BF16)
            dvb = dv[at, :].astype(BF16)
            dqkv_o[at, 2 * half :] = dvb
            total += colsum(dvb.astype(F32))
            moves += copies([(dqkv_o.at[at], dqkv_h.at[at])], osems.at[b, 0:1])
            part_o[at, :] = dot(dqkv_o[at, :], w[:, : 3 * half], 1, 1).astype(BF16)
            moves += copies([(part_o.at[at], part_h.at[at])], osems.at[b, 1:2])
        qvs_o[1:2, :] = total
        for m in moves:
            m.wait()


def attn_bwd(layer, g, own, oth, mid, qkv, att, lse, start, gain, w):
    d = mid.shape[1]
    half = att.shape[1]
    ins = [g, own, oth, mid, qkv, att, lse, start, gain, w]
    specs = [rows_spec(d)] * 4 + [full_spec(qkv.shape), rows_spec(half)]
    specs += [full_spec(a.shape) for a in ins[6:]]
    return pl.pallas_call(
        functools.partial(attn_bwd_kernel, layer, half),
        grid=(LEN // BT,),
        in_specs=specs,
        out_specs=[
            rows_spec(d),
            rows_spec(d),
            ANY,
            ANY,
            full_spec((8, d)),
            full_spec((8, half)),
        ],
        out_shape=[
            jax.ShapeDtypeStruct((LEN, d), F32),
            jax.ShapeDtypeStruct((LEN, d), BF16),
            jax.ShapeDtypeStruct((LEN, 3 * half), BF16),
            jax.ShapeDtypeStruct((LEN, d), BF16),
            jax.ShapeDtypeStruct((8, d), F32),
            jax.ShapeDtypeStruct((8, half), F32),
        ],
        scratch_shapes=[
            pltpu.VMEM((half, LEN), BF16),
            pltpu.VMEM((LEN, half), F32),
            pltpu.VMEM((LEN, half), F32),
            pltpu.VMEM((half, QB), F32),
            pltpu.VMEM((LEN, 3 * half), BF16),
            pltpu.VMEM((LEN, d), BF16),
            pltpu.SemaphoreType.DMA((LEN // BT, 2)),
        ],
        name=f"attn_bwd_{layer}",
        cost_estimate=cost(24),
    )(*ins)


def norm_bwd_kernel(layer, n_dp, place, g, own, oth, x, gain, hot, *refs):
    sums, (near_o, far_o, own_o, oth_o, acc, table, small) = refs[:8], refs[8:]
    sums0, sums0b, sums1, sumg1, sumh0, sumh1, qvs0, qvs1 = sums
    w = near_o.shape[1]
    step = pl.program_id(0)

    @pl.when(step == 0)
    def _():
        acc[...] = jnp.zeros_like(acc)
        table[...] = jnp.zeros_like(table)
        small[...] = jnp.zeros_like(small)

    out, g_gain, g_shift = norm_back(
        g[...], own[...], oth[...], x[...], gain[layer, 0:1, :].astype(F32)
    )
    acc[0:1, :] += colsum(g_gain)
    acc[1:2, :] += colsum(g_shift)

    def select(q):
        far = q ^ 2
        near_o[...] = out[:, w * q : w * (q + 1)]
        far_o[...] = out[:, w * far : w * (far + 1)].astype(BF16)

    for q in range(4):
        pl.when(place[0] == q)(functools.partial(select, q))
    table[0] += dot(hot[...], near_o[...].astype(BF16), 0, 0)
    table[1] += dot(hot[...], far_o[...], 0, 0)

    @pl.when(step == pl.num_programs(0) - 1)
    def _():
        rows = [(acc, 0), (sums0, 0), (sums0b, 0), (sums1, 0)]
        rows += [(acc, 1), (sums0, 1), (sums0b, 1), (sums1, 1)]
        rows += [(sums0, 2), (sums0b, 2), (sums1, 2), (sumg1, 0)]
        cw, qw, f = acc.shape[1] // n_dp, w // n_dp, sumh0.shape[1] // 2
        for c in range(n_dp):
            for k, (ref, r) in enumerate(rows):
                v = ref[r : r + 1, cw * c : cw * (c + 1)]
                small[0, 16 * c + k : 16 * c + k + 1, 0:cw] = v
                small[1, 16 * c + k : 16 * c + k + 1, 0:cw] = v
            for slot in range(2):
                for k, ref in enumerate((sumh0, sumh1)):
                    lo = f * slot + cw * c
                    row = 16 * c + 12 + k
                    small[slot, row : row + 1, 0:cw] = ref[0:1, lo : lo + cw]
                for k, (ref, r) in enumerate(((qvs0, 0), (qvs0, 1), (qvs1, 0), (qvs1, 1))):
                    lo = w * slot + qw * c
                    row = 16 * c + k
                    small[slot, row : row + 1, cw : cw + qw] = ref[r : r + 1, lo : lo + qw]
        for slot, ref in enumerate((own_o, oth_o)):
            ref[:DOC_MOST, :] = table[slot].astype(BF16)
            ref[DOC_MOST:, :] = small[slot].astype(BF16)


def norm_bwd(layer, n_dp, place, g, own, oth, x, gain, hot, sums):
    d = x.shape[1]
    w = d // 4
    r = DOC_MOST + 16 * n_dp
    return pl.pallas_call(
        functools.partial(norm_bwd_kernel, layer, n_dp),
        grid=(LEN // BT,),
        in_specs=[SMEM]
        + [rows_spec(d)] * 4
        + [full_spec(gain.shape), rows_spec(DOC_MOST)]
        + [full_spec(v.shape) for v in sums],
        out_specs=[rows_spec(w), rows_spec(w), full_spec((r, w)), full_spec((r, w))],
        out_shape=[
            jax.ShapeDtypeStruct((LEN, w), F32),
            jax.ShapeDtypeStruct((LEN, w), BF16),
            jax.ShapeDtypeStruct((r, w), BF16),
            jax.ShapeDtypeStruct((r, w), BF16),
        ],
        scratch_shapes=[
            pltpu.VMEM((8, d), F32),
            pltpu.VMEM((2, DOC_MOST, w), F32),
            pltpu.VMEM((2, 16 * n_dp, w), F32),
        ],
        name=f"norm_bwd_{layer}",
        cost_estimate=cost(1),
    )(place, g, own, oth, x, gain, hot, *sums)


def expand_kernel(order, n_dp, rows, flags, own, got, keep, send):
    total = (own[...].astype(F32) + got[...].astype(F32)).astype(BF16)
    n = len(order)
    half = 1 << (n - 1)
    r = rows + 16

    def split(bit):
        for c in range(n_dp):
            pos = sum(((c >> b) & 1) << (n - 1 - j) for j, b in enumerate(order))
            out = keep if pos // half == bit else send
            row = r * (pos % half)
            if rows * c < DOC_MOST:
                out[row : row + rows, :] = total[rows * c : rows * (c + 1)]
            else:
                out[row : row + rows, :] = jnp.zeros((rows, total.shape[1]), BF16)
            lo = DOC_MOST + 16 * c
            out[row + rows : row + r, :] = total[lo : lo + 16]

    pl.when(flags[order[0]] == 0)(lambda: split(0))
    pl.when(flags[order[0]] == 1)(lambda: split(1))


def expand(own, got, order, n_dp, rows, flags):
    w = own.shape[1]
    shape = (n_dp * (rows + 16) // 2, w)
    keep, send = pl.pallas_call(
        functools.partial(expand_kernel, order, n_dp, rows),
        grid=(1,),
        in_specs=[SMEM, full_spec(own.shape), full_spec(own.shape)],
        out_specs=[full_spec(shape)] * 2,
        out_shape=[jax.ShapeDtypeStruct(shape, BF16)] * 2,
        name="expand",
        cost_estimate=cost(0.3),
    )(flags, own, got)
    return Part(keep, send, order)


def core_swap(a):
    return lax.ppermute(a, "mp", [(i, i ^ 1) for i in range(4)])


def y_swap(a):
    return lax.ppermute(a, "mp", [(i, i ^ 2) for i in range(4)])


def dp_swap(a, bit, n_dp):
    return lax.ppermute(a, "dp", [(i, i ^ (1 << bit)) for i in range(n_dp)])


def pick(flag, zero, one):
    return jnp.where(flag == 0, zero, one)


class Place:
    def __init__(self, n_dp):
        mp = lax.axis_index("mp")
        self.n_dp = n_dp
        self.bits = n_dp.bit_length() - 1
        self.y = mp // 2
        self.c = mp % 2
        self.dp = lax.axis_index("dp")

    def dp_bit(self, b):
        return (self.dp >> b) & 1


def row_pieces(a, at):
    rows = a.reshape(2, LEN, a.shape[1])
    return pick(at.y, rows[0], rows[1]), pick(at.y, rows[1], rows[0])


def own_cols(a, at, other):
    w = a.shape[1] // 4
    halves = (a[:, : 2 * w], a[:, 2 * w :])
    h = pick(at.y, halves[1], halves[0]) if other else pick(at.y, halves[0], halves[1])
    return pick(at.c, h[:, :w], h[:, w:])


def bar(*vals):
    return lax.optimization_barrier(vals)


def doc_starts(doc_ids):
    row_index = jnp.broadcast_to(jnp.arange(doc_ids.shape[1], dtype=jnp.int32), doc_ids.shape)
    previous = jnp.concatenate([doc_ids[:, :1] - 1, doc_ids[:, :-1]], axis=1)
    starts = jnp.where(doc_ids != previous, row_index, 0)
    return lax.cummax(starts, axis=1)


def on_device(
    n_dp,
    tokens,
    doc_ids,
    positions_table,
    norm_gain,
    norm_shift,
    joined_projection_weight,
    qv_bias,
    w_out,
    out_bias,
    w_fc,
    fc_bias,
    w_proj,
    cotangent,
):
    at = Place(n_dp)
    d = positions_table.shape[1]
    share = joined_projection_weight.shape[-1]
    f = w_fc.shape[-1]
    bits = list(range(2, at.bits))
    flags = jnp.stack([at.dp_bit(b) for b in range(at.bits)]).astype(jnp.int32)

    b = at.dp_bit(0) ^ at.dp_bit(1)
    flag = b.reshape(1)
    quarter = (2 * at.y + at.c).astype(jnp.int32).reshape(1)
    gain, shift = norm_gain, norm_shift

    a_own = [
        jnp.concatenate([joined_projection_weight[l].reshape(d, 3 * share), w_out[l].T], axis=1)
        for l in range(2)
    ]
    biases = jnp.concatenate([qv_bias.reshape(-1), fc_bias.reshape(-1)]).reshape(-1, d)
    biases = jnp.pad(biases, ((0, -biases.shape[0] % 8), (0, 0)))
    r = d // 2

    def half_rows(w):
        return lax.dynamic_slice_in_dim(w, b * r, r, 0)

    def x_swap(w):
        return dp_swap(w, 0, n_dp)

    def z_swap(w):
        return dp_swap(w, 1, n_dp)

    def by_two(one, lo=0):
        return x_swap(one[lo : lo + r // 2]), z_swap(one[lo + r // 2 : lo + r])

    def plan_one(lo=0):
        return ((lo, r, 0, 0), (0, r, 1, 0))

    def plan_two(lo=0):
        return ((lo, r, 0, 0), (0, r // 2, 1, 0), (0, r // 2, 1, r // 2))

    tok_mine, tok_theirs = row_pieces(tokens, at)
    tok_far = y_swap(tok_theirs)
    a_one0 = y_swap(jnp.concatenate([half_rows(a_own[0]), biases], axis=0))

    starts = doc_starts(doc_ids)
    start = pick(at.y, starts[0:1], starts[1:2])
    place = jnp.arange(LEN, dtype=jnp.int32) - start[0]
    hot = (place[:, None] == jnp.arange(DOC_MOST, dtype=jnp.int32)[None, :]).astype(BF16)
    fc_half, a_own[1] = bar(half_rows(w_fc[0]), a_own[1])
    fc_one0 = y_swap(fc_half)
    tok_far, a_one0, hot, a_own[1] = bar(tok_far, a_one0, hot, a_own[1])
    embedded = dot(hot, positions_table[:DOC_MOST]).astype(BF16)

    a_x, a_z = by_two(a_one0)
    tok = [tok_mine, core_swap(tok_mine), tok_far, core_swap(tok_far)]
    small = a_one0[r:].reshape(-1)
    nq = qv_bias.size
    qvb = jnp.concatenate([qv_bias, small[:nq].reshape(qv_bias.shape)], axis=-1)
    fcb = jnp.concatenate(
        [fc_bias, small[nq : nq + fc_bias.size].reshape(fc_bias.shape)], axis=-1
    )
    send_y = jnp.concatenate([half_rows(w_proj[0]), half_rows(a_own[1])], axis=0)
    a_x, a_z, fc_one0, send_y, embedded, *tok = bar(a_x, a_z, fc_one0, send_y, embedded, *tok)

    fc_two0 = x_swap(fc_one0)
    pj_a1 = y_swap(send_y)
    x0, n0, qkv0, att0, lse0, part, wa0 = attn_fwd(
        0,
        (*tok, embedded, quarter),
        out_bias,
        flag,
        start,
        gain,
        shift,
        qvb,
        a_own[0],
        (plan_two(), (a_one0, a_x, a_z)),
    )
    part, x0, fc_two0, pj_a1 = bar(part, x0, fc_two0, pj_a1)
    far = core_swap(part)
    pj_x, pj_z = by_two(pj_a1)
    far, pj_x, pj_z = bar(far, pj_x, pj_z)
    mlp0 = (
        w_fc,
        (plan_one(), (fc_one0, fc_two0)),
        w_proj,
        (plan_two(), (pj_a1, pj_x, pj_z)),
    )
    a_two1 = x_swap(pj_a1[r:])
    fc_one1 = y_swap(half_rows(w_fc[1]))
    mid0, nn0, hid0, part2 = mlp_fwd(
        0, x0, part, far, out_bias, gain, shift, fcb, flag, mlp0
    )
    part2, mid0, a_two1, fc_one1 = bar(part2, mid0, a_two1, fc_one1)
    far = core_swap(part2)
    (far,) = bar(far)
    fc_two1 = x_swap(fc_one1)
    pj_one1 = y_swap(half_rows(w_proj[1]))
    cot_mine, cot_theirs = row_pieces(cotangent, at)
    cot_far = y_swap(cot_theirs)
    x1, n1, qkv1, att1, lse1, part, wa1 = attn_fwd(
        1,
        (mid0, part2, far),
        out_bias,
        flag,
        start,
        gain,
        shift,
        qvb,
        a_own[1],
        (plan_one(r), (pj_a1, a_two1)),
    )
    part, x1, fc_two1, cot_far, pj_one1 = bar(part, x1, fc_two1, cot_far, pj_one1)
    far = core_swap(part)
    pj_x, pj_z = by_two(pj_one1)
    cot = [cot_mine, core_swap(cot_mine), cot_far, core_swap(cot_far)]
    far, pj_x, pj_z, *cot = bar(far, pj_x, pj_z, *cot)
    mlp1 = (
        w_fc,
        (plan_one(), (fc_one1, fc_two1)),
        w_proj,
        (plan_two(), (pj_one1, pj_x, pj_z)),
    )
    mid1, nn1, act, gh, part_out, part, cot, sumg1, sumh1 = mlp_both(
        1, x1, part, far, (*cot, quarter), out_bias, gain, shift, fcb, flag, mlp1
    )

    def go(*parts):
        for p in parts:
            p.go(n_dp)

    def bar_parts(parts, sent, *vals):
        name = "send" if sent else "got"
        out = bar(*[getattr(p, name) for p in parts], *vals)
        for p, v in zip(parts, out):
            setattr(p, name, v)
        return out[len(parts) :]

    part, part_out, mid1, gh, act = bar(part, part_out, mid1, gh, act)
    far = core_swap(part)
    far_out = core_swap(part_out)
    o_fc, o_pj = ["y", 1, 0] + bits, [0, "y", 1] + bits
    o_a, o_b = [0, 1, "y"] + bits, [1, "y", 0] + bits
    fc1, pj1 = dw_mlp(1, nn1, cot, gh, act, (o_fc, o_pj), flags)
    far, far_out, mid1, part_out = bar_parts([fc1, pj1], True, far, far_out, mid1, part_out)
    go(fc1, pj1)
    gm1, m_low, dqkv, part, sums1, qvs1 = attn_bwd(
        1, cot, part, far, mid1, qkv1, att1, lse1, start, gain, wa1
    )
    part, gm1, m_low, dqkv, far_out, part_out = bar_parts(
        [fc1, pj1], False, part, gm1, m_low, dqkv, far_out, part_out
    )
    far = core_swap(part)
    fc1, pj1 = combine([fc1, pj1], flags)
    result = (
        mid1 + (part_out.astype(F32) + far_out.astype(F32)) + out_bias[1, 1].astype(F32)
    ).astype(BF16)
    out_near, out_send = own_cols(result, at, False), own_cols(result, at, True)
    out_near, out_send, far, m_low = bar_parts([fc1, pj1], True, out_near, out_send, far, m_low)
    aa1, ab1 = dw_attn(1, n1, m_low, dqkv, att1, (o_a, ["y", 1, 0] + bits), flags)
    far, gm1 = bar_parts([aa1, ab1], True, far, gm1)
    go(fc1, pj1, aa1)
    g0, g_low, act, gh, part, sums0b, sumh0 = mlp_bwd(
        0, gm1, part, far, x1, hid0, gain, flag, mlp0
    )
    part, g0, g_low, act, gh = bar_parts([fc1, pj1, aa1], False, part, g0, g_low, act, gh)
    far = core_swap(part)
    fc1, pj1, aa1 = combine([fc1, pj1, aa1], flags)
    far, g_low, act, gh = bar_parts([fc1, pj1, aa1, ab1], True, far, g_low, act, gh)
    go(ab1, fc1, pj1, aa1)
    fc0, pj0 = dw_mlp(0, nn0, g_low, gh, act, (o_fc, o_pj), flags)
    far, fc0.send, pj0.send, g0 = bar_parts(
        [ab1, fc1, pj1, aa1], False, far, fc0.send, pj0.send, g0
    )
    last1 = combine([fc1, pj1], flags, merged=True)
    aa1, ab1 = combine([aa1, ab1], flags)
    far, g0, part = bar_parts([last1, aa1, ab1, fc0, pj0], True, far, g0, part)
    go(fc0, pj0, aa1, ab1, last1)
    gm0, m_low, dqkv, part, sums0, qvs0 = attn_bwd(
        0, g0, part, far, mid0, qkv0, att0, lse0, start, gain, wa0
    )
    part, gm0, m_low, dqkv = bar_parts(
        [fc0, pj0, aa1, ab1, last1], False, part, gm0, m_low, dqkv
    )
    far = core_swap(part)
    fc0, pj0 = combine([fc0, pj0], flags)
    (ab1,) = combine([ab1], flags)
    far, m_low, dqkv = bar_parts([fc0, pj0, ab1], True, far, m_low, dqkv)
    go(fc0, pj0, ab1)
    aa0, ab0 = dw_attn(0, n0, m_low, dqkv, att0, (o_a, o_b), flags)
    aa0.send, ab0.send, far, gm0, part = bar_parts([ab1], False, aa0.send, ab0.send, far, gm0, part)
    last3 = combine([aa1, ab1], flags, merged=True)
    far, gm0, part = bar_parts([aa0, ab0, last3], True, far, gm0, part)
    go(aa0, ab0, last3)
    sums = (sums0, sums0b, sums1, sumg1, sumh0, sumh1, qvs0, qvs1)
    near, far_send, pk, pk_send = norm_bwd(0, n_dp, quarter, gm0, part, far, x0, gain, hot, sums)
    near, far_send, pk, pk_send = bar_parts([fc0, pj0], False, near, far_send, pk, pk_send)
    pk_got = y_swap(pk_send)
    fc0, pj0 = combine([fc0, pj0], flags)
    pk_got, pk, far_send = bar_parts([fc0, pj0], True, pk_got, pk, far_send)
    go(fc0, pj0)
    g_far = y_swap(far_send)
    rows = positions_table.shape[0] // n_dp
    pk = expand(pk, pk_got, [0, 1] + bits, n_dp, rows, flags)
    (pk.send,) = bar_parts([aa0, ab0], False, pk.send)
    aa0, ab0 = combine([aa0, ab0], flags)
    aa0.send, ab0.send, pk.send, out_send, out_near = bar_parts(
        [fc0, pj0, last3], False, aa0.send, ab0.send, pk.send, out_send, out_near
    )
    go(aa0, ab0, pk)
    last0 = combine([fc0, pj0], flags, merged=True)
    last0.send, g_far, near = bar_parts([aa0, ab0, pk], False, last0.send, g_far, near)
    go(last0)
    aa0, ab0, pk = combine([aa0, ab0, pk], flags)
    out_send, out_near = bar_parts([aa0, ab0, pk], True, out_send, out_near)
    go(aa0, ab0, pk)
    g_far = g_far.astype(F32)
    grad_tokens = jnp.concatenate([pick(at.y, near, g_far), pick(at.y, g_far, near)], axis=0)
    out_send, out_near = bar_parts([aa0, ab0, pk], False, out_send, out_near)
    last2 = combine([aa0, ab0], flags, merged=True)
    (pk,) = combine([pk], flags)
    out_send, out_near, grad_tokens = bar_parts([last2, pk], True, out_send, out_near, grad_tokens)
    out_far = y_swap(out_send)
    go(last2, pk)
    out = jnp.concatenate([pick(at.y, out_near, out_far), pick(at.y, out_far, out_near)], axis=0)
    lasts = [last1, last0, last3, last2, pk]
    while len(lasts[0].order) > 1:
        lasts = combine(lasts, flags)
        go(*lasts)
    g_fc, g_pj, g_qkv, g_wo, g_pos, g_gain, g_shift, g_bias, g_fcb, g_qvb = final(
        lasts, f, share, rows, n_dp
    )
    return (
        out,
        grad_tokens,
        g_pos.T,
        g_gain,
        g_shift,
        g_qkv.transpose(0, 2, 1, 3),
        g_qvb,
        g_wo,
        g_bias,
        g_fc,
        g_fcb,
        g_pj.transpose(0, 2, 1),
    )


def solution(mesh):
    n_dp = mesh.shape["dp"]
    in_specs = (
        P("dp", "mp"),
        P("dp", None),
        P(),
        P(),
        P(),
        P(None, None, None, "mp"),
        P(None, None, "mp"),
        P(None, "mp", None),
        P(),
        P(None, None, "mp"),
        P(None, "mp"),
        P(None, "mp", None),
        P("dp", "mp"),
    )
    out_specs = (
        P("dp", "mp"),
        P("dp", "mp"),
        P("dp", "mp"),
        P(None, None, "dp"),
        P(None, None, "dp"),
        P(None, "dp", None, "mp"),
        P(None, None, ("mp", "dp")),
        P(None, "mp", "dp"),
        P(None, None, "dp"),
        P(None, "dp", "mp"),
        P(None, ("mp", "dp")),
        P(None, "mp", "dp"),
    )
    return jax.shard_map(
        functools.partial(on_device, n_dp),
        mesh=mesh,
        in_specs=in_specs,
        out_specs=out_specs,
        check_vma=False,
    )
```
